32 devices in a mesh: dp: 8 (over z, core), tensor: 4 (over y, x).
Axes of the slice: x: 2, y: 2, z: 4, core: 2. Of those that a mesh axis runs over, the one named last changes fastest.
Arguments:
- tokens_in: bfloat16 [3216, 4096], P('dp', 'tensor'), may hold values from -8 to 8
- ln1_gain: float32 [4096], replicated, may hold values from 0.5 to 1.5
- ln1_bias: float32 [4096], replicated, may hold values from -1.75 to 1.75
- w_qkv: bfloat16 [4096, 3, 4096], P(None, None, 'tensor'), may hold values from -6 to 6
- w_out: bfloat16 [4096, 4096], P('tensor'), may hold values from -0.375 to 0.375
- scale_attn: float32 [4096], replicated, may hold values from 0.3 to 3
- ln2_gain: float32 [4096], replicated, may hold values from 0.5 to 1.5
- ln2_bias: float32 [4096], replicated, may hold values from -1.75 to 1.75
- w_gu: bfloat16 [4096, 2, 8192], P(None, None, 'tensor'), may hold values from -0.09375 to 0.09375
- w_down: bfloat16 [8192, 4096], P('tensor'), may hold values from -0.0625 to 0.0625
- scale_mlp: float32 [4096], replicated, may hold values from 0.3 to 3
- out_cotangent: bfloat16 [3216, 4096], P('dp', 'tensor'), may hold values from -8 to 8
Outputs:
- layer_out: float32 [3216, 4096], P('dp', 'tensor')
- input_grad: float32 [3216, 4096], P('dp', 'tensor')
- ln1_gain_grad: float32 [4096], replicated
- ln1_bias_grad: float32 [4096], replicated
- qkv_grad: float32 [4096, 3, 4096], P('dp', None, 'tensor')
- proj_grad: float32 [4096, 4096], P('tensor', 'dp')
- scale_attn_grad: float32 [4096], replicated
- ln2_gain_grad: float32 [4096], replicated
- ln2_bias_grad: float32 [4096], replicated
- gu_grad: float32 [4096, 2, 8192], P('dp', None, 'tensor')
- down_grad: float32 [8192, 4096], P('tensor', 'dp')
- scale_mlp_grad: float32 [4096], replicated
The draws below stay inside these ranges and needn't reach their ends.
All inputs are finite; a program needn't handle non-finite values.
Results may differ from the reference program's by a relative error of at most 0.018.
Values may be sent and summed in bfloat16 or wider, within the bound.
A program may use at most 384 MiB of HBM per device.

```python
import math
import jax
import jax.numpy as jnp
from jax import lax

D = 4096
H = 32
HD = 128
FF = 8192
GRID = 14
EXTRA = 5
IMG_DEV = 2
PATCH = 196
SEQ = 201
IMAGES = 16
TOKENS = 3216


def draw_w_qkv(key, part):
    spread = D ** (-0.5)
    query_w = jax.random.truncated_normal(jax.random.fold_in(key, 21), -4.0, 4.0, (D, H, HD), jnp.float32) * spread
    keys_w = jax.random.truncated_normal(jax.random.fold_in(key, 22), -4.0, 4.0, (D, H, HD), jnp.float32) * spread
    values_w = jax.random.truncated_normal(jax.random.fold_in(key, 23), -4.0, 4.0, (D, H, HD), jnp.float32) * spread
    stacked = jnp.stack([query_w, keys_w, values_w], axis=1)
    return stacked.reshape(D, 3, H * HD).astype(jnp.bfloat16)


def with_spikes(values, own_key, source, target, blocks, factor):
    def block_of(dim):
        return (jnp.arange(values.shape[dim]) // (values.shape[dim] // blocks)).reshape((-1,) + (1,) * (values.ndim - 1 - dim))

    near = jax.random.permutation(own_key, blocks)[block_of(target)]
    second = (block_of(target) + blocks // 2) % blocks
    return jnp.where((block_of(source) == near) | (block_of(source) == second), factor * values, values)


def shard_levels(key, shape, shards, smallest, top_value):
    factor_of = 1.0
    for axis_at, parts in shards:
        draws = jax.random.uniform(jax.random.fold_in(jax.random.fold_in(key, 6), axis_at), (parts,), jnp.float32, smallest / len(shards), top_value / len(shards))
        factor_of = factor_of * jnp.repeat(jnp.exp(draws), shape[axis_at] // parts).reshape((-1,) + (1,) * (len(shape) - 1 - axis_at))
    return factor_of


def normal_values(own_key, shape, width, most, pieces=(), kind=jnp.bfloat16):
    values = jax.random.normal(own_key, shape, jnp.float32) * width
    if len(pieces) > 0:
        values = shard_levels(own_key, shape, pieces, -0.22, 0.18) * values
    return jnp.clip(values, min=-most, max=most).astype(kind)


def heavy_noise(rng, dims, scale, limit, pieces, heavy, held_as=jnp.bfloat16):
    drawn = scale * jax.random.normal(rng, dims, jnp.float32)
    if pieces:
        drawn = drawn * shard_levels(rng, dims, pieces, -0.22, 0.18)
    return jnp.clip(with_spikes(drawn, jax.random.fold_in(rng, 3), *heavy), -limit, limit).astype(held_as)


def setup_inputs(seed: int = 0) -> dict:
    arg_keys = jax.random.split(jax.random.key(seed), 13)
    return {
        "tokens_in": heavy_noise(arg_keys[0], (TOKENS, D), 1.0, 8.0, ((0, 8), (1, 4)), (0, 1, 8, 2.0)),
        "ln1_gain": jnp.clip(1.0 + 0.1 * jax.random.normal(arg_keys[1], (D,), jnp.float32), 0.5, 1.5),
        "ln1_bias": normal_values(arg_keys[2], (D,), 0.3, 1.75, (), jnp.float32),
        "w_qkv": draw_w_qkv(jax.random.fold_in(arg_keys[12], 71), 0),
        "w_out": normal_values(arg_keys[4], (H * HD, D), (D // 16) ** -0.5, 0.375, ((0, 4),)),
        "scale_attn": jnp.clip(jnp.exp(jax.random.uniform(arg_keys[5], (D,), jnp.float32, math.log(0.3), math.log(3.0))), 0.3, 3.0),
        "ln2_gain": jnp.clip(1.0 + 0.1 * jax.random.normal(arg_keys[6], (D,), jnp.float32), 0.5, 1.5),
        "ln2_bias": normal_values(arg_keys[7], (D,), 0.3, 1.75, (), jnp.float32),
        "w_gu": normal_values(arg_keys[8], (D, 2, FF), D ** -0.5, 0.09375, ((2, 4),)),
        "w_down": normal_values(arg_keys[9], (FF, D), FF ** -0.5, 0.0625, ((0, 4),)),
        "scale_mlp": jnp.clip(jnp.exp(jax.random.uniform(arg_keys[10], (D,), jnp.float32, math.log(0.3), math.log(3.0))), 0.3, 3.0),
        "out_cotangent": heavy_noise(arg_keys[11], (TOKENS, D), 1.0, 8.0, ((0, 8), (1, 4)), (0, 1, 8, 2.0)),
    }


EPS = 1e-06
HIGH = lax.Precision.HIGHEST

@jax.custom_vjp
def low(v):
    return lax.optimization_barrier(v.astype(jnp.bfloat16)).astype(jnp.float32)

@jax.custom_vjp
def low_back(v):
    return v

def low_keep(v):
    return (low(v), None)

def low_pass(kept, grad):
    return (grad,)

def back_keep(v):
    return (v, None)

def back_low(kept, grad):
    return (low(grad),)
low.defvjp(low_keep, low_pass)
low_back.defvjp(back_keep, back_low)

def rope_tables():
    quarter = HD // 4
    theta = 2.0 * math.pi * jnp.exp(jnp.arange(quarter, dtype=jnp.float32) * (-4.0 * math.log(100.0) / HD))
    places = jnp.arange(PATCH, dtype=jnp.int32)
    row_pos = ((places // GRID).astype(jnp.float32) + 0.5) * (2.0 / GRID) - 1.0
    col_pos = ((places % GRID).astype(jnp.float32) + 0.5) * (2.0 / GRID) - 1.0
    angles = jnp.concatenate([row_pos[:, None] * theta[None, :], col_pos[:, None] * theta[None, :]], axis=1)
    angles = jnp.concatenate([jnp.zeros((EXTRA, HD // 2), jnp.float32), angles], axis=0)
    return (jnp.cos(angles), jnp.sin(angles))

def rotate(vectors, cosines, sines):
    halfway = HD // 2
    leading = vectors[..., :halfway]
    trailing = vectors[..., halfway:]
    cos_b = cosines[:, None, :]
    sin_b = sines[:, None, :]
    return jnp.concatenate([leading * cos_b - trailing * sin_b, leading * sin_b + trailing * cos_b], axis=-1)

def layer_norm(values, gain_vec, bias_vec):
    center = values - lax.optimization_barrier(jnp.mean(values, axis=-1, keepdims=True))
    inverse = lax.rsqrt(lax.optimization_barrier(jnp.mean(center * center, axis=-1, keepdims=True)) + EPS)
    return center * inverse * gain_vec + bias_vec

def forward(rows_in, gain_one, bias_one, qkv_mat, out_mat, scale_one, gain_two, bias_two, gu_mat, down_mat, scale_two):
    row_count = rows_in.shape[0]
    image_count = row_count // SEQ
    act_one = low(layer_norm(rows_in, gain_one, bias_one))
    raw_all = jnp.dot(act_one, qkv_mat.reshape(D, 3 * H * HD), precision=HIGH)
    raw_all = low_back(raw_all).reshape(image_count, SEQ, 3, H, HD)
    cosines, sines = rope_tables()
    queries = low(rotate(raw_all[:, :, 0], cosines, sines))
    keys_rot = low(rotate(raw_all[:, :, 1], cosines, sines))
    values = low(raw_all[:, :, 2])
    scores = low_back(jnp.einsum('bqhd,bkhd->bhqk', queries, keys_rot, precision=HIGH) * HD ** (-0.5))
    attn_probs = jax.nn.softmax(scores, axis=-1)
    mixed_heads = jnp.einsum('bhqk,bkhd->bqhd', low(attn_probs), values, precision=HIGH)
    mixed_heads = low_back(low(mixed_heads)).reshape(row_count, H * HD)
    attn_sum = low_back(jnp.dot(mixed_heads, out_mat, precision=HIGH))
    residual = rows_in + scale_one * attn_sum
    act_two = low(layer_norm(residual, gain_two, bias_two))
    gate_up = low_back(jnp.dot(act_two, gu_mat.reshape(D, 2 * FF), precision=HIGH)).reshape(row_count, 2, FF)
    hidden = low(jax.nn.silu(gate_up[:, 0]) * gate_up[:, 1])
    branch = low_back(jnp.dot(hidden, down_mat, precision=HIGH))
    return residual + scale_two * branch

def reference(tokens_in, ln1_gain, ln1_bias, w_qkv, w_out, scale_attn, ln2_gain, ln2_bias, w_gu, w_down, scale_mlp, out_cotangent):
    params = tuple((item.astype(jnp.float32) for item in (ln1_gain, ln1_bias, w_qkv, w_out, scale_attn, ln2_gain, ln2_bias, w_gu, w_down, scale_mlp)))
    groups = IMAGES // IMG_DEV
    inputs = tokens_in.astype(jnp.float32).reshape(groups, IMG_DEV * SEQ, D)
    cotangents = out_cotangent.astype(jnp.float32).reshape(groups, IMG_DEV * SEQ, D)

    def one_group(totals, pair):
        rows_in, cot_rows = pair
        result, pullback = jax.vjp(forward, rows_in, *params)
        grads = pullback(cot_rows)
        totals = tuple((acc + grad_part for acc, grad_part in zip(totals, grads[1:])))
        return (totals, (result, grads[0]))
    zeros = tuple((jnp.zeros_like(item) for item in params))
    totals, (results, input_grads) = lax.scan(one_group, zeros, (inputs, cotangents))
    layer_out = results.reshape(TOKENS, D)
    input_grad = input_grads.reshape(TOKENS, D)
    return (layer_out, input_grad, totals[0], totals[1], totals[2], totals[3], totals[4], totals[5], totals[6], totals[7], totals[8], totals[9])
```

```python
import functools
import math

import jax
import jax.numpy as jnp
from jax import lax
from jax.experimental import pallas as pl
from jax.experimental.pallas import tpu as pltpu
from jax.sharding import PartitionSpec as P

D = 4096
HD = 128
GRID = 14
EXTRA = 5
PATCH = 196
SEQ = 201
EPS = 1e-06
LANE = 128
BF = jnp.bfloat16
F32 = jnp.float32
MESH = pl.DeviceIdType.MESH
ROWS = (((0,), (0,)), ((), ()))
COLS = (((1,), (1,)), ((), ()))


def rope_tables():
    quarter = HD // 4
    theta = (
        2.0
        * math.pi
        * jnp.exp(jnp.arange(quarter, dtype=jnp.float32) * (-4.0 * math.log(100.0) / HD))
    )
    places = jnp.arange(PATCH, dtype=jnp.int32)
    row_pos = ((places // GRID).astype(jnp.float32) + 0.5) * (2.0 / GRID) - 1.0
    col_pos = ((places % GRID).astype(jnp.float32) + 0.5) * (2.0 / GRID) - 1.0
    angles = jnp.concatenate(
        [row_pos[:, None] * theta[None, :], col_pos[:, None] * theta[None, :]], axis=1
    )
    angles = jnp.concatenate([jnp.zeros((EXTRA, HD // 2), jnp.float32), angles], axis=0)
    return (jnp.cos(angles), jnp.sin(angles))


def rotate(vectors, cosines, sines):
    halfway = HD // 2
    leading = vectors[..., :halfway]
    trailing = vectors[..., halfway:]
    cos_b = cosines[:, None, :]
    sin_b = sines[:, None, :]
    return jnp.concatenate(
        [leading * cos_b - trailing * sin_b, leading * sin_b + trailing * cos_b], axis=-1
    )


def greet(n):
    me = lax.axis_index("tensor")
    barrier = pltpu.get_barrier_semaphore()
    for k in range(1, n):
        pl.semaphore_signal(
            barrier, inc=1, device_id={"tensor": lax.rem(me + k, n)}, device_id_type=MESH
        )
    pl.semaphore_wait(barrier, n - 1)


def send(src, dst, send_sem, recv_sem, peer):
    return pltpu.make_async_remote_copy(
        src_ref=src,
        dst_ref=dst,
        send_sem=send_sem,
        recv_sem=recv_sem,
        device_id={"tensor": peer},
        device_id_type=MESH,
    )


def chunks(width, body):
    def step(j, carry):
        body(pl.ds(pl.multiple_of(j * LANE, LANE), LANE))
        return carry

    lax.fori_loop(0, width // LANE, step, 0)


def spread(column, rows):
    return jnp.broadcast_to(column, (rows, LANE))


def gather_start(n, own_ref, all_ref, ssem, rsem):
    me = lax.axis_index("tensor")
    copies = []
    for k in range(1, n):
        copy = send(own_ref, all_ref.at[me], ssem.at[k - 1], rsem.at[k - 1], lax.rem(me + k, n))
        copy.start()
        copies.append(copy)
    return copies


def scatter_start(n, w, part_ref, slots, ssem, rsem):
    me = lax.axis_index("tensor")
    copies = []
    for k in range(1, n):
        peer = lax.rem(me + k, n)
        cols = pl.ds(pl.multiple_of(peer * w, w), w)
        copy = send(part_ref.at[:, cols], slots.at[k - 1], ssem.at[k - 1], rsem.at[k - 1], peer)
        copy.start()
        copies.append(copy)
    return copies


def wait_all(copies):
    for copy in copies:
        copy.wait()


def row_stats(n, rows, w, all_ref, acc, mean_ref, inv_ref):
    acc[...] = jnp.zeros_like(acc)

    def add(cols):
        total = all_ref[0, :, cols].astype(F32)
        for k in range(1, n):
            total = total + all_ref[k, :, cols].astype(F32)
        acc[...] += total

    chunks(w, add)
    mean_ref[...] = spread(jnp.sum(acc[...], axis=1, keepdims=True) * (1.0 / D), rows)
    acc[...] = jnp.zeros_like(acc)

    def square(cols):
        mean = mean_ref[...]
        total = jnp.zeros_like(mean)
        for k in range(n):
            center = all_ref[k, :, cols].astype(F32) - mean
            total = total + center * center
        acc[...] += total

    chunks(w, square)
    var = jnp.sum(acc[...], axis=1, keepdims=True) * (1.0 / D)
    inv_ref[...] = spread(lax.rsqrt(var + EPS), rows)


def write_act(n, w, all_ref, mean_ref, inv_ref, gain_ref, bias_ref, act_ref):
    def act(cols):
        for k in range(n):
            wide = pl.ds(pl.multiple_of(k * w + cols.start, LANE), LANE)
            center = all_ref[k, :, cols].astype(F32) - mean_ref[...]
            act_ref[:, wide] = (
                center * inv_ref[...] * gain_ref[:, wide] + bias_ref[:, wide]
            ).astype(BF)

    chunks(w, act)


def first_norm_kernel(n, x_ref, gain_ref, bias_ref, act_ref, mean_ref, inv_ref, all_ref, acc, ssem, rsem):
    rows, w = x_ref.shape
    me = lax.axis_index("tensor")
    greet(n)
    copies = gather_start(n, x_ref, all_ref, ssem, rsem)
    all_ref[me] = x_ref[...]
    wait_all(copies)
    row_stats(n, rows, w, all_ref, acc, mean_ref, inv_ref)
    write_act(n, w, all_ref, mean_ref, inv_ref, gain_ref, bias_ref, act_ref)


def second_norm_kernel(
    n, part_ref, x_ref, scale_ref, gain_ref, bias_ref,
    attn_ref, res_ref, act_ref, mean_ref, inv_ref,
    slots, own_ref, all_ref, acc, ssem, rsem, ssem2, rsem2,
):
    rows, w = x_ref.shape
    me = lax.axis_index("tensor")
    greet(n)
    wait_all(scatter_start(n, w, part_ref, slots, ssem, rsem))

    def add(cols):
        wide = pl.ds(pl.multiple_of(me * w + cols.start, LANE), LANE)
        total = part_ref[:, wide].astype(F32)
        for k in range(n - 1):
            total = total + slots[k, :, cols].astype(F32)
        attn_ref[:, cols] = total
        res = x_ref[:, cols].astype(F32) + scale_ref[:, wide] * total
        res_ref[:, cols] = res
        own_ref[:, cols] = res.astype(BF)

    chunks(w, add)
    copies = gather_start(n, own_ref, all_ref, ssem2, rsem2)
    all_ref[me] = own_ref[...]
    wait_all(copies)
    row_stats(n, rows, w, all_ref, acc, mean_ref, inv_ref)
    write_act(n, w, all_ref, mean_ref, inv_ref, gain_ref, bias_ref, act_ref)


def norm_back(n, w, part_ref, slots, grad_ref, base_ref, mean_ref, inv_ref, gain_ref,
              sums, acc, acc2, stat_own, stats, ssem, rsem, out):
    rows = grad_ref.shape[0]
    me = lax.axis_index("tensor")
    acc[...] = jnp.zeros_like(acc)
    acc2[...] = jnp.zeros_like(acc2)

    def first(cols):
        wide = pl.ds(pl.multiple_of(me * w + cols.start, LANE), LANE)
        total = part_ref[:, wide].astype(F32)
        for k in range(n - 1):
            total = total + slots[k, :, cols].astype(F32)
        grad_ref[:, cols] = total
        normed = (base_ref[:, cols].astype(F32) - mean_ref[...]) * inv_ref[...]
        sums[0:1, cols] = jnp.sum(total * normed, axis=0, keepdims=True)
        sums[1:2, cols] = jnp.sum(total, axis=0, keepdims=True)
        scaled = total * gain_ref[:, wide]
        acc[...] += scaled
        acc2[...] += scaled * normed

    chunks(w, first)
    plain = jnp.sum(acc[...], axis=1, keepdims=True)
    cross = jnp.sum(acc2[...], axis=1, keepdims=True)
    lane = lax.broadcasted_iota(jnp.int32, (rows, LANE), 1)
    stat_own[...] = jnp.where(lane == 0, plain, cross)
    copies = gather_start(n, stat_own, stats, ssem, rsem)
    wait_all(copies)
    both = stat_own[...]
    for k in range(1, n):
        both = both + stats[lax.rem(me + k, n)]
    acc[...] = spread(both[:, 0:1] * (1.0 / D), rows)
    acc2[...] = spread(both[:, 1:2] * (1.0 / D), rows)

    def second(cols):
        wide = pl.ds(pl.multiple_of(me * w + cols.start, LANE), LANE)
        normed = (base_ref[:, cols].astype(F32) - mean_ref[...]) * inv_ref[...]
        scaled = grad_ref[:, cols] * gain_ref[:, wide]
        out(cols, wide, inv_ref[...] * (scaled - acc[...] - normed * acc2[...]))

    chunks(w, second)


def second_back_kernel(
    n, part_ref, cot_ref, res_ref, attn_ref, mean_ref, inv_ref, gain_ref, scale_ref,
    rgrad_ref, agrad_ref, sums_ref,
    slots, grad_ref, own_ref, acc, acc2, stat_own, stats, ssem, rsem, ssem2, rsem2, ssem3, rsem3, lsem,
):
    w = cot_ref.shape[1]
    me = lax.axis_index("tensor")
    greet(n)
    wait_all(scatter_start(n, w, part_ref, slots, ssem, rsem))
    sums_ref[...] = jnp.zeros_like(sums_ref)

    def out(cols, wide, back):
        res_grad = cot_ref[:, cols].astype(F32) + back
        rgrad_ref[:, cols] = res_grad
        sums_ref[2:3, cols] = jnp.sum(res_grad * attn_ref[:, cols], axis=0, keepdims=True)
        own_ref[:, cols] = (scale_ref[:, wide] * res_grad).astype(BF)

    norm_back(n, w, part_ref, slots, grad_ref, res_ref, mean_ref, inv_ref, gain_ref,
              sums_ref, acc, acc2, stat_own, stats, ssem2, rsem2, out)
    mine = pl.ds(pl.multiple_of(me * w, w), w)
    copies = []
    for k in range(1, n):
        copy = send(own_ref, agrad_ref.at[:, mine], ssem3.at[k - 1], rsem3.at[k - 1], lax.rem(me + k, n))
        copy.start()
        copies.append(copy)
    local = pltpu.make_async_copy(own_ref, agrad_ref.at[:, mine], lsem)
    local.start()
    local.wait()
    wait_all(copies)


def branch_kernel(n, part_ref, res_ref, cot_ref, scale_ref, out_ref, sums_ref, slots, ssem, rsem):
    w = cot_ref.shape[1]
    me = lax.axis_index("tensor")
    greet(n)
    wait_all(scatter_start(n, w, part_ref, slots, ssem, rsem))
    sums_ref[...] = jnp.zeros_like(sums_ref)

    def add(cols):
        wide = pl.ds(pl.multiple_of(me * w + cols.start, LANE), LANE)
        total = part_ref[:, wide].astype(F32)
        for k in range(n - 1):
            total = total + slots[k, :, cols].astype(F32)
        out_ref[:, cols] = res_ref[:, cols] + scale_ref[:, wide] * total
        sums_ref[0:1, cols] = jnp.sum(cot_ref[:, cols].astype(F32) * total, axis=0, keepdims=True)

    chunks(w, add)


def first_back_kernel(
    n, m, part_ref, rgrad_ref, x_ref, mean_ref, inv_ref, gain_ref, small_ref,
    igrad_ref, small_out,
    slots, grad_ref, sums, acc, acc2, stat_own, stats, dsums, tsum,
    ssem, rsem, ssem2, rsem2, dss, drs, tss, trs,
):
    w = x_ref.shape[1]
    me = lax.axis_index("tensor")
    you = lax.axis_index("dp")
    barrier = pltpu.get_barrier_semaphore()
    for k in range(1, n):
        pl.semaphore_signal(
            barrier, inc=1, device_id={"tensor": lax.rem(me + k, n)}, device_id_type=MESH
        )
    for k in range(1, m):
        pl.semaphore_signal(
            barrier, inc=1, device_id={"dp": lax.rem(you + k, m)}, device_id_type=MESH
        )
    pl.semaphore_wait(barrier, n + m - 2)
    wait_all(scatter_start(n, w, part_ref, slots, ssem, rsem))
    sums[...] = small_ref[...]

    def out(cols, wide, back):
        igrad_ref[:, cols] = rgrad_ref[:, cols] + back

    norm_back(n, w, part_ref, slots, grad_ref, x_ref, mean_ref, inv_ref, gain_ref,
              sums, acc, acc2, stat_own, stats, ssem2, rsem2, out)
    copies = []
    for k in range(1, m):
        copy = pltpu.make_async_remote_copy(
            src_ref=sums, dst_ref=dsums.at[you], send_sem=dss.at[k - 1], recv_sem=drs.at[k - 1],
            device_id={"dp": lax.rem(you + k, m)}, device_id_type=MESH,
        )
        copy.start()
        copies.append(copy)
    dsums[you] = sums[...]
    wait_all(copies)
    total = dsums[0]
    for k in range(1, m):
        total = total + dsums[k]
    tsum[...] = total
    mine = pl.ds(pl.multiple_of(me * w, w), w)
    copies = []
    for k in range(1, n):
        copy = send(tsum, small_out.at[:, mine], tss.at[k - 1], trs.at[k - 1], lax.rem(me + k, n))
        copy.start()
        copies.append(copy)
    small_out[:, mine] = total
    wait_all(copies)


def vm():
    return pl.BlockSpec(memory_space=pltpu.VMEM)


def sems(count):
    return pltpu.SemaphoreType.DMA((count,))


def call(kernel, ident, outs, scratch, args):
    return pl.pallas_call(
        kernel,
        out_shape=[jax.ShapeDtypeStruct(s, t) for s, t in outs],
        in_specs=[vm()] * len(args),
        out_specs=[vm()] * len(outs),
        scratch_shapes=scratch,
        compiler_params=pltpu.CompilerParams(
            collective_id=ident, has_side_effects=True, vmem_limit_bytes=48 << 20
        ),
        cost_estimate=pl.CostEstimate(flops=30_000_000_000, bytes_accessed=8_000_000, transcendentals=0),
    )(*args)


def local(
    tokens_in, ln1_gain, ln1_bias, w_qkv, w_out, scale_attn, ln2_gain, ln2_bias, w_gu, w_down,
    scale_mlp, out_cotangent, *, n, m,
):
    rows, w = tokens_in.shape
    images = rows // SEQ
    inner = w_qkv.shape[2]
    heads = inner // HD
    hidden_width = w_gu.shape[2]
    scale = HD ** (-0.5)
    cosines, sines = rope_tables()
    wide = (rows, n * w)
    own = (rows, w)
    lanes = (rows, LANE)
    row = lambda v: v.reshape(1, D)

    w_j = jnp.transpose(w_qkv, (1, 0, 2))
    gu_j = lax.optimization_barrier(jnp.transpose(w_gu, (1, 0, 2)))
    cot_all = lax.all_gather(out_cotangent, "tensor", axis=1, tiled=True)

    act_one, mean_one, inv_one = call(
        functools.partial(first_norm_kernel, n), 1,
        [(wide, BF), (lanes, F32), (lanes, F32)],
        [pltpu.VMEM((n,) + own, BF), pltpu.VMEM(lanes, F32), sems(n - 1), sems(n - 1)],
        (tokens_in, row(ln1_gain), row(ln1_bias)),
    )
    raw = [
        jnp.dot(act_one, w_j[j], preferred_element_type=F32).reshape(images, SEQ, heads, HD)
        for j in range(3)
    ]
    queries = rotate(raw[0], cosines, sines).astype(BF)
    keys_rot = rotate(raw[1], cosines, sines).astype(BF)
    values = raw[2].astype(BF)
    scores = jnp.einsum("bqhd,bkhd->bhqk", queries, keys_rot, preferred_element_type=F32) * scale
    row_top = jnp.max(scores, axis=-1, keepdims=True)
    log_total = row_top + jnp.log(jnp.sum(jnp.exp(scores - row_top), axis=-1, keepdims=True))
    probs_low = jnp.exp(scores - log_total).astype(BF)
    mixed = jnp.einsum("bhqk,bkhd->bqhd", probs_low, values, preferred_element_type=F32)
    mixed = mixed.astype(BF).reshape(rows, inner)
    attn_part = jnp.dot(mixed, w_out, preferred_element_type=F32).astype(BF)
    attn_sum, residual, act_two, mean_two, inv_two = call(
        functools.partial(second_norm_kernel, n), 2,
        [(own, F32), (own, F32), (wide, BF), (lanes, F32), (lanes, F32)],
        [pltpu.VMEM((n - 1,) + own, BF), pltpu.VMEM(own, BF), pltpu.VMEM((n,) + own, BF),
         pltpu.VMEM(lanes, F32)] + [sems(n - 1)] * 4,
        (attn_part, tokens_in, row(scale_attn), row(ln2_gain), row(ln2_bias)),
    )
    gate = jnp.dot(act_two, gu_j[0], preferred_element_type=F32)
    up = jnp.dot(act_two, gu_j[1], preferred_element_type=F32)
    sig = jax.nn.sigmoid(gate)
    hidden = (gate * sig * up).astype(BF)
    branch_grad = (scale_mlp * cot_all.astype(F32)).astype(BF)
    hidden_grad = lax.dot_general(branch_grad, w_down, COLS, preferred_element_type=F32)
    gate_grad = (hidden_grad * up * sig * (1.0 + gate * (1.0 - sig))).astype(BF)
    up_grad = (hidden_grad * gate * sig).astype(BF)
    act_two_part = (
        lax.dot_general(gate_grad, gu_j[0], COLS, preferred_element_type=F32)
        + lax.dot_general(up_grad, gu_j[1], COLS, preferred_element_type=F32)
    ).astype(BF)
    down_term = lax.dot_general(hidden, branch_grad, ROWS, preferred_element_type=F32).astype(BF)
    down_sum = lax.psum_scatter(down_term, "dp", scatter_dimension=1, tiled=True).astype(F32)
    gu_term = jnp.stack(
        [
            lax.dot_general(act_two, g, ROWS, preferred_element_type=F32).astype(BF)
            for g in (gate_grad, up_grad)
        ]
    )
    gu_sum = lax.psum_scatter(gu_term, "dp", scatter_dimension=1, tiled=True).astype(F32)

    res_grad, attn_grad, sums_two = call(
        functools.partial(second_back_kernel, n), 3,
        [(own, F32), (wide, BF), ((8, w), F32)],
        [pltpu.VMEM((n - 1,) + own, BF), pltpu.VMEM(own, F32), pltpu.VMEM(own, BF),
         pltpu.VMEM(lanes, F32), pltpu.VMEM(lanes, F32), pltpu.VMEM(lanes, F32),
         pltpu.VMEM((n,) + lanes, F32)] + [sems(n - 1)] * 6 + [pltpu.SemaphoreType.DMA],
        (act_two_part, out_cotangent, residual, attn_sum, mean_two, inv_two, row(ln2_gain), row(scale_attn)),
    )
    mixed_grad = lax.dot_general(attn_grad, w_out, COLS, preferred_element_type=F32)
    mixed_grad = mixed_grad.astype(BF).reshape(images, SEQ, heads, HD)
    scores_again = (
        jnp.einsum("bqhd,bkhd->bhqk", queries, keys_rot, preferred_element_type=F32) * scale
    )
    attn_probs = jnp.exp(scores_again - log_total)
    probs_again = attn_probs.astype(BF)
    prob_grad = jnp.einsum("bqhd,bkhd->bhqk", mixed_grad, values, preferred_element_type=F32)
    row_delta = jnp.sum(attn_probs * prob_grad, axis=-1, keepdims=True)
    score_grad = (attn_probs * (prob_grad - row_delta)).astype(BF)
    query_grad = (
        jnp.einsum("bhqk,bkhd->bqhd", score_grad, keys_rot, preferred_element_type=F32) * scale
    )
    key_grad = (
        jnp.einsum("bhqk,bqhd->bkhd", score_grad, queries, preferred_element_type=F32) * scale
    )
    value_grad = jnp.einsum("bhqk,bqhd->bkhd", probs_again, mixed_grad, preferred_element_type=F32)
    raw_grad = [
        g.astype(BF).reshape(rows, inner)
        for g in (
            rotate(query_grad, cosines, -sines),
            rotate(key_grad, cosines, -sines),
            value_grad,
        )
    ]
    proj_term = lax.dot_general(mixed, attn_grad, ROWS, preferred_element_type=F32).astype(BF)
    proj_sum = lax.psum_scatter(proj_term, "dp", scatter_dimension=1, tiled=True).astype(F32)
    qkv_term = jnp.stack(
        [lax.dot_general(act_one, g, ROWS, preferred_element_type=F32).astype(BF) for g in raw_grad]
    )
    qkv_sum = lax.psum_scatter(qkv_term, "dp", scatter_dimension=1, tiled=True).astype(F32)

    act_one_part = sum(
        lax.dot_general(raw_grad[j], w_j[j], COLS, preferred_element_type=F32) for j in range(3)
    ).astype(BF)
    branch_part = jnp.dot(hidden, w_down, preferred_element_type=F32).astype(BF)
    layer_out, sums_mlp = call(
        functools.partial(branch_kernel, n), 4,
        [(own, F32), ((8, w), F32)],
        [pltpu.VMEM((n - 1,) + own, BF), sems(n - 1), sems(n - 1)],
        (branch_part, residual, out_cotangent, row(scale_mlp)),
    )
    small = jnp.concatenate(
        [jnp.zeros((2, w), F32), sums_two[0:3], sums_mlp[0:1], jnp.zeros((2, w), F32)], axis=0
    )
    input_grad, small_sums = call(
        functools.partial(first_back_kernel, n, m), 5,
        [(own, F32), ((8, n * w), F32)],
        [pltpu.VMEM((n - 1,) + own, BF), pltpu.VMEM(own, F32), pltpu.VMEM((8, w), F32),
         pltpu.VMEM(lanes, F32), pltpu.VMEM(lanes, F32), pltpu.VMEM(lanes, F32),
         pltpu.VMEM((n,) + lanes, F32), pltpu.VMEM((m, 8, w), F32), pltpu.VMEM((8, w), F32)]
        + [sems(n - 1)] * 4 + [sems(m - 1)] * 2 + [sems(n - 1)] * 2,
        (act_one_part, res_grad, tokens_in, mean_one, inv_one, row(ln1_gain), small),
    )
    return (
        layer_out,
        input_grad,
        small_sums[0],
        small_sums[1],
        jnp.transpose(qkv_sum, (1, 0, 2)),
        proj_sum,
        small_sums[4],
        small_sums[2],
        small_sums[3],
        jnp.transpose(gu_sum, (1, 0, 2)),
        down_sum,
        small_sums[5],
    )


def solution(mesh):
    placed = (
        P("dp", "tensor"),
        P(),
        P(),
        P(None, None, "tensor"),
        P("tensor", None),
        P(),
        P(),
        P(),
        P(None, None, "tensor"),
        P("tensor", None),
        P(),
        P("dp", "tensor"),
    )
    return jax.shard_map(
        functools.partial(local, n=mesh.shape["tensor"], m=mesh.shape["dp"]),
        mesh=mesh,
        in_specs=placed,
        out_specs=(
            P("dp", "tensor"),
            P("dp", "tensor"),
            P(),
            P(),
            P("dp", None, "tensor"),
            P("tensor", "dp"),
            P(),
            P(),
            P(),
            P("dp", None, "tensor"),
            P("tensor", "dp"),
            P(),
        ),
        check_vma=False,
    )
```

```python
import functools
import math

import jax
import jax.numpy as jnp
from jax import lax
from jax.experimental import pallas as pl
from jax.experimental.pallas import tpu as pltpu
from jax.sharding import PartitionSpec as P

D = 4096
HD = 128
GRID = 14
EXTRA = 5
PATCH = 196
SEQ = 201
EPS = 1e-06
LANE = 128
BF = jnp.bfloat16
F32 = jnp.float32
MESH = pl.DeviceIdType.MESH
ROWS = (((0,), (0,)), ((), ()))
COLS = (((1,), (1,)), ((), ()))


def rope_tables():
    quarter = HD // 4
    theta = (
        2.0
        * math.pi
        * jnp.exp(jnp.arange(quarter, dtype=jnp.float32) * (-4.0 * math.log(100.0) / HD))
    )
    places = jnp.arange(PATCH, dtype=jnp.int32)
    row_pos = ((places // GRID).astype(jnp.float32) + 0.5) * (2.0 / GRID) - 1.0
    col_pos = ((places % GRID).astype(jnp.float32) + 0.5) * (2.0 / GRID) - 1.0
    angles = jnp.concatenate(
        [row_pos[:, None] * theta[None, :], col_pos[:, None] * theta[None, :]], axis=1
    )
    angles = jnp.concatenate([jnp.zeros((EXTRA, HD // 2), jnp.float32), angles], axis=0)
    return (jnp.cos(angles), jnp.sin(angles))


def rotate(vectors, cosines, sines):
    halfway = HD // 2
    leading = vectors[..., :halfway]
    trailing = vectors[..., halfway:]
    cos_b = cosines[:, None, :]
    sin_b = sines[:, None, :]
    return jnp.concatenate(
        [leading * cos_b - trailing * sin_b, leading * sin_b + trailing * cos_b], axis=-1
    )


def greet(n, m=1):
    me = lax.axis_index("tensor")
    you = lax.axis_index("dp")
    barrier = pltpu.get_barrier_semaphore()
    for k in range(1, n):
        pl.semaphore_signal(
            barrier, inc=1, device_id={"tensor": lax.rem(me + k, n)}, device_id_type=MESH
        )
    for k in range(1, m):
        pl.semaphore_signal(
            barrier, inc=1, device_id={"dp": lax.rem(you + k, m)}, device_id_type=MESH
        )
    pl.semaphore_wait(barrier, n + m - 2)


def send(src, dst, send_sem, recv_sem, peer):
    return pltpu.make_async_remote_copy(
        src_ref=src,
        dst_ref=dst,
        send_sem=send_sem,
        recv_sem=recv_sem,
        device_id={"tensor": peer},
        device_id_type=MESH,
    )


def send_dp(src, dst, send_sem, recv_sem, peer):
    return pltpu.make_async_remote_copy(
        src_ref=src,
        dst_ref=dst,
        send_sem=send_sem,
        recv_sem=recv_sem,
        device_id={"dp": peer},
        device_id_type=MESH,
    )


class Hop:
    def __init__(self, k, m, right_src, left_src, right_dst, left_dst, sem):
        you = lax.axis_index("dp")
        z, last = you // 2, m // 2 - 1
        right = send_dp(right_src, right_dst, sem.at[0], sem.at[1], lax.rem(you + 2, m))
        left = send_dp(left_src, left_dst, sem.at[2], sem.at[3], lax.rem(you + m - 2, m))
        self.steps = [
            (right, (z >= k - 1) & (z < last), z >= k),
            (left, (z <= last - k + 1) & (z > 0), z <= last - k),
        ]

    def start(self):
        for copy, sends, _ in self.steps:
            pl.when(sends)(copy.start)

    def wait(self):
        for copy, sends, gets in self.steps:
            pl.when(sends)(copy.wait_send)
            pl.when(gets)(copy.wait_recv)


class End:
    def __init__(self, m, part_ref, right_dst, left_dst, sem):
        you = lax.axis_index("dp")
        z, last = you // 2, m // 2 - 1
        right = send_dp(part_ref.at[last], right_dst, sem.at[0], sem.at[1], lax.rem(you + 2, m))
        left = send_dp(part_ref.at[0], left_dst, sem.at[2], sem.at[3], lax.rem(you + m - 2, m))
        self.steps = [(right, z == 0, z == 1), (left, z == last, z == last - 1)]

    start = Hop.start
    wait = Hop.wait


class Exchange:
    def __init__(self, m, pieces, full_ref, out_ref, ssem, rsem, lsem):
        you = lax.axis_index("dp")
        piece = lax.rem(lax.axis_index("tensor"), pieces)
        self.copies = []
        for k in range(m):
            peer = lax.rem(you + k, m)
            cols = pl.ds(pl.multiple_of((peer * pieces + piece) * LANE, LANE), LANE)
            if k:
                copy = send_dp(
                    full_ref.at[:, cols], out_ref.at[you], ssem.at[k - 1], rsem.at[k - 1], peer
                )
            else:
                copy = pltpu.make_async_copy(full_ref.at[:, cols], out_ref.at[you], lsem)
            self.copies.append(copy)

    def start(self):
        for copy in self.copies:
            copy.start()

    def wait(self):
        for copy in self.copies:
            copy.wait()


def chunks(width, body):
    def step(j, carry):
        body(pl.ds(pl.multiple_of(j * LANE, LANE), LANE))
        return carry

    lax.fori_loop(0, width // LANE, step, 0)


def spread(column, rows):
    return jnp.broadcast_to(column, (rows, LANE))


def gather_start(n, own_ref, all_ref, ssem, rsem):
    me = lax.axis_index("tensor")
    copies = []
    for k in range(1, n):
        copy = send(own_ref, all_ref.at[me], ssem.at[k - 1], rsem.at[k - 1], lax.rem(me + k, n))
        copy.start()
        copies.append(copy)
    return copies


def scatter_start(n, w, part_ref, slots, ssem, rsem):
    me = lax.axis_index("tensor")
    copies = []
    for k in range(1, n):
        peer = lax.rem(me + k, n)
        cols = pl.ds(pl.multiple_of(peer * w, w), w)
        copy = send(part_ref.at[:, cols], slots.at[k - 1], ssem.at[k - 1], rsem.at[k - 1], peer)
        copy.start()
        copies.append(copy)
    return copies


def wait_all(copies):
    for copy in copies:
        copy.wait()


def row_stats(n, rows, w, all_ref, acc, mean_ref, inv_ref):
    acc[...] = jnp.zeros_like(acc)

    def add(cols):
        total = all_ref[0, :, cols].astype(F32)
        for k in range(1, n):
            total = total + all_ref[k, :, cols].astype(F32)
        acc[...] += total

    chunks(w, add)
    mean_ref[...] = spread(jnp.sum(acc[...], axis=1, keepdims=True) * (1.0 / D), rows)
    acc[...] = jnp.zeros_like(acc)

    def square(cols):
        mean = mean_ref[...]
        total = jnp.zeros_like(mean)
        for k in range(n):
            center = all_ref[k, :, cols].astype(F32) - mean
            total = total + center * center
        acc[...] += total

    chunks(w, square)
    var = jnp.sum(acc[...], axis=1, keepdims=True) * (1.0 / D)
    inv_ref[...] = spread(lax.rsqrt(var + EPS), rows)


def write_act(n, w, all_ref, mean_ref, inv_ref, gain_ref, bias_ref, act_ref):
    def act(cols):
        for k in range(n):
            wide = pl.ds(pl.multiple_of(k * w + cols.start, LANE), LANE)
            center = all_ref[k, :, cols].astype(F32) - mean_ref[...]
            act_ref[:, wide] = (
                center * inv_ref[...] * gain_ref[:, wide] + bias_ref[:, wide]
            ).astype(BF)

    chunks(w, act)


def first_norm_kernel(n, x_ref, gain_ref, bias_ref, act_ref, mean_ref, inv_ref, all_ref, acc, ssem, rsem):
    rows, w = x_ref.shape
    me = lax.axis_index("tensor")
    greet(n)
    copies = gather_start(n, x_ref, all_ref, ssem, rsem)
    all_ref[me] = x_ref[...]
    wait_all(copies)
    row_stats(n, rows, w, all_ref, acc, mean_ref, inv_ref)
    write_act(n, w, all_ref, mean_ref, inv_ref, gain_ref, bias_ref, act_ref)


def second_norm_kernel(
    n, m, pieces, part_ref, x_ref, scale_ref, gain_ref, bias_ref, act_one_ref, cot_ref, mixed_ref,
    attn_ref, res_ref, act_ref, mean_ref, inv_ref, kact_ref, kcot_ref, *refs,
):
    hops = m // 2 - 1
    rights, lefts, refs = refs[:hops], refs[hops:2 * hops], refs[2 * hops:]
    (slots, own_ref, all_ref, acc, ssem, rsem, ssem2, rsem2, hsem,
     ass, ars, als, css, crs, cls) = refs
    rows, w = x_ref.shape
    me = lax.axis_index("tensor")
    greet(n, m)
    copies = scatter_start(n, w, part_ref, slots, ssem, rsem)
    line = [
        Hop(k, m, rights[k - 2] if k > 1 else mixed_ref, lefts[k - 2] if k > 1 else mixed_ref,
            rights[k - 1], lefts[k - 1], hsem.at[k - 1])
        for k in range(1, hops + 1)
    ]
    line[0].start()
    sides = [
        Exchange(m, pieces, act_one_ref, kact_ref, ass, ars, als),
        Exchange(m, pieces, cot_ref, kcot_ref, css, crs, cls),
    ]
    for side in sides:
        side.start()
    wait_all(copies)

    def add(cols):
        wide = pl.ds(pl.multiple_of(me * w + cols.start, LANE), LANE)
        total = part_ref[:, wide].astype(F32)
        for k in range(n - 1):
            total = total + slots[k, :, cols].astype(F32)
        attn_ref[:, cols] = total
        res = x_ref[:, cols].astype(F32) + scale_ref[:, wide] * total
        res_ref[:, cols] = res
        own_ref[:, cols] = res.astype(BF)

    chunks(w, add)
    copies = gather_start(n, own_ref, all_ref, ssem2, rsem2)
    all_ref[me] = own_ref[...]
    line[0].wait()
    if hops > 1:
        line[1].start()
    wait_all(copies)
    row_stats(n, rows, w, all_ref, acc, mean_ref, inv_ref)
    for k in range(1, hops):
        line[k].wait()
        if k + 1 < hops:
            line[k + 1].start()
        if k == 1:
            write_act(n, w, all_ref, mean_ref, inv_ref, gain_ref, bias_ref, act_ref)
    for side in sides:
        side.wait()


def norm_back(n, w, load_total, grad_ref, base_ref, mean_ref, inv_ref, gain_ref,
              sums, acc, acc2, stat_own, stats, ssem, rsem, out):
    rows = grad_ref.shape[0]
    me = lax.axis_index("tensor")
    acc[...] = jnp.zeros_like(acc)
    acc2[...] = jnp.zeros_like(acc2)

    def first(cols):
        wide = pl.ds(pl.multiple_of(me * w + cols.start, LANE), LANE)
        total = load_total(cols, wide)
        grad_ref[:, cols] = total
        normed = (base_ref[:, cols].astype(F32) - mean_ref[...]) * inv_ref[...]
        sums[0:1, cols] = jnp.sum(total * normed, axis=0, keepdims=True)
        sums[1:2, cols] = jnp.sum(total, axis=0, keepdims=True)
        scaled = total * gain_ref[:, wide]
        acc[...] += scaled
        acc2[...] += scaled * normed

    chunks(w, first)
    plain = jnp.sum(acc[...], axis=1, keepdims=True)
    cross = jnp.sum(acc2[...], axis=1, keepdims=True)
    lane = lax.broadcasted_iota(jnp.int32, (rows, LANE), 1)
    stat_own[...] = jnp.where(lane == 0, plain, cross)
    copies = gather_start(n, stat_own, stats, ssem, rsem)
    wait_all(copies)
    both = stat_own[...]
    for k in range(1, n):
        both = both + stats[lax.rem(me + k, n)]
    acc[...] = spread(both[:, 0:1] * (1.0 / D), rows)
    acc2[...] = spread(both[:, 1:2] * (1.0 / D), rows)

    def second(cols):
        wide = pl.ds(pl.multiple_of(me * w + cols.start, LANE), LANE)
        normed = (base_ref[:, cols].astype(F32) - mean_ref[...]) * inv_ref[...]
        scaled = grad_ref[:, cols] * gain_ref[:, wide]
        out(cols, wide, inv_ref[...] * (scaled - acc[...] - normed * acc2[...]))

    chunks(w, second)


def second_back_kernel(
    n, m, part_ref, cot_ref, res_ref, attn_ref, mean_ref, inv_ref, gain_ref, scale_ref,
    right_ref, left_ref, gu_ref, rgrad_ref, agrad_ref, sums_ref, gu_right, gu_left, *refs,
):
    hops = m // 2 - 1
    rights = (right_ref,) + refs[:hops - 1]
    lefts = (left_ref,) + refs[hops - 1:2 * hops - 2]
    (slots, grad_ref, own_ref, acc, acc2, stat_own, stats,
     ssem, rsem, ssem2, rsem2, ssem3, rsem3, lsem, hsem, gsem) = refs[2 * hops - 2:]
    w = cot_ref.shape[1]
    me = lax.axis_index("tensor")
    greet(n, m)
    copies = scatter_start(n, w, part_ref, slots, ssem, rsem)
    line = [
        Hop(k, m, rights[k - 2], lefts[k - 2], rights[k - 1], lefts[k - 1], hsem.at[k - 2])
        for k in range(2, hops + 1)
    ]
    line[0].start()
    first = End(m, gu_ref, gu_right, gu_left, gsem)
    first.start()
    wait_all(copies)
    sums_ref[...] = jnp.zeros_like(sums_ref)

    def load_total(cols, wide):
        total = part_ref[:, wide].astype(F32)
        for k in range(n - 1):
            total = total + slots[k, :, cols].astype(F32)
        return total

    def out(cols, wide, back):
        res_grad = cot_ref[:, cols].astype(F32) + back
        rgrad_ref[:, cols] = res_grad
        sums_ref[2:3, cols] = jnp.sum(res_grad * attn_ref[:, cols], axis=0, keepdims=True)
        own_ref[:, cols] = (scale_ref[:, wide] * res_grad).astype(BF)

    norm_back(n, w, load_total, grad_ref, res_ref, mean_ref, inv_ref, gain_ref,
              sums_ref, acc, acc2, stat_own, stats, ssem2, rsem2, out)
    mine = pl.ds(pl.multiple_of(me * w, w), w)
    copies = []
    for k in range(1, n):
        copy = send(own_ref, agrad_ref.at[:, mine], ssem3.at[k - 1], rsem3.at[k - 1], lax.rem(me + k, n))
        copy.start()
        copies.append(copy)
    local = pltpu.make_async_copy(own_ref, agrad_ref.at[:, mine], lsem)
    local.start()
    for k in range(len(line)):
        line[k].wait()
        if k + 1 < len(line):
            line[k + 1].start()
    local.wait()
    wait_all(copies)
    first.wait()


def first_back_kernel(
    n, m, grad_in, rgrad_ref, x_ref, mean_ref, inv_ref, gain_ref, small_ref,
    igrad_ref, small_out,
    grad_ref, sums, acc, acc2, stat_own, stats, dsums, tsum,
    ssem, rsem, dss, drs, tss, trs,
):
    w = x_ref.shape[1]
    me = lax.axis_index("tensor")
    you = lax.axis_index("dp")
    greet(n, m)
    sums[...] = small_ref[...]

    def load_total(cols, wide):
        return grad_in[:, cols].astype(F32)

    def out(cols, wide, back):
        igrad_ref[:, cols] = rgrad_ref[:, cols] + back

    norm_back(n, w, load_total, grad_ref, x_ref, mean_ref, inv_ref, gain_ref,
              sums, acc, acc2, stat_own, stats, ssem, rsem, out)
    copies = []
    for k in range(1, m):
        copy = send_dp(sums, dsums.at[you], dss.at[k - 1], drs.at[k - 1], lax.rem(you + k, m))
        copy.start()
        copies.append(copy)
    dsums[you] = sums[...]
    wait_all(copies)
    total = dsums[0]
    for k in range(1, m):
        total = total + dsums[k]
    tsum[...] = total
    mine = pl.ds(pl.multiple_of(me * w, w), w)
    copies = []
    for k in range(1, n):
        copy = send(tsum, small_out.at[:, mine], tss.at[k - 1], trs.at[k - 1], lax.rem(me + k, n))
        copy.start()
        copies.append(copy)
    small_out[:, mine] = total
    wait_all(copies)


def exchange_kernel(m, pieces, full_ref, out_ref, ssem, rsem, lsem):
    greet(1, m)
    side = Exchange(m, pieces, full_ref, out_ref, ssem, rsem, lsem)
    side.start()
    side.wait()


def mate_of(you):
    return you + 1 - 2 * lax.rem(you, 2)


def pair_grad_kernel(
    m, act_ref, gate_ref, up_ref, hidden_ref, out_ref, right_ref, left_ref,
    acts, mates, gates, ups, flip, asem, arem, gsem, grem, lsem, hsem,
):
    line = m // 2
    you = lax.axis_index("dp")
    core, mate = lax.rem(you, 2), mate_of(you)
    width = acts.shape[-1]
    tile = 512
    greet(1, m)
    hop = Hop(1, m, hidden_ref, hidden_ref, right_ref, left_ref, hsem)
    copies = [
        send_dp(gate_ref, gates, gsem.at[0], grem.at[0], mate),
        send_dp(up_ref, ups, gsem.at[1], grem.at[1], mate),
    ]
    locals_ = []
    for k in range(line):
        theirs = pl.ds(pl.multiple_of((2 * k + 1 - core) * width, LANE), width)
        ours = pl.ds(pl.multiple_of((2 * k + core) * width, LANE), width)
        copies.append(send_dp(act_ref.at[:, theirs], mates.at[k], asem.at[k], arem.at[k], mate))
        locals_.append(pltpu.make_async_copy(act_ref.at[:, ours], acts.at[k], lsem.at[k]))
    for copy in locals_ + copies:
        copy.start()
    hop.start()
    for copy in locals_:
        copy.wait()
    for k in range(line):
        flip[0, k] = acts[k].T
    for copy in copies:
        copy.wait()
    for k in range(line):
        flip[1, k] = mates[k].T
    for j, (near, far) in enumerate(((gate_ref, gates), (up_ref, ups))):

        def step(i, carry):
            cols = pl.ds(pl.multiple_of(i * tile, tile), tile)
            for k in range(line):
                out_ref[k, j, :, cols] = (
                    jnp.dot(flip[0, k], near[:, cols], preferred_element_type=F32)
                    + jnp.dot(flip[1, k], far[:, cols], preferred_element_type=F32)
                ).astype(BF)
            return carry

        lax.fori_loop(0, gate_ref.shape[1] // tile, step, 0)
    hop.wait()


def gathered_grad_kernel(m, turned, own_ref, *refs):
    hops = m // 2 - 1
    rights, lefts = refs[:hops], refs[hops:2 * hops]
    side_ref, out_ref, blocks, flip, lsem, ssem, rsem = refs[2 * hops:]
    you = lax.axis_index("dp")
    core, mate, z = lax.rem(you, 2), mate_of(you), you // 2
    greet(1, m)
    todo = [(None, own_ref, 0)]
    for k in range(1, hops + 1):
        todo.append((z >= k, rights[k - 1], k))
        todo.append((z < k, lefts[hops - k], k))
    copies = []
    for cond, src, k in todo:
        index = lax.rem(z - k + m // 2, m // 2) * 2 + core
        near = pltpu.make_async_copy(src, blocks.at[index], lsem.at[k])
        far = send_dp(src, blocks.at[index], ssem.at[k], rsem.at[k], mate)
        copies.append((cond, near, far))
    for cond, near, far in copies:

        def go(near=near, far=far):
            near.start()
            far.start()

        go() if cond is None else pl.when(cond)(go)
    for b in range(m):
        flip[b] = side_ref[b].T
    for cond, near, far in copies:

        def done(near=near, far=far):
            near.wait()
            far.wait()

        done() if cond is None else pl.when(cond)(done)
    tile = 512
    for j in range(own_ref.shape[0]):

        def step(i, carry):
            cols = pl.ds(pl.multiple_of(i * tile, tile), tile)
            total = jnp.dot(flip[0], blocks[0, j, :, cols], preferred_element_type=F32)
            for b in range(1, m):
                total = total + jnp.dot(flip[b], blocks[b, j, :, cols], preferred_element_type=F32)
            if turned:
                out_ref[j, cols, :] = total.T
            else:
                out_ref[j, :, cols] = total
            return carry

        lax.fori_loop(0, own_ref.shape[2] // tile, step, 0)


def qkv_kernel(act_ref, w_ref, cos_ref, sin_ref, out_ref):
    raw = jnp.dot(act_ref[...], w_ref[...], preferred_element_type=F32)
    part = pl.program_id(0)

    @pl.when(part < 2)
    def _():
        for h in range(raw.shape[1] // HD):
            cols = slice(h * HD, (h + 1) * HD)
            t = raw[:, cols]
            out_ref[:, cols] = (
                t * cos_ref[...] + pltpu.roll(t, HD // 2, 1) * sin_ref[...]
            ).astype(BF)

    @pl.when(part == 2)
    def _():
        out_ref[...] = raw.astype(BF)


def qkv_matmul(act, w_j, cos2, sin2):
    rows = act.shape[0]
    inner = w_j.shape[2]
    tile = min(512, inner)
    return pl.pallas_call(
        qkv_kernel,
        grid=(3, inner // tile),
        out_shape=jax.ShapeDtypeStruct((3, rows, inner), BF),
        in_specs=[
            pl.BlockSpec((rows, D), lambda j, i: (0, 0)),
            pl.BlockSpec((None, D, tile), lambda j, i: (j, 0, i)),
            pl.BlockSpec((rows, HD), lambda j, i: (0, 0)),
            pl.BlockSpec((rows, HD), lambda j, i: (0, 0)),
        ],
        out_specs=pl.BlockSpec((None, rows, tile), lambda j, i: (j, 0, i)),
        compiler_params=pltpu.CompilerParams(vmem_limit_bytes=40 << 20),
        cost_estimate=pl.CostEstimate(
            flops=2 * rows * D * 3 * inner, bytes_accessed=6 * D * inner, transcendentals=0
        ),
    )(act, w_j, cos2, sin2)


def back_kernel(g_ref, w_ref, out_ref):
    total = None
    for j in range(g_ref.shape[0]):
        term = lax.dot_general(g_ref[j], w_ref[j], COLS, preferred_element_type=F32)
        total = term if total is None else total + term
    out_ref[...] = total.astype(BF)


def back_matmul(grads, w_j):
    parts, rows, inner = grads.shape
    tile = 512
    return pl.pallas_call(
        back_kernel,
        grid=(D // tile,),
        out_shape=jax.ShapeDtypeStruct((rows, D), BF),
        in_specs=[
            pl.BlockSpec((parts, rows, inner), lambda i: (0, 0, 0)),
            pl.BlockSpec((parts, tile, inner), lambda i: (0, i, 0)),
        ],
        out_specs=pl.BlockSpec((rows, tile), lambda i: (0, i)),
        compiler_params=pltpu.CompilerParams(vmem_limit_bytes=40 << 20),
        cost_estimate=pl.CostEstimate(
            flops=2 * rows * D * parts * inner,
            bytes_accessed=2 * D * parts * inner,
            transcendentals=0,
        ),
    )(grads, w_j)


def vm():
    return pl.BlockSpec(memory_space=pltpu.VMEM)


def hb():
    return pl.BlockSpec(memory_space=pltpu.HBM)


def sems(*shape):
    return pltpu.SemaphoreType.DMA(shape)


def call(kernel, ident, outs, scratch, args, micros=30):
    shapes = [jax.ShapeDtypeStruct(o[0], o[1]) for o in outs]
    return list(pl.pallas_call(
        kernel,
        out_shape=shapes,
        in_specs=[hb() if a[1] else vm() for a in args],
        out_specs=[hb() if len(o) > 2 else vm() for o in outs],
        scratch_shapes=scratch,
        compiler_params=pltpu.CompilerParams(
            collective_id=ident, has_side_effects=True, vmem_limit_bytes=56 << 20
        ),
        cost_estimate=pl.CostEstimate(
            flops=micros * 1_000_000, bytes_accessed=8_000, transcendentals=0
        ),
    )(*[a[0] for a in args]))


def line_reduce(part, right, left, m, gate):
    line = m // 2
    z = lax.axis_index("dp") // 2
    take = lambda i: lax.dynamic_index_in_dim(part, jnp.clip(i, 0, line - 1), 0, keepdims=False)
    right = jnp.where(z >= 1, right.astype(F32), 0.0)
    left = jnp.where(z <= line - 2, left.astype(F32), 0.0)
    for t in range(2, line):
        give_r = (take(z + line - t).astype(F32) + right).astype(BF)
        give_l = (take(z - line + t).astype(F32) + left).astype(BF)
        if t == 2:
            give_r, give_l, gate = lax.optimization_barrier((give_r, give_l, gate))
        right = lax.ppermute(
            give_r, "dp", [(2 * i + c, 2 * i + 2 + c) for i in range(t) for c in range(2)]
        ).astype(F32)
        left = lax.ppermute(
            give_l, "dp", [(2 * i + c, 2 * i - 2 + c) for i in range(line - t, line) for c in range(2)]
        ).astype(F32)
    return take(z).astype(F32) + right + left, gate


def line_gather(own, m):
    line = m // 2
    right = left = own
    rights, lefts = [], []
    for k in range(1, line):
        right = lax.ppermute(right, "dp", [(i, i + 2) for i in range(2 * (k - 1), m - 2)])
        left = lax.ppermute(left, "dp", [(i, i - 2) for i in range(2, m - 2 * (k - 1))])
        rights.append(right)
        lefts.append(left)
    return rights, lefts


def local(
    tokens_in, ln1_gain, ln1_bias, w_qkv, w_out, scale_attn, ln2_gain, ln2_bias, w_gu, w_down,
    scale_mlp, out_cotangent, *, n, m,
):
    rows, w = tokens_in.shape
    images = rows // SEQ
    inner = w_qkv.shape[2]
    heads = inner // HD
    hidden_width = w_gu.shape[2]
    scale = HD ** (-0.5)
    line = m // 2
    hops = line - 1
    shard = D // m
    pieces = min(n, shard // LANE)
    cosines, sines = rope_tables()
    cos2 = jnp.tile(jnp.concatenate([cosines, cosines], axis=1), (images, 1))
    sin2 = jnp.tile(jnp.concatenate([-sines, sines], axis=1), (images, 1))
    wide = (rows, n * w)
    own = (rows, w)
    lanes = (rows, LANE)
    row = lambda v: v.reshape(1, D)
    V = lambda *a: [(x, False) for x in a]
    H = lambda *a: [(x, True) for x in a]

    w_j = jnp.transpose(w_qkv, (1, 0, 2))
    gu_j = lax.optimization_barrier(jnp.transpose(w_gu, (1, 0, 2)))

    act_one, mean_one, inv_one = call(
        functools.partial(first_norm_kernel, n), 1,
        [(wide, BF), (lanes, F32), (lanes, F32)],
        [pltpu.VMEM((n,) + own, BF), pltpu.VMEM(lanes, F32), sems(n - 1), sems(n - 1)],
        V(tokens_in, row(ln1_gain), row(ln1_bias)), 50,
    )
    cot_late, act_one = lax.optimization_barrier((out_cotangent, act_one))
    cot_all = lax.all_gather(cot_late, "tensor", axis=1, tiled=True)
    branch_grad = (scale_mlp * cot_all.astype(F32)).astype(BF)
    qkv = qkv_matmul(act_one, w_j, cos2, sin2)
    queries, keys_rot, values = (qkv[j].reshape(images, SEQ, heads, HD) for j in range(3))
    scores = jnp.einsum("bqhd,bkhd->bhqk", queries, keys_rot, preferred_element_type=F32) * scale
    row_top = jnp.max(scores, axis=-1, keepdims=True)
    log_total = row_top + jnp.log(jnp.sum(jnp.exp(scores - row_top), axis=-1, keepdims=True))
    probs_low = jnp.exp(scores - log_total).astype(BF)
    mixed = jnp.einsum("bhqk,bkhd->bqhd", probs_low, values, preferred_element_type=F32)
    mixed = mixed.astype(BF).reshape(rows, inner)
    attn_part = jnp.dot(mixed, w_out, preferred_element_type=F32).astype(BF)
    outs = call(
        functools.partial(second_norm_kernel, n, m, pieces), 2,
        [(own, F32), (own, F32), (wide, BF), (lanes, F32), (lanes, F32)]
        + [((m, rows, LANE), BF, True)] * 2 + [((rows, inner), BF, True)] * (2 * hops),
        [pltpu.VMEM((n - 1,) + own, BF), pltpu.VMEM(own, BF), pltpu.VMEM((n,) + own, BF),
         pltpu.VMEM(lanes, F32)] + [sems(n - 1)] * 4 + [sems(hops, 4)]
        + [sems(m - 1), sems(m - 1), pltpu.SemaphoreType.DMA] * 2,
        V(attn_part, tokens_in, row(scale_attn), row(ln2_gain), row(ln2_bias))
        + H(act_one, branch_grad, mixed), 80,
    )
    attn_sum, residual, act_two, mean_two, inv_two, kact, kcot = outs[:7]
    mixed_right, mixed_left = outs[7:7 + hops], outs[7 + hops:]
    side = lambda k: lax.all_gather(k, "tensor", axis=2, tiled=True)[:, :, :shard]
    side_act, side_cot = side(kact), side(kcot)

    gate = jnp.dot(act_two, gu_j[0], preferred_element_type=F32)
    up = jnp.dot(act_two, gu_j[1], preferred_element_type=F32)
    sig = jax.nn.sigmoid(gate)
    hidden = (gate * sig * up).astype(BF)
    hidden_grad = lax.dot_general(branch_grad, w_down, COLS, preferred_element_type=F32)
    gate_grad = (hidden_grad * up * sig * (1.0 + gate * (1.0 - sig))).astype(BF)
    up_grad = (hidden_grad * gate * sig).astype(BF)
    block = (rows, hidden_width)
    gu_part, hidden_r, hidden_l = call(
        functools.partial(pair_grad_kernel, m), 3,
        [((line, 2, shard, hidden_width), BF), (block, BF, True), (block, BF, True)],
        [pltpu.VMEM((line, rows, shard), BF), pltpu.VMEM((line, rows, shard), BF),
         pltpu.VMEM(block, BF), pltpu.VMEM(block, BF), pltpu.VMEM((2, line, shard, rows), BF),
         sems(line), sems(line), sems(2), sems(2), sems(line), sems(4)],
        H(act_two) + V(gate_grad, up_grad) + H(hidden), 40,
    )
    gu_grads = jnp.stack([gate_grad, up_grad])
    act_two_part = back_matmul(gu_grads, gu_j)
    branch_part = jnp.dot(hidden, w_down, preferred_element_type=F32).astype(BF)
    branch = lax.psum_scatter(branch_part, "tensor", scatter_dimension=1, tiled=True).astype(F32)

    outs = call(
        functools.partial(second_back_kernel, n, m), 4,
        [(own, F32), (wide, BF), ((8, w), F32)] + [(gu_part.shape[1:], BF, True)] * 2
        + [(block, BF, True)] * (2 * hops - 2),
        [pltpu.VMEM((n - 1,) + own, BF), pltpu.VMEM(own, F32), pltpu.VMEM(own, BF),
         pltpu.VMEM(lanes, F32), pltpu.VMEM(lanes, F32), pltpu.VMEM(lanes, F32),
         pltpu.VMEM((n,) + lanes, F32)] + [sems(n - 1)] * 6
        + [pltpu.SemaphoreType.DMA, sems(hops - 1, 4), sems(4)],
        V(act_two_part, out_cotangent, residual, attn_sum, mean_two, inv_two, row(ln2_gain), row(scale_attn))
        + H(hidden_r, hidden_l, gu_part), 80,
    )
    res_grad, attn_grad, sums_two, gu_right, gu_left = outs[:5]
    hidden_right = [hidden_r] + outs[5:4 + hops]
    hidden_left = [hidden_l] + outs[4 + hops:]
    gu_sum, attn_grad = line_reduce(gu_part, gu_right, gu_left, m, attn_grad)
    mixed_grad = lax.dot_general(attn_grad, w_out, COLS, preferred_element_type=F32)
    mixed_grad = mixed_grad.astype(BF).reshape(images, SEQ, heads, HD)
    scores_again = (
        jnp.einsum("bqhd,bkhd->bhqk", queries, keys_rot, preferred_element_type=F32) * scale
    )
    attn_probs = jnp.exp(scores_again - log_total)
    probs_again = attn_probs.astype(BF)
    prob_grad = jnp.einsum("bqhd,bkhd->bhqk", mixed_grad, values, preferred_element_type=F32)
    row_delta = jnp.sum(attn_probs * prob_grad, axis=-1, keepdims=True)
    score_grad = (attn_probs * (prob_grad - row_delta)).astype(BF)
    query_grad = (
        jnp.einsum("bhqk,bkhd->bqhd", score_grad, keys_rot, preferred_element_type=F32) * scale
    )
    key_grad = (
        jnp.einsum("bhqk,bqhd->bkhd", score_grad, queries, preferred_element_type=F32) * scale
    )
    value_grad = jnp.einsum("bhqk,bqhd->bkhd", probs_again, mixed_grad, preferred_element_type=F32)
    raw_grad = jnp.stack(
        [
            g.astype(BF).reshape(rows, inner)
            for g in (
                rotate(query_grad, cosines, -sines),
                rotate(key_grad, cosines, -sines),
                value_grad,
            )
        ]
    )
    raw_right, raw_left = line_gather(raw_grad, m)
    act_one_part = back_matmul(raw_grad, w_j)
    act_one_grad = lax.psum_scatter(act_one_part, "tensor", scatter_dimension=1, tiled=True)
    (kattn,) = call(
        functools.partial(exchange_kernel, m, pieces), 5, [((m, rows, LANE), BF, True)],
        [sems(m - 1), sems(m - 1), pltpu.SemaphoreType.DMA], H(attn_grad), 20,
    )
    side_attn = side(kattn)

    def gathered(ident, mine, rights, lefts, sides, turned):
        parts, _, width = mine.shape
        shape = (parts, width, shard) if turned else (parts, shard, width)
        (out,) = call(
            functools.partial(gathered_grad_kernel, m, turned), ident, [(shape, F32)],
            [pltpu.VMEM((m,) + mine.shape, BF), pltpu.VMEM((m, shard, rows), BF),
             sems(line), sems(line), sems(line)],
            H(mine, *rights, *lefts) + V(sides), 30,
        )
        return out

    lead = lambda arrays: [a[None] for a in arrays]
    down_sum = gathered(6, hidden[None], lead(hidden_right), lead(hidden_left), side_cot, True)[0]
    proj_sum = gathered(7, mixed[None], lead(mixed_right), lead(mixed_left), side_attn, True)[0]
    qkv_sum = gathered(8, raw_grad, raw_right, raw_left, side_act, False)

    own_cols = lambda v: lax.dynamic_slice_in_dim(v, lax.axis_index("tensor") * w, w, 0)
    layer_out = residual + own_cols(scale_mlp) * branch
    sums_mlp = jnp.sum(out_cotangent.astype(F32) * branch, axis=0, keepdims=True)
    small = jnp.concatenate(
        [jnp.zeros((2, w), F32), sums_two[0:3], sums_mlp, jnp.zeros((2, w), F32)], axis=0
    )
    input_grad, small_sums = call(
        functools.partial(first_back_kernel, n, m), 9,
        [(own, F32), ((8, n * w), F32)],
        [pltpu.VMEM(own, F32), pltpu.VMEM((8, w), F32),
         pltpu.VMEM(lanes, F32), pltpu.VMEM(lanes, F32), pltpu.VMEM(lanes, F32),
         pltpu.VMEM((n,) + lanes, F32), pltpu.VMEM((m, 8, w), F32), pltpu.VMEM((8, w), F32)]
        + [sems(n - 1)] * 2 + [sems(m - 1)] * 2 + [sems(n - 1)] * 2,
        V(act_one_grad, res_grad, tokens_in, mean_one, inv_one, row(ln1_gain), small), 20,
    )
    return (
        layer_out,
        input_grad,
        small_sums[0],
        small_sums[1],
        jnp.transpose(qkv_sum, (1, 0, 2)),
        proj_sum,
        small_sums[4],
        small_sums[2],
        small_sums[3],
        jnp.transpose(gu_sum, (1, 0, 2)),
        down_sum,
        small_sums[5],
    )


def solution(mesh):
    placed = (
        P("dp", "tensor"),
        P(),
        P(),
        P(None, None, "tensor"),
        P("tensor", None),
        P(),
        P(),
        P(),
        P(None, None, "tensor"),
        P("tensor", None),
        P(),
        P("dp", "tensor"),
    )
    return jax.shard_map(
        functools.partial(local, n=mesh.shape["tensor"], m=mesh.shape["dp"]),
        mesh=mesh,
        in_specs=placed,
        out_specs=(
            P("dp", "tensor"),
            P("dp", "tensor"),
            P(),
            P(),
            P("dp", None, "tensor"),
            P("tensor", "dp"),
            P(),
            P(),
            P(),
            P("dp", None, "tensor"),
            P("tensor", "dp"),
            P(),
        ),
        check_vma=False,
    )
```

```python
import functools
import math

import jax
import jax.numpy as jnp
from jax import lax
from jax.experimental import pallas as pl
from jax.experimental.pallas import tpu as pltpu
from jax.sharding import PartitionSpec as P

D = 4096
HD = 128
GRID = 14
EXTRA = 5
PATCH = 196
SEQ = 201
EPS = 1e-06
LANE = 128
BF = jnp.bfloat16
F32 = jnp.float32
MESH = pl.DeviceIdType.MESH
ROWS = (((0,), (0,)), ((), ()))
COLS = (((1,), (1,)), ((), ()))


def rope_tables():
    quarter = HD // 4
    theta = (
        2.0
        * math.pi
        * jnp.exp(jnp.arange(quarter, dtype=jnp.float32) * (-4.0 * math.log(100.0) / HD))
    )
    places = jnp.arange(PATCH, dtype=jnp.int32)
    row_pos = ((places // GRID).astype(jnp.float32) + 0.5) * (2.0 / GRID) - 1.0
    col_pos = ((places % GRID).astype(jnp.float32) + 0.5) * (2.0 / GRID) - 1.0
    angles = jnp.concatenate(
        [row_pos[:, None] * theta[None, :], col_pos[:, None] * theta[None, :]], axis=1
    )
    angles = jnp.concatenate([jnp.zeros((EXTRA, HD // 2), jnp.float32), angles], axis=0)
    return (jnp.cos(angles), jnp.sin(angles))


def rotate(vectors, cosines, sines):
    halfway = HD // 2
    leading = vectors[..., :halfway]
    trailing = vectors[..., halfway:]
    cos_b = cosines[:, None, :]
    sin_b = sines[:, None, :]
    return jnp.concatenate(
        [leading * cos_b - trailing * sin_b, leading * sin_b + trailing * cos_b], axis=-1
    )


def greet(n, m=1):
    me = lax.axis_index("tensor")
    you = lax.axis_index("dp")
    barrier = pltpu.get_barrier_semaphore()
    for k in range(1, n):
        pl.semaphore_signal(
            barrier, inc=1, device_id={"tensor": lax.rem(me + k, n)}, device_id_type=MESH
        )
    for k in range(1, m):
        pl.semaphore_signal(
            barrier, inc=1, device_id={"dp": lax.rem(you + k, m)}, device_id_type=MESH
        )
    pl.semaphore_wait(barrier, n + m - 2)


def send(src, dst, send_sem, recv_sem, peer):
    return pltpu.make_async_remote_copy(
        src_ref=src,
        dst_ref=dst,
        send_sem=send_sem,
        recv_sem=recv_sem,
        device_id={"tensor": peer},
        device_id_type=MESH,
    )


def send_dp(src, dst, send_sem, recv_sem, peer):
    return pltpu.make_async_remote_copy(
        src_ref=src,
        dst_ref=dst,
        send_sem=send_sem,
        recv_sem=recv_sem,
        device_id={"dp": peer},
        device_id_type=MESH,
    )


class Hop:
    def __init__(self, k, m, right_src, left_src, right_dst, left_dst, sem):
        you = lax.axis_index("dp")
        z, last = you // 2, m // 2 - 1
        right = send_dp(right_src, right_dst, sem.at[0], sem.at[1], lax.rem(you + 2, m))
        left = send_dp(left_src, left_dst, sem.at[2], sem.at[3], lax.rem(you + m - 2, m))
        self.steps = [
            (right, (z >= k - 1) & (z < last), z >= k),
            (left, (z <= last - k + 1) & (z > 0), z <= last - k),
        ]

    def start(self):
        for copy, sends, _ in self.steps:
            pl.when(sends)(copy.start)

    def wait(self):
        for copy, sends, gets in self.steps:
            pl.when(sends)(copy.wait_send)
            pl.when(gets)(copy.wait_recv)


class End:
    def __init__(self, m, part_ref, right_dst, left_dst, sem):
        you = lax.axis_index("dp")
        z, last = you // 2, m // 2 - 1
        right = send_dp(part_ref.at[last], right_dst, sem.at[0], sem.at[1], lax.rem(you + 2, m))
        left = send_dp(part_ref.at[0], left_dst, sem.at[2], sem.at[3], lax.rem(you + m - 2, m))
        self.steps = [(right, z == 0, z == 1), (left, z == last, z == last - 1)]

    start = Hop.start
    wait = Hop.wait


class Exchange:
    def __init__(self, m, pieces, full_ref, out_ref, ssem, rsem, lsem):
        you = lax.axis_index("dp")
        piece = lax.rem(lax.axis_index("tensor"), pieces)
        self.copies = []
        for k in range(m):
            peer = lax.rem(you + k, m)
            cols = pl.ds(pl.multiple_of((peer * pieces + piece) * LANE, LANE), LANE)
            if k:
                copy = send_dp(
                    full_ref.at[:, cols], out_ref.at[you], ssem.at[k - 1], rsem.at[k - 1], peer
                )
            else:
                copy = pltpu.make_async_copy(full_ref.at[:, cols], out_ref.at[you], lsem)
            self.copies.append(copy)

    def start(self):
        for copy in self.copies:
            copy.start()

    def wait(self):
        for copy in self.copies:
            copy.wait()


def chunks(width, body):
    def step(j, carry):
        body(pl.ds(pl.multiple_of(j * LANE, LANE), LANE))
        return carry

    lax.fori_loop(0, width // LANE, step, 0)


def spread(column, rows):
    return jnp.broadcast_to(column, (rows, LANE))


def gather_start(n, own_ref, all_ref, ssem, rsem):
    me = lax.axis_index("tensor")
    copies = []
    for k in range(1, n):
        copy = send(own_ref, all_ref.at[me], ssem.at[k - 1], rsem.at[k - 1], lax.rem(me + k, n))
        copy.start()
        copies.append(copy)
    return copies


def scatter_start(n, w, part_ref, slots, ssem, rsem):
    me = lax.axis_index("tensor")
    copies = []
    for k in range(1, n):
        peer = lax.rem(me + k, n)
        cols = pl.ds(pl.multiple_of(peer * w, w), w)
        copy = send(part_ref.at[:, cols], slots.at[k - 1], ssem.at[k - 1], rsem.at[k - 1], peer)
        copy.start()
        copies.append(copy)
    return copies


def wait_all(copies):
    for copy in copies:
        copy.wait()


def row_stats(n, rows, w, all_ref, acc, mean_ref, inv_ref):
    acc[...] = jnp.zeros_like(acc)

    def add(cols):
        total = all_ref[0, :, cols].astype(F32)
        for k in range(1, n):
            total = total + all_ref[k, :, cols].astype(F32)
        acc[...] += total

    chunks(w, add)
    mean_ref[...] = spread(jnp.sum(acc[...], axis=1, keepdims=True) * (1.0 / D), rows)
    acc[...] = jnp.zeros_like(acc)

    def square(cols):
        mean = mean_ref[...]
        total = jnp.zeros_like(mean)
        for k in range(n):
            center = all_ref[k, :, cols].astype(F32) - mean
            total = total + center * center
        acc[...] += total

    chunks(w, square)
    var = jnp.sum(acc[...], axis=1, keepdims=True) * (1.0 / D)
    inv_ref[...] = spread(lax.rsqrt(var + EPS), rows)


def write_act(n, w, all_ref, mean_ref, inv_ref, gain_ref, bias_ref, act_ref):
    def act(cols):
        for k in range(n):
            wide = pl.ds(pl.multiple_of(k * w + cols.start, LANE), LANE)
            center = all_ref[k, :, cols].astype(F32) - mean_ref[...]
            act_ref[:, wide] = (
                center * inv_ref[...] * gain_ref[:, wide] + bias_ref[:, wide]
            ).astype(BF)

    chunks(w, act)


def first_norm_kernel(n, x_ref, gain_ref, bias_ref, act_ref, mean_ref, inv_ref, all_ref, acc, ssem, rsem):
    rows, w = x_ref.shape
    me = lax.axis_index("tensor")
    greet(n)
    copies = gather_start(n, x_ref, all_ref, ssem, rsem)
    all_ref[me] = x_ref[...]
    wait_all(copies)
    row_stats(n, rows, w, all_ref, acc, mean_ref, inv_ref)
    write_act(n, w, all_ref, mean_ref, inv_ref, gain_ref, bias_ref, act_ref)


def second_norm_kernel(
    n, m, pieces, part_ref, x_ref, scale_ref, gain_ref, bias_ref, act_one_ref, mixed_ref,
    attn_ref, res_ref, act_ref, mean_ref, inv_ref, kact_ref, *refs,
):
    hops = m // 2 - 1
    rights, lefts, refs = refs[:hops], refs[hops:2 * hops], refs[2 * hops:]
    (slots, own_ref, all_ref, acc, ssem, rsem, ssem2, rsem2, hsem,
     ass, ars, als) = refs
    rows, w = x_ref.shape
    me = lax.axis_index("tensor")
    greet(n, m)
    copies = scatter_start(n, w, part_ref, slots, ssem, rsem)
    line = [
        Hop(k, m, rights[k - 2] if k > 1 else mixed_ref, lefts[k - 2] if k > 1 else mixed_ref,
            rights[k - 1], lefts[k - 1], hsem.at[k - 1])
        for k in range(1, hops + 1)
    ]
    line[0].start()
    side = Exchange(m, pieces, act_one_ref, kact_ref, ass, ars, als)
    side.start()
    wait_all(copies)

    def add(cols):
        wide = pl.ds(pl.multiple_of(me * w + cols.start, LANE), LANE)
        total = part_ref[:, wide].astype(F32)
        for k in range(n - 1):
            total = total + slots[k, :, cols].astype(F32)
        attn_ref[:, cols] = total
        res = x_ref[:, cols].astype(F32) + scale_ref[:, wide] * total
        res_ref[:, cols] = res
        own_ref[:, cols] = res.astype(BF)

    chunks(w, add)
    copies = gather_start(n, own_ref, all_ref, ssem2, rsem2)
    all_ref[me] = own_ref[...]
    line[0].wait()
    if hops > 1:
        line[1].start()
    wait_all(copies)
    row_stats(n, rows, w, all_ref, acc, mean_ref, inv_ref)
    for k in range(1, hops):
        line[k].wait()
        if k + 1 < hops:
            line[k + 1].start()
        if k == 1:
            write_act(n, w, all_ref, mean_ref, inv_ref, gain_ref, bias_ref, act_ref)
    side.wait()


def norm_back(n, w, load_total, grad_ref, base_ref, mean_ref, inv_ref, gain_ref,
              sums, acc, acc2, stat_own, stats, ssem, rsem, out):
    rows = grad_ref.shape[0]
    me = lax.axis_index("tensor")
    acc[...] = jnp.zeros_like(acc)
    acc2[...] = jnp.zeros_like(acc2)

    def first(cols):
        wide = pl.ds(pl.multiple_of(me * w + cols.start, LANE), LANE)
        total = load_total(cols, wide)
        grad_ref[:, cols] = total
        normed = (base_ref[:, cols].astype(F32) - mean_ref[...]) * inv_ref[...]
        sums[0:1, cols] = jnp.sum(total * normed, axis=0, keepdims=True)
        sums[1:2, cols] = jnp.sum(total, axis=0, keepdims=True)
        scaled = total * gain_ref[:, wide]
        acc[...] += scaled
        acc2[...] += scaled * normed

    chunks(w, first)
    plain = jnp.sum(acc[...], axis=1, keepdims=True)
    cross = jnp.sum(acc2[...], axis=1, keepdims=True)
    lane = lax.broadcasted_iota(jnp.int32, (rows, LANE), 1)
    stat_own[...] = jnp.where(lane == 0, plain, cross)
    copies = gather_start(n, stat_own, stats, ssem, rsem)
    wait_all(copies)
    both = stat_own[...]
    for k in range(1, n):
        both = both + stats[lax.rem(me + k, n)]
    acc[...] = spread(both[:, 0:1] * (1.0 / D), rows)
    acc2[...] = spread(both[:, 1:2] * (1.0 / D), rows)

    def second(cols):
        wide = pl.ds(pl.multiple_of(me * w + cols.start, LANE), LANE)
        normed = (base_ref[:, cols].astype(F32) - mean_ref[...]) * inv_ref[...]
        scaled = grad_ref[:, cols] * gain_ref[:, wide]
        out(cols, wide, inv_ref[...] * (scaled - acc[...] - normed * acc2[...]))

    chunks(w, second)


def second_back_kernel(
    n, m, pieces, part_ref, cot_ref, res_ref, attn_ref, mean_ref, inv_ref, gain_ref, scale_ref,
    hidden_ref, bgrad_ref, act_two_ref,
    rgrad_ref, agrad_ref, sums_ref, terms_ref, right_ref, left_ref, kact_ref,
    slots, grad_ref, own_ref, acc, acc2, stat_own, stats, acts, mates, far, flip,
    ssem, rsem, ssem2, rsem2, ssem3, rsem3, lsem, psem, prem, plsem, fsem, esem, ass, ars, als,
):
    w = cot_ref.shape[1]
    line = m // 2
    me = lax.axis_index("tensor")
    greet(n, m)
    copies = scatter_start(n, w, part_ref, slots, ssem, rsem)
    pair = PairTerms(m, [bgrad_ref], [hidden_ref], [far], acts, mates, flip, psem, prem, plsem, fsem)
    pair.start()
    side = Exchange(m, pieces, act_two_ref, kact_ref, ass, ars, als)
    side.start()
    pair.arrive()
    pair.compute(terms_ref, [(line - 1, 0), (0, 0)])
    first = End(m, terms_ref, right_ref, left_ref, esem)
    first.start()
    pair.compute(terms_ref, [(k, 0) for k in range(1, line - 1)])
    wait_all(copies)
    sums_ref[...] = jnp.zeros_like(sums_ref)

    def load_total(cols, wide):
        total = part_ref[:, wide].astype(F32)
        for k in range(n - 1):
            total = total + slots[k, :, cols].astype(F32)
        return total

    def out(cols, wide, back):
        res_grad = cot_ref[:, cols].astype(F32) + back
        rgrad_ref[:, cols] = res_grad
        sums_ref[2:3, cols] = jnp.sum(res_grad * attn_ref[:, cols], axis=0, keepdims=True)
        own_ref[:, cols] = (scale_ref[:, wide] * res_grad).astype(BF)

    norm_back(n, w, load_total, grad_ref, res_ref, mean_ref, inv_ref, gain_ref,
              sums_ref, acc, acc2, stat_own, stats, ssem2, rsem2, out)
    mine = pl.ds(pl.multiple_of(me * w, w), w)
    copies = []
    for k in range(1, n):
        copy = send(own_ref, agrad_ref.at[:, mine], ssem3.at[k - 1], rsem3.at[k - 1], lax.rem(me + k, n))
        copy.start()
        copies.append(copy)
    local = pltpu.make_async_copy(own_ref, agrad_ref.at[:, mine], lsem)
    local.start()
    local.wait()
    wait_all(copies)
    side.wait()
    first.wait()


def first_back_kernel(
    n, grad_in, rgrad_ref, x_ref, mean_ref, inv_ref, gain_ref, small_ref,
    igrad_ref, sums,
    grad_ref, acc, acc2, stat_own, stats, ssem, rsem,
):
    w = x_ref.shape[1]
    greet(n)
    sums[...] = small_ref[...]

    def load_total(cols, wide):
        return grad_in[:, cols].astype(F32)

    def out(cols, wide, back):
        igrad_ref[:, cols] = rgrad_ref[:, cols] + back

    norm_back(n, w, load_total, grad_ref, x_ref, mean_ref, inv_ref, gain_ref,
              sums, acc, acc2, stat_own, stats, ssem, rsem, out)


def mate_of(you):
    return you + 1 - 2 * lax.rem(you, 2)


class PairTerms:
    def __init__(self, m, sides, grads, fars, acts, mates, flip, psem, prem, plsem, fsem):
        self.line = line = m // 2
        you = lax.axis_index("dp")
        core, mate = lax.rem(you, 2), mate_of(you)
        shard = acts.shape[-1]
        self.grads, self.fars, self.acts, self.mates, self.flip = grads, fars, acts, mates, flip
        unique = []
        for side in sides:
            if side not in unique:
                unique.append(side)
        self.which = [unique.index(side) for side in sides]
        self.far_copies = [
            send_dp(grad, far, fsem.at[2 * i], fsem.at[2 * i + 1], mate)
            for i, (grad, far) in enumerate(zip(grads, fars))
        ]
        self.near_copies = []
        for s, side in enumerate(unique):
            for k in range(line):
                at = s * line + k
                theirs = pl.ds(pl.multiple_of((2 * k + 1 - core) * shard, LANE), shard)
                ours = pl.ds(pl.multiple_of((2 * k + core) * shard, LANE), shard)
                self.far_copies.append(
                    send_dp(side.at[:, theirs], mates.at[at], psem.at[at], prem.at[at], mate)
                )
                self.near_copies.append(
                    pltpu.make_async_copy(side.at[:, ours], acts.at[at], plsem.at[at])
                )

    def start(self):
        for copy in self.near_copies + self.far_copies:
            copy.start()

    def arrive(self):
        for copy in self.near_copies:
            copy.wait()
        for at in range(len(self.near_copies)):
            self.flip[0, at] = self.acts[at].T
        for copy in self.far_copies:
            copy.wait()
        for at in range(len(self.near_copies)):
            self.flip[1, at] = self.mates[at].T

    def compute(self, out_ref, which, tile=512):
        for k, j in which:
            near, far = self.grads[j], self.fars[j]
            at = self.which[j] * self.line + k

            def step(i, carry):
                cols = pl.ds(pl.multiple_of(i * tile, tile), tile)
                out_ref[k, j, :, cols] = (
                    jnp.dot(self.flip[0, at], near[:, cols], preferred_element_type=F32)
                    + jnp.dot(self.flip[1, at], far[:, cols], preferred_element_type=F32)
                ).astype(BF)
                return carry

            lax.fori_loop(0, near.shape[1] // tile, step, 0)


def pair_grad_kernel(
    m, pieces, count, act_ref, agrad_ref, *refs,
):
    grads, (terms_ref, kattn_ref), fars = refs[:count], refs[count:count + 2], refs[count + 2:2 * count + 2]
    acts, mates, flip, psem, prem, plsem, fsem, ass, ars, als = refs[2 * count + 2:]
    greet(1, m)
    pair = PairTerms(m, [act_ref] * count, grads, fars, acts, mates, flip, psem, prem, plsem, fsem)
    pair.start()
    side = Exchange(m, pieces, agrad_ref, kattn_ref, ass, ars, als)
    side.start()
    pair.arrive()
    pair.compute(terms_ref, [(k, j) for k in range(m // 2) for j in range(count)])
    side.wait()


class SmallSums:
    def __init__(self, n, m, sums, out, parts, total, dss, drs, tss, trs):
        self.out, self.sums, self.parts, self.total = out, sums, parts, total
        me, you = lax.axis_index("tensor"), lax.axis_index("dp")
        w = sums.shape[1]
        self.m, self.you = m, you
        self.mine = pl.ds(pl.multiple_of(me * w, w), w)
        self.dp = [
            send_dp(sums, parts.at[you], dss.at[k - 1], drs.at[k - 1], lax.rem(you + k, m))
            for k in range(1, m)
        ]
        self.tensor = [
            send(total, out.at[:, self.mine], tss.at[k - 1], trs.at[k - 1], lax.rem(me + k, n))
            for k in range(1, n)
        ]

    def start(self):
        for copy in self.dp:
            copy.start()

    def finish(self):
        self.parts[self.you] = self.sums[...]
        wait_all(self.dp)
        total = self.parts[0]
        for k in range(1, self.m):
            total = total + self.parts[k]
        self.total[...] = total
        for copy in self.tensor:
            copy.start()
        self.out[:, self.mine] = total
        wait_all(self.tensor)


def gathered_grad_kernel(m, turned, n, own_ref, *refs):
    hops = m // 2 - 1
    rights, lefts = refs[:hops], refs[hops:2 * hops]
    small = None
    if n:
        side_ref, sums, out_ref, small_ref, blocks, flip, lsem, ssem, rsem = refs[2 * hops:2 * hops + 9]
        small = SmallSums(n, m, sums, small_ref, *refs[2 * hops + 9:])
    else:
        side_ref, out_ref, blocks, flip, lsem, ssem, rsem = refs[2 * hops:]
    you = lax.axis_index("dp")
    core, mate, z = lax.rem(you, 2), mate_of(you), you // 2
    greet(max(n, 1), m)
    if small:
        small.start()
    todo = [(None, own_ref, 0)]
    for k in range(1, hops + 1):
        todo.append((z >= k, rights[k - 1], k))
        todo.append((z < k, lefts[hops - k], k))
    copies = []
    for cond, src, k in todo:
        index = lax.rem(z - k + m // 2, m // 2) * 2 + core
        near = pltpu.make_async_copy(src, blocks.at[index], lsem.at[k])
        far = send_dp(src, blocks.at[index], ssem.at[k], rsem.at[k], mate)
        copies.append((cond, near, far))
    for cond, near, far in copies:

        def go(near=near, far=far):
            near.start()
            far.start()

        go() if cond is None else pl.when(cond)(go)
    for b in range(m):
        flip[b] = side_ref[b].T
    for cond, near, far in copies:

        def done(near=near, far=far):
            near.wait()
            far.wait()

        done() if cond is None else pl.when(cond)(done)
    tile = 512
    for j in range(own_ref.shape[0]):

        def step(i, carry):
            cols = pl.ds(pl.multiple_of(i * tile, tile), tile)
            total = jnp.dot(flip[0], blocks[0, j, :, cols], preferred_element_type=F32)
            for b in range(1, m):
                total = total + jnp.dot(flip[b], blocks[b, j, :, cols], preferred_element_type=F32)
            if turned:
                out_ref[j, cols, :] = total.T
            else:
                out_ref[j, :, cols] = total
            return carry

        lax.fori_loop(0, own_ref.shape[2] // tile, step, 0)
    if small:
        small.finish()


def qkv_kernel(act_ref, w_ref, cos_ref, sin_ref, out_ref):
    raw = jnp.dot(act_ref[...], w_ref[...], preferred_element_type=F32)
    part = pl.program_id(0)

    @pl.when(part < 2)
    def _():
        for h in range(raw.shape[1] // HD):
            cols = slice(h * HD, (h + 1) * HD)
            t = raw[:, cols]
            out_ref[:, cols] = (
                t * cos_ref[...] + pltpu.roll(t, HD // 2, 1) * sin_ref[...]
            ).astype(BF)

    @pl.when(part == 2)
    def _():
        out_ref[...] = raw.astype(BF)


def qkv_matmul(act, w_j, cos2, sin2):
    rows = act.shape[0]
    inner = w_j.shape[2]
    tile = min(512, inner)
    return pl.pallas_call(
        qkv_kernel,
        grid=(3, inner // tile),
        out_shape=jax.ShapeDtypeStruct((3, rows, inner), BF),
        in_specs=[
            pl.BlockSpec((rows, D), lambda j, i: (0, 0)),
            pl.BlockSpec((None, D, tile), lambda j, i: (j, 0, i)),
            pl.BlockSpec((rows, HD), lambda j, i: (0, 0)),
            pl.BlockSpec((rows, HD), lambda j, i: (0, 0)),
        ],
        out_specs=pl.BlockSpec((None, rows, tile), lambda j, i: (j, 0, i)),
        compiler_params=pltpu.CompilerParams(vmem_limit_bytes=40 << 20),
        cost_estimate=pl.CostEstimate(
            flops=2 * rows * D * 3 * inner, bytes_accessed=6 * D * inner, transcendentals=0
        ),
    )(act, w_j, cos2, sin2)


def back_kernel(g_ref, w_ref, out_ref):
    total = None
    inner = w_ref.shape[2]
    for j in range(w_ref.shape[0]):
        g = g_ref[:, j * inner:(j + 1) * inner]
        term = lax.dot_general(g, w_ref[j], COLS, preferred_element_type=F32)
        total = term if total is None else total + term
    out_ref[...] = total.astype(BF)


def back_matmul(grads, w_j):
    parts, _, inner = w_j.shape
    rows = grads.shape[0]
    tile = 512
    return pl.pallas_call(
        back_kernel,
        grid=(D // tile,),
        out_shape=jax.ShapeDtypeStruct((rows, D), BF),
        in_specs=[
            pl.BlockSpec((rows, parts * inner), lambda i: (0, 0)),
            pl.BlockSpec((parts, tile, inner), lambda i: (0, i, 0)),
        ],
        out_specs=pl.BlockSpec((rows, tile), lambda i: (0, i)),
        compiler_params=pltpu.CompilerParams(vmem_limit_bytes=40 << 20),
        cost_estimate=pl.CostEstimate(
            flops=2 * rows * D * parts * inner,
            bytes_accessed=2 * D * parts * inner,
            transcendentals=0,
        ),
    )(grads, w_j)


def vm():
    return pl.BlockSpec(memory_space=pltpu.VMEM)


def hb():
    return pl.BlockSpec(memory_space=pltpu.HBM)


def sems(*shape):
    return pltpu.SemaphoreType.DMA(shape)


def call(kernel, ident, outs, scratch, args, micros=30):
    shapes = [jax.ShapeDtypeStruct(o[0], o[1]) for o in outs]
    return list(pl.pallas_call(
        kernel,
        out_shape=shapes,
        in_specs=[hb() if a[1] else vm() for a in args],
        out_specs=[hb() if len(o) > 2 else vm() for o in outs],
        scratch_shapes=scratch,
        compiler_params=pltpu.CompilerParams(
            collective_id=ident, has_side_effects=True, vmem_limit_bytes=56 << 20
        ),
        cost_estimate=pl.CostEstimate(
            flops=micros * 1_000_000_000, bytes_accessed=8_000_000, transcendentals=0
        ),
    )(*[a[0] for a in args]))


class LineReduce:
    def __init__(self, part, m, first=None):
        self.part, self.m, self.line = part, m, m // 2
        self.z = lax.axis_index("dp") // 2
        self.t = 1
        self.right = self.left = None
        if first is not None:
            self.t = 2
            self.right = jnp.where(self.z >= 1, first[0].astype(F32), 0.0)
            self.left = jnp.where(self.z <= self.line - 2, first[1].astype(F32), 0.0)

    def take(self, i):
        i = jnp.clip(i, 0, self.line - 1)
        return lax.dynamic_index_in_dim(self.part, i, 0, keepdims=False)

    def give(self):
        right, left = self.take(self.z + self.line - self.t), self.take(self.z - self.line + self.t)
        if self.right is not None:
            right = (right.astype(F32) + self.right).astype(BF)
            left = (left.astype(F32) + self.left).astype(BF)
        return right, left

    def step(self, given):
        line, t = self.line, self.t
        self.right = lax.ppermute(
            given[0], "dp", [(2 * i + c, 2 * i + 2 + c) for i in range(t) for c in range(2)]
        ).astype(F32)
        self.left = lax.ppermute(
            given[1], "dp",
            [(2 * i + c, 2 * i - 2 + c) for i in range(line - t, line) for c in range(2)],
        ).astype(F32)
        self.t += 1

    def finish(self):
        while self.t < self.line:
            self.step(self.give())
        return self.take(self.z).astype(F32) + self.right + self.left


class LineGather:
    def __init__(self, own, m):
        self.m, self.own = m, own
        self.rights, self.lefts = [], []

    def step(self):
        m, k = self.m, len(self.rights) + 1
        right = self.rights[-1] if self.rights else self.own
        left = self.lefts[-1] if self.lefts else self.own
        self.rights.append(lax.ppermute(right, "dp", [(i, i + 2) for i in range(2 * (k - 1), m - 2)]))
        self.lefts.append(lax.ppermute(left, "dp", [(i, i - 2) for i in range(2, m - 2 * (k - 1))]))

    def finish(self):
        while len(self.rights) < self.m // 2 - 1:
            self.step()
        return self.rights, self.lefts


def tie(*values):
    return lax.optimization_barrier(values)


def local(
    tokens_in, ln1_gain, ln1_bias, w_qkv, w_out, scale_attn, ln2_gain, ln2_bias, w_gu, w_down,
    scale_mlp, out_cotangent, *, n, m,
):
    rows, w = tokens_in.shape
    images = rows // SEQ
    inner = w_qkv.shape[2]
    heads = inner // HD
    hidden_width = w_gu.shape[2]
    scale = HD ** (-0.5)
    line = m // 2
    hops = line - 1
    shard = D // m
    pieces = min(n, shard // LANE)
    cosines, sines = rope_tables()
    cos2 = jnp.tile(jnp.concatenate([cosines, cosines], axis=1), (images, 1))
    sin2 = jnp.tile(jnp.concatenate([-sines, sines], axis=1), (images, 1))
    wide = (rows, n * w)
    own = (rows, w)
    lanes = (rows, LANE)
    row = lambda v: v.reshape(1, D)
    V = lambda *a: [(x, False) for x in a]
    H = lambda *a: [(x, True) for x in a]

    w_j = jnp.transpose(w_qkv, (1, 0, 2))
    gu_j = lax.optimization_barrier(jnp.transpose(w_gu, (1, 0, 2)))

    act_one, mean_one, inv_one = call(
        functools.partial(first_norm_kernel, n), 1,
        [(wide, BF), (lanes, F32), (lanes, F32)],
        [pltpu.VMEM((n,) + own, BF), pltpu.VMEM(lanes, F32), sems(n - 1), sems(n - 1)],
        V(tokens_in, row(ln1_gain), row(ln1_bias)), 50,
    )
    cot_late, act_one = lax.optimization_barrier((out_cotangent, act_one))
    cot_all = lax.all_gather(cot_late, "tensor", axis=1, tiled=True)
    branch_grad = (scale_mlp * cot_all.astype(F32)).astype(BF)
    qkv = qkv_matmul(act_one, w_j, cos2, sin2)
    queries, keys_rot, values = (qkv[j].reshape(images, SEQ, heads, HD) for j in range(3))
    scores = jnp.einsum("bqhd,bkhd->bhqk", queries, keys_rot, preferred_element_type=F32) * scale
    row_top = jnp.max(scores, axis=-1, keepdims=True)
    log_total = row_top + jnp.log(jnp.sum(jnp.exp(scores - row_top), axis=-1, keepdims=True))
    probs_low = jnp.exp(scores - log_total).astype(BF)
    mixed = jnp.einsum("bhqk,bkhd->bqhd", probs_low, values, preferred_element_type=F32)
    mixed = mixed.astype(BF).reshape(rows, inner)
    attn_part = jnp.dot(mixed, w_out, preferred_element_type=F32).astype(BF)
    outs = call(
        functools.partial(second_norm_kernel, n, m, pieces), 2,
        [(own, F32), (own, F32), (wide, BF), (lanes, F32), (lanes, F32)]
        + [((m, rows, LANE), BF, True)] + [((rows, inner), BF, True)] * (2 * hops),
        [pltpu.VMEM((n - 1,) + own, BF), pltpu.VMEM(own, BF), pltpu.VMEM((n,) + own, BF),
         pltpu.VMEM(lanes, F32)] + [sems(n - 1)] * 4 + [sems(hops, 4)]
        + [sems(m - 1), sems(m - 1), pltpu.SemaphoreType.DMA],
        V(attn_part, tokens_in, row(scale_attn), row(ln2_gain), row(ln2_bias))
        + H(act_one, mixed), 80,
    )
    attn_sum, residual, act_two, mean_two, inv_two, kact = outs[:6]
    mixed_right, mixed_left = outs[6:6 + hops], outs[6 + hops:]
    side = lambda k: lax.all_gather(k, "tensor", axis=2, tiled=True)[:, :, :shard]
    side_one = side(kact)

    gate = jnp.dot(act_two, gu_j[0], preferred_element_type=F32)
    up = jnp.dot(act_two, gu_j[1], preferred_element_type=F32)
    sig = jax.nn.sigmoid(gate)
    hidden = (gate * sig * up).astype(BF)
    hidden_grad = lax.dot_general(branch_grad, w_down, COLS, preferred_element_type=F32)
    gate_grad = (hidden_grad * up * sig * (1.0 + gate * (1.0 - sig))).astype(BF)
    up_grad = (hidden_grad * gate * sig).astype(BF)
    gu_grads = jnp.concatenate([gate_grad, up_grad], axis=1)
    gu_line = LineGather(gu_grads, m)
    gu_line.step()
    act_two_part = back_matmul(gu_grads, gu_j)
    block = (rows, hidden_width)
    lane_shape = (line, 1, shard, hidden_width)
    outs = call(
        functools.partial(second_back_kernel, n, m, pieces), 4,
        [(own, F32), (wide, BF), ((8, w), F32), (lane_shape, BF)] + [(lane_shape[1:], BF, True)] * 2
        + [((m, rows, LANE), BF, True)],
        [pltpu.VMEM((n - 1,) + own, BF), pltpu.VMEM(own, F32), pltpu.VMEM(own, BF),
         pltpu.VMEM(lanes, F32), pltpu.VMEM(lanes, F32), pltpu.VMEM(lanes, F32),
         pltpu.VMEM((n,) + lanes, F32), pltpu.VMEM((line, rows, shard), BF),
         pltpu.VMEM((line, rows, shard), BF), pltpu.VMEM(block, BF), pltpu.VMEM((2, line, shard, rows), BF)]
        + [sems(n - 1)] * 6 + [pltpu.SemaphoreType.DMA] + [sems(line)] * 3 + [sems(2), sems(4)]
        + [sems(m - 1), sems(m - 1), pltpu.SemaphoreType.DMA],
        V(act_two_part, out_cotangent, residual, attn_sum, mean_two, inv_two, row(ln2_gain), row(scale_attn), hidden)
        + H(branch_grad, act_two), 80,
    )
    res_grad, attn_grad, sums_two, down_terms, down_right, down_left, kact_two = outs
    down_line = LineReduce(down_terms, m, (down_right, down_left))
    attn_grad, gu_r, gu_l, give_r, give_l = tie(
        attn_grad, gu_line.rights[-1], gu_line.lefts[-1], *down_line.give()
    )
    gu_line.rights[-1], gu_line.lefts[-1] = gu_r, gu_l
    gu_line.step()
    down_line.step((give_r, give_l))
    side_two = side(kact_two)
    mixed_grad = lax.dot_general(attn_grad, w_out, COLS, preferred_element_type=F32)
    mixed_grad = mixed_grad.astype(BF).reshape(images, SEQ, heads, HD)
    scores_again = (
        jnp.einsum("bqhd,bkhd->bhqk", queries, keys_rot, preferred_element_type=F32) * scale
    )
    attn_probs = jnp.exp(scores_again - log_total)
    probs_again = attn_probs.astype(BF)
    prob_grad = jnp.einsum("bqhd,bkhd->bhqk", mixed_grad, values, preferred_element_type=F32)
    row_delta = jnp.sum(attn_probs * prob_grad, axis=-1, keepdims=True)
    score_grad = (attn_probs * (prob_grad - row_delta)).astype(BF)
    query_grad = (
        jnp.einsum("bhqk,bkhd->bqhd", score_grad, keys_rot, preferred_element_type=F32) * scale
    )
    key_grad = (
        jnp.einsum("bhqk,bqhd->bkhd", score_grad, queries, preferred_element_type=F32) * scale
    )
    value_grad = jnp.einsum("bhqk,bqhd->bkhd", probs_again, mixed_grad, preferred_element_type=F32)
    raw_grad = [
        g.astype(BF).reshape(rows, inner)
        for g in (
            rotate(query_grad, cosines, -sines),
            rotate(key_grad, cosines, -sines),
            value_grad,
        )
    ]
    *raw_grad, hidden_late = tie(*raw_grad, hidden)
    value_line = LineGather(raw_grad[2], m)
    value_line.step()
    query_in, gu_r, gu_l, down_r, down_l = tie(
        raw_grad[0], gu_line.rights[-1], gu_line.lefts[-1], down_line.right, down_line.left
    )
    gu_line.rights[-1], gu_line.lefts[-1] = gu_r, gu_l
    down_line.right, down_line.left = down_r, down_l
    two_terms, kattn = call(
        functools.partial(pair_grad_kernel, m, pieces, 2), 5,
        [((line, 2, shard, inner), BF), ((m, rows, LANE), BF, True)],
        [pltpu.VMEM((rows, inner), BF)] * 2
        + [pltpu.VMEM((line, rows, shard), BF)] * 2 + [pltpu.VMEM((2, line, shard, rows), BF)]
        + [sems(line)] * 3 + [sems(4)] + [sems(m - 1), sems(m - 1), pltpu.SemaphoreType.DMA],
        H(act_one, attn_grad) + V(query_in, raw_grad[1]), 30,
    )
    two_line = LineReduce(two_terms, m)
    act_one_part = back_matmul(jnp.concatenate(raw_grad, axis=1), w_j)
    act_one_grad = lax.psum_scatter(act_one_part, "tensor", scatter_dimension=1, tiled=True)
    branch_part = jnp.dot(hidden_late, w_down, preferred_element_type=F32).astype(BF)
    branch = lax.psum_scatter(branch_part, "tensor", scatter_dimension=1, tiled=True).astype(F32)
    side_attn = side(kattn)

    def gathered(ident, mine, rights, lefts, sides, turned, sums=None):
        parts, _, width = mine.shape
        shape = (parts, width, shard) if turned else (parts, shard, width)
        small = sums is not None
        outs = call(
            functools.partial(gathered_grad_kernel, m, turned, n if small else 0), ident,
            [(shape, F32)] + ([((8, n * w), F32)] if small else []),
            [pltpu.VMEM((m,) + mine.shape, BF), pltpu.VMEM((m, shard, rows), BF),
             sems(line), sems(line), sems(line)]
            + ([pltpu.VMEM((m, 8, w), F32), pltpu.VMEM((8, w), F32)]
               + [sems(m - 1)] * 2 + [sems(n - 1)] * 2 if small else []),
            H(mine, *rights, *lefts) + V(sides) + (V(sums) if small else []), 30,
        )
        return outs if small else outs[0]

    lead = lambda arrays: [a[None] for a in arrays]
    down_sum = down_line.finish()[0].T
    gu_sum = gathered(
        6, gu_grads[None], *(lead(v) for v in gu_line.finish()), side_two, False
    ).reshape(shard, 2, hidden_width)
    proj_sum = gathered(7, mixed[None], lead(mixed_right), lead(mixed_left), side_attn, True)[0]

    own_cols = lambda v: lax.dynamic_slice_in_dim(v, lax.axis_index("tensor") * w, w, 0)
    layer_out = residual + own_cols(scale_mlp) * branch
    sums_mlp = jnp.sum(out_cotangent.astype(F32) * branch, axis=0, keepdims=True)
    small = jnp.concatenate(
        [jnp.zeros((2, w), F32), sums_two[0:3], sums_mlp, jnp.zeros((2, w), F32)], axis=0
    )
    input_grad, sums = call(
        functools.partial(first_back_kernel, n), 9,
        [(own, F32), ((8, w), F32)],
        [pltpu.VMEM(own, F32),
         pltpu.VMEM(lanes, F32), pltpu.VMEM(lanes, F32), pltpu.VMEM(lanes, F32),
         pltpu.VMEM((n,) + lanes, F32)] + [sems(n - 1)] * 2,
        V(act_one_grad, res_grad, tokens_in, mean_one, inv_one, row(ln1_gain), small), 20,
    )
    value_sum, small_sums = gathered(
        8, raw_grad[2][None], *(lead(v) for v in value_line.finish()), side_one, False, sums
    )
    qkv_sum = jnp.concatenate([two_line.finish(), value_sum], axis=0)
    return (
        layer_out,
        input_grad,
        small_sums[0],
        small_sums[1],
        jnp.transpose(qkv_sum, (1, 0, 2)),
        proj_sum,
        small_sums[4],
        small_sums[2],
        small_sums[3],
        gu_sum,
        down_sum,
        small_sums[5],
    )


def solution(mesh):
    placed = (
        P("dp", "tensor"),
        P(),
        P(),
        P(None, None, "tensor"),
        P("tensor", None),
        P(),
        P(),
        P(),
        P(None, None, "tensor"),
        P("tensor", None),
        P(),
        P("dp", "tensor"),
    )
    return jax.shard_map(
        functools.partial(local, n=mesh.shape["tensor"], m=mesh.shape["dp"]),
        mesh=mesh,
        in_specs=placed,
        out_specs=(
            P("dp", "tensor"),
            P("dp", "tensor"),
            P(),
            P(),
            P("dp", None, "tensor"),
            P("tensor", "dp"),
            P(),
            P(),
            P(),
            P("dp", None, "tensor"),
            P("tensor", "dp"),
            P(),
        ),
        check_vma=False,
    )
```

```python
import functools
import math

import jax
import jax.numpy as jnp
from jax import lax
from jax.experimental import pallas as pl
from jax.experimental.pallas import tpu as pltpu
from jax.sharding import PartitionSpec as P

D = 4096
HD = 128
GRID = 14
EXTRA = 5
PATCH = 196
SEQ = 201
EPS = 1e-06
LANE = 128
BF = jnp.bfloat16
F32 = jnp.float32
MESH = pl.DeviceIdType.MESH
ROWS = (((0,), (0,)), ((), ()))
COLS = (((1,), (1,)), ((), ()))


def rope_tables():
    quarter = HD // 4
    theta = (
        2.0
        * math.pi
        * jnp.exp(jnp.arange(quarter, dtype=jnp.float32) * (-4.0 * math.log(100.0) / HD))
    )
    places = jnp.arange(PATCH, dtype=jnp.int32)
    row_pos = ((places // GRID).astype(jnp.float32) + 0.5) * (2.0 / GRID) - 1.0
    col_pos = ((places % GRID).astype(jnp.float32) + 0.5) * (2.0 / GRID) - 1.0
    angles = jnp.concatenate(
        [row_pos[:, None] * theta[None, :], col_pos[:, None] * theta[None, :]], axis=1
    )
    angles = jnp.concatenate([jnp.zeros((EXTRA, HD // 2), jnp.float32), angles], axis=0)
    return (jnp.cos(angles), jnp.sin(angles))


def rotate(vectors, cosines, sines):
    halfway = HD // 2
    leading = vectors[..., :halfway]
    trailing = vectors[..., halfway:]
    cos_b = cosines[:, None, :]
    sin_b = sines[:, None, :]
    return jnp.concatenate(
        [leading * cos_b - trailing * sin_b, leading * sin_b + trailing * cos_b], axis=-1
    )


def greet(n, m=1):
    me = lax.axis_index("tensor")
    you = lax.axis_index("dp")
    barrier = pltpu.get_barrier_semaphore()
    for k in range(1, n):
        pl.semaphore_signal(
            barrier, inc=1, device_id={"tensor": lax.rem(me + k, n)}, device_id_type=MESH
        )
    for k in range(1, m):
        pl.semaphore_signal(
            barrier, inc=1, device_id={"dp": lax.rem(you + k, m)}, device_id_type=MESH
        )
    pl.semaphore_wait(barrier, n + m - 2)


def send(src, dst, send_sem, recv_sem, peer):
    return pltpu.make_async_remote_copy(
        src_ref=src,
        dst_ref=dst,
        send_sem=send_sem,
        recv_sem=recv_sem,
        device_id={"tensor": peer},
        device_id_type=MESH,
    )


def send_dp(src, dst, send_sem, recv_sem, peer):
    return pltpu.make_async_remote_copy(
        src_ref=src,
        dst_ref=dst,
        send_sem=send_sem,
        recv_sem=recv_sem,
        device_id={"dp": peer},
        device_id_type=MESH,
    )


class Hop:
    def __init__(self, k, m, right_src, left_src, right_dst, left_dst, sem):
        you = lax.axis_index("dp")
        z, last = you // 2, m // 2 - 1
        right = send_dp(right_src, right_dst, sem.at[0], sem.at[1], lax.rem(you + 2, m))
        left = send_dp(left_src, left_dst, sem.at[2], sem.at[3], lax.rem(you + m - 2, m))
        self.steps = [
            (right, (z >= k - 1) & (z < last), z >= k),
            (left, (z <= last - k + 1) & (z > 0), z <= last - k),
        ]

    def start(self):
        for copy, sends, _ in self.steps:
            pl.when(sends)(copy.start)

    def wait(self):
        for copy, sends, gets in self.steps:
            pl.when(sends)(copy.wait_send)
            pl.when(gets)(copy.wait_recv)


class End:
    def __init__(self, m, part_ref, right_dst, left_dst, sem):
        you = lax.axis_index("dp")
        z, last = you // 2, m // 2 - 1
        right = send_dp(part_ref.at[last], right_dst, sem.at[0], sem.at[1], lax.rem(you + 2, m))
        left = send_dp(part_ref.at[0], left_dst, sem.at[2], sem.at[3], lax.rem(you + m - 2, m))
        self.steps = [(right, z == 0, z == 1), (left, z == last, z == last - 1)]

    start = Hop.start
    wait = Hop.wait


class Exchange:
    def __init__(self, m, pieces, full_ref, out_ref, ssem, rsem, lsem):
        you = lax.axis_index("dp")
        piece = lax.rem(lax.axis_index("tensor"), pieces)
        self.copies = []
        for k in range(m):
            peer = lax.rem(you + k, m)
            cols = pl.ds(pl.multiple_of((peer * pieces + piece) * LANE, LANE), LANE)
            if k:
                copy = send_dp(
                    full_ref.at[:, cols], out_ref.at[you], ssem.at[k - 1], rsem.at[k - 1], peer
                )
            else:
                copy = pltpu.make_async_copy(full_ref.at[:, cols], out_ref.at[you], lsem)
            self.copies.append(copy)

    def start(self):
        for copy in self.copies:
            copy.start()

    def wait(self):
        for copy in self.copies:
            copy.wait()


def chunks(width, body):
    def step(j, carry):
        body(pl.ds(pl.multiple_of(j * LANE, LANE), LANE))
        return carry

    lax.fori_loop(0, width // LANE, step, 0)


def spread(column, rows):
    return jnp.broadcast_to(column, (rows, LANE))


def gather_start(n, own_ref, all_ref, ssem, rsem):
    me = lax.axis_index("tensor")
    copies = []
    for k in range(1, n):
        copy = send(own_ref, all_ref.at[me], ssem.at[k - 1], rsem.at[k - 1], lax.rem(me + k, n))
        copy.start()
        copies.append(copy)
    return copies


def scatter_start(n, w, part_ref, slots, ssem, rsem):
    me = lax.axis_index("tensor")
    copies = []
    for k in range(1, n):
        peer = lax.rem(me + k, n)
        cols = pl.ds(pl.multiple_of(peer * w, w), w)
        copy = send(part_ref.at[:, cols], slots.at[k - 1], ssem.at[k - 1], rsem.at[k - 1], peer)
        copy.start()
        copies.append(copy)
    return copies


def wait_all(copies):
    for copy in copies:
        copy.wait()


def row_stats(n, rows, w, all_ref, acc, mean_ref, inv_ref):
    acc[...] = jnp.zeros_like(acc)

    def add(cols):
        total = all_ref[0, :, cols].astype(F32)
        for k in range(1, n):
            total = total + all_ref[k, :, cols].astype(F32)
        acc[...] += total

    chunks(w, add)
    mean_ref[...] = spread(jnp.sum(acc[...], axis=1, keepdims=True) * (1.0 / D), rows)
    acc[...] = jnp.zeros_like(acc)

    def square(cols):
        mean = mean_ref[...]
        total = jnp.zeros_like(mean)
        for k in range(n):
            center = all_ref[k, :, cols].astype(F32) - mean
            total = total + center * center
        acc[...] += total

    chunks(w, square)
    var = jnp.sum(acc[...], axis=1, keepdims=True) * (1.0 / D)
    inv_ref[...] = spread(lax.rsqrt(var + EPS), rows)


def write_act(n, w, all_ref, mean_ref, inv_ref, gain_ref, bias_ref, act_ref):
    def act(cols):
        for k in range(n):
            wide = pl.ds(pl.multiple_of(k * w + cols.start, LANE), LANE)
            center = all_ref[k, :, cols].astype(F32) - mean_ref[...]
            act_ref[:, wide] = (
                center * inv_ref[...] * gain_ref[:, wide] + bias_ref[:, wide]
            ).astype(BF)

    chunks(w, act)


def first_norm_kernel(n, x_ref, gain_ref, bias_ref, act_ref, mean_ref, inv_ref, all_ref, acc, ssem, rsem):
    rows, w = x_ref.shape
    me = lax.axis_index("tensor")
    greet(n)
    copies = gather_start(n, x_ref, all_ref, ssem, rsem)
    all_ref[me] = x_ref[...]
    wait_all(copies)
    row_stats(n, rows, w, all_ref, acc, mean_ref, inv_ref)
    write_act(n, w, all_ref, mean_ref, inv_ref, gain_ref, bias_ref, act_ref)


def second_norm_kernel(
    n, m, pieces, part_ref, x_ref, scale_ref, gain_ref, bias_ref, act_one_ref, cot_ref, mixed_ref,
    attn_ref, res_ref, act_ref, mean_ref, inv_ref, kact_ref, kcot_ref, *refs,
):
    hops = m // 2 - 1
    rights, lefts, refs = refs[:hops], refs[hops:2 * hops], refs[2 * hops:]
    (slots, own_ref, all_ref, acc, ssem, rsem, ssem2, rsem2, hsem,
     ass, ars, als, css, crs, cls) = refs
    rows, w = x_ref.shape
    me = lax.axis_index("tensor")
    greet(n, m)
    copies = scatter_start(n, w, part_ref, slots, ssem, rsem)
    line = [
        Hop(k, m, rights[k - 2] if k > 1 else mixed_ref, lefts[k - 2] if k > 1 else mixed_ref,
            rights[k - 1], lefts[k - 1], hsem.at[k - 1])
        for k in range(1, hops + 1)
    ]
    line[0].start()
    sides = [
        Exchange(m, pieces, act_one_ref, kact_ref, ass, ars, als),
        Exchange(m, pieces, cot_ref, kcot_ref, css, crs, cls),
    ]
    for side in sides:
        side.start()
    wait_all(copies)

    def add(cols):
        wide = pl.ds(pl.multiple_of(me * w + cols.start, LANE), LANE)
        total = part_ref[:, wide].astype(F32)
        for k in range(n - 1):
            total = total + slots[k, :, cols].astype(F32)
        attn_ref[:, cols] = total
        res = x_ref[:, cols].astype(F32) + scale_ref[:, wide] * total
        res_ref[:, cols] = res
        own_ref[:, cols] = res.astype(BF)

    chunks(w, add)
    copies = gather_start(n, own_ref, all_ref, ssem2, rsem2)
    all_ref[me] = own_ref[...]
    for k in range(hops - 1):
        line[k].wait()
        line[k + 1].start()
    wait_all(copies)
    row_stats(n, rows, w, all_ref, acc, mean_ref, inv_ref)
    write_act(n, w, all_ref, mean_ref, inv_ref, gain_ref, bias_ref, act_ref)
    line[-1].wait()
    for side in sides:
        side.wait()


def norm_back(n, w, load_total, grad_ref, base_ref, mean_ref, inv_ref, gain_ref,
              sums, acc, acc2, stat_own, stats, ssem, rsem, out):
    rows = grad_ref.shape[0]
    me = lax.axis_index("tensor")
    acc[...] = jnp.zeros_like(acc)
    acc2[...] = jnp.zeros_like(acc2)

    def first(cols):
        wide = pl.ds(pl.multiple_of(me * w + cols.start, LANE), LANE)
        total = load_total(cols, wide)
        grad_ref[:, cols] = total
        normed = (base_ref[:, cols].astype(F32) - mean_ref[...]) * inv_ref[...]
        sums[0:1, cols] = jnp.sum(total * normed, axis=0, keepdims=True)
        sums[1:2, cols] = jnp.sum(total, axis=0, keepdims=True)
        scaled = total * gain_ref[:, wide]
        acc[...] += scaled
        acc2[...] += scaled * normed

    chunks(w, first)
    plain = jnp.sum(acc[...], axis=1, keepdims=True)
    cross = jnp.sum(acc2[...], axis=1, keepdims=True)
    lane = lax.broadcasted_iota(jnp.int32, (rows, LANE), 1)
    stat_own[...] = jnp.where(lane == 0, plain, cross)
    copies = gather_start(n, stat_own, stats, ssem, rsem)
    wait_all(copies)
    both = stat_own[...]
    for k in range(1, n):
        both = both + stats[lax.rem(me + k, n)]
    acc[...] = spread(both[:, 0:1] * (1.0 / D), rows)
    acc2[...] = spread(both[:, 1:2] * (1.0 / D), rows)

    def second(cols):
        wide = pl.ds(pl.multiple_of(me * w + cols.start, LANE), LANE)
        normed = (base_ref[:, cols].astype(F32) - mean_ref[...]) * inv_ref[...]
        scaled = grad_ref[:, cols] * gain_ref[:, wide]
        out(cols, wide, inv_ref[...] * (scaled - acc[...] - normed * acc2[...]))

    chunks(w, second)


def second_back_kernel(
    n, m, part_ref, cot_ref, res_ref, attn_ref, mean_ref, inv_ref, gain_ref, scale_ref,
    right_ref, left_ref, gu_ref, rgrad_ref, agrad_ref, sums_ref, gu_right, gu_left, *refs,
):
    hops = m // 2 - 1
    rights = (right_ref,) + refs[:hops - 1]
    lefts = (left_ref,) + refs[hops - 1:2 * hops - 2]
    (slots, grad_ref, own_ref, acc, acc2, stat_own, stats,
     ssem, rsem, ssem2, rsem2, ssem3, rsem3, lsem, hsem, gsem) = refs[2 * hops - 2:]
    w = cot_ref.shape[1]
    me = lax.axis_index("tensor")
    greet(n, m)
    copies = scatter_start(n, w, part_ref, slots, ssem, rsem)
    line = [
        Hop(k, m, rights[k - 2], lefts[k - 2], rights[k - 1], lefts[k - 1], hsem.at[k - 2])
        for k in range(2, hops + 1)
    ]
    line[0].start()
    first = End(m, gu_ref, gu_right, gu_left, gsem)
    first.start()
    wait_all(copies)
    sums_ref[...] = jnp.zeros_like(sums_ref)

    def load_total(cols, wide):
        total = part_ref[:, wide].astype(F32)
        for k in range(n - 1):
            total = total + slots[k, :, cols].astype(F32)
        return total

    def out(cols, wide, back):
        res_grad = cot_ref[:, cols].astype(F32) + back
        rgrad_ref[:, cols] = res_grad
        sums_ref[2:3, cols] = jnp.sum(res_grad * attn_ref[:, cols], axis=0, keepdims=True)
        own_ref[:, cols] = (scale_ref[:, wide] * res_grad).astype(BF)

    norm_back(n, w, load_total, grad_ref, res_ref, mean_ref, inv_ref, gain_ref,
              sums_ref, acc, acc2, stat_own, stats, ssem2, rsem2, out)
    mine = pl.ds(pl.multiple_of(me * w, w), w)
    copies = []
    for k in range(1, n):
        copy = send(own_ref, agrad_ref.at[:, mine], ssem3.at[k - 1], rsem3.at[k - 1], lax.rem(me + k, n))
        copy.start()
        copies.append(copy)
    local = pltpu.make_async_copy(own_ref, agrad_ref.at[:, mine], lsem)
    local.start()
    for k in range(len(line)):
        line[k].wait()
        if k + 1 < len(line):
            line[k + 1].start()
    local.wait()
    wait_all(copies)
    first.wait()


def first_back_kernel(
    n, grad_in, rgrad_ref, x_ref, mean_ref, inv_ref, gain_ref, small_ref,
    igrad_ref, sums,
    grad_ref, acc, acc2, stat_own, stats, ssem, rsem,
):
    w = x_ref.shape[1]
    greet(n)
    sums[...] = small_ref[...]

    def load_total(cols, wide):
        return grad_in[:, cols].astype(F32)

    def out(cols, wide, back):
        igrad_ref[:, cols] = rgrad_ref[:, cols] + back

    norm_back(n, w, load_total, grad_ref, x_ref, mean_ref, inv_ref, gain_ref,
              sums, acc, acc2, stat_own, stats, ssem, rsem, out)


def mate_of(you):
    return you + 1 - 2 * lax.rem(you, 2)


def pair_grad_kernel(
    m, act_ref, gate_ref, up_ref, hidden_ref, out_ref, right_ref, left_ref,
    acts, mates, gates, ups, flip, asem, arem, gsem, grem, lsem, hsem,
):
    line = m // 2
    you = lax.axis_index("dp")
    core, mate = lax.rem(you, 2), mate_of(you)
    width = acts.shape[-1]
    tile = 512
    greet(1, m)
    hop = Hop(1, m, hidden_ref, hidden_ref, right_ref, left_ref, hsem)
    copies = [
        send_dp(gate_ref, gates, gsem.at[0], grem.at[0], mate),
        send_dp(up_ref, ups, gsem.at[1], grem.at[1], mate),
    ]
    locals_ = []
    for k in range(line):
        theirs = pl.ds(pl.multiple_of((2 * k + 1 - core) * width, LANE), width)
        ours = pl.ds(pl.multiple_of((2 * k + core) * width, LANE), width)
        copies.append(send_dp(act_ref.at[:, theirs], mates.at[k], asem.at[k], arem.at[k], mate))
        locals_.append(pltpu.make_async_copy(act_ref.at[:, ours], acts.at[k], lsem.at[k]))
    for copy in locals_ + copies:
        copy.start()
    hop.start()
    for copy in locals_:
        copy.wait()
    for k in range(line):
        flip[0, k] = acts[k].T
    for copy in copies:
        copy.wait()
    for k in range(line):
        flip[1, k] = mates[k].T
    for j, (near, far) in enumerate(((gate_ref, gates), (up_ref, ups))):

        def step(i, carry):
            cols = pl.ds(pl.multiple_of(i * tile, tile), tile)
            for k in range(line):
                out_ref[k, j, :, cols] = (
                    jnp.dot(flip[0, k], near[:, cols], preferred_element_type=F32)
                    + jnp.dot(flip[1, k], far[:, cols], preferred_element_type=F32)
                ).astype(BF)
            return carry

        lax.fori_loop(0, gate_ref.shape[1] // tile, step, 0)
    hop.wait()


class SmallSums:
    def __init__(self, n, m, sums, out, parts, total, dss, drs, tss, trs):
        self.out, self.sums, self.parts, self.total = out, sums, parts, total
        me, you = lax.axis_index("tensor"), lax.axis_index("dp")
        w = sums.shape[1]
        self.m, self.you = m, you
        self.mine = pl.ds(pl.multiple_of(me * w, w), w)
        self.dp = [
            send_dp(sums, parts.at[you], dss.at[k - 1], drs.at[k - 1], lax.rem(you + k, m))
            for k in range(1, m)
        ]
        self.tensor = [
            send(total, out.at[:, self.mine], tss.at[k - 1], trs.at[k - 1], lax.rem(me + k, n))
            for k in range(1, n)
        ]

    def start(self):
        for copy in self.dp:
            copy.start()

    def finish(self):
        self.parts[self.you] = self.sums[...]
        wait_all(self.dp)
        total = self.parts[0]
        for k in range(1, self.m):
            total = total + self.parts[k]
        self.total[...] = total
        for copy in self.tensor:
            copy.start()
        self.out[:, self.mine] = total
        wait_all(self.tensor)


def gathered_grad_kernel(m, turned, first, last, n, *refs):
    hops = m // 2 - 1
    you = lax.axis_index("dp")
    core, mate, z = lax.rem(you, 2), mate_of(you), you // 2
    todo = []
    refs = list(refs)
    for k in range(first, last + 1):
        if k == 0:
            todo.append((None, refs.pop(0), z))
        else:
            todo.append((z >= k, refs.pop(0), z - k))
            todo.append((z <= hops - k, refs.pop(0), z + k))
    side_ref = refs.pop(0)
    before = refs.pop(0) if first else None
    sums = refs.pop(0) if n else None
    out_ref = refs.pop(0)
    small_ref = refs.pop(0) if n else None
    blocks, flip, lsem, ssem, rsem = refs[:5]
    small = SmallSums(n, m, sums, small_ref, *refs[5:]) if n else None
    greet(max(n, 1), m)
    if small:
        small.start()
    copies = []
    for at, (cond, src, chip) in enumerate(todo):
        near = pltpu.make_async_copy(src, blocks.at[at, core], lsem.at[at])
        far = send_dp(src, blocks.at[at, core], ssem.at[at], rsem.at[at], mate)
        copies.append((cond, near, far))

    def when(cond, body):
        body() if cond is None else pl.when(cond)(body)

    def go(near, far):
        near.start()
        far.start()

    def done(near, far):
        near.wait()
        far.wait()

    def turn(at, chip):
        for c in range(2):
            flip[at, c] = side_ref[2 * chip + c].T

    for cond, near, far in copies:
        when(cond, functools.partial(go, near, far))
    for at, (cond, _, chip) in enumerate(todo):
        when(cond, functools.partial(turn, at, chip))
    for cond, near, far in copies:
        when(cond, functools.partial(done, near, far))
    tile = 512
    parts, width = out_ref.shape[0], blocks.shape[-1]
    if before is not None:
        out_ref[...] = before[...]
    for at, (cond, _, chip) in enumerate(todo):
        for j in range(parts):

            def step(i, carry, at=at, j=j):
                cols = pl.ds(pl.multiple_of(i * tile, tile), tile)
                total = jnp.dot(
                    flip[at, 0], blocks[at, 0, j, :, cols], preferred_element_type=F32
                ) + jnp.dot(flip[at, 1], blocks[at, 1, j, :, cols], preferred_element_type=F32)
                if turned:
                    if first or at:
                        out_ref[j, cols, :] += total.T
                    else:
                        out_ref[j, cols, :] = total.T
                elif first or at:
                    out_ref[j, :, cols] += total
                else:
                    out_ref[j, :, cols] = total
                return carry

            def run(step=step):
                lax.fori_loop(0, width // tile, step, 0)

            when(cond, run)
    if small:
        small.finish()


def qkv_kernel(act_ref, w_ref, cos_ref, sin_ref, out_ref):
    raw = jnp.dot(act_ref[...], w_ref[...], preferred_element_type=F32)
    part = pl.program_id(0)

    @pl.when(part < 2)
    def _():
        for h in range(raw.shape[1] // HD):
            cols = slice(h * HD, (h + 1) * HD)
            t = raw[:, cols]
            out_ref[:, cols] = (
                t * cos_ref[...] + pltpu.roll(t, HD // 2, 1) * sin_ref[...]
            ).astype(BF)

    @pl.when(part == 2)
    def _():
        out_ref[...] = raw.astype(BF)


def qkv_matmul(act, w_j, cos2, sin2):
    rows = act.shape[0]
    inner = w_j.shape[2]
    tile = min(512, inner)
    return pl.pallas_call(
        qkv_kernel,
        grid=(3, inner // tile),
        out_shape=jax.ShapeDtypeStruct((3, rows, inner), BF),
        in_specs=[
            pl.BlockSpec((rows, D), lambda j, i: (0, 0)),
            pl.BlockSpec((None, D, tile), lambda j, i: (j, 0, i)),
            pl.BlockSpec((rows, HD), lambda j, i: (0, 0)),
            pl.BlockSpec((rows, HD), lambda j, i: (0, 0)),
        ],
        out_specs=pl.BlockSpec((None, rows, tile), lambda j, i: (j, 0, i)),
        compiler_params=pltpu.CompilerParams(vmem_limit_bytes=40 << 20),
        cost_estimate=pl.CostEstimate(
            flops=2 * rows * D * 3 * inner, bytes_accessed=6 * D * inner, transcendentals=0
        ),
    )(act, w_j, cos2, sin2)


def attention_probs(q, k, same):
    scores = lax.dot_general(k, q, COLS, preferred_element_type=F32) * (HD ** (-0.5))
    scores = jnp.where(same, scores, -jnp.inf)
    top = jnp.max(scores, axis=0, keepdims=True)
    weight = jnp.exp(scores - top)
    return weight / jnp.sum(weight, axis=0, keepdims=True)


def same_image(rows):
    one = lax.broadcasted_iota(jnp.int32, (rows, rows), 0)
    two = lax.broadcasted_iota(jnp.int32, (rows, rows), 1)
    image = lambda i: sum((i >= SEQ * k).astype(jnp.int32) for k in range(1, rows // SEQ))
    return image(one) == image(two)


def attention_kernel(qkv_ref, w_ref, mixed_ref, part_ref):
    rows, inner = mixed_ref.shape

    def head(h, carry):
        cols = pl.ds(pl.multiple_of(h * HD, HD), HD)
        probs = attention_probs(qkv_ref[0, :, cols], qkv_ref[1, :, cols], same_image(rows))
        value = qkv_ref[2, :, cols].astype(F32).T.astype(BF)
        mixed = jnp.dot(value, probs.astype(BF), preferred_element_type=F32)
        mixed_ref[:, cols] = mixed.T.astype(BF)
        return carry

    lax.fori_loop(0, inner // HD, head, 0)

    def tile(i, carry):
        cols = pl.ds(pl.multiple_of(i * 512, 512), 512)
        part_ref[:, cols] = jnp.dot(
            mixed_ref[...], w_ref[:, cols], preferred_element_type=F32
        ).astype(BF)
        return carry

    lax.fori_loop(0, D // 512, tile, 0)


def attention_back_kernel(
    m, pieces, agrad_ref, w_ref, qkv_ref, cos_ref, sin_ref, full_ref, out_ref, kattn_ref,
    mgrad, ass, ars, als,
):
    rows, inner = mgrad.shape
    greet(1, m)
    side = Exchange(m, pieces, full_ref, kattn_ref, ass, ars, als)
    side.start()
    step = min(256, inner)

    def tile(i, carry):
        cols = pl.ds(pl.multiple_of(i * step, step), step)
        mgrad[:, cols] = lax.dot_general(
            agrad_ref[...], w_ref[cols, :], COLS, preferred_element_type=F32
        ).astype(BF)
        return carry

    lax.fori_loop(0, inner // step, tile, 0)

    def back(t):
        return t * cos_ref[...] - pltpu.roll(t, HD // 2, 1) * sin_ref[...]

    def head(h, carry):
        cols = pl.ds(pl.multiple_of(h * HD, HD), HD)
        q, k, v = qkv_ref[0, :, cols], qkv_ref[1, :, cols], qkv_ref[2, :, cols]
        grad = mgrad[:, cols]
        probs = attention_probs(q, k, same_image(rows))
        prob_grad = lax.dot_general(v, grad, COLS, preferred_element_type=F32)
        delta = jnp.sum(probs * prob_grad, axis=0, keepdims=True)
        score_grad = (probs * (prob_grad - delta)).astype(BF)
        scale = HD ** (-0.5)
        flipped = k.astype(F32).T.astype(BF)
        q_grad = jnp.dot(flipped, score_grad, preferred_element_type=F32).T * scale
        k_grad = jnp.dot(score_grad, q, preferred_element_type=F32) * scale
        out_ref[0, :, cols] = back(q_grad).astype(BF)
        out_ref[1, :, cols] = back(k_grad).astype(BF)
        out_ref[2, :, cols] = jnp.dot(
            probs.astype(BF), grad, preferred_element_type=F32
        ).astype(BF)
        return carry

    lax.fori_loop(0, inner // HD, head, 0)
    side.wait()


def plain(kernel, outs, args, scratch=(), micros=15):
    return list(pl.pallas_call(
        kernel,
        out_shape=[jax.ShapeDtypeStruct(*o) for o in outs],
        in_specs=[vm()] * len(args),
        out_specs=[vm()] * len(outs),
        scratch_shapes=list(scratch),
        compiler_params=pltpu.CompilerParams(vmem_limit_bytes=48 << 20),
        cost_estimate=pl.CostEstimate(
            flops=micros * 100_000_000, bytes_accessed=800_000, transcendentals=0
        ),
    )(*args))


def back_kernel(g_ref, w_ref, out_ref):
    total = None
    for j in range(g_ref.shape[0]):
        term = lax.dot_general(g_ref[j], w_ref[j], COLS, preferred_element_type=F32)
        total = term if total is None else total + term
    out_ref[...] = total.astype(BF)


def back_matmul(grads, w_j):
    parts, rows, inner = grads.shape
    tile = 512
    return pl.pallas_call(
        back_kernel,
        grid=(D // tile,),
        out_shape=jax.ShapeDtypeStruct((rows, D), BF),
        in_specs=[
            pl.BlockSpec((parts, rows, inner), lambda i: (0, 0, 0)),
            pl.BlockSpec((parts, tile, inner), lambda i: (0, i, 0)),
        ],
        out_specs=pl.BlockSpec((rows, tile), lambda i: (0, i)),
        compiler_params=pltpu.CompilerParams(vmem_limit_bytes=40 << 20),
        cost_estimate=pl.CostEstimate(
            flops=rows * D * parts * inner * 100 // 500,
            bytes_accessed=800_000,
            transcendentals=0,
        ),
    )(grads, w_j)


def vm():
    return pl.BlockSpec(memory_space=pltpu.VMEM)


def hb():
    return pl.BlockSpec(memory_space=pltpu.HBM)


def sems(*shape):
    return pltpu.SemaphoreType.DMA(shape)


def call(kernel, ident, outs, scratch, args, micros=30):
    shapes = [jax.ShapeDtypeStruct(o[0], o[1]) for o in outs]
    return list(pl.pallas_call(
        kernel,
        out_shape=shapes,
        in_specs=[hb() if a[1] else vm() for a in args],
        out_specs=[hb() if len(o) > 2 else vm() for o in outs],
        scratch_shapes=scratch,
        compiler_params=pltpu.CompilerParams(
            collective_id=ident, has_side_effects=True, vmem_limit_bytes=56 << 20
        ),
        cost_estimate=pl.CostEstimate(
            flops=micros * 100_000_000, bytes_accessed=800_000, transcendentals=0
        ),
    )(*[a[0] for a in args]))


def line_reduce(part, right, left, m, gate):
    line = m // 2
    z = lax.axis_index("dp") // 2
    take = lambda i: lax.dynamic_index_in_dim(part, jnp.clip(i, 0, line - 1), 0, keepdims=False)
    right = jnp.where(z >= 1, right.astype(F32), 0.0)
    left = jnp.where(z <= line - 2, left.astype(F32), 0.0)
    steps = []
    for t in range(2, line):
        give_r = (take(z + line - t).astype(F32) + right).astype(BF)
        give_l = (take(z - line + t).astype(F32) + left).astype(BF)
        if t == 2:
            give_r, give_l, gate = lax.optimization_barrier((give_r, give_l, gate))
        sent = (
            lax.ppermute(
                give_r, "dp", [(2 * i + c, 2 * i + 2 + c) for i in range(t) for c in range(2)]
            ),
            lax.ppermute(
                give_l, "dp",
                [(2 * i + c, 2 * i - 2 + c) for i in range(line - t, line) for c in range(2)],
            ),
        )
        right, left = (v.astype(F32) for v in sent)
        steps.append(sent)
    return take(z).astype(F32) + right + left, gate, steps[0]


def line_gather(own, m, also):
    line = m // 2
    right = left = own
    rights, lefts = [], []
    for k in range(1, line):
        if k == 2:
            right, left, also = lax.optimization_barrier((right, left, also))
        right = lax.ppermute(right, "dp", [(i, i + 2) for i in range(2 * (k - 1), m - 2)])
        left = lax.ppermute(left, "dp", [(i, i - 2) for i in range(2, m - 2 * (k - 1))])
        rights.append(right)
        lefts.append(left)
    return rights, lefts, also


def local(
    tokens_in, ln1_gain, ln1_bias, w_qkv, w_out, scale_attn, ln2_gain, ln2_bias, w_gu, w_down,
    scale_mlp, out_cotangent, *, n, m,
):
    rows, w = tokens_in.shape
    images = rows // SEQ
    inner = w_qkv.shape[2]
    heads = inner // HD
    hidden_width = w_gu.shape[2]
    scale = HD ** (-0.5)
    line = m // 2
    hops = line - 1
    shard = D // m
    pieces = min(n, shard // LANE)
    cosines, sines = rope_tables()
    cos2 = jnp.tile(jnp.concatenate([cosines, cosines], axis=1), (images, 1))
    sin2 = jnp.tile(jnp.concatenate([-sines, sines], axis=1), (images, 1))
    wide = (rows, n * w)
    own = (rows, w)
    lanes = (rows, LANE)
    row = lambda v: v.reshape(1, D)
    V = lambda *a: [(x, False) for x in a]
    H = lambda *a: [(x, True) for x in a]

    w_j = jnp.transpose(w_qkv, (1, 0, 2))
    gu_j = lax.optimization_barrier(jnp.transpose(w_gu, (1, 0, 2)))

    act_one, mean_one, inv_one = call(
        functools.partial(first_norm_kernel, n), 1,
        [(wide, BF), (lanes, F32), (lanes, F32)],
        [pltpu.VMEM((n,) + own, BF), pltpu.VMEM(lanes, F32), sems(n - 1), sems(n - 1)],
        V(tokens_in, row(ln1_gain), row(ln1_bias)), 50,
    )
    cot_late, act_one = lax.optimization_barrier((out_cotangent, act_one))
    cot_all = lax.all_gather(cot_late, "tensor", axis=1, tiled=True)
    branch_grad = (scale_mlp * cot_all.astype(F32)).astype(BF)
    qkv = qkv_matmul(act_one, w_j, cos2, sin2)
    mixed, attn_part = plain(
        attention_kernel, [((rows, inner), BF), (wide, BF)], (qkv, w_out)
    )
    outs = call(
        functools.partial(second_norm_kernel, n, m, pieces), 2,
        [(own, F32), (own, F32), (wide, BF), (lanes, F32), (lanes, F32)]
        + [((m, rows, LANE), BF, True)] * 2 + [((rows, inner), BF, True)] * (2 * hops),
        [pltpu.VMEM((n - 1,) + own, BF), pltpu.VMEM(own, BF), pltpu.VMEM((n,) + own, BF),
         pltpu.VMEM(lanes, F32)] + [sems(n - 1)] * 4 + [sems(hops, 4)]
        + [sems(m - 1), sems(m - 1), pltpu.SemaphoreType.DMA] * 2,
        V(attn_part, tokens_in, row(scale_attn), row(ln2_gain), row(ln2_bias))
        + H(act_one, branch_grad, mixed), 80,
    )
    attn_sum, residual, act_two, mean_two, inv_two, kact, kcot = outs[:7]
    mixed_right, mixed_left = outs[7:7 + hops], outs[7 + hops:]
    side = lambda k: lax.all_gather(k, "tensor", axis=2, tiled=True)[:, :, :shard]
    side_act, side_cot = side(kact), side(kcot)

    gate = jnp.dot(act_two, gu_j[0], preferred_element_type=F32)
    up = jnp.dot(act_two, gu_j[1], preferred_element_type=F32)
    sig = jax.nn.sigmoid(gate)
    hidden = (gate * sig * up).astype(BF)
    hidden_grad = lax.dot_general(branch_grad, w_down, COLS, preferred_element_type=F32)
    gate_grad = (hidden_grad * up * sig * (1.0 + gate * (1.0 - sig))).astype(BF)
    up_grad = (hidden_grad * gate * sig).astype(BF)
    block = (rows, hidden_width)
    gu_part, hidden_r, hidden_l = call(
        functools.partial(pair_grad_kernel, m), 3,
        [((line, 2, shard, hidden_width), BF), (block, BF, True), (block, BF, True)],
        [pltpu.VMEM((line, rows, shard), BF), pltpu.VMEM((line, rows, shard), BF),
         pltpu.VMEM(block, BF), pltpu.VMEM(block, BF), pltpu.VMEM((2, line, shard, rows), BF),
         sems(line), sems(line), sems(2), sems(2), sems(line), sems(4)],
        H(act_two) + V(gate_grad, up_grad) + H(hidden), 40,
    )
    gu_grads = jnp.stack([gate_grad, up_grad])
    act_two_part = back_matmul(gu_grads, gu_j)

    outs = call(
        functools.partial(second_back_kernel, n, m), 4,
        [(own, F32), (wide, BF), ((8, w), F32)] + [(gu_part.shape[1:], BF, True)] * 2
        + [(block, BF, True)] * (2 * hops - 2),
        [pltpu.VMEM((n - 1,) + own, BF), pltpu.VMEM(own, F32), pltpu.VMEM(own, BF),
         pltpu.VMEM(lanes, F32), pltpu.VMEM(lanes, F32), pltpu.VMEM(lanes, F32),
         pltpu.VMEM((n,) + lanes, F32)] + [sems(n - 1)] * 6
        + [pltpu.SemaphoreType.DMA, sems(hops - 1, 4), sems(4)],
        V(act_two_part, out_cotangent, residual, attn_sum, mean_two, inv_two, row(ln2_gain), row(scale_attn))
        + H(hidden_r, hidden_l, gu_part), 80,
    )
    res_grad, attn_grad, sums_two, gu_right, gu_left = outs[:5]
    hidden_right = [hidden_r] + outs[5:4 + hops]
    hidden_left = [hidden_l] + outs[4 + hops:]
    gu_sum, attn_grad, gu_step = line_reduce(gu_part, gu_right, gu_left, m, attn_grad)
    raw_grad, kattn = call(
        functools.partial(attention_back_kernel, m, pieces), 5,
        [((3, rows, inner), BF), ((m, rows, LANE), BF, True)],
        [pltpu.VMEM((rows, inner), BF), sems(m - 1), sems(m - 1), pltpu.SemaphoreType.DMA],
        V(attn_grad, w_out, qkv, cos2, sin2) + H(attn_grad), 25,
    )
    side_attn = side(kattn)
    act_one_part = back_matmul(raw_grad, w_j)
    raw_right, raw_left, act_one_part = line_gather(raw_grad, m, act_one_part)
    act_one_grad = lax.psum_scatter(act_one_part, "tensor", scatter_dimension=1, tiled=True)
    hidden_late = lax.optimization_barrier((hidden, raw_right[1], raw_left[1]) + gu_step)[0]
    branch_part = jnp.dot(hidden_late, w_down, preferred_element_type=F32).astype(BF)
    branch = lax.psum_scatter(branch_part, "tensor", scatter_dimension=1, tiled=True).astype(F32)
    act_one_part = back_matmul(raw_grad, w_j)
    act_one_grad = lax.psum_scatter(act_one_part, "tensor", scatter_dimension=1, tiled=True)
    def gathered(ident, mine, rights, lefts, sides, turned, first=0, last=hops, before=None, sums=None):
        parts, _, width = mine.shape
        shape = (parts, width, shard) if turned else (parts, shard, width)
        small = sums is not None
        blocks = []
        for k in range(first, last + 1):
            blocks += [rights[k - 1], lefts[k - 1]] if k else [mine]
        count = len(blocks)
        outs = call(
            functools.partial(gathered_grad_kernel, m, turned, first, last, n if small else 0), ident,
            [(shape, F32)] + ([((8, n * w), F32)] if small else []),
            [pltpu.VMEM((count, 2) + mine.shape, BF), pltpu.VMEM((count, 2, shard, rows), BF),
             sems(count), sems(count), sems(count)]
            + ([pltpu.VMEM((m, 8, w), F32), pltpu.VMEM((8, w), F32)]
               + [sems(m - 1)] * 2 + [sems(n - 1)] * 2 if small else []),
            H(*blocks) + V(sides) + (V(before) if first else []) + (V(sums) if small else []), 30,
        )
        return outs if small else outs[0]

    lead = lambda arrays: [a[None] for a in arrays]
    down_sum = gathered(6, hidden[None], lead(hidden_right), lead(hidden_left), side_cot, True)[0]
    proj_sum = gathered(7, mixed[None], lead(mixed_right), lead(mixed_left), side_attn, True)[0]

    own_cols = lambda v: lax.dynamic_slice_in_dim(v, lax.axis_index("tensor") * w, w, 0)
    layer_out = residual + own_cols(scale_mlp) * branch
    sums_mlp = jnp.sum(out_cotangent.astype(F32) * branch, axis=0, keepdims=True)
    small = jnp.concatenate(
        [jnp.zeros((2, w), F32), sums_two[0:3], sums_mlp, jnp.zeros((2, w), F32)], axis=0
    )
    input_grad, sums = call(
        functools.partial(first_back_kernel, n), 9,
        [(own, F32), ((8, w), F32)],
        [pltpu.VMEM(own, F32),
         pltpu.VMEM(lanes, F32), pltpu.VMEM(lanes, F32), pltpu.VMEM(lanes, F32),
         pltpu.VMEM((n,) + lanes, F32)] + [sems(n - 1)] * 2,
        V(act_one_grad, res_grad, tokens_in, mean_one, inv_one, row(ln1_gain), small), 20,
    )
    qkv_part = gathered(8, raw_grad, raw_right, raw_left, side_act, False, 0, hops - 1)
    qkv_sum, small_sums = gathered(
        10, raw_grad, raw_right, raw_left, side_act, False, hops, hops, qkv_part, sums
    )
    return (
        layer_out,
        input_grad,
        small_sums[0],
        small_sums[1],
        jnp.transpose(qkv_sum, (1, 0, 2)),
        proj_sum,
        small_sums[4],
        small_sums[2],
        small_sums[3],
        jnp.transpose(gu_sum, (1, 0, 2)),
        down_sum,
        small_sums[5],
    )


def solution(mesh):
    placed = (
        P("dp", "tensor"),
        P(),
        P(),
        P(None, None, "tensor"),
        P("tensor", None),
        P(),
        P(),
        P(),
        P(None, None, "tensor"),
        P("tensor", None),
        P(),
        P("dp", "tensor"),
    )
    return jax.shard_map(
        functools.partial(local, n=mesh.shape["tensor"], m=mesh.shape["dp"]),
        mesh=mesh,
        in_specs=placed,
        out_specs=(
            P("dp", "tensor"),
            P("dp", "tensor"),
            P(),
            P(),
            P("dp", None, "tensor"),
            P("tensor", "dp"),
            P(),
            P(),
            P(),
            P("dp", None, "tensor"),
            P("tensor", "dp"),
            P(),
        ),
        check_vma=False,
    )
```

```python
import functools
import math

import jax
import jax.numpy as jnp
from jax import lax
from jax.experimental import pallas as pl
from jax.experimental.pallas import tpu as pltpu
from jax.sharding import PartitionSpec as P

D = 4096
HD = 128
GRID = 14
EXTRA = 5
PATCH = 196
SEQ = 201
EPS = 1e-06
LANE = 128
BF = jnp.bfloat16
F32 = jnp.float32
MESH = pl.DeviceIdType.MESH
ROWS = (((0,), (0,)), ((), ()))
COLS = (((1,), (1,)), ((), ()))


def rope_tables():
    quarter = HD // 4
    theta = (
        2.0
        * math.pi
        * jnp.exp(jnp.arange(quarter, dtype=jnp.float32) * (-4.0 * math.log(100.0) / HD))
    )
    places = jnp.arange(PATCH, dtype=jnp.int32)
    row_pos = ((places // GRID).astype(jnp.float32) + 0.5) * (2.0 / GRID) - 1.0
    col_pos = ((places % GRID).astype(jnp.float32) + 0.5) * (2.0 / GRID) - 1.0
    angles = jnp.concatenate(
        [row_pos[:, None] * theta[None, :], col_pos[:, None] * theta[None, :]], axis=1
    )
    angles = jnp.concatenate([jnp.zeros((EXTRA, HD // 2), jnp.float32), angles], axis=0)
    return (jnp.cos(angles), jnp.sin(angles))


def rotate(vectors, cosines, sines):
    halfway = HD // 2
    leading = vectors[..., :halfway]
    trailing = vectors[..., halfway:]
    cos_b = cosines[:, None, :]
    sin_b = sines[:, None, :]
    return jnp.concatenate(
        [leading * cos_b - trailing * sin_b, leading * sin_b + trailing * cos_b], axis=-1
    )


def greet(n, m=1):
    me = lax.axis_index("tensor")
    you = lax.axis_index("dp")
    barrier = pltpu.get_barrier_semaphore()
    for k in range(1, n):
        pl.semaphore_signal(
            barrier, inc=1, device_id={"tensor": lax.rem(me + k, n)}, device_id_type=MESH
        )
    for k in range(1, m):
        pl.semaphore_signal(
            barrier, inc=1, device_id={"dp": lax.rem(you + k, m)}, device_id_type=MESH
        )
    pl.semaphore_wait(barrier, n + m - 2)


def send(src, dst, send_sem, recv_sem, peer):
    return pltpu.make_async_remote_copy(
        src_ref=src,
        dst_ref=dst,
        send_sem=send_sem,
        recv_sem=recv_sem,
        device_id={"tensor": peer},
        device_id_type=MESH,
    )


def send_dp(src, dst, send_sem, recv_sem, peer):
    return pltpu.make_async_remote_copy(
        src_ref=src,
        dst_ref=dst,
        send_sem=send_sem,
        recv_sem=recv_sem,
        device_id={"dp": peer},
        device_id_type=MESH,
    )


class Hop:
    def __init__(self, k, m, right_src, left_src, right_dst, left_dst, sem):
        you = lax.axis_index("dp")
        z, last = you // 2, m // 2 - 1
        right = send_dp(right_src, right_dst, sem.at[0], sem.at[1], lax.rem(you + 2, m))
        left = send_dp(left_src, left_dst, sem.at[2], sem.at[3], lax.rem(you + m - 2, m))
        self.steps = [
            (right, (z >= k - 1) & (z < last), z >= k),
            (left, (z <= last - k + 1) & (z > 0), z <= last - k),
        ]

    def start(self):
        for copy, sends, _ in self.steps:
            pl.when(sends)(copy.start)

    def wait(self):
        for copy, sends, gets in self.steps:
            pl.when(sends)(copy.wait_send)
            pl.when(gets)(copy.wait_recv)


class End:
    def __init__(self, m, part_ref, right_dst, left_dst, sem):
        you = lax.axis_index("dp")
        z, last = you // 2, m // 2 - 1
        right = send_dp(part_ref.at[last], right_dst, sem.at[0], sem.at[1], lax.rem(you + 2, m))
        left = send_dp(part_ref.at[0], left_dst, sem.at[2], sem.at[3], lax.rem(you + m - 2, m))
        self.steps = [(right, z == 0, z == 1), (left, z == last, z == last - 1)]

    start = Hop.start
    wait = Hop.wait


class Exchange:
    def __init__(self, m, pieces, full_ref, out_ref, ssem, rsem, lsem):
        you = lax.axis_index("dp")
        piece = lax.rem(lax.axis_index("tensor"), pieces)
        self.copies = []
        for k in range(m):
            peer = lax.rem(you + k, m)
            cols = pl.ds(pl.multiple_of((peer * pieces + piece) * LANE, LANE), LANE)
            if k:
                copy = send_dp(
                    full_ref.at[:, cols], out_ref.at[you], ssem.at[k - 1], rsem.at[k - 1], peer
                )
            else:
                copy = pltpu.make_async_copy(full_ref.at[:, cols], out_ref.at[you], lsem)
            self.copies.append(copy)

    def start(self):
        for copy in self.copies:
            copy.start()

    def wait(self):
        for copy in self.copies:
            copy.wait()


def chunks(width, body):
    def step(j, carry):
        body(pl.ds(pl.multiple_of(j * LANE, LANE), LANE))
        return carry

    lax.fori_loop(0, width // LANE, step, 0)


def spread(column, rows):
    return jnp.broadcast_to(column, (rows, LANE))


def beside(me):
    return me + 1 - 2 * lax.rem(me, 2), me + 2 - 4 * (me // 2)


class Gather:
    def __init__(self, n, own_ref, dest, ssem, rsem):
        me = lax.axis_index("tensor")
        w = own_ref.shape[1]
        self.square = n == 4
        if self.square:
            x, y = beside(me)
            half = w // 2
            part = lambda i: own_ref.at[:, i * half:(i + 1) * half]
            to = lambda i, src, owner, at, peer: send(
                src, dest(owner, at * half, half), ssem.at[i], rsem.at[i], peer
            )
            self.copies = [
                to(0, part(0), me, 0, x), to(1, part(1), me, 1, y),
                to(2, part(1), me, 1, x), to(3, part(0), me, 0, y),
            ]
            self.passed = [
                to(4, dest(x, 0, half), x, 0, y), to(5, dest(y, half, half), y, 1, x)
            ]
        else:
            self.copies = [
                send(own_ref, dest(me, 0, w), ssem.at[k - 1], rsem.at[k - 1], lax.rem(me + k, n))
                for k in range(1, n)
            ]

    def start(self):
        for copy in self.copies:
            copy.start()

    def relay(self):
        if self.square:
            for copy, passed in zip(self.copies, self.passed):
                copy.wait_recv()
                passed.start()

    def wait(self):
        if self.square:
            for copy in self.copies:
                copy.wait_send()
            for copy in self.copies[2:]:
                copy.wait_recv()
            wait_all(self.passed)
        else:
            wait_all(self.copies)


class Scatter:
    def __init__(self, n, w, part_ref, slots, come, go, ssem, rsem):
        me = lax.axis_index("tensor")
        self.n, self.w, self.part, self.slots, self.come, self.go = n, w, part_ref, slots, come, go
        self.square = n == 4
        cols = lambda owner, at, size: part_ref.at[:, pl.ds(pl.multiple_of(owner * w + at, LANE), size)]
        if self.square:
            x, y = beside(me)
            far = 3 - me
            half = w // 2
            self.half, self.x, self.y = half, x, y
            to = lambda i, src, dst, peer: send(src, dst, ssem.at[i], rsem.at[i], peer)
            low, high = slice(0, half), slice(half, w)
            self.first = [
                to(0, cols(far, 0, half), come.at[0], x), to(1, cols(far, half, half), come.at[1], y)
            ]
            self.second = [
                to(2, cols(x, 0, half), slots.at[0, :, low], x),
                to(3, cols(y, half, half), slots.at[1, :, high], y),
            ]
            self.third = [
                to(4, go.at[0], slots.at[0, :, high], x), to(5, go.at[1], slots.at[1, :, low], y)
            ]
            self.order = [(far, 0), (far, 1), (x, 0), (y, 1), (x, 1), (y, 0), (me, 0), (me, 1)]
        else:
            self.first = [
                send(cols(lax.rem(me + k, n), 0, w), slots.at[k - 1], ssem.at[k - 1], rsem.at[k - 1],
                     lax.rem(me + k, n))
                for k in range(1, n)
            ]
            self.second = self.third = []

    def start(self):
        for copy in self.first + self.second:
            copy.start()

    def relay(self):
        if self.square:
            half = self.half
            for i, (owner, at) in enumerate(((self.x, half), (self.y, 0))):
                self.first[1 - i].wait_recv()

                def add(cols, i=i, owner=owner, at=at):
                    wide = pl.ds(pl.multiple_of(owner * self.w + at + cols.start, LANE), LANE)
                    self.go[i, :, cols] = (
                        self.part[:, wide].astype(F32) + self.come[1 - i, :, cols].astype(F32)
                    ).astype(BF)

                chunks(half, add)
                self.third[i].start()

    def wait(self):
        if self.square:
            for copy in self.first:
                copy.wait_send()
            wait_all(self.second + self.third)
        else:
            wait_all(self.first)

    def total(self, cols, wide):
        total = self.part[:, wide].astype(F32)
        for k in range(self.slots.shape[0]):
            total = total + self.slots[k, :, cols].astype(F32)
        return total


def scatter_room(n, rows, w):
    count, half = (2, w // 2) if n == 4 else (n - 1, LANE)
    return [
        pltpu.VMEM((count, rows, w), BF), pltpu.VMEM((2, rows, half), BF), pltpu.VMEM((2, rows, half), BF),
        sems(6 if n == 4 else n - 1), sems(6 if n == 4 else n - 1),
    ]


def gather_sems(n):
    return [sems(6 if n == 4 else n - 1)] * 2


def stream(count, fetch, compute):
    fetch(0, 0).start()

    def step(i, carry):
        slot = lax.rem(i, 2)

        @pl.when(i + 1 < count)
        def _():
            fetch(i + 1, 1 - slot).start()

        fetch(i, slot).wait()
        compute(i, slot)
        return carry

    lax.fori_loop(0, count, step, 0)


def wait_all(copies):
    for copy in copies:
        copy.wait()


def row_stats(n, rows, w, all_ref, acc, mean_ref, inv_ref):
    acc[...] = jnp.zeros_like(acc)

    def add(cols):
        total = all_ref[0, :, cols].astype(F32)
        for k in range(1, n):
            total = total + all_ref[k, :, cols].astype(F32)
        acc[...] += total

    chunks(w, add)
    mean_ref[...] = spread(jnp.sum(acc[...], axis=1, keepdims=True) * (1.0 / D), rows)
    acc[...] = jnp.zeros_like(acc)

    def square(cols):
        mean = mean_ref[...]
        total = jnp.zeros_like(mean)
        for k in range(n):
            center = all_ref[k, :, cols].astype(F32) - mean
            total = total + center * center
        acc[...] += total

    chunks(w, square)
    var = jnp.sum(acc[...], axis=1, keepdims=True) * (1.0 / D)
    inv_ref[...] = spread(lax.rsqrt(var + EPS), rows)


def write_act(n, w, all_ref, mean_ref, inv_ref, gain_ref, bias_ref, act_ref):
    def act(cols):
        for k in range(n):
            wide = pl.ds(pl.multiple_of(k * w + cols.start, LANE), LANE)
            center = all_ref[k, :, cols].astype(F32) - mean_ref[...]
            act_ref[:, wide] = (
                center * inv_ref[...] * gain_ref[:, wide] + bias_ref[:, wide]
            ).astype(BF)

    chunks(w, act)


def first_norm_kernel(n, x_ref, gain_ref, bias_ref, act_ref, mean_ref, inv_ref, all_ref, acc, ssem, rsem):
    rows, w = x_ref.shape
    me = lax.axis_index("tensor")
    greet(n)
    dest = lambda owner, at, size: all_ref.at[owner, :, pl.ds(at, size)]
    gather = Gather(n, x_ref, dest, ssem, rsem)
    gather.start()
    all_ref[me] = x_ref[...]
    gather.relay()
    gather.wait()
    row_stats(n, rows, w, all_ref, acc, mean_ref, inv_ref)
    write_act(n, w, all_ref, mean_ref, inv_ref, gain_ref, bias_ref, act_ref)


def second_norm_kernel(
    n, m, pieces, part_ref, x_ref, scale_ref, gain_ref, bias_ref, bgrad_ref, act_one_ref, cot_ref,
    mixed_ref, w_down_ref,
    attn_ref, res_ref, act_ref, mean_ref, inv_ref, hgrad_ref, kact_ref, kcot_ref, *refs,
):
    hops = m // 2 - 1
    rights, lefts, refs = refs[:hops], refs[hops:2 * hops], refs[2 * hops:]
    (slots, come, go, ssem, rsem, own_ref, all_ref, acc, ssem2, rsem2, hsem,
     ass, ars, als, css, crs, cls, wbuf, wsem) = refs
    rows, w = x_ref.shape
    me = lax.axis_index("tensor")
    greet(n, m)
    scatter = Scatter(n, w, part_ref, slots, come, go, ssem, rsem)
    scatter.start()
    line = [
        Hop(k, m, rights[k - 2] if k > 1 else mixed_ref, lefts[k - 2] if k > 1 else mixed_ref,
            rights[k - 1], lefts[k - 1], hsem.at[k - 1])
        for k in range(1, hops + 1)
    ]
    line[0].start()
    sides = [
        Exchange(m, pieces, act_one_ref, kact_ref, ass, ars, als),
        Exchange(m, pieces, cot_ref, kcot_ref, css, crs, cls),
    ]
    for side in sides:
        side.start()
    tile = wbuf.shape[1]
    count = hgrad_ref.shape[1] // tile

    def fetch(i, slot):
        return pltpu.make_async_copy(
            w_down_ref.at[pl.ds(pl.multiple_of(i * tile, tile), tile), :], wbuf.at[slot], wsem.at[slot]
        )

    def compute(i, slot):
        hgrad_ref[:, pl.ds(pl.multiple_of(i * tile, tile), tile)] = lax.dot_general(
            bgrad_ref[...], wbuf[slot], COLS, preferred_element_type=F32
        )

        @pl.when(i == count // 2)
        def _():
            scatter.relay()

    stream(count, fetch, compute)
    scatter.wait()

    def add(cols):
        wide = pl.ds(pl.multiple_of(me * w + cols.start, LANE), LANE)
        total = scatter.total(cols, wide)
        attn_ref[:, cols] = total
        res = x_ref[:, cols].astype(F32) + scale_ref[:, wide] * total
        res_ref[:, cols] = res
        own_ref[:, cols] = res.astype(BF)

    chunks(w, add)
    dest = lambda owner, at, size: all_ref.at[owner, :, pl.ds(at, size)]
    gather = Gather(n, own_ref, dest, ssem2, rsem2)
    gather.start()
    all_ref[me] = own_ref[...]
    line[0].wait()
    if hops > 1:
        line[1].start()
    gather.relay()
    for k in range(1, hops - 1):
        line[k].wait()
        line[k + 1].start()
    gather.wait()
    row_stats(n, rows, w, all_ref, acc, mean_ref, inv_ref)
    write_act(n, w, all_ref, mean_ref, inv_ref, gain_ref, bias_ref, act_ref)
    line[-1].wait()
    for side in sides:
        side.wait()


def norm_back(n, w, load_total, grad_ref, base_ref, mean_ref, inv_ref, gain_ref,
              sums, acc, acc2, stat_own, stats, ssem, rsem, out):
    rows = grad_ref.shape[0]
    me = lax.axis_index("tensor")
    acc[...] = jnp.zeros_like(acc)
    acc2[...] = jnp.zeros_like(acc2)

    def first(cols):
        wide = pl.ds(pl.multiple_of(me * w + cols.start, LANE), LANE)
        total = load_total(cols, wide)
        grad_ref[:, cols] = total
        normed = (base_ref[:, cols].astype(F32) - mean_ref[...]) * inv_ref[...]
        sums[0:1, cols] = jnp.sum(total * normed, axis=0, keepdims=True)
        sums[1:2, cols] = jnp.sum(total, axis=0, keepdims=True)
        scaled = total * gain_ref[:, wide]
        acc[...] += scaled
        acc2[...] += scaled * normed

    chunks(w, first)
    plain = jnp.sum(acc[...], axis=1, keepdims=True)
    cross = jnp.sum(acc2[...], axis=1, keepdims=True)
    lane = lax.broadcasted_iota(jnp.int32, (rows, LANE), 1)
    stat_own[...] = jnp.where(lane == 0, plain, cross)
    copies = [
        send(stat_own, stats.at[me], ssem.at[k - 1], rsem.at[k - 1], lax.rem(me + k, n))
        for k in range(1, n)
    ]
    for copy in copies:
        copy.start()
    wait_all(copies)
    both = stat_own[...]
    for k in range(1, n):
        both = both + stats[lax.rem(me + k, n)]
    acc[...] = spread(both[:, 0:1] * (1.0 / D), rows)
    acc2[...] = spread(both[:, 1:2] * (1.0 / D), rows)

    def second(cols):
        wide = pl.ds(pl.multiple_of(me * w + cols.start, LANE), LANE)
        normed = (base_ref[:, cols].astype(F32) - mean_ref[...]) * inv_ref[...]
        scaled = grad_ref[:, cols] * gain_ref[:, wide]
        out(cols, wide, inv_ref[...] * (scaled - acc[...] - normed * acc2[...]))

    chunks(w, second)


def second_back_kernel(
    n, m, grads_ref, cot_ref, res_ref, attn_ref, mean_ref, inv_ref, gain_ref, scale_ref,
    right_ref, left_ref, gu_ref, w_ref, rgrad_ref, agrad_ref, sums_ref, gu_right, gu_left, *refs,
):
    hops = m // 2 - 1
    rights = (right_ref,) + refs[:hops - 1]
    lefts = (left_ref,) + refs[hops - 1:2 * hops - 2]
    (part_ref, slots, come, go, ssem, rsem, grad_ref, own_ref, acc, acc2, stat_own, stats,
     ssem2, rsem2, ssem3, rsem3, lsem, hsem, gsem, wbuf, wsem) = refs[2 * hops - 2:]
    w = cot_ref.shape[1]
    me = lax.axis_index("tensor")
    greet(n, m)
    line = [
        Hop(k, m, rights[k - 2], lefts[k - 2], rights[k - 1], lefts[k - 1], hsem.at[k - 2])
        for k in range(2, hops + 1)
    ]
    line[0].start()
    first = End(m, gu_ref, gu_right, gu_left, gsem)
    first.start()
    scatter = Scatter(n, w, part_ref, slots, come, go, ssem, rsem)
    tile = wbuf.shape[2]
    inner = w_ref.shape[2]
    count = D // tile

    def spot(i):
        if not scatter.square:
            return pl.ds(pl.multiple_of(i * tile, LANE), tile)
        at = 0
        for k, (owner, half) in enumerate(scatter.order):
            at = at + jnp.where(i == k, owner * w + half * tile, 0)
        return pl.ds(pl.multiple_of(at, LANE), tile)

    def fetch(i, slot):
        return pltpu.make_async_copy(w_ref.at[:, spot(i), :], wbuf.at[slot], wsem.at[slot])

    def compute(i, slot):
        total = None
        for j in range(w_ref.shape[0]):
            term = lax.dot_general(
                grads_ref[:, j * inner:(j + 1) * inner], wbuf[slot, j], COLS,
                preferred_element_type=F32,
            )
            total = term if total is None else total + term
        part_ref[:, spot(i)] = total.astype(BF)
        if scatter.square:
            for k, copy in enumerate(scatter.first + scatter.second):
                pl.when(i == k)(copy.start)
            pl.when(i == 5)(scatter.relay)

    stream(count, fetch, compute)
    if not scatter.square:
        scatter.start()
    scatter.wait()
    sums_ref[...] = jnp.zeros_like(sums_ref)

    def out(cols, wide, back):
        res_grad = cot_ref[:, cols].astype(F32) + back
        rgrad_ref[:, cols] = res_grad
        sums_ref[2:3, cols] = jnp.sum(res_grad * attn_ref[:, cols], axis=0, keepdims=True)
        own_ref[:, cols] = (scale_ref[:, wide] * res_grad).astype(BF)

    norm_back(n, w, scatter.total, grad_ref, res_ref, mean_ref, inv_ref, gain_ref,
              sums_ref, acc, acc2, stat_own, stats, ssem2, rsem2, out)
    dest = lambda owner, at, size: agrad_ref.at[:, pl.ds(pl.multiple_of(owner * w + at, LANE), size)]
    gather = Gather(n, own_ref, dest, ssem3, rsem3)
    gather.start()
    local = pltpu.make_async_copy(own_ref, dest(me, 0, w), lsem)
    local.start()
    gather.relay()
    for k in range(len(line)):
        line[k].wait()
        if k + 1 < len(line):
            line[k + 1].start()
    local.wait()
    gather.wait()
    first.wait()


def first_back_kernel(
    n, grad_in, rgrad_ref, x_ref, mean_ref, inv_ref, gain_ref, small_ref,
    igrad_ref, sums,
    grad_ref, acc, acc2, stat_own, stats, ssem, rsem,
):
    w = x_ref.shape[1]
    greet(n)
    sums[...] = small_ref[...]

    def load_total(cols, wide):
        return grad_in[:, cols].astype(F32)

    def out(cols, wide, back):
        igrad_ref[:, cols] = rgrad_ref[:, cols] + back

    norm_back(n, w, load_total, grad_ref, x_ref, mean_ref, inv_ref, gain_ref,
              sums, acc, acc2, stat_own, stats, ssem, rsem, out)


def mate_of(you):
    return you + 1 - 2 * lax.rem(you, 2)


def pair_grad_kernel(
    m, act_ref, gate_ref, up_ref, hidden_ref, out_ref, right_ref, left_ref,
    acts, mates, gates, ups, flip, asem, arem, gsem, grem, lsem, hsem,
):
    line = m // 2
    you = lax.axis_index("dp")
    core, mate = lax.rem(you, 2), mate_of(you)
    width = acts.shape[-1]
    tile = 512
    greet(1, m)
    hop = Hop(1, m, hidden_ref, hidden_ref, right_ref, left_ref, hsem)
    copies = [
        send_dp(gate_ref, gates, gsem.at[0], grem.at[0], mate),
        send_dp(up_ref, ups, gsem.at[1], grem.at[1], mate),
    ]
    locals_ = []
    for k in range(line):
        theirs = pl.ds(pl.multiple_of((2 * k + 1 - core) * width, LANE), width)
        ours = pl.ds(pl.multiple_of((2 * k + core) * width, LANE), width)
        copies.append(send_dp(act_ref.at[:, theirs], mates.at[k], asem.at[k], arem.at[k], mate))
        locals_.append(pltpu.make_async_copy(act_ref.at[:, ours], acts.at[k], lsem.at[k]))
    for copy in locals_ + copies:
        copy.start()
    hop.start()
    for copy in locals_:
        copy.wait()
    for k in range(line):
        flip[0, k] = acts[k].T
    for copy in copies:
        copy.wait()
    for k in range(line):
        flip[1, k] = mates[k].T
    for j, (near, far) in enumerate(((gate_ref, gates), (up_ref, ups))):

        def step(i, carry):
            cols = pl.ds(pl.multiple_of(i * tile, tile), tile)
            for k in range(line):
                out_ref[k, j, :, cols] = (
                    jnp.dot(flip[0, k], near[:, cols], preferred_element_type=F32)
                    + jnp.dot(flip[1, k], far[:, cols], preferred_element_type=F32)
                ).astype(BF)
            return carry

        lax.fori_loop(0, gate_ref.shape[1] // tile, step, 0)
    hop.wait()


class SmallSums:
    def __init__(self, n, m, sums, out, parts, total, dss, drs, tss, trs):
        self.out, self.sums, self.parts, self.total = out, sums, parts, total
        me, you = lax.axis_index("tensor"), lax.axis_index("dp")
        w = sums.shape[1]
        self.m, self.you = m, you
        self.mine = pl.ds(pl.multiple_of(me * w, w), w)
        self.dp = [
            send_dp(sums, parts.at[you], dss.at[k - 1], drs.at[k - 1], lax.rem(you + k, m))
            for k in range(1, m)
        ]
        self.tensor = [
            send(total, out.at[:, self.mine], tss.at[k - 1], trs.at[k - 1], lax.rem(me + k, n))
            for k in range(1, n)
        ]

    def start(self):
        for copy in self.dp:
            copy.start()

    def finish(self):
        self.parts[self.you] = self.sums[...]
        wait_all(self.dp)
        total = self.parts[0]
        for k in range(1, self.m):
            total = total + self.parts[k]
        self.total[...] = total
        for copy in self.tensor:
            copy.start()
        self.out[:, self.mine] = total
        wait_all(self.tensor)


def gathered_grad_kernel(m, turned, first, last, n, *refs):
    hops = m // 2 - 1
    you = lax.axis_index("dp")
    core, mate, z = lax.rem(you, 2), mate_of(you), you // 2
    todo = []
    refs = list(refs)
    for k in range(first, last + 1):
        if k == 0:
            todo.append((None, refs.pop(0), z))
        else:
            todo.append((z >= k, refs.pop(0), z - k))
            todo.append((z <= hops - k, refs.pop(0), z + k))
    side_ref = refs.pop(0)
    before = refs.pop(0) if first else None
    sums = refs.pop(0) if n else None
    out_ref = refs.pop(0)
    small_ref = refs.pop(0) if n else None
    blocks, flip, lsem, ssem, rsem = refs[:5]
    small = SmallSums(n, m, sums, small_ref, *refs[5:]) if n else None
    greet(max(n, 1), m)
    if small:
        small.start()
    copies = []
    for at, (cond, src, chip) in enumerate(todo):
        near = pltpu.make_async_copy(src, blocks.at[at, core], lsem.at[at])
        far = send_dp(src, blocks.at[at, core], ssem.at[at], rsem.at[at], mate)
        copies.append((cond, near, far))

    def when(cond, body):
        body() if cond is None else pl.when(cond)(body)

    def go(near, far):
        near.start()
        far.start()

    def done(near, far):
        near.wait()
        far.wait()

    def turn(at, chip):
        for c in range(2):
            flip[at, c] = side_ref[2 * chip + c].T

    for cond, near, far in copies:
        when(cond, functools.partial(go, near, far))
    for at, (cond, _, chip) in enumerate(todo):
        when(cond, functools.partial(turn, at, chip))
    for cond, near, far in copies:
        when(cond, functools.partial(done, near, far))
    tile = 512
    parts, width = out_ref.shape[0], blocks.shape[-1]
    if before is not None:
        out_ref[...] = before[...]
    for at, (cond, _, chip) in enumerate(todo):
        for j in range(parts):

            def step(i, carry, at=at, j=j):
                cols = pl.ds(pl.multiple_of(i * tile, tile), tile)
                total = jnp.dot(
                    flip[at, 0], blocks[at, 0, j, :, cols], preferred_element_type=F32
                ) + jnp.dot(flip[at, 1], blocks[at, 1, j, :, cols], preferred_element_type=F32)
                if turned:
                    if first or at:
                        out_ref[j, cols, :] += total.T
                    else:
                        out_ref[j, cols, :] = total.T
                elif first or at:
                    out_ref[j, :, cols] += total
                else:
                    out_ref[j, :, cols] = total
                return carry

            def run(step=step):
                lax.fori_loop(0, width // tile, step, 0)

            when(cond, run)
    if small:
        small.finish()


def qkv_kernel(act_ref, w_ref, cos_ref, sin_ref, out_ref):
    raw = jnp.dot(act_ref[...], w_ref[...], preferred_element_type=F32)
    part = pl.program_id(0)

    @pl.when(part < 2)
    def _():
        for h in range(raw.shape[1] // HD):
            cols = slice(h * HD, (h + 1) * HD)
            t = raw[:, cols]
            out_ref[:, cols] = (
                t * cos_ref[...] + pltpu.roll(t, HD // 2, 1) * sin_ref[...]
            ).astype(BF)

    @pl.when(part == 2)
    def _():
        out_ref[...] = raw.astype(BF)


def qkv_matmul(act, w_j, cos2, sin2):
    rows = act.shape[0]
    inner = w_j.shape[2]
    tile = min(512, inner)
    return pl.pallas_call(
        qkv_kernel,
        grid=(3, inner // tile),
        out_shape=jax.ShapeDtypeStruct((3, rows, inner), BF),
        in_specs=[
            pl.BlockSpec((rows, D), lambda j, i: (0, 0)),
            pl.BlockSpec((None, D, tile), lambda j, i: (j, 0, i)),
            pl.BlockSpec((rows, HD), lambda j, i: (0, 0)),
            pl.BlockSpec((rows, HD), lambda j, i: (0, 0)),
        ],
        out_specs=pl.BlockSpec((None, rows, tile), lambda j, i: (j, 0, i)),
        compiler_params=pltpu.CompilerParams(vmem_limit_bytes=40 << 20),
        cost_estimate=pl.CostEstimate(
            flops=2 * rows * D * 3 * inner, bytes_accessed=6 * D * inner, transcendentals=0
        ),
    )(act, w_j, cos2, sin2)


def attention_probs(q, k, same):
    scores = lax.dot_general(k, q, COLS, preferred_element_type=F32) * (HD ** (-0.5))
    scores = jnp.where(same, scores, -jnp.inf)
    top = jnp.max(scores, axis=0, keepdims=True)
    weight = jnp.exp(scores - top)
    return weight / jnp.sum(weight, axis=0, keepdims=True)


def same_image(rows):
    one = lax.broadcasted_iota(jnp.int32, (rows, rows), 0)
    two = lax.broadcasted_iota(jnp.int32, (rows, rows), 1)
    image = lambda i: sum((i >= SEQ * k).astype(jnp.int32) for k in range(1, rows // SEQ))
    return image(one) == image(two)


def attention_kernel(qkv_ref, w_ref, mixed_ref, part_ref):
    rows, inner = mixed_ref.shape

    def head(h, carry):
        cols = pl.ds(pl.multiple_of(h * HD, HD), HD)
        probs = attention_probs(qkv_ref[0, :, cols], qkv_ref[1, :, cols], same_image(rows))
        value = qkv_ref[2, :, cols].astype(F32).T.astype(BF)
        mixed = jnp.dot(value, probs.astype(BF), preferred_element_type=F32)
        mixed_ref[:, cols] = mixed.T.astype(BF)
        return carry

    lax.fori_loop(0, inner // HD, head, 0)

    def tile(i, carry):
        cols = pl.ds(pl.multiple_of(i * 512, 512), 512)
        part_ref[:, cols] = jnp.dot(
            mixed_ref[...], w_ref[:, cols], preferred_element_type=F32
        ).astype(BF)
        return carry

    lax.fori_loop(0, D // 512, tile, 0)


def attention_back_kernel(
    m, pieces, agrad_ref, w_ref, qkv_ref, cos_ref, sin_ref, full_ref, out_ref, kattn_ref,
    mgrad, ass, ars, als,
):
    rows, inner = mgrad.shape
    greet(1, m)
    side = Exchange(m, pieces, full_ref, kattn_ref, ass, ars, als)
    side.start()
    step = min(256, inner)

    def tile(i, carry):
        cols = pl.ds(pl.multiple_of(i * step, step), step)
        mgrad[:, cols] = lax.dot_general(
            agrad_ref[...], w_ref[cols, :], COLS, preferred_element_type=F32
        ).astype(BF)
        return carry

    lax.fori_loop(0, inner // step, tile, 0)

    def back(t):
        return t * cos_ref[...] - pltpu.roll(t, HD // 2, 1) * sin_ref[...]

    def head(h, carry):
        cols = pl.ds(pl.multiple_of(h * HD, HD), HD)
        q, k, v = qkv_ref[0, :, cols], qkv_ref[1, :, cols], qkv_ref[2, :, cols]
        grad = mgrad[:, cols]
        probs = attention_probs(q, k, same_image(rows))
        prob_grad = lax.dot_general(v, grad, COLS, preferred_element_type=F32)
        delta = jnp.sum(probs * prob_grad, axis=0, keepdims=True)
        score_grad = (probs * (prob_grad - delta)).astype(BF)
        scale = HD ** (-0.5)
        flipped = k.astype(F32).T.astype(BF)
        q_grad = jnp.dot(flipped, score_grad, preferred_element_type=F32).T * scale
        k_grad = jnp.dot(score_grad, q, preferred_element_type=F32) * scale
        out_ref[0, :, cols] = back(q_grad).astype(BF)
        out_ref[1, :, cols] = back(k_grad).astype(BF)
        out_ref[2, :, cols] = jnp.dot(
            probs.astype(BF), grad, preferred_element_type=F32
        ).astype(BF)
        return carry

    lax.fori_loop(0, inner // HD, head, 0)
    side.wait()


def plain(kernel, outs, args, scratch=(), micros=15):
    return list(pl.pallas_call(
        kernel,
        out_shape=[jax.ShapeDtypeStruct(*o) for o in outs],
        in_specs=[vm()] * len(args),
        out_specs=[vm()] * len(outs),
        scratch_shapes=list(scratch),
        compiler_params=pltpu.CompilerParams(vmem_limit_bytes=48 << 20),
        cost_estimate=pl.CostEstimate(
            flops=micros * 100_000_000, bytes_accessed=800_000, transcendentals=0
        ),
    )(*args))


def back_kernel(g_ref, w_ref, out_ref):
    total = None
    for j in range(g_ref.shape[0]):
        term = lax.dot_general(g_ref[j], w_ref[j], COLS, preferred_element_type=F32)
        total = term if total is None else total + term
    out_ref[...] = total.astype(BF)


def back_matmul(grads, w_j):
    parts, rows, inner = grads.shape
    tile = 512
    return pl.pallas_call(
        back_kernel,
        grid=(D // tile,),
        out_shape=jax.ShapeDtypeStruct((rows, D), BF),
        in_specs=[
            pl.BlockSpec((parts, rows, inner), lambda i: (0, 0, 0)),
            pl.BlockSpec((parts, tile, inner), lambda i: (0, i, 0)),
        ],
        out_specs=pl.BlockSpec((rows, tile), lambda i: (0, i)),
        compiler_params=pltpu.CompilerParams(vmem_limit_bytes=40 << 20),
        cost_estimate=pl.CostEstimate(
            flops=rows * D * parts * inner * 100 // 500,
            bytes_accessed=800_000,
            transcendentals=0,
        ),
    )(grads, w_j)


def vm():
    return pl.BlockSpec(memory_space=pltpu.VMEM)


def hb():
    return pl.BlockSpec(memory_space=pltpu.HBM)


def sems(*shape):
    return pltpu.SemaphoreType.DMA(shape)


def call(kernel, ident, outs, scratch, args, micros=30):
    shapes = [jax.ShapeDtypeStruct(o[0], o[1]) for o in outs]
    return list(pl.pallas_call(
        kernel,
        out_shape=shapes,
        in_specs=[hb() if a[1] else vm() for a in args],
        out_specs=[hb() if len(o) > 2 else vm() for o in outs],
        scratch_shapes=scratch,
        compiler_params=pltpu.CompilerParams(
            collective_id=ident, has_side_effects=True, vmem_limit_bytes=56 << 20
        ),
        cost_estimate=pl.CostEstimate(
            flops=micros * 100_000_000, bytes_accessed=800_000, transcendentals=0
        ),
    )(*[a[0] for a in args]))


class LineReduce:
    def __init__(self, part, right, left, m):
        self.part, self.line, self.t = part, m // 2, 2
        self.z = lax.axis_index("dp") // 2
        self.right = jnp.where(self.z >= 1, right.astype(F32), 0.0)
        self.left = jnp.where(self.z <= self.line - 2, left.astype(F32), 0.0)

    def take(self, i):
        i = jnp.clip(i, 0, self.line - 1)
        return lax.dynamic_index_in_dim(self.part, i, 0, keepdims=False).astype(F32)

    def step(self, after):
        line, t = self.line, self.t
        right = (self.take(self.z + line - t) + self.right).astype(BF)
        left = (self.take(self.z - line + t) + self.left).astype(BF)
        right, left = lax.optimization_barrier((right, left) + tuple(after))[:2]
        self.given = right, left
        self.right = lax.ppermute(
            right, "dp", [(2 * i + c, 2 * i + 2 + c) for i in range(t) for c in range(2)]
        ).astype(F32)
        self.left = lax.ppermute(
            left, "dp",
            [(2 * i + c, 2 * i - 2 + c) for i in range(line - t, line) for c in range(2)],
        ).astype(F32)
        self.t += 1

    def finish(self, after):
        while self.t < self.line:
            self.step(after)
        return self.take(self.z) + self.right + self.left


def line_gather(own, m, meanwhile):
    line = m // 2
    right = left = own
    rights, lefts = [], []
    for k in range(1, line):
        right = lax.ppermute(right, "dp", [(i, i + 2) for i in range(2 * (k - 1), m - 2)])
        left = lax.ppermute(left, "dp", [(i, i - 2) for i in range(2, m - 2 * (k - 1))])
        if k in meanwhile and k < line - 1:
            right, left = lax.optimization_barrier((right, left) + meanwhile[k](right, left))[:2]
        rights.append(right)
        lefts.append(left)
    return rights, lefts


def local(
    tokens_in, ln1_gain, ln1_bias, w_qkv, w_out, scale_attn, ln2_gain, ln2_bias, w_gu, w_down,
    scale_mlp, out_cotangent, *, n, m,
):
    rows, w = tokens_in.shape
    images = rows // SEQ
    inner = w_qkv.shape[2]
    heads = inner // HD
    hidden_width = w_gu.shape[2]
    scale = HD ** (-0.5)
    line = m // 2
    hops = line - 1
    shard = D // m
    pieces = min(n, shard // LANE)
    cosines, sines = rope_tables()
    cos2 = jnp.tile(jnp.concatenate([cosines, cosines], axis=1), (images, 1))
    sin2 = jnp.tile(jnp.concatenate([-sines, sines], axis=1), (images, 1))
    wide = (rows, n * w)
    own = (rows, w)
    lanes = (rows, LANE)
    row = lambda v: v.reshape(1, D)
    V = lambda *a: [(x, False) for x in a]
    H = lambda *a: [(x, True) for x in a]

    w_j = jnp.transpose(w_qkv, (1, 0, 2))
    gu_j = lax.optimization_barrier(jnp.transpose(w_gu, (1, 0, 2)))

    act_one, mean_one, inv_one = call(
        functools.partial(first_norm_kernel, n), 1,
        [(wide, BF), (lanes, F32), (lanes, F32)],
        [pltpu.VMEM((n,) + own, BF), pltpu.VMEM(lanes, F32)] + gather_sems(n),
        V(tokens_in, row(ln1_gain), row(ln1_bias)), 50,
    )
    cot_late, act_one = lax.optimization_barrier((out_cotangent, act_one))
    cot_all = lax.all_gather(cot_late, "tensor", axis=1, tiled=True)
    branch_grad = (scale_mlp * cot_all.astype(F32)).astype(BF)
    qkv = qkv_matmul(act_one, w_j, cos2, sin2)
    mixed, attn_part = plain(
        attention_kernel, [((rows, inner), BF), (wide, BF)], (qkv, w_out)
    )
    tile = min(512, hidden_width)
    outs = call(
        functools.partial(second_norm_kernel, n, m, pieces), 2,
        [(own, F32), (own, F32), (wide, BF), (lanes, F32), (lanes, F32), ((rows, hidden_width), F32)]
        + [((m, rows, LANE), BF, True)] * 2 + [((rows, inner), BF, True)] * (2 * hops),
        scatter_room(n, rows, w)
        + [pltpu.VMEM(own, BF), pltpu.VMEM((n,) + own, BF), pltpu.VMEM(lanes, F32)]
        + gather_sems(n) + [sems(hops, 4)]
        + [sems(m - 1), sems(m - 1), pltpu.SemaphoreType.DMA] * 2
        + [pltpu.VMEM((2, tile, D), BF), sems(2)],
        V(attn_part, tokens_in, row(scale_attn), row(ln2_gain), row(ln2_bias), branch_grad)
        + H(act_one, branch_grad, mixed, w_down), 80,
    )
    attn_sum, residual, act_two, mean_two, inv_two, hidden_grad, kact, kcot = outs[:8]
    mixed_right, mixed_left = outs[8:8 + hops], outs[8 + hops:]
    side = lambda k: lax.all_gather(k, "tensor", axis=2, tiled=True)[:, :, :shard]
    side_act, side_cot = side(kact), side(kcot)

    gate = jnp.dot(act_two, gu_j[0], preferred_element_type=F32)
    up = jnp.dot(act_two, gu_j[1], preferred_element_type=F32)
    sig = jax.nn.sigmoid(gate)
    hidden = (gate * sig * up).astype(BF)
    gate_grad = (hidden_grad * up * sig * (1.0 + gate * (1.0 - sig))).astype(BF)
    up_grad = (hidden_grad * gate * sig).astype(BF)
    block = (rows, hidden_width)
    gu_part, hidden_r, hidden_l = call(
        functools.partial(pair_grad_kernel, m), 3,
        [((line, 2, shard, hidden_width), BF), (block, BF, True), (block, BF, True)],
        [pltpu.VMEM((line, rows, shard), BF), pltpu.VMEM((line, rows, shard), BF),
         pltpu.VMEM(block, BF), pltpu.VMEM(block, BF), pltpu.VMEM((2, line, shard, rows), BF),
         sems(line), sems(line), sems(2), sems(2), sems(line), sems(4)],
        H(act_two) + V(gate_grad, up_grad) + H(hidden), 40,
    )
    gu_grads = jnp.concatenate([gate_grad, up_grad], axis=1)
    tile = w // 2 if n == 4 else min(512, w)
    outs = call(
        functools.partial(second_back_kernel, n, m), 4,
        [(own, F32), (wide, BF), ((8, w), F32)] + [(gu_part.shape[1:], BF, True)] * 2
        + [(block, BF, True)] * (2 * hops - 2),
        [pltpu.VMEM(wide, BF)] + scatter_room(n, rows, w)
        + [pltpu.VMEM(own, F32), pltpu.VMEM(own, BF),
         pltpu.VMEM(lanes, F32), pltpu.VMEM(lanes, F32), pltpu.VMEM(lanes, F32),
         pltpu.VMEM((n,) + lanes, F32)] + [sems(n - 1)] * 2 + gather_sems(n)
        + [pltpu.SemaphoreType.DMA, sems(hops - 1, 4), sems(4)]
        + [pltpu.VMEM((2, 2, tile, hidden_width), BF), sems(2)],
        V(gu_grads, out_cotangent, residual, attn_sum, mean_two, inv_two, row(ln2_gain), row(scale_attn))
        + H(hidden_r, hidden_l, gu_part, gu_j), 80,
    )
    res_grad, attn_grad, sums_two, gu_right, gu_left = outs[:5]
    hidden_right = [hidden_r] + outs[5:4 + hops]
    hidden_left = [hidden_l] + outs[4 + hops:]
    gu_line = LineReduce(gu_part, gu_right, gu_left, m)
    raw_grad, kattn = call(
        functools.partial(attention_back_kernel, m, pieces), 5,
        [((3, rows, inner), BF), ((m, rows, LANE), BF, True)],
        [pltpu.VMEM((rows, inner), BF), sems(m - 1), sems(m - 1), pltpu.SemaphoreType.DMA],
        V(attn_grad, w_out, qkv, cos2, sin2) + H(attn_grad), 25,
    )
    side_attn = side(kattn)
    def gathered(ident, mine, rights, lefts, sides, turned, first=0, last=hops, before=None, sums=None):
        parts, _, width = mine.shape
        shape = (parts, width, shard) if turned else (parts, shard, width)
        small = sums is not None
        blocks = []
        for k in range(first, last + 1):
            blocks += [rights[k - 1], lefts[k - 1]] if k else [mine]
        count = len(blocks)
        outs = call(
            functools.partial(gathered_grad_kernel, m, turned, first, last, n if small else 0), ident,
            [(shape, F32)] + ([((8, n * w), F32)] if small else []),
            [pltpu.VMEM((count, 2) + mine.shape, BF), pltpu.VMEM((count, 2, shard, rows), BF),
             sems(count), sems(count), sems(count)]
            + ([pltpu.VMEM((m, 8, w), F32), pltpu.VMEM((8, w), F32)]
               + [sems(m - 1)] * 2 + [sems(n - 1)] * 2 if small else []),
            H(*blocks) + V(sides) + (V(before) if first else []) + (V(sums) if small else []), 30,
        )
        return outs if small else outs[0]

    lead = lambda arrays: [a[None] for a in arrays]
    done = {}

    def after_one(right, left):
        part = back_matmul(raw_grad, w_j)
        done["grad"] = lax.psum_scatter(part, "tensor", scatter_dimension=1, tiled=True)
        return (part,)

    def after_two(right, left):
        gu_line.step((right, left))
        late = lax.optimization_barrier((side_cot,) + gu_line.given)
        down = gathered(6, hidden[None], lead(hidden_right), lead(hidden_left), late[0], True)[0]
        down, late = lax.optimization_barrier((down, hidden))
        part = jnp.dot(late, w_down, preferred_element_type=F32).astype(BF)
        done["branch"] = lax.psum_scatter(part, "tensor", scatter_dimension=1, tiled=True)
        done["down"], done["part"] = down, part
        return ()

    raw_right, raw_left = line_gather(raw_grad, m, {1: after_one, 2: after_two})
    act_one_grad, down_sum = done["grad"], done["down"]
    branch = done["branch"].astype(F32)
    proj_sum = gathered(7, mixed[None], lead(mixed_right), lead(mixed_left), side_attn, True)[0]
    gu_sum = gu_line.finish((raw_right[-1], raw_left[-1], down_sum, proj_sum, done["part"]))

    own_cols = lambda v: lax.dynamic_slice_in_dim(v, lax.axis_index("tensor") * w, w, 0)
    layer_out = residual + own_cols(scale_mlp) * branch
    sums_mlp = jnp.sum(out_cotangent.astype(F32) * branch, axis=0, keepdims=True)
    small = jnp.concatenate(
        [jnp.zeros((2, w), F32), sums_two[0:3], sums_mlp, jnp.zeros((2, w), F32)], axis=0
    )
    input_grad, sums = call(
        functools.partial(first_back_kernel, n), 9,
        [(own, F32), ((8, w), F32)],
        [pltpu.VMEM(own, F32),
         pltpu.VMEM(lanes, F32), pltpu.VMEM(lanes, F32), pltpu.VMEM(lanes, F32),
         pltpu.VMEM((n,) + lanes, F32)] + [sems(n - 1)] * 2,
        V(act_one_grad, res_grad, tokens_in, mean_one, inv_one, row(ln1_gain), small), 20,
    )
    qkv_part = gathered(8, raw_grad, raw_right, raw_left, side_act, False, 0, hops - 1)
    qkv_sum, small_sums = gathered(
        10, raw_grad, raw_right, raw_left, side_act, False, hops, hops, qkv_part, sums
    )
    return (
        layer_out,
        input_grad,
        small_sums[0],
        small_sums[1],
        jnp.transpose(qkv_sum, (1, 0, 2)),
        proj_sum,
        small_sums[4],
        small_sums[2],
        small_sums[3],
        jnp.transpose(gu_sum, (1, 0, 2)),
        down_sum,
        small_sums[5],
    )


def solution(mesh):
    placed = (
        P("dp", "tensor"),
        P(),
        P(),
        P(None, None, "tensor"),
        P("tensor", None),
        P(),
        P(),
        P(),
        P(None, None, "tensor"),
        P("tensor", None),
        P(),
        P("dp", "tensor"),
    )
    return jax.shard_map(
        functools.partial(local, n=mesh.shape["tensor"], m=mesh.shape["dp"]),
        mesh=mesh,
        in_specs=placed,
        out_specs=(
            P("dp", "tensor"),
            P("dp", "tensor"),
            P(),
            P(),
            P("dp", None, "tensor"),
            P("tensor", "dp"),
            P(),
            P(),
            P(),
            P("dp", None, "tensor"),
            P("tensor", "dp"),
            P(),
        ),
        check_vma=False,
    )
```

```python
import functools
import math

import jax
import jax.numpy as jnp
from jax import lax
from jax.experimental import pallas as pl
from jax.experimental.pallas import tpu as pltpu
from jax.sharding import PartitionSpec as P

D = 4096
HD = 128
GRID = 14
EXTRA = 5
PATCH = 196
SEQ = 201
EPS = 1e-06
LANE = 128
BF = jnp.bfloat16
F32 = jnp.float32
MESH = pl.DeviceIdType.MESH
ROWS = (((0,), (0,)), ((), ()))
COLS = (((1,), (1,)), ((), ()))


def rope_tables():
    quarter = HD // 4
    theta = (
        2.0
        * math.pi
        * jnp.exp(jnp.arange(quarter, dtype=jnp.float32) * (-4.0 * math.log(100.0) / HD))
    )
    places = jnp.arange(PATCH, dtype=jnp.int32)
    row_pos = ((places // GRID).astype(jnp.float32) + 0.5) * (2.0 / GRID) - 1.0
    col_pos = ((places % GRID).astype(jnp.float32) + 0.5) * (2.0 / GRID) - 1.0
    angles = jnp.concatenate(
        [row_pos[:, None] * theta[None, :], col_pos[:, None] * theta[None, :]], axis=1
    )
    angles = jnp.concatenate([jnp.zeros((EXTRA, HD // 2), jnp.float32), angles], axis=0)
    return (jnp.cos(angles), jnp.sin(angles))


def rotate(vectors, cosines, sines):
    halfway = HD // 2
    leading = vectors[..., :halfway]
    trailing = vectors[..., halfway:]
    cos_b = cosines[:, None, :]
    sin_b = sines[:, None, :]
    return jnp.concatenate(
        [leading * cos_b - trailing * sin_b, leading * sin_b + trailing * cos_b], axis=-1
    )


def greet(n, m=1):
    me = lax.axis_index("tensor")
    you = lax.axis_index("dp")
    barrier = pltpu.get_barrier_semaphore()
    for k in range(1, n):
        pl.semaphore_signal(
            barrier, inc=1, device_id={"tensor": lax.rem(me + k, n)}, device_id_type=MESH
        )
    for k in range(1, m):
        pl.semaphore_signal(
            barrier, inc=1, device_id={"dp": lax.rem(you + k, m)}, device_id_type=MESH
        )
    pl.semaphore_wait(barrier, n + m - 2)


def send(src, dst, send_sem, recv_sem, peer):
    return pltpu.make_async_remote_copy(
        src_ref=src,
        dst_ref=dst,
        send_sem=send_sem,
        recv_sem=recv_sem,
        device_id={"tensor": peer},
        device_id_type=MESH,
    )


def send_dp(src, dst, send_sem, recv_sem, peer):
    return pltpu.make_async_remote_copy(
        src_ref=src,
        dst_ref=dst,
        send_sem=send_sem,
        recv_sem=recv_sem,
        device_id={"dp": peer},
        device_id_type=MESH,
    )


class Hop:
    def __init__(self, k, m, right_src, left_src, right_dst, left_dst, sem):
        you = lax.axis_index("dp")
        z, last = you // 2, m // 2 - 1
        right = send_dp(right_src, right_dst, sem.at[0], sem.at[1], lax.rem(you + 2, m))
        left = send_dp(left_src, left_dst, sem.at[2], sem.at[3], lax.rem(you + m - 2, m))
        self.steps = [
            (right, (z >= k - 1) & (z < last), z >= k),
            (left, (z <= last - k + 1) & (z > 0), z <= last - k),
        ]

    def start(self):
        for copy, sends, _ in self.steps:
            pl.when(sends)(copy.start)

    def wait(self):
        for copy, sends, gets in self.steps:
            pl.when(sends)(copy.wait_send)
            pl.when(gets)(copy.wait_recv)


class End:
    def __init__(self, m, part_ref, at, right_dst, left_dst, sem):
        you = lax.axis_index("dp")
        z, last = you // 2, m // 2 - 1
        some = pl.ds(at, right_dst.shape[1])
        right = send_dp(
            part_ref.at[last, :, some], right_dst, sem.at[0], sem.at[1], lax.rem(you + 2, m)
        )
        left = send_dp(
            part_ref.at[0, :, some], left_dst, sem.at[2], sem.at[3], lax.rem(you + m - 2, m)
        )
        self.steps = [(right, z == 0, z == 1), (left, z == last, z == last - 1)]

    start = Hop.start
    wait = Hop.wait


class Exchange:
    def __init__(self, m, pieces, full_ref, out_ref, ssem, rsem, lsem):
        you = lax.axis_index("dp")
        piece = lax.rem(lax.axis_index("tensor"), pieces)
        self.copies = []
        for k in range(m):
            peer = lax.rem(you + k, m)
            cols = pl.ds(pl.multiple_of((peer * pieces + piece) * LANE, LANE), LANE)
            if k:
                copy = send_dp(
                    full_ref.at[:, cols], out_ref.at[you], ssem.at[k - 1], rsem.at[k - 1], peer
                )
            else:
                copy = pltpu.make_async_copy(full_ref.at[:, cols], out_ref.at[you], lsem)
            self.copies.append(copy)

    def start(self):
        for copy in self.copies:
            copy.start()

    def wait(self):
        for copy in self.copies:
            copy.wait()


def chunks(width, body):
    def step(j, carry):
        body(pl.ds(pl.multiple_of(j * LANE, LANE), LANE))
        return carry

    lax.fori_loop(0, width // LANE, step, 0)


def spread(column, rows):
    return jnp.broadcast_to(column, (rows, LANE))


def beside(me):
    return me + 1 - 2 * lax.rem(me, 2), me + 2 - 4 * (me // 2)


class Gather:
    def __init__(self, n, own_ref, dest, ssem, rsem):
        me = lax.axis_index("tensor")
        w = own_ref.shape[1]
        self.square = n == 4
        if self.square:
            x, y = beside(me)
            half = w // 2
            part = lambda i: own_ref.at[:, i * half:(i + 1) * half]
            to = lambda i, src, owner, at, peer: send(
                src, dest(owner, at * half, half), ssem.at[i], rsem.at[i], peer
            )
            self.copies = [
                to(0, part(0), me, 0, x), to(1, part(1), me, 1, y),
                to(2, part(1), me, 1, x), to(3, part(0), me, 0, y),
            ]
            self.passed = [
                to(4, dest(x, 0, half), x, 0, y), to(5, dest(y, half, half), y, 1, x)
            ]
        else:
            self.copies = [
                send(own_ref, dest(me, 0, w), ssem.at[k - 1], rsem.at[k - 1], lax.rem(me + k, n))
                for k in range(1, n)
            ]

    def start(self):
        for copy in self.copies:
            copy.start()

    def relay(self):
        if self.square:
            for copy, passed in zip(self.copies, self.passed):
                copy.wait_recv()
                passed.start()

    def wait(self):
        if self.square:
            for copy in self.copies:
                copy.wait_send()
            for copy in self.copies[2:]:
                copy.wait_recv()
            wait_all(self.passed)
        else:
            wait_all(self.copies)


class Scatter:
    def __init__(self, n, w, part_ref, slots, come, go, ssem, rsem):
        me = lax.axis_index("tensor")
        self.n, self.w, self.part, self.slots, self.come, self.go = n, w, part_ref, slots, come, go
        self.square = n == 4
        cols = lambda owner, at, size: part_ref.at[:, pl.ds(pl.multiple_of(owner * w + at, LANE), size)]
        if self.square:
            x, y = beside(me)
            far = 3 - me
            half = w // 2
            self.half, self.x, self.y = half, x, y
            to = lambda i, src, dst, peer: send(src, dst, ssem.at[i], rsem.at[i], peer)
            low, high = slice(0, half), slice(half, w)
            self.first = [
                to(0, cols(far, 0, half), come.at[0], x), to(1, cols(far, half, half), come.at[1], y)
            ]
            self.second = [
                to(2, cols(x, 0, half), slots.at[0, :, low], x),
                to(3, cols(y, half, half), slots.at[1, :, high], y),
            ]
            self.third = [
                to(4, go.at[0], slots.at[0, :, high], x), to(5, go.at[1], slots.at[1, :, low], y)
            ]
            self.order = [(far, 0), (far, 1), (x, 0), (y, 1), (x, 1), (y, 0), (me, 0), (me, 1)]
        else:
            self.first = [
                send(cols(lax.rem(me + k, n), 0, w), slots.at[k - 1], ssem.at[k - 1], rsem.at[k - 1],
                     lax.rem(me + k, n))
                for k in range(1, n)
            ]
            self.second = self.third = []

    def start(self):
        for copy in self.first + self.second:
            copy.start()

    def relay(self):
        if self.square:
            half = self.half
            for i, (owner, at) in enumerate(((self.x, half), (self.y, 0))):
                self.first[1 - i].wait_recv()

                def add(cols, i=i, owner=owner, at=at):
                    wide = pl.ds(pl.multiple_of(owner * self.w + at + cols.start, LANE), LANE)
                    self.go[i, :, cols] = (
                        self.part[:, wide].astype(F32) + self.come[1 - i, :, cols].astype(F32)
                    ).astype(BF)

                chunks(half, add)
                self.third[i].start()

    def wait(self):
        if self.square:
            for copy in self.first:
                copy.wait_send()
            wait_all(self.second + self.third)
        else:
            wait_all(self.first)

    def total(self, cols, wide):
        total = self.part[:, wide].astype(F32)
        for k in range(self.slots.shape[0]):
            total = total + self.slots[k, :, cols].astype(F32)
        return total


def scatter_room(n, rows, w):
    count, half = (2, w // 2) if n == 4 else (n - 1, LANE)
    return [
        pltpu.VMEM((count, rows, w), BF), pltpu.VMEM((2, rows, half), BF), pltpu.VMEM((2, rows, half), BF),
        sems(6 if n == 4 else n - 1), sems(6 if n == 4 else n - 1),
    ]


def gather_sems(n):
    return [sems(6 if n == 4 else n - 1)] * 2


def stream(count, fetch, compute):
    fetch(0, 0).start()

    def step(i, carry):
        slot = lax.rem(i, 2)

        @pl.when(i + 1 < count)
        def _():
            fetch(i + 1, 1 - slot).start()

        fetch(i, slot).wait()
        compute(i, slot)
        return carry

    lax.fori_loop(0, count, step, 0)


def wait_all(copies):
    for copy in copies:
        copy.wait()


def row_stats(n, rows, w, all_ref, acc, mean_ref, inv_ref):
    acc[...] = jnp.zeros_like(acc)

    def add(cols):
        total = all_ref[0, :, cols].astype(F32)
        for k in range(1, n):
            total = total + all_ref[k, :, cols].astype(F32)
        acc[...] += total

    chunks(w, add)
    mean_ref[...] = spread(jnp.sum(acc[...], axis=1, keepdims=True) * (1.0 / D), rows)
    acc[...] = jnp.zeros_like(acc)

    def square(cols):
        mean = mean_ref[...]
        total = jnp.zeros_like(mean)
        for k in range(n):
            center = all_ref[k, :, cols].astype(F32) - mean
            total = total + center * center
        acc[...] += total

    chunks(w, square)
    var = jnp.sum(acc[...], axis=1, keepdims=True) * (1.0 / D)
    inv_ref[...] = spread(lax.rsqrt(var + EPS), rows)


def write_act(n, w, all_ref, mean_ref, inv_ref, gain_ref, bias_ref, act_ref):
    def act(cols):
        for k in range(n):
            wide = pl.ds(pl.multiple_of(k * w + cols.start, LANE), LANE)
            center = all_ref[k, :, cols].astype(F32) - mean_ref[...]
            act_ref[:, wide] = (
                center * inv_ref[...] * gain_ref[:, wide] + bias_ref[:, wide]
            ).astype(BF)

    chunks(w, act)


def part_rows(w_ref, out_ref, ibuf, obuf, isem, osem, also):
    size = ibuf.shape[1]
    count = w_ref.shape[0] // size

    def rows_of(i):
        return pl.ds(pl.multiple_of(i * size, size), size)

    def fetch(i, slot):
        return pltpu.make_async_copy(w_ref.at[rows_of(i)], ibuf.at[slot], isem.at[slot])

    def put(i, slot):
        return pltpu.make_async_copy(obuf.at[slot], out_ref.at[:, rows_of(i)], osem.at[slot])

    fetch(0, 0).start()

    def step(i, carry):
        slot = lax.rem(i, 2)
        also(i)

        @pl.when(i + 1 < count)
        def _():
            fetch(i + 1, 1 - slot).start()

        fetch(i, slot).wait()

        @pl.when(i >= 2)
        def _():
            put(i - 2, slot).wait()

        obuf[slot] = jnp.swapaxes(ibuf[slot], 0, 1)
        put(i, slot).start()
        return carry

    lax.fori_loop(0, count, step, 0)
    for i in (count - 2, count - 1):
        put(i, i % 2).wait()


def first_norm_kernel(
    n, x_ref, gain_ref, bias_ref, w_ref, act_ref, mean_ref, inv_ref, parted_ref,
    all_ref, acc, ssem, rsem, ibuf, obuf, isem, osem,
):
    rows, w = x_ref.shape
    me = lax.axis_index("tensor")
    greet(n)
    dest = lambda owner, at, size: all_ref.at[owner, :, pl.ds(at, size)]
    gather = Gather(n, x_ref, dest, ssem, rsem)
    gather.start()
    all_ref[me] = x_ref[...]
    part_rows(w_ref, parted_ref, ibuf, obuf, isem, osem, lambda i: pl.when(i == 12)(gather.relay))
    gather.wait()
    row_stats(n, rows, w, all_ref, acc, mean_ref, inv_ref)
    write_act(n, w, all_ref, mean_ref, inv_ref, gain_ref, bias_ref, act_ref)


def second_norm_kernel(
    n, m, part_ref, x_ref, scale_ref, gain_ref, bias_ref, bgrad_ref, mixed_ref, w_down_ref,
    attn_ref, res_ref, act_ref, mean_ref, inv_ref, hgrad_ref, *refs,
):
    hops = m // 2 - 1
    rights, lefts, refs = refs[:hops], refs[hops:2 * hops], refs[2 * hops:]
    (slots, come, go, ssem, rsem, own_ref, all_ref, acc, ssem2, rsem2, hsem,
     wbuf, wsem) = refs
    rows, w = x_ref.shape
    me = lax.axis_index("tensor")
    greet(n, m)
    scatter = Scatter(n, w, part_ref, slots, come, go, ssem, rsem)
    scatter.start()
    line = [
        Hop(k, m, rights[k - 2] if k > 1 else mixed_ref, lefts[k - 2] if k > 1 else mixed_ref,
            rights[k - 1], lefts[k - 1], hsem.at[k - 1])
        for k in range(1, hops + 1)
    ]
    line[0].start()
    tile = wbuf.shape[1]
    count = hgrad_ref.shape[1] // tile

    def fetch(i, slot):
        return pltpu.make_async_copy(
            w_down_ref.at[pl.ds(pl.multiple_of(i * tile, tile), tile), :], wbuf.at[slot], wsem.at[slot]
        )

    def compute(i, slot):
        hgrad_ref[:, pl.ds(pl.multiple_of(i * tile, tile), tile)] = lax.dot_general(
            bgrad_ref[...], wbuf[slot], COLS, preferred_element_type=F32
        )

        @pl.when(i == count // 2)
        def _():
            scatter.relay()

    stream(count, fetch, compute)
    scatter.wait()

    def add(cols):
        wide = pl.ds(pl.multiple_of(me * w + cols.start, LANE), LANE)
        total = scatter.total(cols, wide)
        attn_ref[:, cols] = total
        res = x_ref[:, cols].astype(F32) + scale_ref[:, wide] * total
        res_ref[:, cols] = res
        own_ref[:, cols] = res.astype(BF)

    chunks(w, add)
    dest = lambda owner, at, size: all_ref.at[owner, :, pl.ds(at, size)]
    gather = Gather(n, own_ref, dest, ssem2, rsem2)
    gather.start()
    all_ref[me] = own_ref[...]
    line[0].wait()
    if hops > 1:
        line[1].start()
    gather.relay()
    for k in range(1, hops - 1):
        line[k].wait()
        line[k + 1].start()
    gather.wait()
    row_stats(n, rows, w, all_ref, acc, mean_ref, inv_ref)
    write_act(n, w, all_ref, mean_ref, inv_ref, gain_ref, bias_ref, act_ref)
    line[-1].wait()


def norm_back(n, w, load_total, grad_ref, base_ref, mean_ref, inv_ref, gain_ref,
              sums, acc, acc2, stat_own, stats, ssem, rsem, out):
    rows = grad_ref.shape[0]
    me = lax.axis_index("tensor")
    acc[...] = jnp.zeros_like(acc)
    acc2[...] = jnp.zeros_like(acc2)

    def first(cols):
        wide = pl.ds(pl.multiple_of(me * w + cols.start, LANE), LANE)
        total = load_total(cols, wide)
        grad_ref[:, cols] = total
        normed = (base_ref[:, cols].astype(F32) - mean_ref[...]) * inv_ref[...]
        sums[0:1, cols] = jnp.sum(total * normed, axis=0, keepdims=True)
        sums[1:2, cols] = jnp.sum(total, axis=0, keepdims=True)
        scaled = total * gain_ref[:, wide]
        acc[...] += scaled
        acc2[...] += scaled * normed

    chunks(w, first)
    plain = jnp.sum(acc[...], axis=1, keepdims=True)
    cross = jnp.sum(acc2[...], axis=1, keepdims=True)
    lane = lax.broadcasted_iota(jnp.int32, (rows, LANE), 1)
    stat_own[...] = jnp.where(lane == 0, plain, cross)
    copies = [
        send(stat_own, stats.at[me], ssem.at[k - 1], rsem.at[k - 1], lax.rem(me + k, n))
        for k in range(1, n)
    ]
    for copy in copies:
        copy.start()
    wait_all(copies)
    both = stat_own[...]
    for k in range(1, n):
        both = both + stats[lax.rem(me + k, n)]
    acc[...] = spread(both[:, 0:1] * (1.0 / D), rows)
    acc2[...] = spread(both[:, 1:2] * (1.0 / D), rows)

    def second(cols):
        wide = pl.ds(pl.multiple_of(me * w + cols.start, LANE), LANE)
        normed = (base_ref[:, cols].astype(F32) - mean_ref[...]) * inv_ref[...]
        scaled = grad_ref[:, cols] * gain_ref[:, wide]
        out(cols, wide, inv_ref[...] * (scaled - acc[...] - normed * acc2[...]))

    chunks(w, second)


def second_back_kernel(
    n, m, grads_ref, cot_ref, res_ref, attn_ref, mean_ref, inv_ref, gain_ref, scale_ref,
    right_ref, left_ref, gu_ref, w_ref, rgrad_ref, agrad_ref, sums_ref, gu_right, gu_left, *refs,
):
    hops = m // 2 - 1
    rights = (right_ref,) + refs[:hops - 1]
    lefts = (left_ref,) + refs[hops - 1:2 * hops - 2]
    (part_ref, slots, come, go, ssem, rsem, grad_ref, own_ref, acc, acc2, stat_own, stats,
     ssem2, rsem2, ssem3, rsem3, lsem, hsem, gsem, wbuf, wsem) = refs[2 * hops - 2:]
    w = cot_ref.shape[1]
    me = lax.axis_index("tensor")
    greet(n, m)
    line = [
        Hop(k, m, rights[k - 2], lefts[k - 2], rights[k - 1], lefts[k - 1], hsem.at[k - 2])
        for k in range(2, hops + 1)
    ]
    line[0].start()
    first = End(m, gu_ref, 0, gu_right, gu_left, gsem)
    first.start()
    scatter = Scatter(n, w, part_ref, slots, come, go, ssem, rsem)
    tile = wbuf.shape[2]
    inner = w_ref.shape[2]
    count = D // tile

    def spot(i):
        if not scatter.square:
            return pl.ds(pl.multiple_of(i * tile, LANE), tile)
        at = 0
        for k, (owner, half) in enumerate(scatter.order):
            at = at + jnp.where(i == k, owner * w + half * tile, 0)
        return pl.ds(pl.multiple_of(at, LANE), tile)

    def fetch(i, slot):
        return pltpu.make_async_copy(w_ref.at[:, spot(i), :], wbuf.at[slot], wsem.at[slot])

    def compute(i, slot):
        total = None
        for j in range(w_ref.shape[0]):
            term = lax.dot_general(
                grads_ref[:, j * inner:(j + 1) * inner], wbuf[slot, j], COLS,
                preferred_element_type=F32,
            )
            total = term if total is None else total + term
        part_ref[:, spot(i)] = total.astype(BF)
        if scatter.square:
            for k, copy in enumerate(scatter.first + scatter.second):
                pl.when(i == k)(copy.start)
            pl.when(i == 5)(scatter.relay)

    stream(count, fetch, compute)
    if not scatter.square:
        scatter.start()
    scatter.wait()
    sums_ref[...] = jnp.zeros_like(sums_ref)

    def out(cols, wide, back):
        res_grad = cot_ref[:, cols].astype(F32) + back
        rgrad_ref[:, cols] = res_grad
        sums_ref[2:3, cols] = jnp.sum(res_grad * attn_ref[:, cols], axis=0, keepdims=True)
        own_ref[:, cols] = (scale_ref[:, wide] * res_grad).astype(BF)

    norm_back(n, w, scatter.total, grad_ref, res_ref, mean_ref, inv_ref, gain_ref,
              sums_ref, acc, acc2, stat_own, stats, ssem2, rsem2, out)
    dest = lambda owner, at, size: agrad_ref.at[:, pl.ds(pl.multiple_of(owner * w + at, LANE), size)]
    gather = Gather(n, own_ref, dest, ssem3, rsem3)
    gather.start()
    local = pltpu.make_async_copy(own_ref, dest(me, 0, w), lsem)
    local.start()
    gather.relay()
    for k in range(len(line)):
        line[k].wait()
        if k + 1 < len(line):
            line[k + 1].start()
    local.wait()
    gather.wait()
    first.wait()


def first_back_kernel(
    n, grad_in, rgrad_ref, x_ref, mean_ref, inv_ref, gain_ref, small_ref,
    igrad_ref, sums,
    grad_ref, acc, acc2, stat_own, stats, ssem, rsem,
):
    w = x_ref.shape[1]
    greet(n)
    sums[...] = small_ref[...]

    def load_total(cols, wide):
        return grad_in[:, cols].astype(F32)

    def out(cols, wide, back):
        igrad_ref[:, cols] = rgrad_ref[:, cols] + back

    norm_back(n, w, load_total, grad_ref, x_ref, mean_ref, inv_ref, gain_ref,
              sums, acc, acc2, stat_own, stats, ssem, rsem, out)


def mate_of(you):
    return you + 1 - 2 * lax.rem(you, 2)


def pair_grad_kernel(
    m, pieces, act_ref, gate_ref, up_ref, hidden_ref, cot_ref, out_ref, right_ref, left_ref, kcot_ref,
    acts, mates, gates, ups, flip, asem, arem, gsem, grem, lsem, hsem, css, crs, cls,
):
    line = m // 2
    you = lax.axis_index("dp")
    core, mate = lax.rem(you, 2), mate_of(you)
    width = acts.shape[-1]
    tile = 512
    greet(1, m)
    hop = Hop(1, m, hidden_ref, hidden_ref, right_ref, left_ref, hsem)
    copies = [
        send_dp(gate_ref, gates, gsem.at[0], grem.at[0], mate),
        send_dp(up_ref, ups, gsem.at[1], grem.at[1], mate),
    ]
    locals_ = []
    for k in range(line):
        theirs = pl.ds(pl.multiple_of((2 * k + 1 - core) * width, LANE), width)
        ours = pl.ds(pl.multiple_of((2 * k + core) * width, LANE), width)
        copies.append(send_dp(act_ref.at[:, theirs], mates.at[k], asem.at[k], arem.at[k], mate))
        locals_.append(pltpu.make_async_copy(act_ref.at[:, ours], acts.at[k], lsem.at[k]))
    for copy in locals_ + copies:
        copy.start()
    hop.start()
    side = Exchange(m, pieces, cot_ref, kcot_ref, css, crs, cls)
    side.start()
    for copy in locals_:
        copy.wait()
    for k in range(line):
        flip[0, k] = acts[k].T
    for copy in copies:
        copy.wait()
    for k in range(line):
        flip[1, k] = mates[k].T
    for j, (near, far) in enumerate(((gate_ref, gates), (up_ref, ups))):

        def step(i, carry):
            cols = pl.ds(pl.multiple_of(i * tile, tile), tile)
            for k in range(line):
                out_ref[k, j, :, cols] = (
                    jnp.dot(flip[0, k], near[:, cols], preferred_element_type=F32)
                    + jnp.dot(flip[1, k], far[:, cols], preferred_element_type=F32)
                ).astype(BF)
            return carry

        lax.fori_loop(0, gate_ref.shape[1] // tile, step, 0)
    hop.wait()
    side.wait()


class SmallSums:
    def __init__(self, n, m, sums, out, parts, total, dss, drs, tss, trs):
        self.out, self.sums, self.parts, self.total = out, sums, parts, total
        me, you = lax.axis_index("tensor"), lax.axis_index("dp")
        w = sums.shape[1]
        self.m, self.you = m, you
        self.mine = pl.ds(pl.multiple_of(me * w, w), w)
        self.dp = [
            send_dp(sums, parts.at[you], dss.at[k - 1], drs.at[k - 1], lax.rem(you + k, m))
            for k in range(1, m)
        ]
        self.tensor = [
            send(total, out.at[:, self.mine], tss.at[k - 1], trs.at[k - 1], lax.rem(me + k, n))
            for k in range(1, n)
        ]

    def start(self):
        for copy in self.dp:
            copy.start()

    def finish(self):
        self.parts[self.you] = self.sums[...]
        wait_all(self.dp)
        total = self.parts[0]
        for k in range(1, self.m):
            total = total + self.parts[k]
        self.total[...] = total
        for copy in self.tensor:
            copy.start()
        self.out[:, self.mine] = total
        wait_all(self.tensor)


def small_sums_kernel(n, m, sums, out_ref, parts, total, *room):
    greet(n, m)
    small = SmallSums(n, m, sums, out_ref, parts, total, *room)
    small.start()
    small.finish()


def gathered_grad_kernel(m, turned, first, last, *refs):
    hops = m // 2 - 1
    you = lax.axis_index("dp")
    core, mate, z = lax.rem(you, 2), mate_of(you), you // 2
    todo = []
    refs = list(refs)
    for k in range(first, last + 1):
        if k == 0:
            todo.append((None, refs.pop(0), z))
        else:
            todo.append((z >= k, refs.pop(0), z - k))
            todo.append((z <= hops - k, refs.pop(0), z + k))
    side_ref = refs.pop(0)
    before = refs.pop(0) if first else None
    out_ref, blocks, flip, lsem, ssem, rsem = refs
    greet(1, m)
    copies = []
    for at, (cond, src, chip) in enumerate(todo):
        near = pltpu.make_async_copy(src, blocks.at[at, core], lsem.at[at])
        far = send_dp(src, blocks.at[at, core], ssem.at[at], rsem.at[at], mate)
        copies.append((cond, near, far))

    def when(cond, body):
        body() if cond is None else pl.when(cond)(body)

    def go(near, far):
        near.start()
        far.start()

    def done(near, far):
        near.wait()
        far.wait()

    def turn(at, chip):
        for c in range(2):
            flip[at, c] = side_ref[2 * chip + c].T

    for cond, near, far in copies:
        when(cond, functools.partial(go, near, far))
    for at, (cond, _, chip) in enumerate(todo):
        when(cond, functools.partial(turn, at, chip))
    for cond, near, far in copies:
        when(cond, functools.partial(done, near, far))
    tile = 512
    parts, width = out_ref.shape[0], blocks.shape[-1]
    if before is not None:
        out_ref[...] = before[...]
    for at, (cond, _, chip) in enumerate(todo):
        for j in range(parts):

            def step(i, carry, at=at, j=j):
                cols = pl.ds(pl.multiple_of(i * tile, tile), tile)
                total = jnp.dot(
                    flip[at, 0], blocks[at, 0, j, :, cols], preferred_element_type=F32
                ) + jnp.dot(flip[at, 1], blocks[at, 1, j, :, cols], preferred_element_type=F32)
                if turned:
                    if first or at:
                        out_ref[j, cols, :] += total.T
                    else:
                        out_ref[j, cols, :] = total.T
                elif first or at:
                    out_ref[j, :, cols] += total
                else:
                    out_ref[j, :, cols] = total
                return carry

            def run(step=step):
                lax.fori_loop(0, width // tile, step, 0)

            when(cond, run)


def qkv_kernel(act_ref, w_ref, cos_ref, sin_ref, out_ref):
    raw = jnp.dot(act_ref[...], w_ref[...], preferred_element_type=F32)
    part = pl.program_id(0)

    @pl.when(part < 2)
    def _():
        for h in range(raw.shape[1] // HD):
            cols = slice(h * HD, (h + 1) * HD)
            t = raw[:, cols]
            out_ref[:, cols] = (
                t * cos_ref[...] + pltpu.roll(t, HD // 2, 1) * sin_ref[...]
            ).astype(BF)

    @pl.when(part == 2)
    def _():
        out_ref[...] = raw.astype(BF)


def qkv_matmul(act, w_j, cos2, sin2):
    rows = act.shape[0]
    inner = w_j.shape[2]
    tile = min(512, inner)
    return pl.pallas_call(
        qkv_kernel,
        grid=(3, inner // tile),
        out_shape=jax.ShapeDtypeStruct((3, rows, inner), BF),
        in_specs=[
            pl.BlockSpec((rows, D), lambda j, i: (0, 0)),
            pl.BlockSpec((None, D, tile), lambda j, i: (j, 0, i)),
            pl.BlockSpec((rows, HD), lambda j, i: (0, 0)),
            pl.BlockSpec((rows, HD), lambda j, i: (0, 0)),
        ],
        out_specs=pl.BlockSpec((None, rows, tile), lambda j, i: (j, 0, i)),
        compiler_params=pltpu.CompilerParams(vmem_limit_bytes=40 << 20),
        cost_estimate=pl.CostEstimate(
            flops=2 * rows * D * 3 * inner, bytes_accessed=6 * D * inner, transcendentals=0
        ),
    )(act, w_j, cos2, sin2)


def attention_probs(q, k, same):
    scores = lax.dot_general(k, q, COLS, preferred_element_type=F32) * (HD ** (-0.5))
    scores = jnp.where(same, scores, -jnp.inf)
    top = jnp.max(scores, axis=0, keepdims=True)
    weight = jnp.exp(scores - top)
    return weight / jnp.sum(weight, axis=0, keepdims=True)


def same_image(rows):
    one = lax.broadcasted_iota(jnp.int32, (rows, rows), 0)
    two = lax.broadcasted_iota(jnp.int32, (rows, rows), 1)
    image = lambda i: sum((i >= SEQ * k).astype(jnp.int32) for k in range(1, rows // SEQ))
    return image(one) == image(two)


def attention_kernel(
    m, pieces, qkv_ref, w_ref, act_ref, mixed_ref, part_ref, kact_ref, ass, ars, als
):
    rows, inner = mixed_ref.shape
    greet(1, m)
    side = Exchange(m, pieces, act_ref, kact_ref, ass, ars, als)
    side.start()

    def head(h, carry):
        cols = pl.ds(pl.multiple_of(h * HD, HD), HD)
        probs = attention_probs(qkv_ref[0, :, cols], qkv_ref[1, :, cols], same_image(rows))
        value = qkv_ref[2, :, cols].astype(F32).T.astype(BF)
        mixed = jnp.dot(value, probs.astype(BF), preferred_element_type=F32)
        mixed_ref[:, cols] = mixed.T.astype(BF)
        return carry

    lax.fori_loop(0, inner // HD, head, 0)

    def tile(i, carry):
        cols = pl.ds(pl.multiple_of(i * 512, 512), 512)
        part_ref[:, cols] = jnp.dot(
            mixed_ref[...], w_ref[:, cols], preferred_element_type=F32
        ).astype(BF)
        return carry

    lax.fori_loop(0, D // 512, tile, 0)
    side.wait()


def attention_back_kernel(
    m, pieces, agrad_ref, w_ref, qkv_ref, cos_ref, sin_ref, full_ref, gu_ref,
    out_ref, kattn_ref, gu_right, gu_left, mgrad, ass, ars, als, gsem,
):
    rows, inner = mgrad.shape
    greet(1, m)
    rest = End(m, gu_ref, gu_ref.shape[2] - gu_right.shape[1], gu_right, gu_left, gsem)
    rest.start()
    side = Exchange(m, pieces, full_ref, kattn_ref, ass, ars, als)
    side.start()
    step = min(256, inner)

    def tile(i, carry):
        cols = pl.ds(pl.multiple_of(i * step, step), step)
        mgrad[:, cols] = lax.dot_general(
            agrad_ref[...], w_ref[cols, :], COLS, preferred_element_type=F32
        ).astype(BF)
        return carry

    lax.fori_loop(0, inner // step, tile, 0)

    def back(t):
        return t * cos_ref[...] - pltpu.roll(t, HD // 2, 1) * sin_ref[...]

    def head(h, carry):
        cols = pl.ds(pl.multiple_of(h * HD, HD), HD)
        q, k, v = qkv_ref[0, :, cols], qkv_ref[1, :, cols], qkv_ref[2, :, cols]
        grad = mgrad[:, cols]
        probs = attention_probs(q, k, same_image(rows))
        prob_grad = lax.dot_general(v, grad, COLS, preferred_element_type=F32)
        delta = jnp.sum(probs * prob_grad, axis=0, keepdims=True)
        score_grad = (probs * (prob_grad - delta)).astype(BF)
        scale = HD ** (-0.5)
        flipped = k.astype(F32).T.astype(BF)
        q_grad = jnp.dot(flipped, score_grad, preferred_element_type=F32).T * scale
        k_grad = jnp.dot(score_grad, q, preferred_element_type=F32) * scale
        out_ref[0, :, cols] = back(q_grad).astype(BF)
        out_ref[1, :, cols] = back(k_grad).astype(BF)
        out_ref[2, :, cols] = jnp.dot(
            probs.astype(BF), grad, preferred_element_type=F32
        ).astype(BF)
        return carry

    lax.fori_loop(0, inner // HD, head, 0)
    side.wait()
    rest.wait()


def back_kernel(g_ref, w_ref, out_ref):
    total = None
    for j in range(g_ref.shape[0]):
        term = lax.dot_general(g_ref[j], w_ref[j], COLS, preferred_element_type=F32)
        total = term if total is None else total + term
    out_ref[...] = total.astype(BF)


def back_matmul(grads, w_j):
    parts, rows, inner = grads.shape
    tile = 512
    return pl.pallas_call(
        back_kernel,
        grid=(D // tile,),
        out_shape=jax.ShapeDtypeStruct((rows, D), BF),
        in_specs=[
            pl.BlockSpec((parts, rows, inner), lambda i: (0, 0, 0)),
            pl.BlockSpec((parts, tile, inner), lambda i: (0, i, 0)),
        ],
        out_specs=pl.BlockSpec((rows, tile), lambda i: (0, i)),
        compiler_params=pltpu.CompilerParams(vmem_limit_bytes=40 << 20),
        cost_estimate=pl.CostEstimate(
            flops=rows * D * parts * inner * 100 // 500,
            bytes_accessed=800_000,
            transcendentals=0,
        ),
    )(grads, w_j)


def vm():
    return pl.BlockSpec(memory_space=pltpu.VMEM)


def hb():
    return pl.BlockSpec(memory_space=pltpu.HBM)


def sems(*shape):
    return pltpu.SemaphoreType.DMA(shape)


def call(kernel, ident, outs, scratch, args, micros=30):
    shapes = [jax.ShapeDtypeStruct(o[0], o[1]) for o in outs]
    return list(pl.pallas_call(
        kernel,
        out_shape=shapes,
        in_specs=[hb() if a[1] else vm() for a in args],
        out_specs=[hb() if len(o) > 2 else vm() for o in outs],
        scratch_shapes=scratch,
        compiler_params=pltpu.CompilerParams(
            collective_id=ident, has_side_effects=True, vmem_limit_bytes=56 << 20
        ),
        cost_estimate=pl.CostEstimate(
            flops=micros * 100_000_000, bytes_accessed=800_000, transcendentals=0
        ),
    )(*[a[0] for a in args]))


class LineReduce:
    def __init__(self, part, right, left, m):
        self.part, self.line, self.t = part, m // 2, 2
        self.z = lax.axis_index("dp") // 2
        self.right = jnp.where(self.z >= 1, right.astype(F32), 0.0)
        self.left = jnp.where(self.z <= self.line - 2, left.astype(F32), 0.0)

    def take(self, i):
        i = jnp.clip(i, 0, self.line - 1)
        return lax.dynamic_index_in_dim(self.part, i, 0, keepdims=False).astype(F32)

    def step(self, after):
        line, t = self.line, self.t
        right = (self.take(self.z + line - t) + self.right).astype(BF)
        left = (self.take(self.z - line + t) + self.left).astype(BF)
        right, left = lax.optimization_barrier((right, left) + tuple(after))[:2]
        self.given = right, left
        self.right = lax.ppermute(
            right, "dp", [(2 * i + c, 2 * i + 2 + c) for i in range(t) for c in range(2)]
        ).astype(F32)
        self.left = lax.ppermute(
            left, "dp",
            [(2 * i + c, 2 * i - 2 + c) for i in range(line - t, line) for c in range(2)],
        ).astype(F32)
        self.t += 1

    def finish(self, after):
        while self.t < self.line:
            self.step(after)
        return self.take(self.z) + self.right + self.left


def line_gather(own, m, meanwhile):
    line = m // 2
    right = left = own
    rights, lefts = [], []
    for k in range(1, line):
        right = lax.ppermute(right, "dp", [(i, i + 2) for i in range(2 * (k - 1), m - 2)])
        left = lax.ppermute(left, "dp", [(i, i - 2) for i in range(2, m - 2 * (k - 1))])
        if k in meanwhile and k < line - 1:
            right, left = lax.optimization_barrier((right, left) + meanwhile[k](right, left))[:2]
        rights.append(right)
        lefts.append(left)
    return rights, lefts


def local(
    tokens_in, ln1_gain, ln1_bias, w_qkv, w_out, scale_attn, ln2_gain, ln2_bias, w_gu, w_down,
    scale_mlp, out_cotangent, *, n, m,
):
    rows, w = tokens_in.shape
    images = rows // SEQ
    inner = w_qkv.shape[2]
    heads = inner // HD
    hidden_width = w_gu.shape[2]
    scale = HD ** (-0.5)
    line = m // 2
    hops = line - 1
    shard = D // m
    pieces = min(n, shard // LANE)
    cosines, sines = rope_tables()
    cos2 = jnp.tile(jnp.concatenate([cosines, cosines], axis=1), (images, 1))
    sin2 = jnp.tile(jnp.concatenate([-sines, sines], axis=1), (images, 1))
    wide = (rows, n * w)
    own = (rows, w)
    lanes = (rows, LANE)
    row = lambda v: v.reshape(1, D)
    V = lambda *a: [(x, False) for x in a]
    H = lambda *a: [(x, True) for x in a]

    w_j = jnp.transpose(w_qkv, (1, 0, 2))

    act_one, mean_one, inv_one, gu_j = call(
        functools.partial(first_norm_kernel, n), 1,
        [(wide, BF), (lanes, F32), (lanes, F32), ((2, D, hidden_width), BF, True)],
        [pltpu.VMEM((n,) + own, BF), pltpu.VMEM(lanes, F32)] + gather_sems(n)
        + [pltpu.VMEM((2, 128, 2, hidden_width), BF), pltpu.VMEM((2, 2, 128, hidden_width), BF),
           sems(2), sems(2)],
        V(tokens_in, row(ln1_gain), row(ln1_bias)) + H(w_gu), 50,
    )
    cot_late, act_one = lax.optimization_barrier((out_cotangent, act_one))
    cot_all = lax.all_gather(cot_late, "tensor", axis=1, tiled=True)
    branch_grad = (scale_mlp * cot_all.astype(F32)).astype(BF)
    qkv = qkv_matmul(act_one, w_j, cos2, sin2)
    mixed, attn_part, kact = call(
        functools.partial(attention_kernel, m, pieces), 12,
        [((rows, inner), BF), (wide, BF), ((m, rows, LANE), BF, True)],
        [sems(m - 1), sems(m - 1), pltpu.SemaphoreType.DMA], V(qkv, w_out) + H(act_one), 15,
    )
    tile = min(512, hidden_width)
    outs = call(
        functools.partial(second_norm_kernel, n, m), 2,
        [(own, F32), (own, F32), (wide, BF), (lanes, F32), (lanes, F32), ((rows, hidden_width), F32)]
        + [((rows, inner), BF, True)] * (2 * hops),
        scatter_room(n, rows, w)
        + [pltpu.VMEM(own, BF), pltpu.VMEM((n,) + own, BF), pltpu.VMEM(lanes, F32)]
        + gather_sems(n) + [sems(hops, 4)]
        + [pltpu.VMEM((2, tile, D), BF), sems(2)],
        V(attn_part, tokens_in, row(scale_attn), row(ln2_gain), row(ln2_bias), branch_grad)
        + H(mixed, w_down), 80,
    )
    attn_sum, residual, act_two, mean_two, inv_two, hidden_grad = outs[:6]
    mixed_right, mixed_left = outs[6:6 + hops], outs[6 + hops:]
    side = lambda k: lax.all_gather(k, "tensor", axis=2, tiled=True)[:, :, :shard]
    side_act = side(kact)

    gate = jnp.dot(act_two, gu_j[0], preferred_element_type=F32)
    up = jnp.dot(act_two, gu_j[1], preferred_element_type=F32)
    sig = jax.nn.sigmoid(gate)
    hidden = (gate * sig * up).astype(BF)
    gate_grad = (hidden_grad * up * sig * (1.0 + gate * (1.0 - sig))).astype(BF)
    up_grad = (hidden_grad * gate * sig).astype(BF)
    block = (rows, hidden_width)
    gu_part, hidden_r, hidden_l, kcot = call(
        functools.partial(pair_grad_kernel, m, pieces), 3,
        [((line, 2, shard, hidden_width), BF), (block, BF, True), (block, BF, True),
         ((m, rows, LANE), BF, True)],
        [pltpu.VMEM((line, rows, shard), BF), pltpu.VMEM((line, rows, shard), BF),
         pltpu.VMEM(block, BF), pltpu.VMEM(block, BF), pltpu.VMEM((2, line, shard, rows), BF),
         sems(line), sems(line), sems(2), sems(2), sems(line), sems(4),
         sems(m - 1), sems(m - 1), pltpu.SemaphoreType.DMA],
        H(act_two) + V(gate_grad, up_grad) + H(hidden, branch_grad), 40,
    )
    side_cot = side(kcot)
    gu_grads = jnp.concatenate([gate_grad, up_grad], axis=1)
    cut = shard * 3 // 4
    tile = w // 2 if n == 4 else min(512, w)
    outs = call(
        functools.partial(second_back_kernel, n, m), 4,
        [(own, F32), (wide, BF), ((8, w), F32)] + [((2, cut, hidden_width), BF, True)] * 2
        + [(block, BF, True)] * (2 * hops - 2),
        [pltpu.VMEM(wide, BF)] + scatter_room(n, rows, w)
        + [pltpu.VMEM(own, F32), pltpu.VMEM(own, BF),
         pltpu.VMEM(lanes, F32), pltpu.VMEM(lanes, F32), pltpu.VMEM(lanes, F32),
         pltpu.VMEM((n,) + lanes, F32)] + [sems(n - 1)] * 2 + gather_sems(n)
        + [pltpu.SemaphoreType.DMA, sems(hops - 1, 4), sems(4)]
        + [pltpu.VMEM((2, 2, tile, hidden_width), BF), sems(2)],
        V(gu_grads, out_cotangent, residual, attn_sum, mean_two, inv_two, row(ln2_gain), row(scale_attn))
        + H(hidden_r, hidden_l, gu_part, gu_j), 80,
    )
    res_grad, attn_grad, sums_two, gu_right, gu_left = outs[:5]
    hidden_right = [hidden_r] + outs[5:4 + hops]
    hidden_left = [hidden_l] + outs[4 + hops:]
    raw_grad, kattn, gu_right_b, gu_left_b = call(
        functools.partial(attention_back_kernel, m, pieces), 5,
        [((3, rows, inner), BF), ((m, rows, LANE), BF, True)]
        + [((2, shard - cut, hidden_width), BF, True)] * 2,
        [pltpu.VMEM((rows, inner), BF), sems(m - 1), sems(m - 1), pltpu.SemaphoreType.DMA, sems(4)],
        V(attn_grad, w_out, qkv, cos2, sin2) + H(attn_grad, gu_part), 25,
    )
    gu_line = LineReduce(
        gu_part,
        jnp.concatenate([gu_right, gu_right_b], axis=1),
        jnp.concatenate([gu_left, gu_left_b], axis=1),
        m,
    )
    side_attn = side(kattn)
    def gathered(ident, mine, rights, lefts, sides, turned, first=0, last=hops, before=None):
        parts, _, width = mine.shape
        shape = (parts, width, shard) if turned else (parts, shard, width)
        blocks = []
        for k in range(first, last + 1):
            blocks += [rights[k - 1], lefts[k - 1]] if k else [mine]
        count = len(blocks)
        (out,) = call(
            functools.partial(gathered_grad_kernel, m, turned, first, last), ident, [(shape, F32)],
            [pltpu.VMEM((count, 2) + mine.shape, BF), pltpu.VMEM((count, 2, shard, rows), BF),
             sems(count), sems(count), sems(count)],
            H(*blocks) + V(sides) + (V(before) if first else []), 30,
        )
        return out

    lead = lambda arrays: [a[None] for a in arrays]
    done = {}

    def after_one(right, left):
        part = back_matmul(raw_grad, w_j)
        done["grad"] = lax.psum_scatter(part, "tensor", scatter_dimension=1, tiled=True)
        return (part,)

    def after_two(right, left):
        gu_line.step((right, left))
        late = lax.optimization_barrier((hidden, side_cot) + gu_line.given)
        part = jnp.dot(late[0], w_down, preferred_element_type=F32).astype(BF)
        done["branch"] = lax.psum_scatter(part, "tensor", scatter_dimension=1, tiled=True)
        done["down"] = gathered(
            6, hidden[None], lead(hidden_right), lead(hidden_left), late[1], True
        )[0]
        done["part"] = part
        return ()

    raw_right, raw_left = line_gather(raw_grad, m, {1: after_one, 2: after_two})
    act_one_grad, down_sum = done["grad"], done["down"]
    branch = done["branch"].astype(F32)
    proj_sum = gathered(7, mixed[None], lead(mixed_right), lead(mixed_left), side_attn, True)[0]
    gu_sum = gu_line.finish((raw_right[-1], raw_left[-1], down_sum, proj_sum, done["branch"]))

    own_cols = lambda v: lax.dynamic_slice_in_dim(v, lax.axis_index("tensor") * w, w, 0)
    layer_out = residual + own_cols(scale_mlp) * branch
    sums_mlp = jnp.sum(out_cotangent.astype(F32) * branch, axis=0, keepdims=True)
    small = jnp.concatenate(
        [jnp.zeros((2, w), F32), sums_two[0:3], sums_mlp, jnp.zeros((2, w), F32)], axis=0
    )
    input_grad, sums = call(
        functools.partial(first_back_kernel, n), 9,
        [(own, F32), ((8, w), F32)],
        [pltpu.VMEM(own, F32),
         pltpu.VMEM(lanes, F32), pltpu.VMEM(lanes, F32), pltpu.VMEM(lanes, F32),
         pltpu.VMEM((n,) + lanes, F32)] + [sems(n - 1)] * 2,
        V(act_one_grad, res_grad, tokens_in, mean_one, inv_one, row(ln1_gain), small), 20,
    )
    qkv_part = gathered(8, raw_grad, raw_right, raw_left, side_act, False, 0, hops - 1)
    qkv_sum = gathered(
        10, raw_grad, raw_right, raw_left, side_act, False, hops, hops, qkv_part
    )
    qkv_sum, sums = lax.optimization_barrier((qkv_sum, sums))
    (small_sums,) = call(
        functools.partial(small_sums_kernel, n, m), 11, [((8, n * w), F32)],
        [pltpu.VMEM((m, 8, w), F32), pltpu.VMEM((8, w), F32)] + [sems(m - 1)] * 2 + [sems(n - 1)] * 2,
        V(sums), 10,
    )
    return (
        layer_out,
        input_grad,
        small_sums[0],
        small_sums[1],
        jnp.transpose(qkv_sum, (1, 0, 2)),
        proj_sum,
        small_sums[4],
        small_sums[2],
        small_sums[3],
        jnp.transpose(gu_sum, (1, 0, 2)),
        down_sum,
        small_sums[5],
    )


def solution(mesh):
    placed = (
        P("dp", "tensor"),
        P(),
        P(),
        P(None, None, "tensor"),
        P("tensor", None),
        P(),
        P(),
        P(),
        P(None, None, "tensor"),
        P("tensor", None),
        P(),
        P("dp", "tensor"),
    )
    return jax.shard_map(
        functools.partial(local, n=mesh.shape["tensor"], m=mesh.shape["dp"]),
        mesh=mesh,
        in_specs=placed,
        out_specs=(
            P("dp", "tensor"),
            P("dp", "tensor"),
            P(),
            P(),
            P("dp", None, "tensor"),
            P("tensor", "dp"),
            P(),
            P(),
            P(),
            P("dp", None, "tensor"),
            P("tensor", "dp"),
            P(),
        ),
        check_vma=False,
    )
```

```python
import functools
import math

import jax
import jax.numpy as jnp
from jax import lax
from jax.experimental import pallas as pl
from jax.experimental.pallas import tpu as pltpu
from jax.sharding import PartitionSpec as P

D = 4096
HD = 128
GRID = 14
EXTRA = 5
PATCH = 196
SEQ = 201
EPS = 1e-06
LANE = 128
BF = jnp.bfloat16
F32 = jnp.float32
MESH = pl.DeviceIdType.MESH
ROWS = (((0,), (0,)), ((), ()))
COLS = (((1,), (1,)), ((), ()))


def rope_tables():
    quarter = HD // 4
    theta = (
        2.0
        * math.pi
        * jnp.exp(jnp.arange(quarter, dtype=jnp.float32) * (-4.0 * math.log(100.0) / HD))
    )
    places = jnp.arange(PATCH, dtype=jnp.int32)
    row_pos = ((places // GRID).astype(jnp.float32) + 0.5) * (2.0 / GRID) - 1.0
    col_pos = ((places % GRID).astype(jnp.float32) + 0.5) * (2.0 / GRID) - 1.0
    angles = jnp.concatenate(
        [row_pos[:, None] * theta[None, :], col_pos[:, None] * theta[None, :]], axis=1
    )
    angles = jnp.concatenate([jnp.zeros((EXTRA, HD // 2), jnp.float32), angles], axis=0)
    return (jnp.cos(angles), jnp.sin(angles))


def rotate(vectors, cosines, sines):
    halfway = HD // 2
    leading = vectors[..., :halfway]
    trailing = vectors[..., halfway:]
    cos_b = cosines[:, None, :]
    sin_b = sines[:, None, :]
    return jnp.concatenate(
        [leading * cos_b - trailing * sin_b, leading * sin_b + trailing * cos_b], axis=-1
    )


def greet(n, m=1):
    me = lax.axis_index("tensor")
    you = lax.axis_index("dp")
    barrier = pltpu.get_barrier_semaphore()
    for k in range(1, n):
        pl.semaphore_signal(
            barrier, inc=1, device_id={"tensor": lax.rem(me + k, n)}, device_id_type=MESH
        )
    for k in range(1, m):
        pl.semaphore_signal(
            barrier, inc=1, device_id={"dp": lax.rem(you + k, m)}, device_id_type=MESH
        )
    pl.semaphore_wait(barrier, n + m - 2)


def send(src, dst, send_sem, recv_sem, peer):
    return pltpu.make_async_remote_copy(
        src_ref=src,
        dst_ref=dst,
        send_sem=send_sem,
        recv_sem=recv_sem,
        device_id={"tensor": peer},
        device_id_type=MESH,
    )


def send_dp(src, dst, send_sem, recv_sem, peer):
    return pltpu.make_async_remote_copy(
        src_ref=src,
        dst_ref=dst,
        send_sem=send_sem,
        recv_sem=recv_sem,
        device_id={"dp": peer},
        device_id_type=MESH,
    )


class Hop:
    def __init__(self, k, m, right_src, left_src, right_dst, left_dst, sem):
        you = lax.axis_index("dp")
        z, last = you // 2, m // 2 - 1
        right = send_dp(right_src, right_dst, sem.at[0], sem.at[1], lax.rem(you + 2, m))
        left = send_dp(left_src, left_dst, sem.at[2], sem.at[3], lax.rem(you + m - 2, m))
        self.steps = [
            (right, (z >= k - 1) & (z < last), z >= k),
            (left, (z <= last - k + 1) & (z > 0), z <= last - k),
        ]

    def start(self):
        for copy, sends, _ in self.steps:
            pl.when(sends)(copy.start)

    def wait(self):
        for copy, sends, gets in self.steps:
            pl.when(sends)(copy.wait_send)
            pl.when(gets)(copy.wait_recv)


class End:
    def __init__(self, m, part_ref, at, right_dst, left_dst, sem):
        you = lax.axis_index("dp")
        z, last = you // 2, m // 2 - 1
        some = pl.ds(at, right_dst.shape[1])
        right = send_dp(
            part_ref.at[last, :, some], right_dst, sem.at[0], sem.at[1], lax.rem(you + 2, m)
        )
        left = send_dp(
            part_ref.at[0, :, some], left_dst, sem.at[2], sem.at[3], lax.rem(you + m - 2, m)
        )
        self.steps = [(right, z == 0, z == 1), (left, z == last, z == last - 1)]

    start = Hop.start
    wait = Hop.wait


class Exchange:
    def __init__(self, m, pieces, full_ref, out_ref, ssem, rsem, lsem):
        you = lax.axis_index("dp")
        piece = lax.rem(lax.axis_index("tensor"), pieces)
        self.copies = []
        for k in range(m):
            peer = lax.rem(you + k, m)
            cols = pl.ds(pl.multiple_of((peer * pieces + piece) * LANE, LANE), LANE)
            if k:
                copy = send_dp(
                    full_ref.at[:, cols], out_ref.at[you], ssem.at[k - 1], rsem.at[k - 1], peer
                )
            else:
                copy = pltpu.make_async_copy(full_ref.at[:, cols], out_ref.at[you], lsem)
            self.copies.append(copy)

    def start(self):
        for copy in self.copies:
            copy.start()

    def wait(self):
        for copy in self.copies:
            copy.wait()


def chunks(width, body):
    def step(j, carry):
        body(pl.ds(pl.multiple_of(j * LANE, LANE), LANE))
        return carry

    lax.fori_loop(0, width // LANE, step, 0)


def spread(column, rows):
    return jnp.broadcast_to(column, (rows, LANE))


def beside(me):
    return me + 1 - 2 * lax.rem(me, 2), me + 2 - 4 * (me // 2)


class Gather:
    def __init__(self, n, own_ref, dest, ssem, rsem):
        me = lax.axis_index("tensor")
        w = own_ref.shape[1]
        self.square = n == 4
        if self.square:
            x, y = beside(me)
            half = w // 2
            part = lambda i: own_ref.at[:, i * half:(i + 1) * half]
            to = lambda i, src, owner, at, peer: send(
                src, dest(owner, at * half, half), ssem.at[i], rsem.at[i], peer
            )
            self.copies = [
                to(0, part(0), me, 0, x), to(1, part(1), me, 1, y),
                to(2, part(1), me, 1, x), to(3, part(0), me, 0, y),
            ]
            self.passed = [
                to(4, dest(x, 0, half), x, 0, y), to(5, dest(y, half, half), y, 1, x)
            ]
        else:
            self.copies = [
                send(own_ref, dest(me, 0, w), ssem.at[k - 1], rsem.at[k - 1], lax.rem(me + k, n))
                for k in range(1, n)
            ]

    def start(self):
        for copy in self.copies:
            copy.start()

    def relay(self):
        if self.square:
            for copy, passed in zip(self.copies, self.passed):
                copy.wait_recv()
                passed.start()

    def wait(self):
        if self.square:
            for copy in self.copies:
                copy.wait_send()
            for copy in self.copies[2:]:
                copy.wait_recv()
            wait_all(self.passed)
        else:
            wait_all(self.copies)


class Scatter:
    def __init__(self, n, w, part_ref, slots, come, go, ssem, rsem):
        me = lax.axis_index("tensor")
        self.n, self.w, self.part, self.slots, self.come, self.go = n, w, part_ref, slots, come, go
        self.square = n == 4
        cols = lambda owner, at, size: part_ref.at[:, pl.ds(pl.multiple_of(owner * w + at, LANE), size)]
        if self.square:
            x, y = beside(me)
            far = 3 - me
            half = w // 2
            self.half, self.x, self.y = half, x, y
            to = lambda i, src, dst, peer: send(src, dst, ssem.at[i], rsem.at[i], peer)
            low, high = slice(0, half), slice(half, w)
            self.first = [
                to(0, cols(far, 0, half), come.at[0], x), to(1, cols(far, half, half), come.at[1], y)
            ]
            self.second = [
                to(2, cols(x, 0, half), slots.at[0, :, low], x),
                to(3, cols(y, half, half), slots.at[1, :, high], y),
            ]
            self.third = [
                to(4, go.at[0], slots.at[0, :, high], x), to(5, go.at[1], slots.at[1, :, low], y)
            ]
            self.order = [(far, 0), (far, 1), (x, 0), (y, 1), (x, 1), (y, 0), (me, 0), (me, 1)]
        else:
            self.first = [
                send(cols(lax.rem(me + k, n), 0, w), slots.at[k - 1], ssem.at[k - 1], rsem.at[k - 1],
                     lax.rem(me + k, n))
                for k in range(1, n)
            ]
            self.second = self.third = []

    def start(self):
        for copy in self.first + self.second:
            copy.start()

    def relay(self):
        if self.square:
            half = self.half
            for i, (owner, at) in enumerate(((self.x, half), (self.y, 0))):
                self.first[1 - i].wait_recv()

                def add(cols, i=i, owner=owner, at=at):
                    wide = pl.ds(pl.multiple_of(owner * self.w + at + cols.start, LANE), LANE)
                    self.go[i, :, cols] = (
                        self.part[:, wide].astype(F32) + self.come[1 - i, :, cols].astype(F32)
                    ).astype(BF)

                chunks(half, add)
                self.third[i].start()

    def wait(self):
        if self.square:
            for copy in self.first:
                copy.wait_send()
            wait_all(self.second + self.third)
        else:
            wait_all(self.first)

    def total(self, cols, wide):
        total = self.part[:, wide].astype(F32)
        for k in range(self.slots.shape[0]):
            total = total + self.slots[k, :, cols].astype(F32)
        return total


def scatter_room(n, rows, w):
    count, half = (2, w // 2) if n == 4 else (n - 1, LANE)
    return [
        pltpu.VMEM((count, rows, w), BF), pltpu.VMEM((2, rows, half), BF), pltpu.VMEM((2, rows, half), BF),
        sems(6 if n == 4 else n - 1), sems(6 if n == 4 else n - 1),
    ]


def gather_sems(n):
    return [sems(6 if n == 4 else n - 1)] * 2


def stream(count, fetch, compute):
    fetch(0, 0).start()

    def step(i, carry):
        slot = lax.rem(i, 2)

        @pl.when(i + 1 < count)
        def _():
            fetch(i + 1, 1 - slot).start()

        fetch(i, slot).wait()
        compute(i, slot)
        return carry

    lax.fori_loop(0, count, step, 0)


def wait_all(copies):
    for copy in copies:
        copy.wait()


def row_stats(n, rows, w, all_ref, acc, mean_ref, inv_ref):
    acc[...] = jnp.zeros_like(acc)

    def add(cols):
        total = all_ref[0, :, cols].astype(F32)
        for k in range(1, n):
            total = total + all_ref[k, :, cols].astype(F32)
        acc[...] += total

    chunks(w, add)
    mean_ref[...] = spread(jnp.sum(acc[...], axis=1, keepdims=True) * (1.0 / D), rows)
    acc[...] = jnp.zeros_like(acc)

    def square(cols):
        mean = mean_ref[...]
        total = jnp.zeros_like(mean)
        for k in range(n):
            center = all_ref[k, :, cols].astype(F32) - mean
            total = total + center * center
        acc[...] += total

    chunks(w, square)
    var = jnp.sum(acc[...], axis=1, keepdims=True) * (1.0 / D)
    inv_ref[...] = spread(lax.rsqrt(var + EPS), rows)


def write_act(n, w, all_ref, mean_ref, inv_ref, gain_ref, bias_ref, act_ref):
    def act(cols):
        for k in range(n):
            wide = pl.ds(pl.multiple_of(k * w + cols.start, LANE), LANE)
            center = all_ref[k, :, cols].astype(F32) - mean_ref[...]
            act_ref[:, wide] = (
                center * inv_ref[...] * gain_ref[:, wide] + bias_ref[:, wide]
            ).astype(BF)

    chunks(w, act)


def part_rows(w_ref, out_ref, ibuf, obuf, isem, osem, also):
    size = ibuf.shape[1]
    count = w_ref.shape[0] // size

    def rows_of(i):
        return pl.ds(pl.multiple_of(i * size, size), size)

    def fetch(i, slot):
        return pltpu.make_async_copy(w_ref.at[rows_of(i)], ibuf.at[slot], isem.at[slot])

    def put(i, slot):
        return pltpu.make_async_copy(obuf.at[slot], out_ref.at[:, rows_of(i)], osem.at[slot])

    fetch(0, 0).start()

    def step(i, carry):
        slot = lax.rem(i, 2)
        also(i)

        @pl.when(i + 1 < count)
        def _():
            fetch(i + 1, 1 - slot).start()

        fetch(i, slot).wait()

        @pl.when(i >= 2)
        def _():
            put(i - 2, slot).wait()

        obuf[slot] = jnp.swapaxes(ibuf[slot], 0, 1)
        put(i, slot).start()
        return carry

    lax.fori_loop(0, count, step, 0)
    for i in (count - 2, count - 1):
        put(i, i % 2).wait()


def first_norm_kernel(
    n, x_ref, gain_ref, bias_ref, w_ref, act_ref, mean_ref, inv_ref, parted_ref,
    all_ref, acc, ssem, rsem, ibuf, obuf, isem, osem,
):
    rows, w = x_ref.shape
    me = lax.axis_index("tensor")
    greet(n)
    dest = lambda owner, at, size: all_ref.at[owner, :, pl.ds(at, size)]
    gather = Gather(n, x_ref, dest, ssem, rsem)
    gather.start()
    all_ref[me] = x_ref[...]
    part_rows(w_ref, parted_ref, ibuf, obuf, isem, osem, lambda i: pl.when(i == 12)(gather.relay))
    gather.wait()
    row_stats(n, rows, w, all_ref, acc, mean_ref, inv_ref)
    write_act(n, w, all_ref, mean_ref, inv_ref, gain_ref, bias_ref, act_ref)


def second_norm_kernel(
    n, m, pieces, part_ref, x_ref, scale_ref, gain_ref, bias_ref, bgrad_ref, cot_ref, mixed_ref, w_down_ref,
    attn_ref, res_ref, act_ref, mean_ref, inv_ref, hgrad_ref, kcot_ref, *refs,
):
    hops = m // 2 - 1
    rights, lefts, refs = refs[:hops], refs[hops:2 * hops], refs[2 * hops:]
    (slots, come, go, ssem, rsem, own_ref, all_ref, acc, ssem2, rsem2, hsem,
     css, crs, cls, wbuf, wsem) = refs
    rows, w = x_ref.shape
    me = lax.axis_index("tensor")
    greet(n, m)
    scatter = Scatter(n, w, part_ref, slots, come, go, ssem, rsem)
    scatter.start()
    line = [
        Hop(k, m, rights[k - 2] if k > 1 else mixed_ref, lefts[k - 2] if k > 1 else mixed_ref,
            rights[k - 1], lefts[k - 1], hsem.at[k - 1])
        for k in range(1, hops + 1)
    ]
    line[0].start()
    side = Exchange(m, pieces, cot_ref, kcot_ref, css, crs, cls)
    side.start()
    tile = wbuf.shape[1]
    count = hgrad_ref.shape[1] // tile

    def fetch(i, slot):
        return pltpu.make_async_copy(
            w_down_ref.at[pl.ds(pl.multiple_of(i * tile, tile), tile), :], wbuf.at[slot], wsem.at[slot]
        )

    def compute(i, slot):
        hgrad_ref[:, pl.ds(pl.multiple_of(i * tile, tile), tile)] = lax.dot_general(
            bgrad_ref[...], wbuf[slot], COLS, preferred_element_type=F32
        )

        @pl.when(i == count // 2)
        def _():
            scatter.relay()

    stream(count, fetch, compute)
    scatter.wait()

    def add(cols):
        wide = pl.ds(pl.multiple_of(me * w + cols.start, LANE), LANE)
        total = scatter.total(cols, wide)
        attn_ref[:, cols] = total
        res = x_ref[:, cols].astype(F32) + scale_ref[:, wide] * total
        res_ref[:, cols] = res
        own_ref[:, cols] = res.astype(BF)

    chunks(w, add)
    dest = lambda owner, at, size: all_ref.at[owner, :, pl.ds(at, size)]
    gather = Gather(n, own_ref, dest, ssem2, rsem2)
    gather.start()
    all_ref[me] = own_ref[...]
    line[0].wait()
    if hops > 1:
        line[1].start()
    gather.relay()
    for k in range(1, hops - 1):
        line[k].wait()
        line[k + 1].start()
    gather.wait()
    row_stats(n, rows, w, all_ref, acc, mean_ref, inv_ref)
    write_act(n, w, all_ref, mean_ref, inv_ref, gain_ref, bias_ref, act_ref)
    line[-1].wait()
    side.wait()


def norm_back(n, w, load_total, grad_ref, base_ref, mean_ref, inv_ref, gain_ref,
              sums, acc, acc2, stat_own, stats, ssem, rsem, out):
    rows = grad_ref.shape[0]
    me = lax.axis_index("tensor")
    acc[...] = jnp.zeros_like(acc)
    acc2[...] = jnp.zeros_like(acc2)

    def first(cols):
        wide = pl.ds(pl.multiple_of(me * w + cols.start, LANE), LANE)
        total = load_total(cols, wide)
        grad_ref[:, cols] = total
        normed = (base_ref[:, cols].astype(F32) - mean_ref[...]) * inv_ref[...]
        sums[0:1, cols] = jnp.sum(total * normed, axis=0, keepdims=True)
        sums[1:2, cols] = jnp.sum(total, axis=0, keepdims=True)
        scaled = total * gain_ref[:, wide]
        acc[...] += scaled
        acc2[...] += scaled * normed

    chunks(w, first)
    plain = jnp.sum(acc[...], axis=1, keepdims=True)
    cross = jnp.sum(acc2[...], axis=1, keepdims=True)
    lane = lax.broadcasted_iota(jnp.int32, (rows, LANE), 1)
    stat_own[...] = jnp.where(lane == 0, plain, cross)
    copies = [
        send(stat_own, stats.at[me], ssem.at[k - 1], rsem.at[k - 1], lax.rem(me + k, n))
        for k in range(1, n)
    ]
    for copy in copies:
        copy.start()
    wait_all(copies)
    both = stat_own[...]
    for k in range(1, n):
        both = both + stats[lax.rem(me + k, n)]
    acc[...] = spread(both[:, 0:1] * (1.0 / D), rows)
    acc2[...] = spread(both[:, 1:2] * (1.0 / D), rows)

    def second(cols):
        wide = pl.ds(pl.multiple_of(me * w + cols.start, LANE), LANE)
        normed = (base_ref[:, cols].astype(F32) - mean_ref[...]) * inv_ref[...]
        scaled = grad_ref[:, cols] * gain_ref[:, wide]
        out(cols, wide, inv_ref[...] * (scaled - acc[...] - normed * acc2[...]))

    chunks(w, second)


def second_back_kernel(
    n, m, grads_ref, cot_ref, res_ref, attn_ref, mean_ref, inv_ref, gain_ref, scale_ref,
    right_ref, left_ref, gu_ref, w_ref, rgrad_ref, agrad_ref, sums_ref, gu_right, gu_left, *refs,
):
    hops = m // 2 - 1
    rights = (right_ref,) + refs[:hops - 1]
    lefts = (left_ref,) + refs[hops - 1:2 * hops - 2]
    (part_ref, slots, come, go, ssem, rsem, grad_ref, own_ref, acc, acc2, stat_own, stats,
     ssem2, rsem2, ssem3, rsem3, lsem, hsem, gsem, wbuf, wsem) = refs[2 * hops - 2:]
    w = cot_ref.shape[1]
    me = lax.axis_index("tensor")
    greet(n, m)
    line = [
        Hop(k, m, rights[k - 2], lefts[k - 2], rights[k - 1], lefts[k - 1], hsem.at[k - 2])
        for k in range(2, hops + 1)
    ]
    line[0].start()
    first = End(m, gu_ref, 0, gu_right, gu_left, gsem)
    first.start()
    scatter = Scatter(n, w, part_ref, slots, come, go, ssem, rsem)
    tile = wbuf.shape[2]
    inner = w_ref.shape[2]
    count = D // tile

    def spot(i):
        if not scatter.square:
            return pl.ds(pl.multiple_of(i * tile, LANE), tile)
        at = 0
        for k, (owner, half) in enumerate(scatter.order):
            at = at + jnp.where(i == k, owner * w + half * tile, 0)
        return pl.ds(pl.multiple_of(at, LANE), tile)

    def fetch(i, slot):
        return pltpu.make_async_copy(w_ref.at[:, spot(i), :], wbuf.at[slot], wsem.at[slot])

    def compute(i, slot):
        total = None
        for j in range(w_ref.shape[0]):
            term = lax.dot_general(
                grads_ref[:, j * inner:(j + 1) * inner], wbuf[slot, j], COLS,
                preferred_element_type=F32,
            )
            total = term if total is None else total + term
        part_ref[:, spot(i)] = total.astype(BF)
        if scatter.square:
            for k, copy in enumerate(scatter.first + scatter.second):
                pl.when(i == k)(copy.start)
            pl.when(i == 5)(scatter.relay)

    stream(count, fetch, compute)
    if not scatter.square:
        scatter.start()
    scatter.wait()
    sums_ref[...] = jnp.zeros_like(sums_ref)

    def out(cols, wide, back):
        res_grad = cot_ref[:, cols].astype(F32) + back
        rgrad_ref[:, cols] = res_grad
        sums_ref[2:3, cols] = jnp.sum(res_grad * attn_ref[:, cols], axis=0, keepdims=True)
        own_ref[:, cols] = (scale_ref[:, wide] * res_grad).astype(BF)

    norm_back(n, w, scatter.total, grad_ref, res_ref, mean_ref, inv_ref, gain_ref,
              sums_ref, acc, acc2, stat_own, stats, ssem2, rsem2, out)
    dest = lambda owner, at, size: agrad_ref.at[:, pl.ds(pl.multiple_of(owner * w + at, LANE), size)]
    gather = Gather(n, own_ref, dest, ssem3, rsem3)
    gather.start()
    local = pltpu.make_async_copy(own_ref, dest(me, 0, w), lsem)
    local.start()
    gather.relay()
    for k in range(len(line)):
        line[k].wait()
        if k + 1 < len(line):
            line[k + 1].start()
    local.wait()
    gather.wait()
    first.wait()


def first_back_kernel(
    n, grad_in, rgrad_ref, x_ref, mean_ref, inv_ref, gain_ref, small_ref,
    part_ref, res_ref, cot_ref, scale_ref,
    igrad_ref, sums, out_ref,
    slots, come, go, ssem, rsem, grad_ref, acc, acc2, stat_own, stats, ssem2, rsem2,
):
    w = x_ref.shape[1]
    greet(n)
    scatter = Scatter(n, w, part_ref, slots, come, go, ssem, rsem)
    scatter.start()
    sums[...] = small_ref[...]

    def load_total(cols, wide):
        return grad_in[:, cols].astype(F32)

    def out(cols, wide, back):
        igrad_ref[:, cols] = rgrad_ref[:, cols] + back

    norm_back(n, w, load_total, grad_ref, x_ref, mean_ref, inv_ref, gain_ref,
              sums, acc, acc2, stat_own, stats, ssem2, rsem2, out)
    scatter.relay()
    scatter.wait()
    me = lax.axis_index("tensor")

    def add(cols):
        wide = pl.ds(pl.multiple_of(me * w + cols.start, LANE), LANE)
        total = scatter.total(cols, wide)
        out_ref[:, cols] = res_ref[:, cols] + scale_ref[:, wide] * total
        sums[5:6, cols] = jnp.sum(cot_ref[:, cols].astype(F32) * total, axis=0, keepdims=True)

    chunks(w, add)


def mate_of(you):
    return you + 1 - 2 * lax.rem(you, 2)


def pair_grad_kernel(
    m, act_ref, gate_ref, up_ref, hidden_ref, out_ref, right_ref, left_ref,
    acts, mates, gates, ups, flip, asem, arem, gsem, grem, lsem, hsem,
):
    line = m // 2
    you = lax.axis_index("dp")
    core, mate = lax.rem(you, 2), mate_of(you)
    width = acts.shape[-1]
    tile = 512
    greet(1, m)
    hop = Hop(1, m, hidden_ref, hidden_ref, right_ref, left_ref, hsem)
    copies = [
        send_dp(gate_ref, gates, gsem.at[0], grem.at[0], mate),
        send_dp(up_ref, ups, gsem.at[1], grem.at[1], mate),
    ]
    locals_ = []
    for k in range(line):
        theirs = pl.ds(pl.multiple_of((2 * k + 1 - core) * width, LANE), width)
        ours = pl.ds(pl.multiple_of((2 * k + core) * width, LANE), width)
        copies.append(send_dp(act_ref.at[:, theirs], mates.at[k], asem.at[k], arem.at[k], mate))
        locals_.append(pltpu.make_async_copy(act_ref.at[:, ours], acts.at[k], lsem.at[k]))
    for copy in locals_ + copies:
        copy.start()
    hop.start()
    for copy in locals_:
        copy.wait()
    for k in range(line):
        flip[0, k] = acts[k].T
    for copy in copies:
        copy.wait()
    for k in range(line):
        flip[1, k] = mates[k].T
    for j, (near, far) in enumerate(((gate_ref, gates), (up_ref, ups))):

        def step(i, carry):
            cols = pl.ds(pl.multiple_of(i * tile, tile), tile)
            for k in range(line):
                out_ref[k, j, :, cols] = (
                    jnp.dot(flip[0, k], near[:, cols], preferred_element_type=F32)
                    + jnp.dot(flip[1, k], far[:, cols], preferred_element_type=F32)
                ).astype(BF)
            return carry

        lax.fori_loop(0, gate_ref.shape[1] // tile, step, 0)
    hop.wait()


class SmallSums:
    def __init__(self, n, m, sums, out, parts, total, dss, drs, tss, trs):
        self.out, self.sums, self.parts, self.total = out, sums, parts, total
        me, you = lax.axis_index("tensor"), lax.axis_index("dp")
        w = sums.shape[1]
        self.m, self.you = m, you
        self.mine = pl.ds(pl.multiple_of(me * w, w), w)
        self.dp = [
            send_dp(sums, parts.at[you], dss.at[k - 1], drs.at[k - 1], lax.rem(you + k, m))
            for k in range(1, m)
        ]
        self.tensor = [
            send(total, out.at[:, self.mine], tss.at[k - 1], trs.at[k - 1], lax.rem(me + k, n))
            for k in range(1, n)
        ]

    def start(self):
        for copy in self.dp:
            copy.start()

    def finish(self):
        self.parts[self.you] = self.sums[...]
        wait_all(self.dp)
        total = self.parts[0]
        for k in range(1, self.m):
            total = total + self.parts[k]
        self.total[...] = total
        for copy in self.tensor:
            copy.start()
        self.out[:, self.mine] = total
        wait_all(self.tensor)


def small_sums_kernel(n, m, sums, out_ref, parts, total, *room):
    greet(n, m)
    small = SmallSums(n, m, sums, out_ref, parts, total, *room)
    small.start()
    small.finish()


def gathered_grad_kernel(m, turned, first, last, *refs):
    hops = m // 2 - 1
    you = lax.axis_index("dp")
    core, mate, z = lax.rem(you, 2), mate_of(you), you // 2
    todo = []
    refs = list(refs)
    for k in range(first, last + 1):
        if k == 0:
            todo.append((None, refs.pop(0), z))
        else:
            todo.append((z >= k, refs.pop(0), z - k))
            todo.append((z <= hops - k, refs.pop(0), z + k))
    side_ref = refs.pop(0)
    before = refs.pop(0) if first else None
    out_ref, blocks, flip, lsem, ssem, rsem = refs
    greet(1, m)
    copies = []
    for at, (cond, src, chip) in enumerate(todo):
        near = pltpu.make_async_copy(src, blocks.at[at, core], lsem.at[at])
        far = send_dp(src, blocks.at[at, core], ssem.at[at], rsem.at[at], mate)
        copies.append((cond, near, far))

    def when(cond, body):
        body() if cond is None else pl.when(cond)(body)

    def go(near, far):
        near.start()
        far.start()

    def done(near, far):
        near.wait()
        far.wait()

    def turn(at, chip):
        for c in range(2):
            flip[at, c] = side_ref[2 * chip + c].T

    for cond, near, far in copies:
        when(cond, functools.partial(go, near, far))
    for at, (cond, _, chip) in enumerate(todo):
        when(cond, functools.partial(turn, at, chip))
    for cond, near, far in copies:
        when(cond, functools.partial(done, near, far))
    tile = 512
    parts, width = out_ref.shape[0], blocks.shape[-1]
    if before is not None:
        out_ref[...] = before[...]
    for at, (cond, _, chip) in enumerate(todo):
        for j in range(parts):

            def step(i, carry, at=at, j=j):
                cols = pl.ds(pl.multiple_of(i * tile, tile), tile)
                total = jnp.dot(
                    flip[at, 0], blocks[at, 0, j, :, cols], preferred_element_type=F32
                ) + jnp.dot(flip[at, 1], blocks[at, 1, j, :, cols], preferred_element_type=F32)
                if turned:
                    if first or at:
                        out_ref[j, cols, :] += total.T
                    else:
                        out_ref[j, cols, :] = total.T
                elif first or at:
                    out_ref[j, :, cols] += total
                else:
                    out_ref[j, :, cols] = total
                return carry

            def run(step=step):
                lax.fori_loop(0, width // tile, step, 0)

            when(cond, run)


def qkv_kernel(act_ref, w_ref, cos_ref, sin_ref, out_ref):
    raw = jnp.dot(act_ref[...], w_ref[...], preferred_element_type=F32)
    part = pl.program_id(0)

    @pl.when(part < 2)
    def _():
        for h in range(raw.shape[1] // HD):
            cols = slice(h * HD, (h + 1) * HD)
            t = raw[:, cols]
            out_ref[:, cols] = (
                t * cos_ref[...] + pltpu.roll(t, HD // 2, 1) * sin_ref[...]
            ).astype(BF)

    @pl.when(part == 2)
    def _():
        out_ref[...] = raw.astype(BF)


def qkv_matmul(act, w_j, cos2, sin2):
    rows = act.shape[0]
    inner = w_j.shape[2]
    tile = min(512, inner)
    return pl.pallas_call(
        qkv_kernel,
        grid=(3, inner // tile),
        out_shape=jax.ShapeDtypeStruct((3, rows, inner), BF),
        in_specs=[
            pl.BlockSpec((rows, D), lambda j, i: (0, 0)),
            pl.BlockSpec((None, D, tile), lambda j, i: (j, 0, i)),
            pl.BlockSpec((rows, HD), lambda j, i: (0, 0)),
            pl.BlockSpec((rows, HD), lambda j, i: (0, 0)),
        ],
        out_specs=pl.BlockSpec((None, rows, tile), lambda j, i: (j, 0, i)),
        compiler_params=pltpu.CompilerParams(vmem_limit_bytes=40 << 20),
        cost_estimate=pl.CostEstimate(
            flops=2 * rows * D * 3 * inner, bytes_accessed=6 * D * inner, transcendentals=0
        ),
    )(act, w_j, cos2, sin2)


def attention_probs(q, k, same):
    scores = lax.dot_general(k, q, COLS, preferred_element_type=F32) * (HD ** (-0.5))
    scores = jnp.where(same, scores, -jnp.inf)
    top = jnp.max(scores, axis=0, keepdims=True)
    weight = jnp.exp(scores - top)
    return weight / jnp.sum(weight, axis=0, keepdims=True)


def same_image(rows):
    one = lax.broadcasted_iota(jnp.int32, (rows, rows), 0)
    two = lax.broadcasted_iota(jnp.int32, (rows, rows), 1)
    image = lambda i: sum((i >= SEQ * k).astype(jnp.int32) for k in range(1, rows // SEQ))
    return image(one) == image(two)


def attention_kernel(
    m, pieces, qkv_ref, w_ref, act_ref, mixed_ref, part_ref, kact_ref, ass, ars, als
):
    rows, inner = mixed_ref.shape
    greet(1, m)
    side = Exchange(m, pieces, act_ref, kact_ref, ass, ars, als)
    side.start()

    def head(h, carry):
        cols = pl.ds(pl.multiple_of(h * HD, HD), HD)
        probs = attention_probs(qkv_ref[0, :, cols], qkv_ref[1, :, cols], same_image(rows))
        value = qkv_ref[2, :, cols].astype(F32).T.astype(BF)
        mixed = jnp.dot(value, probs.astype(BF), preferred_element_type=F32)
        mixed_ref[:, cols] = mixed.T.astype(BF)
        return carry

    lax.fori_loop(0, inner // HD, head, 0)

    def tile(i, carry):
        cols = pl.ds(pl.multiple_of(i * 512, 512), 512)
        part_ref[:, cols] = jnp.dot(
            mixed_ref[...], w_ref[:, cols], preferred_element_type=F32
        ).astype(BF)
        return carry

    lax.fori_loop(0, D // 512, tile, 0)
    side.wait()


def attention_back_kernel(
    m, pieces, agrad_ref, w_ref, qkv_ref, cos_ref, sin_ref, full_ref, gu_ref,
    out_ref, kattn_ref, gu_right, gu_left, mgrad, ass, ars, als, gsem,
):
    rows, inner = mgrad.shape
    greet(1, m)
    rest = End(m, gu_ref, gu_ref.shape[2] - gu_right.shape[1], gu_right, gu_left, gsem)
    rest.start()
    side = Exchange(m, pieces, full_ref, kattn_ref, ass, ars, als)
    side.start()
    step = min(256, inner)

    def tile(i, carry):
        cols = pl.ds(pl.multiple_of(i * step, step), step)
        mgrad[:, cols] = lax.dot_general(
            agrad_ref[...], w_ref[cols, :], COLS, preferred_element_type=F32
        ).astype(BF)
        return carry

    lax.fori_loop(0, inner // step, tile, 0)

    def back(t):
        return t * cos_ref[...] - pltpu.roll(t, HD // 2, 1) * sin_ref[...]

    def head(h, carry):
        cols = pl.ds(pl.multiple_of(h * HD, HD), HD)
        q, k, v = qkv_ref[0, :, cols], qkv_ref[1, :, cols], qkv_ref[2, :, cols]
        grad = mgrad[:, cols]
        probs = attention_probs(q, k, same_image(rows))
        prob_grad = lax.dot_general(v, grad, COLS, preferred_element_type=F32)
        delta = jnp.sum(probs * prob_grad, axis=0, keepdims=True)
        score_grad = (probs * (prob_grad - delta)).astype(BF)
        scale = HD ** (-0.5)
        flipped = k.astype(F32).T.astype(BF)
        q_grad = jnp.dot(flipped, score_grad, preferred_element_type=F32).T * scale
        k_grad = jnp.dot(score_grad, q, preferred_element_type=F32) * scale
        out_ref[0, :, cols] = back(q_grad).astype(BF)
        out_ref[1, :, cols] = back(k_grad).astype(BF)
        out_ref[2, :, cols] = jnp.dot(
            probs.astype(BF), grad, preferred_element_type=F32
        ).astype(BF)
        return carry

    lax.fori_loop(0, inner // HD, head, 0)
    side.wait()
    rest.wait()


def back_kernel(g_ref, w_ref, out_ref):
    total = None
    for j in range(g_ref.shape[0]):
        term = lax.dot_general(g_ref[j], w_ref[j], COLS, preferred_element_type=F32)
        total = term if total is None else total + term
    out_ref[...] = total.astype(BF)


def back_matmul(grads, w_j):
    parts, rows, inner = grads.shape
    tile = 512
    return pl.pallas_call(
        back_kernel,
        grid=(D // tile,),
        out_shape=jax.ShapeDtypeStruct((rows, D), BF),
        in_specs=[
            pl.BlockSpec((parts, rows, inner), lambda i: (0, 0, 0)),
            pl.BlockSpec((parts, tile, inner), lambda i: (0, i, 0)),
        ],
        out_specs=pl.BlockSpec((rows, tile), lambda i: (0, i)),
        compiler_params=pltpu.CompilerParams(vmem_limit_bytes=40 << 20),
        cost_estimate=pl.CostEstimate(
            flops=rows * D * parts * inner * 100 // 500,
            bytes_accessed=800_000,
            transcendentals=0,
        ),
    )(grads, w_j)


def vm():
    return pl.BlockSpec(memory_space=pltpu.VMEM)


def hb():
    return pl.BlockSpec(memory_space=pltpu.HBM)


def sems(*shape):
    return pltpu.SemaphoreType.DMA(shape)


def call(kernel, ident, outs, scratch, args, micros=30):
    shapes = [jax.ShapeDtypeStruct(o[0], o[1]) for o in outs]
    return list(pl.pallas_call(
        kernel,
        out_shape=shapes,
        in_specs=[hb() if a[1] else vm() for a in args],
        out_specs=[hb() if len(o) > 2 else vm() for o in outs],
        scratch_shapes=scratch,
        compiler_params=pltpu.CompilerParams(
            collective_id=ident, has_side_effects=True, vmem_limit_bytes=56 << 20
        ),
        cost_estimate=pl.CostEstimate(
            flops=micros * 100_000_000, bytes_accessed=800_000, transcendentals=0
        ),
    )(*[a[0] for a in args]))


class LineReduce:
    def __init__(self, part, right, left, m):
        self.part, self.line, self.t = part, m // 2, 2
        self.z = lax.axis_index("dp") // 2
        self.right = jnp.where(self.z >= 1, right.astype(F32), 0.0)
        self.left = jnp.where(self.z <= self.line - 2, left.astype(F32), 0.0)

    def take(self, i):
        i = jnp.clip(i, 0, self.line - 1)
        return lax.dynamic_index_in_dim(self.part, i, 0, keepdims=False).astype(F32)

    def step(self, after):
        line, t = self.line, self.t
        right = (self.take(self.z + line - t) + self.right).astype(BF)
        left = (self.take(self.z - line + t) + self.left).astype(BF)
        right, left = lax.optimization_barrier((right, left) + tuple(after))[:2]
        self.given = right, left
        self.right = lax.ppermute(
            right, "dp", [(2 * i + c, 2 * i + 2 + c) for i in range(t) for c in range(2)]
        ).astype(F32)
        self.left = lax.ppermute(
            left, "dp",
            [(2 * i + c, 2 * i - 2 + c) for i in range(line - t, line) for c in range(2)],
        ).astype(F32)
        self.t += 1

    def finish(self, after):
        while self.t < self.line:
            self.step(after)
        return self.take(self.z) + self.right + self.left


def line_gather(own, m, meanwhile):
    line = m // 2
    right = left = own
    rights, lefts = [], []
    for k in range(1, line):
        right = lax.ppermute(right, "dp", [(i, i + 2) for i in range(2 * (k - 1), m - 2)])
        left = lax.ppermute(left, "dp", [(i, i - 2) for i in range(2, m - 2 * (k - 1))])
        if k in meanwhile and k < line - 1:
            right, left = lax.optimization_barrier((right, left) + meanwhile[k](right, left))[:2]
        rights.append(right)
        lefts.append(left)
    return rights, lefts


def local(
    tokens_in, ln1_gain, ln1_bias, w_qkv, w_out, scale_attn, ln2_gain, ln2_bias, w_gu, w_down,
    scale_mlp, out_cotangent, *, n, m,
):
    rows, w = tokens_in.shape
    images = rows // SEQ
    inner = w_qkv.shape[2]
    heads = inner // HD
    hidden_width = w_gu.shape[2]
    scale = HD ** (-0.5)
    line = m // 2
    hops = line - 1
    shard = D // m
    pieces = min(n, shard // LANE)
    cosines, sines = rope_tables()
    cos2 = jnp.tile(jnp.concatenate([cosines, cosines], axis=1), (images, 1))
    sin2 = jnp.tile(jnp.concatenate([-sines, sines], axis=1), (images, 1))
    wide = (rows, n * w)
    own = (rows, w)
    lanes = (rows, LANE)
    row = lambda v: v.reshape(1, D)
    V = lambda *a: [(x, False) for x in a]
    H = lambda *a: [(x, True) for x in a]

    w_j = jnp.transpose(w_qkv, (1, 0, 2))

    act_one, mean_one, inv_one, gu_j = call(
        functools.partial(first_norm_kernel, n), 1,
        [(wide, BF), (lanes, F32), (lanes, F32), ((2, D, hidden_width), BF, True)],
        [pltpu.VMEM((n,) + own, BF), pltpu.VMEM(lanes, F32)] + gather_sems(n)
        + [pltpu.VMEM((2, 128, 2, hidden_width), BF), pltpu.VMEM((2, 2, 128, hidden_width), BF),
           sems(2), sems(2)],
        V(tokens_in, row(ln1_gain), row(ln1_bias)) + H(w_gu), 50,
    )
    cot_late, act_one = lax.optimization_barrier((out_cotangent, act_one))
    cot_all = lax.all_gather(cot_late, "tensor", axis=1, tiled=True)
    branch_grad = (scale_mlp * cot_all.astype(F32)).astype(BF)
    qkv = qkv_matmul(act_one, w_j, cos2, sin2)
    mixed, attn_part, kact = call(
        functools.partial(attention_kernel, m, pieces), 12,
        [((rows, inner), BF), (wide, BF), ((m, rows, LANE), BF, True)],
        [sems(m - 1), sems(m - 1), pltpu.SemaphoreType.DMA], V(qkv, w_out) + H(act_one), 15,
    )
    tile = min(512, hidden_width)
    outs = call(
        functools.partial(second_norm_kernel, n, m, pieces), 2,
        [(own, F32), (own, F32), (wide, BF), (lanes, F32), (lanes, F32), ((rows, hidden_width), F32)]
        + [((m, rows, LANE), BF, True)] + [((rows, inner), BF, True)] * (2 * hops),
        scatter_room(n, rows, w)
        + [pltpu.VMEM(own, BF), pltpu.VMEM((n,) + own, BF), pltpu.VMEM(lanes, F32)]
        + gather_sems(n) + [sems(hops, 4)]
        + [sems(m - 1), sems(m - 1), pltpu.SemaphoreType.DMA]
        + [pltpu.VMEM((2, tile, D), BF), sems(2)],
        V(attn_part, tokens_in, row(scale_attn), row(ln2_gain), row(ln2_bias), branch_grad)
        + H(branch_grad, mixed, w_down), 80,
    )
    attn_sum, residual, act_two, mean_two, inv_two, hidden_grad, kcot = outs[:7]
    mixed_right, mixed_left = outs[7:7 + hops], outs[7 + hops:]
    kact, act_two = lax.optimization_barrier((kact, act_two))
    side = lambda k: lax.all_gather(k, "tensor", axis=2, tiled=True)[:, :, :shard]
    side_act = side(kact)

    gate = jnp.dot(act_two, gu_j[0], preferred_element_type=F32)
    up = jnp.dot(act_two, gu_j[1], preferred_element_type=F32)
    sig = jax.nn.sigmoid(gate)
    hidden = (gate * sig * up).astype(BF)
    gate_grad = (hidden_grad * up * sig * (1.0 + gate * (1.0 - sig))).astype(BF)
    up_grad = (hidden_grad * gate * sig).astype(BF)
    block = (rows, hidden_width)
    gu_part, hidden_r, hidden_l = call(
        functools.partial(pair_grad_kernel, m), 3,
        [((line, 2, shard, hidden_width), BF), (block, BF, True), (block, BF, True)],
        [pltpu.VMEM((line, rows, shard), BF), pltpu.VMEM((line, rows, shard), BF),
         pltpu.VMEM(block, BF), pltpu.VMEM(block, BF), pltpu.VMEM((2, line, shard, rows), BF),
         sems(line), sems(line), sems(2), sems(2), sems(line), sems(4)],
        H(act_two) + V(gate_grad, up_grad) + H(hidden), 40,
    )
    gu_grads = jnp.concatenate([gate_grad, up_grad], axis=1)
    cut = shard * 7 // 8
    tile = w // 2 if n == 4 else min(512, w)
    outs = call(
        functools.partial(second_back_kernel, n, m), 4,
        [(own, F32), (wide, BF), ((8, w), F32)] + [((2, cut, hidden_width), BF, True)] * 2
        + [(block, BF, True)] * (2 * hops - 2),
        [pltpu.VMEM(wide, BF)] + scatter_room(n, rows, w)
        + [pltpu.VMEM(own, F32), pltpu.VMEM(own, BF),
         pltpu.VMEM(lanes, F32), pltpu.VMEM(lanes, F32), pltpu.VMEM(lanes, F32),
         pltpu.VMEM((n,) + lanes, F32)] + [sems(n - 1)] * 2 + gather_sems(n)
        + [pltpu.SemaphoreType.DMA, sems(hops - 1, 4), sems(4)]
        + [pltpu.VMEM((2, 2, tile, hidden_width), BF), sems(2)],
        V(gu_grads, out_cotangent, residual, attn_sum, mean_two, inv_two, row(ln2_gain), row(scale_attn))
        + H(hidden_r, hidden_l, gu_part, gu_j), 80,
    )
    res_grad, attn_grad, sums_two, gu_right, gu_left = outs[:5]
    hidden_right = [hidden_r] + outs[5:4 + hops]
    hidden_left = [hidden_l] + outs[4 + hops:]
    raw_grad, kattn, gu_right_b, gu_left_b = call(
        functools.partial(attention_back_kernel, m, pieces), 5,
        [((3, rows, inner), BF), ((m, rows, LANE), BF, True)]
        + [((2, shard - cut, hidden_width), BF, True)] * 2,
        [pltpu.VMEM((rows, inner), BF), sems(m - 1), sems(m - 1), pltpu.SemaphoreType.DMA, sems(4)],
        V(attn_grad, w_out, qkv, cos2, sin2) + H(attn_grad, gu_part), 25,
    )
    gu_line = LineReduce(
        gu_part,
        jnp.concatenate([gu_right, gu_right_b], axis=1),
        jnp.concatenate([gu_left, gu_left_b], axis=1),
        m,
    )
    kcot, raw_grad = lax.optimization_barrier((kcot, raw_grad))
    side_cot, side_attn = side(kcot), side(kattn)
    def gathered(ident, mine, rights, lefts, sides, turned, first=0, last=hops, before=None):
        parts, _, width = mine.shape
        shape = (parts, width, shard) if turned else (parts, shard, width)
        blocks = []
        for k in range(first, last + 1):
            blocks += [rights[k - 1], lefts[k - 1]] if k else [mine]
        count = len(blocks)
        (out,) = call(
            functools.partial(gathered_grad_kernel, m, turned, first, last), ident, [(shape, F32)],
            [pltpu.VMEM((count, 2) + mine.shape, BF), pltpu.VMEM((count, 2, shard, rows), BF),
             sems(count), sems(count), sems(count)],
            H(*blocks) + V(sides) + (V(before) if first else []), 30,
        )
        return out

    lead = lambda arrays: [a[None] for a in arrays]
    done = {}

    def after_one(right, left):
        part = back_matmul(raw_grad, w_j)
        done["grad"] = lax.psum_scatter(part, "tensor", scatter_dimension=1, tiled=True)
        return (part,)

    def after_two(right, left):
        gu_line.step((right, left))
        late = lax.optimization_barrier((side_cot, side_attn) + gu_line.given)
        done["attn"] = late[1]
        done["down"] = gathered(
            6, hidden[None], lead(hidden_right), lead(hidden_left), late[0], True
        )[0]
        return ()

    raw_right, raw_left = line_gather(raw_grad, m, {1: after_one, 2: after_two})
    act_one_grad, down_sum = done["grad"], done["down"]
    proj_sum = gathered(7, mixed[None], lead(mixed_right), lead(mixed_left), done["attn"], True)[0]
    branch_part = jnp.dot(hidden, w_down, preferred_element_type=F32).astype(BF)
    gu_sum = gu_line.finish((raw_right[-1], raw_left[-1], down_sum, proj_sum))

    small = jnp.concatenate([jnp.zeros((2, w), F32), sums_two[0:3], jnp.zeros((3, w), F32)], axis=0)
    input_grad, sums, layer_out = call(
        functools.partial(first_back_kernel, n), 9,
        [(own, F32), ((8, w), F32), (own, F32)],
        scatter_room(n, rows, w)
        + [pltpu.VMEM(own, F32),
           pltpu.VMEM(lanes, F32), pltpu.VMEM(lanes, F32), pltpu.VMEM(lanes, F32),
           pltpu.VMEM((n,) + lanes, F32)] + [sems(n - 1)] * 2,
        V(act_one_grad, res_grad, tokens_in, mean_one, inv_one, row(ln1_gain), small,
          branch_part, residual, out_cotangent, row(scale_mlp)), 20,
    )
    qkv_part = gathered(8, raw_grad, raw_right, raw_left, side_act, False, 0, hops - 1)
    qkv_sum = gathered(
        10, raw_grad, raw_right, raw_left, side_act, False, hops, hops, qkv_part
    )
    gu_sum = jnp.transpose(gu_sum, (1, 0, 2))
    gu_sum, sums = lax.optimization_barrier((gu_sum, sums))
    (small_sums,) = call(
        functools.partial(small_sums_kernel, n, m), 11, [((8, n * w), F32)],
        [pltpu.VMEM((m, 8, w), F32), pltpu.VMEM((8, w), F32)] + [sems(m - 1)] * 2 + [sems(n - 1)] * 2,
        V(sums), 10,
    )
    return (
        layer_out,
        input_grad,
        small_sums[0],
        small_sums[1],
        jnp.transpose(qkv_sum, (1, 0, 2)),
        proj_sum,
        small_sums[4],
        small_sums[2],
        small_sums[3],
        gu_sum,
        down_sum,
        small_sums[5],
    )


def solution(mesh):
    placed = (
        P("dp", "tensor"),
        P(),
        P(),
        P(None, None, "tensor"),
        P("tensor", None),
        P(),
        P(),
        P(),
        P(None, None, "tensor"),
        P("tensor", None),
        P(),
        P("dp", "tensor"),
    )
    return jax.shard_map(
        functools.partial(local, n=mesh.shape["tensor"], m=mesh.shape["dp"]),
        mesh=mesh,
        in_specs=placed,
        out_specs=(
            P("dp", "tensor"),
            P("dp", "tensor"),
            P(),
            P(),
            P("dp", None, "tensor"),
            P("tensor", "dp"),
            P(),
            P(),
            P(),
            P("dp", None, "tensor"),
            P("tensor", "dp"),
            P(),
        ),
        check_vma=False,
    )
```

```python
import functools
import math

import jax
import jax.numpy as jnp
from jax import lax
from jax.experimental import pallas as pl
from jax.experimental.pallas import tpu as pltpu
from jax.sharding import PartitionSpec as P

D = 4096
HD = 128
GRID = 14
EXTRA = 5
PATCH = 196
SEQ = 201
EPS = 1e-06
LANE = 128
BF = jnp.bfloat16
F32 = jnp.float32
MESH = pl.DeviceIdType.MESH
ROWS = (((0,), (0,)), ((), ()))
COLS = (((1,), (1,)), ((), ()))


def rope_tables():
    quarter = HD // 4
    theta = (
        2.0
        * math.pi
        * jnp.exp(jnp.arange(quarter, dtype=jnp.float32) * (-4.0 * math.log(100.0) / HD))
    )
    places = jnp.arange(PATCH, dtype=jnp.int32)
    row_pos = ((places // GRID).astype(jnp.float32) + 0.5) * (2.0 / GRID) - 1.0
    col_pos = ((places % GRID).astype(jnp.float32) + 0.5) * (2.0 / GRID) - 1.0
    angles = jnp.concatenate(
        [row_pos[:, None] * theta[None, :], col_pos[:, None] * theta[None, :]], axis=1
    )
    angles = jnp.concatenate([jnp.zeros((EXTRA, HD // 2), jnp.float32), angles], axis=0)
    return (jnp.cos(angles), jnp.sin(angles))


def rotate(vectors, cosines, sines):
    halfway = HD // 2
    leading = vectors[..., :halfway]
    trailing = vectors[..., halfway:]
    cos_b = cosines[:, None, :]
    sin_b = sines[:, None, :]
    return jnp.concatenate(
        [leading * cos_b - trailing * sin_b, leading * sin_b + trailing * cos_b], axis=-1
    )


def greet(n, m=1):
    me = lax.axis_index("tensor")
    you = lax.axis_index("dp")
    barrier = pltpu.get_barrier_semaphore()
    for k in range(1, n):
        pl.semaphore_signal(
            barrier, inc=1, device_id={"tensor": lax.rem(me + k, n)}, device_id_type=MESH
        )
    for k in range(1, m):
        pl.semaphore_signal(
            barrier, inc=1, device_id={"dp": lax.rem(you + k, m)}, device_id_type=MESH
        )
    pl.semaphore_wait(barrier, n + m - 2)


def send(src, dst, send_sem, recv_sem, peer):
    return pltpu.make_async_remote_copy(
        src_ref=src,
        dst_ref=dst,
        send_sem=send_sem,
        recv_sem=recv_sem,
        device_id={"tensor": peer},
        device_id_type=MESH,
    )


def send_dp(src, dst, send_sem, recv_sem, peer):
    return pltpu.make_async_remote_copy(
        src_ref=src,
        dst_ref=dst,
        send_sem=send_sem,
        recv_sem=recv_sem,
        device_id={"dp": peer},
        device_id_type=MESH,
    )


class Hop:
    def __init__(self, k, m, right_src, left_src, right_dst, left_dst, sem):
        you = lax.axis_index("dp")
        z, last = you // 2, m // 2 - 1
        right = send_dp(right_src, right_dst, sem.at[0], sem.at[1], lax.rem(you + 2, m))
        left = send_dp(left_src, left_dst, sem.at[2], sem.at[3], lax.rem(you + m - 2, m))
        self.steps = [
            (right, (z >= k - 1) & (z < last), z >= k),
            (left, (z <= last - k + 1) & (z > 0), z <= last - k),
        ]

    def start(self):
        for copy, sends, _ in self.steps:
            pl.when(sends)(copy.start)

    def wait(self):
        for copy, sends, gets in self.steps:
            pl.when(sends)(copy.wait_send)
            pl.when(gets)(copy.wait_recv)


class End:
    def __init__(self, m, part_ref, at, right_dst, left_dst, sem):
        you = lax.axis_index("dp")
        z, last = you // 2, m // 2 - 1
        some = pl.ds(at, right_dst.shape[1])
        right = send_dp(
            part_ref.at[last, :, some], right_dst, sem.at[0], sem.at[1], lax.rem(you + 2, m)
        )
        left = send_dp(
            part_ref.at[0, :, some], left_dst, sem.at[2], sem.at[3], lax.rem(you + m - 2, m)
        )
        self.steps = [(right, z == 0, z == 1), (left, z == last, z == last - 1)]

    start = Hop.start
    wait = Hop.wait


class Exchange:
    def __init__(self, m, pieces, full_ref, out_ref, ssem, rsem, lsem):
        you = lax.axis_index("dp")
        piece = lax.rem(lax.axis_index("tensor"), pieces)
        self.copies = []
        for k in range(m):
            peer = lax.rem(you + k, m)
            cols = pl.ds(pl.multiple_of((peer * pieces + piece) * LANE, LANE), LANE)
            if k:
                copy = send_dp(
                    full_ref.at[:, cols], out_ref.at[you], ssem.at[k - 1], rsem.at[k - 1], peer
                )
            else:
                copy = pltpu.make_async_copy(full_ref.at[:, cols], out_ref.at[you], lsem)
            self.copies.append(copy)

    def start(self):
        for copy in self.copies:
            copy.start()

    def wait(self):
        for copy in self.copies:
            copy.wait()


def chunks(width, body):
    def step(j, carry):
        body(pl.ds(pl.multiple_of(j * LANE, LANE), LANE))
        return carry

    lax.fori_loop(0, width // LANE, step, 0)


def spread(column, rows):
    return jnp.broadcast_to(column, (rows, LANE))


def beside(me):
    return me + 1 - 2 * lax.rem(me, 2), me + 2 - 4 * (me // 2)


class Gather:
    def __init__(self, n, own_ref, dest, ssem, rsem):
        me = lax.axis_index("tensor")
        w = own_ref.shape[1]
        self.square = n == 4
        if self.square:
            x, y = beside(me)
            half = w // 2
            part = lambda i: own_ref.at[:, i * half:(i + 1) * half]
            to = lambda i, src, owner, at, peer: send(
                src, dest(owner, at * half, half), ssem.at[i], rsem.at[i], peer
            )
            self.copies = [
                to(0, part(0), me, 0, x), to(1, part(1), me, 1, y),
                to(2, part(1), me, 1, x), to(3, part(0), me, 0, y),
            ]
            self.passed = [
                to(4, dest(x, 0, half), x, 0, y), to(5, dest(y, half, half), y, 1, x)
            ]
        else:
            self.copies = [
                send(own_ref, dest(me, 0, w), ssem.at[k - 1], rsem.at[k - 1], lax.rem(me + k, n))
                for k in range(1, n)
            ]

    def start(self):
        for copy in self.copies:
            copy.start()

    def relay(self):
        if self.square:
            for copy, passed in zip(self.copies, self.passed):
                copy.wait_recv()
                passed.start()

    def wait(self):
        if self.square:
            for copy in self.copies:
                copy.wait_send()
            for copy in self.copies[2:]:
                copy.wait_recv()
            wait_all(self.passed)
        else:
            wait_all(self.copies)


class Scatter:
    def __init__(self, n, w, part_ref, slots, come, go, ssem, rsem):
        me = lax.axis_index("tensor")
        self.n, self.w, self.part, self.slots, self.come, self.go = n, w, part_ref, slots, come, go
        self.square = n == 4
        cols = lambda owner, at, size: part_ref.at[:, pl.ds(pl.multiple_of(owner * w + at, LANE), size)]
        if self.square:
            x, y = beside(me)
            far = 3 - me
            half = w // 2
            self.half, self.x, self.y = half, x, y
            to = lambda i, src, dst, peer: send(src, dst, ssem.at[i], rsem.at[i], peer)
            low, high = slice(0, half), slice(half, w)
            self.first = [
                to(0, cols(far, 0, half), come.at[0], x), to(1, cols(far, half, half), come.at[1], y)
            ]
            self.second = [
                to(2, cols(x, 0, half), slots.at[0, :, low], x),
                to(3, cols(y, half, half), slots.at[1, :, high], y),
            ]
            self.third = [
                to(4, go.at[0], slots.at[0, :, high], x), to(5, go.at[1], slots.at[1, :, low], y)
            ]
            self.order = [(far, 0), (far, 1), (x, 0), (y, 1), (x, 1), (y, 0), (me, 0), (me, 1)]
        else:
            self.first = [
                send(cols(lax.rem(me + k, n), 0, w), slots.at[k - 1], ssem.at[k - 1], rsem.at[k - 1],
                     lax.rem(me + k, n))
                for k in range(1, n)
            ]
            self.second = self.third = []

    def start(self):
        for copy in self.first + self.second:
            copy.start()

    def relay(self):
        if self.square:
            half = self.half
            for i, (owner, at) in enumerate(((self.x, half), (self.y, 0))):
                self.first[1 - i].wait_recv()

                def add(cols, i=i, owner=owner, at=at):
                    wide = pl.ds(pl.multiple_of(owner * self.w + at + cols.start, LANE), LANE)
                    self.go[i, :, cols] = (
                        self.part[:, wide].astype(F32) + self.come[1 - i, :, cols].astype(F32)
                    ).astype(BF)

                chunks(half, add)
                self.third[i].start()

    def wait(self):
        if self.square:
            for copy in self.first:
                copy.wait_send()
            wait_all(self.second + self.third)
        else:
            wait_all(self.first)

    def total(self, cols, wide):
        total = self.part[:, wide].astype(F32)
        for k in range(self.slots.shape[0]):
            total = total + self.slots[k, :, cols].astype(F32)
        return total


def scatter_room(n, rows, w):
    count, half = (2, w // 2) if n == 4 else (n - 1, LANE)
    return [
        pltpu.VMEM((count, rows, w), BF), pltpu.VMEM((2, rows, half), BF), pltpu.VMEM((2, rows, half), BF),
        sems(6 if n == 4 else n - 1), sems(6 if n == 4 else n - 1),
    ]


def gather_sems(n):
    return [sems(6 if n == 4 else n - 1)] * 2


def stream(count, fetch, compute):
    fetch(0, 0).start()

    def step(i, carry):
        slot = lax.rem(i, 2)

        @pl.when(i + 1 < count)
        def _():
            fetch(i + 1, 1 - slot).start()

        fetch(i, slot).wait()
        compute(i, slot)
        return carry

    lax.fori_loop(0, count, step, 0)


def wait_all(copies):
    for copy in copies:
        copy.wait()


def row_stats(n, rows, w, all_ref, acc, mean_ref, inv_ref):
    acc[...] = jnp.zeros_like(acc)

    def add(cols):
        total = all_ref[0, :, cols].astype(F32)
        for k in range(1, n):
            total = total + all_ref[k, :, cols].astype(F32)
        acc[...] += total

    chunks(w, add)
    mean_ref[...] = spread(jnp.sum(acc[...], axis=1, keepdims=True) * (1.0 / D), rows)
    acc[...] = jnp.zeros_like(acc)

    def square(cols):
        mean = mean_ref[...]
        total = jnp.zeros_like(mean)
        for k in range(n):
            center = all_ref[k, :, cols].astype(F32) - mean
            total = total + center * center
        acc[...] += total

    chunks(w, square)
    var = jnp.sum(acc[...], axis=1, keepdims=True) * (1.0 / D)
    inv_ref[...] = spread(lax.rsqrt(var + EPS), rows)


def write_act(n, w, all_ref, mean_ref, inv_ref, gain_ref, bias_ref, act_ref):
    def act(cols):
        for k in range(n):
            wide = pl.ds(pl.multiple_of(k * w + cols.start, LANE), LANE)
            center = all_ref[k, :, cols].astype(F32) - mean_ref[...]
            act_ref[:, wide] = (
                center * inv_ref[...] * gain_ref[:, wide] + bias_ref[:, wide]
            ).astype(BF)

    chunks(w, act)


def part_rows(w_ref, out_ref, ibuf, obuf, isem, osem, also):
    size = ibuf.shape[1]
    count = w_ref.shape[0] // size

    def rows_of(i):
        return pl.ds(pl.multiple_of(i * size, size), size)

    def fetch(i, slot):
        return pltpu.make_async_copy(w_ref.at[rows_of(i)], ibuf.at[slot], isem.at[slot])

    def put(i, slot):
        return pltpu.make_async_copy(obuf.at[slot], out_ref.at[:, rows_of(i)], osem.at[slot])

    fetch(0, 0).start()

    def step(i, carry):
        slot = lax.rem(i, 2)
        also(i)

        @pl.when(i + 1 < count)
        def _():
            fetch(i + 1, 1 - slot).start()

        fetch(i, slot).wait()

        @pl.when(i >= 2)
        def _():
            put(i - 2, slot).wait()

        obuf[slot] = jnp.swapaxes(ibuf[slot], 0, 1)
        put(i, slot).start()
        return carry

    lax.fori_loop(0, count, step, 0)
    for i in (count - 2, count - 1):
        put(i, i % 2).wait()


def first_norm_kernel(
    n, x_ref, gain_ref, bias_ref, w_ref, act_ref, mean_ref, inv_ref, parted_ref,
    all_ref, acc, ssem, rsem, ibuf, obuf, isem, osem,
):
    rows, w = x_ref.shape
    me = lax.axis_index("tensor")
    greet(n)
    dest = lambda owner, at, size: all_ref.at[owner, :, pl.ds(at, size)]
    gather = Gather(n, x_ref, dest, ssem, rsem)
    gather.start()
    all_ref[me] = x_ref[...]
    part_rows(w_ref, parted_ref, ibuf, obuf, isem, osem, lambda i: pl.when(i == 12)(gather.relay))
    gather.wait()
    row_stats(n, rows, w, all_ref, acc, mean_ref, inv_ref)
    write_act(n, w, all_ref, mean_ref, inv_ref, gain_ref, bias_ref, act_ref)


def second_norm_kernel(
    n, m, pieces, part_ref, x_ref, scale_ref, gain_ref, bias_ref, bgrad_ref, cot_ref, act_one_ref, mixed_ref,
    w_down_ref, attn_ref, res_ref, act_ref, mean_ref, inv_ref, hgrad_ref, kcot_ref, kact_ref, *refs,
):
    hops = m // 2 - 1
    rights, lefts, refs = refs[:hops], refs[hops:2 * hops], refs[2 * hops:]
    (slots, come, go, ssem, rsem, own_ref, all_ref, acc, ssem2, rsem2, hsem,
     css, crs, cls, ass, ars, als, wbuf, wsem) = refs
    rows, w = x_ref.shape
    me = lax.axis_index("tensor")
    greet(n, m)
    scatter = Scatter(n, w, part_ref, slots, come, go, ssem, rsem)
    scatter.start()
    line = [
        Hop(k, m, rights[k - 2] if k > 1 else mixed_ref, lefts[k - 2] if k > 1 else mixed_ref,
            rights[k - 1], lefts[k - 1], hsem.at[k - 1])
        for k in range(1, hops + 1)
    ]
    line[0].start()
    side = Exchange(m, pieces, cot_ref, kcot_ref, css, crs, cls)
    side.start()
    tile = wbuf.shape[1]
    count = hgrad_ref.shape[1] // tile

    def fetch(i, slot):
        return pltpu.make_async_copy(
            w_down_ref.at[pl.ds(pl.multiple_of(i * tile, tile), tile), :], wbuf.at[slot], wsem.at[slot]
        )

    def compute(i, slot):
        hgrad_ref[:, pl.ds(pl.multiple_of(i * tile, tile), tile)] = lax.dot_general(
            bgrad_ref[...], wbuf[slot], COLS, preferred_element_type=F32
        )

        @pl.when(i == count // 2)
        def _():
            scatter.relay()

    stream(count, fetch, compute)
    scatter.wait()

    def add(cols):
        wide = pl.ds(pl.multiple_of(me * w + cols.start, LANE), LANE)
        total = scatter.total(cols, wide)
        attn_ref[:, cols] = total
        res = x_ref[:, cols].astype(F32) + scale_ref[:, wide] * total
        res_ref[:, cols] = res
        own_ref[:, cols] = res.astype(BF)

    chunks(w, add)
    dest = lambda owner, at, size: all_ref.at[owner, :, pl.ds(at, size)]
    gather = Gather(n, own_ref, dest, ssem2, rsem2)
    gather.start()
    all_ref[me] = own_ref[...]
    line[0].wait()
    if hops > 1:
        line[1].start()
    gather.relay()
    for k in range(1, hops - 1):
        line[k].wait()
        line[k + 1].start()
    other = Exchange(m, pieces, act_one_ref, kact_ref, ass, ars, als)
    other.start()
    gather.wait()
    row_stats(n, rows, w, all_ref, acc, mean_ref, inv_ref)
    write_act(n, w, all_ref, mean_ref, inv_ref, gain_ref, bias_ref, act_ref)
    line[-1].wait()
    side.wait()
    other.wait()


def norm_back(n, w, load_total, grad_ref, base_ref, mean_ref, inv_ref, gain_ref,
              sums, acc, acc2, stat_own, stats, ssem, rsem, out):
    rows = grad_ref.shape[0]
    me = lax.axis_index("tensor")
    acc[...] = jnp.zeros_like(acc)
    acc2[...] = jnp.zeros_like(acc2)

    def first(cols):
        wide = pl.ds(pl.multiple_of(me * w + cols.start, LANE), LANE)
        total = load_total(cols, wide)
        grad_ref[:, cols] = total
        normed = (base_ref[:, cols].astype(F32) - mean_ref[...]) * inv_ref[...]
        sums[0:1, cols] = jnp.sum(total * normed, axis=0, keepdims=True)
        sums[1:2, cols] = jnp.sum(total, axis=0, keepdims=True)
        scaled = total * gain_ref[:, wide]
        acc[...] += scaled
        acc2[...] += scaled * normed

    chunks(w, first)
    ones = jnp.ones((8, LANE), F32)
    high = lax.Precision.HIGHEST
    plain = lax.dot_general(ones, acc[...], COLS, precision=high, preferred_element_type=F32)
    cross = lax.dot_general(ones, acc2[...], COLS, precision=high, preferred_element_type=F32)
    line = lax.broadcasted_iota(jnp.int32, (8, rows), 0)
    stat_own[...] = jnp.where(line < 4, plain, cross)
    copies = [
        send(stat_own, stats.at[me], ssem.at[k - 1], rsem.at[k - 1], lax.rem(me + k, n))
        for k in range(1, n)
    ]
    for copy in copies:
        copy.start()
    wait_all(copies)
    both = stat_own[...]
    for k in range(1, n):
        both = both + stats[lax.rem(me + k, n)]
    both = both * (1.0 / D)
    pick = lax.broadcasted_iota(jnp.int32, (8, LANE), 0)
    acc[...] = lax.dot_general(
        both, (pick == 0).astype(F32), ROWS, precision=high, preferred_element_type=F32
    )
    acc2[...] = lax.dot_general(
        both, (pick == 4).astype(F32), ROWS, precision=high, preferred_element_type=F32
    )

    def second(cols):
        wide = pl.ds(pl.multiple_of(me * w + cols.start, LANE), LANE)
        normed = (base_ref[:, cols].astype(F32) - mean_ref[...]) * inv_ref[...]
        scaled = grad_ref[:, cols] * gain_ref[:, wide]
        out(cols, wide, inv_ref[...] * (scaled - acc[...] - normed * acc2[...]))

    chunks(w, second)


def second_back_kernel(
    n, m, gate_ref, up_ref, cot_ref, res_ref, attn_ref, mean_ref, inv_ref, gain_ref, scale_ref,
    right_ref, left_ref, gu_ref, w_ref, rgrad_ref, agrad_ref, sums_ref, gu_right, gu_left, *refs,
):
    hops = m // 2 - 1
    rights = (right_ref,) + refs[:hops - 1]
    lefts = (left_ref,) + refs[hops - 1:2 * hops - 2]
    (part_ref, slots, come, go, ssem, rsem, grad_ref, own_ref, acc, acc2, stat_own, stats,
     ssem2, rsem2, ssem3, rsem3, lsem, hsem, gsem, wbuf, wsem) = refs[2 * hops - 2:]
    w = cot_ref.shape[1]
    me = lax.axis_index("tensor")
    greet(n, m)
    line = [
        Hop(k, m, rights[k - 2], lefts[k - 2], rights[k - 1], lefts[k - 1], hsem.at[k - 2])
        for k in range(2, hops + 1)
    ]
    line[0].start()
    first = End(m, gu_ref, 0, gu_right, gu_left, gsem)
    first.start()
    scatter = Scatter(n, w, part_ref, slots, come, go, ssem, rsem)
    tile = wbuf.shape[2]
    count = D // tile

    def spot(i):
        if not scatter.square:
            return pl.ds(pl.multiple_of(i * tile, LANE), tile)
        at = 0
        for k, (owner, half) in enumerate(scatter.order):
            at = at + jnp.where(i == k, owner * w + half * tile, 0)
        return pl.ds(pl.multiple_of(at, LANE), tile)

    def fetch(i, slot):
        return pltpu.make_async_copy(w_ref.at[:, spot(i), :], wbuf.at[slot], wsem.at[slot])

    def compute(i, slot):
        part_ref[:, spot(i)] = (
            lax.dot_general(gate_ref[...], wbuf[slot, 0], COLS, preferred_element_type=F32)
            + lax.dot_general(up_ref[...], wbuf[slot, 1], COLS, preferred_element_type=F32)
        ).astype(BF)
        if scatter.square:
            for k, copy in enumerate(scatter.first + scatter.second):
                pl.when(i == k)(copy.start)
            pl.when(i == 5)(scatter.relay)

    stream(count, fetch, compute)
    if not scatter.square:
        scatter.start()
    scatter.wait()
    sums_ref[...] = jnp.zeros_like(sums_ref)

    def out(cols, wide, back):
        res_grad = cot_ref[:, cols].astype(F32) + back
        rgrad_ref[:, cols] = res_grad
        sums_ref[2:3, cols] = jnp.sum(res_grad * attn_ref[:, cols], axis=0, keepdims=True)
        own_ref[:, cols] = (scale_ref[:, wide] * res_grad).astype(BF)

    norm_back(n, w, scatter.total, grad_ref, res_ref, mean_ref, inv_ref, gain_ref,
              sums_ref, acc, acc2, stat_own, stats, ssem2, rsem2, out)
    dest = lambda owner, at, size: agrad_ref.at[:, pl.ds(pl.multiple_of(owner * w + at, LANE), size)]
    gather = Gather(n, own_ref, dest, ssem3, rsem3)
    gather.start()
    local = pltpu.make_async_copy(own_ref, dest(me, 0, w), lsem)
    local.start()
    gather.relay()
    for k in range(len(line)):
        line[k].wait()
        if k + 1 < len(line):
            line[k + 1].start()
    local.wait()
    gather.wait()
    first.wait()


def first_back_kernel(
    n, grad_in, rgrad_ref, x_ref, mean_ref, inv_ref, gain_ref, small_ref,
    part_ref, res_ref, cot_ref, scale_ref,
    igrad_ref, sums, out_ref,
    slots, come, go, ssem, rsem, grad_ref, acc, acc2, stat_own, stats, ssem2, rsem2,
):
    w = x_ref.shape[1]
    greet(n)
    scatter = Scatter(n, w, part_ref, slots, come, go, ssem, rsem)
    scatter.start()
    sums[...] = small_ref[...]
    scatter.relay()

    def load_total(cols, wide):
        return grad_in[:, cols].astype(F32)

    def out(cols, wide, back):
        igrad_ref[:, cols] = rgrad_ref[:, cols] + back

    norm_back(n, w, load_total, grad_ref, x_ref, mean_ref, inv_ref, gain_ref,
              sums, acc, acc2, stat_own, stats, ssem2, rsem2, out)
    scatter.wait()
    me = lax.axis_index("tensor")

    def add(cols):
        wide = pl.ds(pl.multiple_of(me * w + cols.start, LANE), LANE)
        total = scatter.total(cols, wide)
        out_ref[:, cols] = res_ref[:, cols] + scale_ref[:, wide] * total
        sums[5:6, cols] = jnp.sum(cot_ref[:, cols].astype(F32) * total, axis=0, keepdims=True)

    chunks(w, add)


def mate_of(you):
    return you + 1 - 2 * lax.rem(you, 2)


def pair_grad_kernel(
    m, act_ref, gate_ref, up_ref, hidden_ref, out_ref, right_ref, left_ref,
    acts, mates, gates, ups, flip, asem, arem, gsem, grem, lsem, hsem,
):
    line = m // 2
    you = lax.axis_index("dp")
    core, mate = lax.rem(you, 2), mate_of(you)
    width = acts.shape[-1]
    tile = 512
    greet(1, m)
    hop = Hop(1, m, hidden_ref, hidden_ref, right_ref, left_ref, hsem)
    copies = [
        send_dp(gate_ref, gates, gsem.at[0], grem.at[0], mate),
        send_dp(up_ref, ups, gsem.at[1], grem.at[1], mate),
    ]
    locals_ = []
    for k in range(line):
        theirs = pl.ds(pl.multiple_of((2 * k + 1 - core) * width, LANE), width)
        ours = pl.ds(pl.multiple_of((2 * k + core) * width, LANE), width)
        copies.append(send_dp(act_ref.at[:, theirs], mates.at[k], asem.at[k], arem.at[k], mate))
        locals_.append(pltpu.make_async_copy(act_ref.at[:, ours], acts.at[k], lsem.at[k]))
    for copy in locals_ + copies:
        copy.start()
    hop.start()
    for copy in locals_:
        copy.wait()
    for k in range(line):
        flip[0, k] = acts[k].T
    for copy in copies:
        copy.wait()
    for k in range(line):
        flip[1, k] = mates[k].T
    for j, (near, far) in enumerate(((gate_ref, gates), (up_ref, ups))):

        def step(i, carry):
            cols = pl.ds(pl.multiple_of(i * tile, tile), tile)
            for k in range(line):
                out_ref[k, j, :, cols] = (
                    jnp.dot(flip[0, k], near[:, cols], preferred_element_type=F32)
                    + jnp.dot(flip[1, k], far[:, cols], preferred_element_type=F32)
                ).astype(BF)
            return carry

        lax.fori_loop(0, gate_ref.shape[1] // tile, step, 0)
    hop.wait()


class SmallSums:
    def __init__(self, n, m, sums, out, parts, total, dss, drs, tss, trs):
        self.out, self.sums, self.parts, self.total = out, sums, parts, total
        me, you = lax.axis_index("tensor"), lax.axis_index("dp")
        w = sums.shape[1]
        self.m, self.you = m, you
        self.mine = pl.ds(pl.multiple_of(me * w, w), w)
        self.dp = [
            send_dp(sums, parts.at[you], dss.at[k - 1], drs.at[k - 1], lax.rem(you + k, m))
            for k in range(1, m)
        ]
        self.tensor = [
            send(total, out.at[:, self.mine], tss.at[k - 1], trs.at[k - 1], lax.rem(me + k, n))
            for k in range(1, n)
        ]

    def start(self):
        for copy in self.dp:
            copy.start()

    def finish(self):
        self.parts[self.you] = self.sums[...]
        wait_all(self.dp)
        total = self.parts[0]
        for k in range(1, self.m):
            total = total + self.parts[k]
        self.total[...] = total
        for copy in self.tensor:
            copy.start()
        self.out[:, self.mine] = total
        wait_all(self.tensor)


def small_sums_kernel(n, m, sums, out_ref, parts, total, *room):
    greet(n, m)
    small = SmallSums(n, m, sums, out_ref, parts, total, *room)
    small.start()
    small.finish()


def gathered_grad_kernel(m, turned, first, last, *refs):
    hops = m // 2 - 1
    you = lax.axis_index("dp")
    core, mate, z = lax.rem(you, 2), mate_of(you), you // 2
    todo = []
    refs = list(refs)
    for k in range(first, last + 1):
        if k == 0:
            todo.append((None, refs.pop(0), z))
        else:
            todo.append((z >= k, refs.pop(0), z - k))
            todo.append((z <= hops - k, refs.pop(0), z + k))
    side_ref = refs.pop(0)
    before = refs.pop(0) if first else None
    out_ref, blocks, flip, lsem, ssem, rsem = refs
    greet(1, m)
    copies = []
    for at, (cond, src, chip) in enumerate(todo):
        near = pltpu.make_async_copy(src, blocks.at[at, core], lsem.at[at])
        far = send_dp(src, blocks.at[at, core], ssem.at[at], rsem.at[at], mate)
        copies.append((cond, near, far))

    def when(cond, body):
        body() if cond is None else pl.when(cond)(body)

    def go(near, far):
        near.start()
        far.start()

    def done(near, far):
        near.wait()
        far.wait()

    def turn(at, chip):
        for c in range(2):
            flip[at, c] = side_ref[2 * chip + c].T

    for cond, near, far in copies:
        when(cond, functools.partial(go, near, far))
    for at, (cond, _, chip) in enumerate(todo):
        when(cond, functools.partial(turn, at, chip))
    for cond, near, far in copies:
        when(cond, functools.partial(done, near, far))
    tile = 512
    parts, width = out_ref.shape[0], blocks.shape[-1]
    if before is not None:
        out_ref[...] = before[...]
    for at, (cond, _, chip) in enumerate(todo):
        for j in range(parts):

            def step(i, carry, at=at, j=j):
                cols = pl.ds(pl.multiple_of(i * tile, tile), tile)
                total = jnp.dot(
                    flip[at, 0], blocks[at, 0, j, :, cols], preferred_element_type=F32
                ) + jnp.dot(flip[at, 1], blocks[at, 1, j, :, cols], preferred_element_type=F32)
                if turned:
                    if first or at:
                        out_ref[j, cols, :] += total.T
                    else:
                        out_ref[j, cols, :] = total.T
                elif first or at:
                    out_ref[j, :, cols] += total
                else:
                    out_ref[j, :, cols] = total
                return carry

            def run(step=step):
                lax.fori_loop(0, width // tile, step, 0)

            when(cond, run)


def qkv_kernel(act_ref, w_ref, cos_ref, sin_ref, out_ref):
    raw = jnp.dot(act_ref[...], w_ref[...], preferred_element_type=F32)
    part = pl.program_id(0)

    @pl.when(part < 2)
    def _():
        for h in range(raw.shape[1] // HD):
            cols = slice(h * HD, (h + 1) * HD)
            t = raw[:, cols]
            out_ref[:, cols] = (
                t * cos_ref[...] + pltpu.roll(t, HD // 2, 1) * sin_ref[...]
            ).astype(BF)

    @pl.when(part == 2)
    def _():
        out_ref[...] = raw.astype(BF)


def qkv_matmul(act, w_j, cos2, sin2):
    rows = act.shape[0]
    inner = w_j.shape[2]
    tile = min(512, inner)
    return pl.pallas_call(
        qkv_kernel,
        grid=(3, inner // tile),
        out_shape=jax.ShapeDtypeStruct((3, rows, inner), BF),
        in_specs=[
            pl.BlockSpec((rows, D), lambda j, i: (0, 0)),
            pl.BlockSpec((None, D, tile), lambda j, i: (j, 0, i)),
            pl.BlockSpec((rows, HD), lambda j, i: (0, 0)),
            pl.BlockSpec((rows, HD), lambda j, i: (0, 0)),
        ],
        out_specs=pl.BlockSpec((None, rows, tile), lambda j, i: (j, 0, i)),
        compiler_params=pltpu.CompilerParams(vmem_limit_bytes=40 << 20),
        cost_estimate=pl.CostEstimate(
            flops=2 * rows * D * 3 * inner, bytes_accessed=6 * D * inner, transcendentals=0
        ),
    )(act, w_j, cos2, sin2)


def attention_probs(q, k, same):
    scores = lax.dot_general(k, q, COLS, preferred_element_type=F32) * (HD ** (-0.5))
    scores = jnp.where(same, scores, -jnp.inf)
    top = jnp.max(scores, axis=0, keepdims=True)
    weight = jnp.exp(scores - top)
    return weight / jnp.sum(weight, axis=0, keepdims=True)


def same_image(rows):
    one = lax.broadcasted_iota(jnp.int32, (rows, rows), 0)
    two = lax.broadcasted_iota(jnp.int32, (rows, rows), 1)
    image = lambda i: sum((i >= SEQ * k).astype(jnp.int32) for k in range(1, rows // SEQ))
    return image(one) == image(two)


def attention_kernel(qkv_ref, w_ref, mixed_ref, part_ref):
    rows, inner = mixed_ref.shape

    def head(h, carry):
        cols = pl.ds(pl.multiple_of(h * HD, HD), HD)
        probs = attention_probs(qkv_ref[0, :, cols], qkv_ref[1, :, cols], same_image(rows))
        value = qkv_ref[2, :, cols].astype(F32).T.astype(BF)
        mixed = jnp.dot(value, probs.astype(BF), preferred_element_type=F32)
        mixed_ref[:, cols] = mixed.T.astype(BF)
        return carry

    lax.fori_loop(0, inner // HD, head, 0)

    def tile(i, carry):
        cols = pl.ds(pl.multiple_of(i * 512, 512), 512)
        part_ref[:, cols] = jnp.dot(
            mixed_ref[...], w_ref[:, cols], preferred_element_type=F32
        ).astype(BF)
        return carry

    lax.fori_loop(0, D // 512, tile, 0)


def attention_back_kernel(
    m, pieces, agrad_ref, w_ref, qkv_ref, cos_ref, sin_ref, full_ref, gu_ref,
    out_ref, kattn_ref, gu_right, gu_left, mgrad, ass, ars, als, gsem,
):
    rows, inner = mgrad.shape
    greet(1, m)
    rest = End(m, gu_ref, gu_ref.shape[2] - gu_right.shape[1], gu_right, gu_left, gsem)
    rest.start()
    side = Exchange(m, pieces, full_ref, kattn_ref, ass, ars, als)
    side.start()
    step = min(256, inner)

    def tile(i, carry):
        cols = pl.ds(pl.multiple_of(i * step, step), step)
        mgrad[:, cols] = lax.dot_general(
            agrad_ref[...], w_ref[cols, :], COLS, preferred_element_type=F32
        ).astype(BF)
        return carry

    lax.fori_loop(0, inner // step, tile, 0)

    def back(t):
        return t * cos_ref[...] - pltpu.roll(t, HD // 2, 1) * sin_ref[...]

    def head(h, carry):
        cols = pl.ds(pl.multiple_of(h * HD, HD), HD)
        q, k, v = qkv_ref[0, :, cols], qkv_ref[1, :, cols], qkv_ref[2, :, cols]
        grad = mgrad[:, cols]
        probs = attention_probs(q, k, same_image(rows))
        prob_grad = lax.dot_general(v, grad, COLS, preferred_element_type=F32)
        delta = jnp.sum(probs * prob_grad, axis=0, keepdims=True)
        score_grad = (probs * (prob_grad - delta)).astype(BF)
        scale = HD ** (-0.5)
        flipped = k.astype(F32).T.astype(BF)
        q_grad = jnp.dot(flipped, score_grad, preferred_element_type=F32).T * scale
        k_grad = jnp.dot(score_grad, q, preferred_element_type=F32) * scale
        out_ref[0, :, cols] = back(q_grad).astype(BF)
        out_ref[1, :, cols] = back(k_grad).astype(BF)
        out_ref[2, :, cols] = jnp.dot(
            probs.astype(BF), grad, preferred_element_type=F32
        ).astype(BF)
        return carry

    lax.fori_loop(0, inner // HD, head, 0)
    side.wait()
    rest.wait()


def gate_kernel(act_ref, w_ref, hgrad_ref, hidden_ref, gate_ref, up_ref):
    gate = jnp.dot(act_ref[...], w_ref[0], preferred_element_type=F32)
    up = jnp.dot(act_ref[...], w_ref[1], preferred_element_type=F32)
    sig = jax.nn.sigmoid(gate)
    grad = hgrad_ref[...]
    hidden_ref[...] = (gate * sig * up).astype(BF)
    gate_ref[...] = (grad * up * sig * (1.0 + gate * (1.0 - sig))).astype(BF)
    up_ref[...] = (grad * gate * sig).astype(BF)


def gate_matmul(act, w_j, hidden_grad):
    rows, width = hidden_grad.shape
    tile = min(256, width)
    block = pl.BlockSpec((rows, tile), lambda i: (0, i))
    return pl.pallas_call(
        gate_kernel,
        grid=(width // tile,),
        out_shape=[jax.ShapeDtypeStruct((rows, width), BF)] * 3,
        in_specs=[
            pl.BlockSpec((rows, D), lambda i: (0, 0)),
            pl.BlockSpec((2, D, tile), lambda i: (0, 0, i)),
            block,
        ],
        out_specs=[block] * 3,
        compiler_params=pltpu.CompilerParams(vmem_limit_bytes=48 << 20),
    )(act, w_j, hidden_grad)


def back_kernel(g_ref, w_ref, out_ref):
    total = None
    for j in range(g_ref.shape[0]):
        term = lax.dot_general(g_ref[j], w_ref[j], COLS, preferred_element_type=F32)
        total = term if total is None else total + term
    out_ref[...] = total.astype(BF)


def back_matmul(grads, w_j):
    parts, rows, inner = grads.shape
    tile = 512
    return pl.pallas_call(
        back_kernel,
        grid=(D // tile,),
        out_shape=jax.ShapeDtypeStruct((rows, D), BF),
        in_specs=[
            pl.BlockSpec((parts, rows, inner), lambda i: (0, 0, 0)),
            pl.BlockSpec((parts, tile, inner), lambda i: (0, i, 0)),
        ],
        out_specs=pl.BlockSpec((rows, tile), lambda i: (0, i)),
        compiler_params=pltpu.CompilerParams(vmem_limit_bytes=40 << 20),
        cost_estimate=pl.CostEstimate(
            flops=rows * D * parts * inner * 100 // 500,
            bytes_accessed=800_000,
            transcendentals=0,
        ),
    )(grads, w_j)


def vm():
    return pl.BlockSpec(memory_space=pltpu.VMEM)


def hb():
    return pl.BlockSpec(memory_space=pltpu.HBM)


def sems(*shape):
    return pltpu.SemaphoreType.DMA(shape)


def call(kernel, ident, outs, scratch, args, micros=30):
    shapes = [jax.ShapeDtypeStruct(o[0], o[1]) for o in outs]
    return list(pl.pallas_call(
        kernel,
        out_shape=shapes,
        in_specs=[hb() if a[1] else vm() for a in args],
        out_specs=[hb() if len(o) > 2 else vm() for o in outs],
        scratch_shapes=scratch,
        compiler_params=pltpu.CompilerParams(
            collective_id=ident, has_side_effects=True, vmem_limit_bytes=56 << 20
        ),
        cost_estimate=pl.CostEstimate(
            flops=micros * 100_000_000, bytes_accessed=800_000, transcendentals=0
        ),
    )(*[a[0] for a in args]))


class LineReduce:
    def __init__(self, part, right, left, m):
        self.part, self.line, self.t = part, m // 2, 2
        self.z = lax.axis_index("dp") // 2
        self.right = jnp.where(self.z >= 1, right.astype(F32), 0.0)
        self.left = jnp.where(self.z <= self.line - 2, left.astype(F32), 0.0)

    def take(self, i):
        i = jnp.clip(i, 0, self.line - 1)
        return lax.dynamic_index_in_dim(self.part, i, 0, keepdims=False).astype(F32)

    def step(self, after):
        line, t = self.line, self.t
        right = (self.take(self.z + line - t) + self.right).astype(BF)
        left = (self.take(self.z - line + t) + self.left).astype(BF)
        right, left = lax.optimization_barrier((right, left) + tuple(after))[:2]
        self.given = right, left
        self.right = lax.ppermute(
            right, "dp", [(2 * i + c, 2 * i + 2 + c) for i in range(t) for c in range(2)]
        ).astype(F32)
        self.left = lax.ppermute(
            left, "dp",
            [(2 * i + c, 2 * i - 2 + c) for i in range(line - t, line) for c in range(2)],
        ).astype(F32)
        self.t += 1

    def finish(self, after):
        while self.t < self.line:
            self.step(after)
        return self.take(self.z) + self.right + self.left


def line_gather(own, m, meanwhile):
    line = m // 2
    right = left = own
    rights, lefts = [], []
    for k in range(1, line):
        right = lax.ppermute(right, "dp", [(i, i + 2) for i in range(2 * (k - 1), m - 2)])
        left = lax.ppermute(left, "dp", [(i, i - 2) for i in range(2, m - 2 * (k - 1))])
        if k in meanwhile and k < line - 1:
            right, left = lax.optimization_barrier((right, left) + meanwhile[k](right, left))[:2]
        rights.append(right)
        lefts.append(left)
    return rights, lefts


def local(
    tokens_in, ln1_gain, ln1_bias, w_qkv, w_out, scale_attn, ln2_gain, ln2_bias, w_gu, w_down,
    scale_mlp, out_cotangent, *, n, m,
):
    rows, w = tokens_in.shape
    images = rows // SEQ
    inner = w_qkv.shape[2]
    heads = inner // HD
    hidden_width = w_gu.shape[2]
    scale = HD ** (-0.5)
    line = m // 2
    hops = line - 1
    shard = D // m
    pieces = min(n, shard // LANE)
    cosines, sines = rope_tables()
    cos2 = jnp.tile(jnp.concatenate([cosines, cosines], axis=1), (images, 1))
    sin2 = jnp.tile(jnp.concatenate([-sines, sines], axis=1), (images, 1))
    wide = (rows, n * w)
    own = (rows, w)
    lanes = (rows, LANE)
    row = lambda v: v.reshape(1, D)
    V = lambda *a: [(x, False) for x in a]
    H = lambda *a: [(x, True) for x in a]

    w_j = jnp.transpose(w_qkv, (1, 0, 2))

    act_one, mean_one, inv_one, gu_j = call(
        functools.partial(first_norm_kernel, n), 1,
        [(wide, BF), (lanes, F32), (lanes, F32), ((2, D, hidden_width), BF, True)],
        [pltpu.VMEM((n,) + own, BF), pltpu.VMEM(lanes, F32)] + gather_sems(n)
        + [pltpu.VMEM((2, 128, 2, hidden_width), BF), pltpu.VMEM((2, 2, 128, hidden_width), BF),
           sems(2), sems(2)],
        V(tokens_in, row(ln1_gain), row(ln1_bias)) + H(w_gu), 50,
    )
    cot_late, act_one = lax.optimization_barrier((out_cotangent, act_one))
    cot_all = lax.all_gather(cot_late, "tensor", axis=1, tiled=True)
    branch_grad = (scale_mlp * cot_all.astype(F32)).astype(BF)
    qkv = qkv_matmul(act_one, w_j, cos2, sin2)
    mixed, attn_part = pl.pallas_call(
        attention_kernel,
        out_shape=[jax.ShapeDtypeStruct((rows, inner), BF), jax.ShapeDtypeStruct(wide, BF)],
        in_specs=[vm()] * 2,
        out_specs=[vm()] * 2,
        compiler_params=pltpu.CompilerParams(vmem_limit_bytes=48 << 20),
    )(qkv, w_out)
    tile = min(512, hidden_width)
    outs = call(
        functools.partial(second_norm_kernel, n, m, pieces), 2,
        [(own, F32), (own, F32), (wide, BF), (lanes, F32), (lanes, F32), ((rows, hidden_width), F32)]
        + [((m, rows, LANE), BF, True)] * 2 + [((rows, inner), BF, True)] * (2 * hops),
        scatter_room(n, rows, w)
        + [pltpu.VMEM(own, BF), pltpu.VMEM((n,) + own, BF), pltpu.VMEM(lanes, F32)]
        + gather_sems(n) + [sems(hops, 4)]
        + [sems(m - 1), sems(m - 1), pltpu.SemaphoreType.DMA] * 2
        + [pltpu.VMEM((2, tile, D), BF), sems(2)],
        V(attn_part, tokens_in, row(scale_attn), row(ln2_gain), row(ln2_bias), branch_grad)
        + H(branch_grad, act_one, mixed, w_down), 80,
    )
    attn_sum, residual, act_two, mean_two, inv_two, hidden_grad, kcot, kact = outs[:8]
    mixed_right, mixed_left = outs[8:8 + hops], outs[8 + hops:]
    side = lambda k: lax.all_gather(k, "tensor", axis=2, tiled=True)[:, :, :shard]
    side_act = side(kact)

    hidden, gate_grad, up_grad = gate_matmul(act_two, gu_j, hidden_grad)
    block = (rows, hidden_width)
    gu_part, hidden_r, hidden_l = call(
        functools.partial(pair_grad_kernel, m), 3,
        [((line, 2, shard, hidden_width), BF), (block, BF, True), (block, BF, True)],
        [pltpu.VMEM((line, rows, shard), BF), pltpu.VMEM((line, rows, shard), BF),
         pltpu.VMEM(block, BF), pltpu.VMEM(block, BF), pltpu.VMEM((2, line, shard, rows), BF),
         sems(line), sems(line), sems(2), sems(2), sems(line), sems(4)],
        H(act_two) + V(gate_grad, up_grad) + H(hidden), 40,
    )
    cut = shard * 7 // 8
    tile = w // 2 if n == 4 else min(512, w)
    outs = call(
        functools.partial(second_back_kernel, n, m), 4,
        [(own, F32), (wide, BF), ((8, w), F32)] + [((2, cut, hidden_width), BF, True)] * 2
        + [(block, BF, True)] * (2 * hops - 2),
        [pltpu.VMEM(wide, BF)] + scatter_room(n, rows, w)
        + [pltpu.VMEM(own, F32), pltpu.VMEM(own, BF),
         pltpu.VMEM(lanes, F32), pltpu.VMEM(lanes, F32), pltpu.VMEM((8, rows), F32),
         pltpu.VMEM((n, 8, rows), F32)] + [sems(n - 1)] * 2 + gather_sems(n)
        + [pltpu.SemaphoreType.DMA, sems(hops - 1, 4), sems(4)]
        + [pltpu.VMEM((2, 2, tile, hidden_width), BF), sems(2)],
        V(gate_grad, up_grad, out_cotangent, residual, attn_sum, mean_two, inv_two, row(ln2_gain), row(scale_attn))
        + H(hidden_r, hidden_l, gu_part, gu_j), 80,
    )
    res_grad, attn_grad, sums_two, gu_right, gu_left = outs[:5]
    hidden_right = [hidden_r] + outs[5:4 + hops]
    hidden_left = [hidden_l] + outs[4 + hops:]
    raw_grad, kattn, gu_right_b, gu_left_b = call(
        functools.partial(attention_back_kernel, m, pieces), 5,
        [((3, rows, inner), BF), ((m, rows, LANE), BF, True)]
        + [((2, shard - cut, hidden_width), BF, True)] * 2,
        [pltpu.VMEM((rows, inner), BF), sems(m - 1), sems(m - 1), pltpu.SemaphoreType.DMA, sems(4)],
        V(attn_grad, w_out, qkv, cos2, sin2) + H(attn_grad, gu_part), 25,
    )
    gu_line = LineReduce(
        gu_part,
        jnp.concatenate([gu_right, gu_right_b], axis=1),
        jnp.concatenate([gu_left, gu_left_b], axis=1),
        m,
    )
    kcot, raw_grad = lax.optimization_barrier((kcot, raw_grad))
    side_cot, side_attn = side(kcot), side(kattn)
    def gathered(ident, mine, rights, lefts, sides, turned, first=0, last=hops, before=None):
        parts, _, width = mine.shape
        shape = (parts, width, shard) if turned else (parts, shard, width)
        blocks = []
        for k in range(first, last + 1):
            blocks += [rights[k - 1], lefts[k - 1]] if k else [mine]
        count = len(blocks)
        (out,) = call(
            functools.partial(gathered_grad_kernel, m, turned, first, last), ident, [(shape, F32)],
            [pltpu.VMEM((count, 2) + mine.shape, BF), pltpu.VMEM((count, 2, shard, rows), BF),
             sems(count), sems(count), sems(count)],
            H(*blocks) + V(sides) + (V(before) if first else []), 30,
        )
        return out

    lead = lambda arrays: [a[None] for a in arrays]
    done = {}

    def after_one(right, left):
        part = back_matmul(raw_grad, w_j)
        done["grad"] = lax.psum_scatter(part, "tensor", scatter_dimension=1, tiled=True)
        return (part,)

    def after_two(right, left):
        gu_line.step((right, left))
        late = lax.optimization_barrier((side_cot, side_attn) + gu_line.given)
        done["attn"] = late[1]
        done["down"] = gathered(
            6, hidden[None], lead(hidden_right), lead(hidden_left), late[0], True
        )[0]
        return ()

    raw_right, raw_left = line_gather(raw_grad, m, {1: after_one, 2: after_two})
    act_one_grad, down_sum = done["grad"], done["down"]
    proj_sum = gathered(7, mixed[None], lead(mixed_right), lead(mixed_left), done["attn"], True)[0]
    branch_part = jnp.dot(hidden, w_down, preferred_element_type=F32).astype(BF)
    qkv_part = gathered(8, raw_grad, raw_right, raw_left, side_act, False, 0, hops - 1)
    gu_sum = gu_line.finish((raw_right[-1], raw_left[-1], down_sum, proj_sum, qkv_part))

    small = jnp.concatenate([jnp.zeros((2, w), F32), sums_two[0:3], jnp.zeros((3, w), F32)], axis=0)
    input_grad, sums, layer_out = call(
        functools.partial(first_back_kernel, n), 9,
        [(own, F32), ((8, w), F32), (own, F32)],
        scatter_room(n, rows, w)
        + [pltpu.VMEM(own, F32),
           pltpu.VMEM(lanes, F32), pltpu.VMEM(lanes, F32), pltpu.VMEM((8, rows), F32),
           pltpu.VMEM((n, 8, rows), F32)] + [sems(n - 1)] * 2,
        V(act_one_grad, res_grad, tokens_in, mean_one, inv_one, row(ln1_gain), small,
          branch_part, residual, out_cotangent, row(scale_mlp)), 20,
    )
    qkv_sum = gathered(
        10, raw_grad, raw_right, raw_left, side_act, False, hops, hops, qkv_part
    )
    gu_sum = jnp.transpose(gu_sum, (1, 0, 2))
    qkv_sum, sums = lax.optimization_barrier((qkv_sum, sums))
    (small_sums,) = call(
        functools.partial(small_sums_kernel, n, m), 11, [((8, n * w), F32)],
        [pltpu.VMEM((m, 8, w), F32), pltpu.VMEM((8, w), F32)] + [sems(m - 1)] * 2 + [sems(n - 1)] * 2,
        V(sums), 10,
    )
    return (
        layer_out,
        input_grad,
        small_sums[0],
        small_sums[1],
        jnp.transpose(qkv_sum, (1, 0, 2)),
        proj_sum,
        small_sums[4],
        small_sums[2],
        small_sums[3],
        gu_sum,
        down_sum,
        small_sums[5],
    )


def solution(mesh):
    placed = (
        P("dp", "tensor"),
        P(),
        P(),
        P(None, None, "tensor"),
        P("tensor", None),
        P(),
        P(),
        P(),
        P(None, None, "tensor"),
        P("tensor", None),
        P(),
        P("dp", "tensor"),
    )
    return jax.shard_map(
        functools.partial(local, n=mesh.shape["tensor"], m=mesh.shape["dp"]),
        mesh=mesh,
        in_specs=placed,
        out_specs=(
            P("dp", "tensor"),
            P("dp", "tensor"),
            P(),
            P(),
            P("dp", None, "tensor"),
            P("tensor", "dp"),
            P(),
            P(),
            P(),
            P("dp", None, "tensor"),
            P("tensor", "dp"),
            P(),
        ),
        check_vma=False,
    )
```

```python
import functools
import math

import jax
import jax.numpy as jnp
from jax import lax
from jax.experimental import pallas as pl
from jax.experimental.pallas import tpu as pltpu
from jax.sharding import PartitionSpec as P

D = 4096
HD = 128
GRID = 14
EXTRA = 5
PATCH = 196
SEQ = 201
EPS = 1e-06
LANE = 128
BF = jnp.bfloat16
F32 = jnp.float32
MESH = pl.DeviceIdType.MESH
ROWS = (((0,), (0,)), ((), ()))
COLS = (((1,), (1,)), ((), ()))


def rope_tables():
    quarter = HD // 4
    theta = (
        2.0
        * math.pi
        * jnp.exp(jnp.arange(quarter, dtype=jnp.float32) * (-4.0 * math.log(100.0) / HD))
    )
    places = jnp.arange(PATCH, dtype=jnp.int32)
    row_pos = ((places // GRID).astype(jnp.float32) + 0.5) * (2.0 / GRID) - 1.0
    col_pos = ((places % GRID).astype(jnp.float32) + 0.5) * (2.0 / GRID) - 1.0
    angles = jnp.concatenate(
        [row_pos[:, None] * theta[None, :], col_pos[:, None] * theta[None, :]], axis=1
    )
    angles = jnp.concatenate([jnp.zeros((EXTRA, HD // 2), jnp.float32), angles], axis=0)
    return (jnp.cos(angles), jnp.sin(angles))


def rotate(vectors, cosines, sines):
    halfway = HD // 2
    leading = vectors[..., :halfway]
    trailing = vectors[..., halfway:]
    cos_b = cosines[:, None, :]
    sin_b = sines[:, None, :]
    return jnp.concatenate(
        [leading * cos_b - trailing * sin_b, leading * sin_b + trailing * cos_b], axis=-1
    )


def greet(n, m=1):
    me = lax.axis_index("tensor")
    you = lax.axis_index("dp")
    barrier = pltpu.get_barrier_semaphore()
    for k in range(1, n):
        pl.semaphore_signal(
            barrier, inc=1, device_id={"tensor": lax.rem(me + k, n)}, device_id_type=MESH
        )
    for k in range(1, m):
        pl.semaphore_signal(
            barrier, inc=1, device_id={"dp": lax.rem(you + k, m)}, device_id_type=MESH
        )
    pl.semaphore_wait(barrier, n + m - 2)


def send(src, dst, send_sem, recv_sem, peer):
    return pltpu.make_async_remote_copy(
        src_ref=src,
        dst_ref=dst,
        send_sem=send_sem,
        recv_sem=recv_sem,
        device_id={"tensor": peer},
        device_id_type=MESH,
    )


def send_dp(src, dst, send_sem, recv_sem, peer):
    return pltpu.make_async_remote_copy(
        src_ref=src,
        dst_ref=dst,
        send_sem=send_sem,
        recv_sem=recv_sem,
        device_id={"dp": peer},
        device_id_type=MESH,
    )


class Hop:
    def __init__(self, k, m, right_src, left_src, right_dst, left_dst, sem):
        you = lax.axis_index("dp")
        z, last = you // 2, m // 2 - 1
        right = send_dp(right_src, right_dst, sem.at[0], sem.at[1], lax.rem(you + 2, m))
        left = send_dp(left_src, left_dst, sem.at[2], sem.at[3], lax.rem(you + m - 2, m))
        self.steps = [
            (right, (z >= k - 1) & (z < last), z >= k),
            (left, (z <= last - k + 1) & (z > 0), z <= last - k),
        ]

    def start(self):
        for copy, sends, _ in self.steps:
            pl.when(sends)(copy.start)

    def wait(self):
        for copy, sends, gets in self.steps:
            pl.when(sends)(copy.wait_send)
            pl.when(gets)(copy.wait_recv)


class End:
    def __init__(self, m, part_ref, at, right_dst, left_dst, sem):
        you = lax.axis_index("dp")
        z, last = you // 2, m // 2 - 1
        some = pl.ds(at, right_dst.shape[1])
        right = send_dp(
            part_ref.at[last, :, some], right_dst, sem.at[0], sem.at[1], lax.rem(you + 2, m)
        )
        left = send_dp(
            part_ref.at[0, :, some], left_dst, sem.at[2], sem.at[3], lax.rem(you + m - 2, m)
        )
        self.steps = [(right, z == 0, z == 1), (left, z == last, z == last - 1)]

    start = Hop.start
    wait = Hop.wait


class Exchange:
    def __init__(self, m, pieces, full_ref, out_ref, ssem, rsem, lsem):
        you = lax.axis_index("dp")
        piece = lax.rem(lax.axis_index("tensor"), pieces)
        self.copies = []
        for k in range(m):
            peer = lax.rem(you + k, m)
            cols = pl.ds(pl.multiple_of((peer * pieces + piece) * LANE, LANE), LANE)
            if k:
                copy = send_dp(
                    full_ref.at[:, cols], out_ref.at[you], ssem.at[k - 1], rsem.at[k - 1], peer
                )
            else:
                copy = pltpu.make_async_copy(full_ref.at[:, cols], out_ref.at[you], lsem)
            self.copies.append(copy)

    def start(self):
        for copy in self.copies:
            copy.start()

    def wait(self):
        for copy in self.copies:
            copy.wait()


def chunks(width, body):
    def step(j, carry):
        body(pl.ds(pl.multiple_of(j * LANE, LANE), LANE))
        return carry

    lax.fori_loop(0, width // LANE, step, 0)


def spread(column, rows):
    return jnp.broadcast_to(column, (rows, LANE))


def beside(me):
    return me + 1 - 2 * lax.rem(me, 2), me + 2 - 4 * (me // 2)


class Gather:
    def __init__(self, n, own_ref, dest, ssem, rsem):
        me = lax.axis_index("tensor")
        w = own_ref.shape[1]
        self.square = n == 4
        if self.square:
            x, y = beside(me)
            half = w // 2
            part = lambda i: own_ref.at[:, i * half:(i + 1) * half]
            to = lambda i, src, owner, at, peer: send(
                src, dest(owner, at * half, half), ssem.at[i], rsem.at[i], peer
            )
            self.copies = [
                to(0, part(0), me, 0, x), to(1, part(1), me, 1, y),
                to(2, part(1), me, 1, x), to(3, part(0), me, 0, y),
            ]
            self.passed = [
                to(4, dest(x, 0, half), x, 0, y), to(5, dest(y, half, half), y, 1, x)
            ]
        else:
            self.copies = [
                send(own_ref, dest(me, 0, w), ssem.at[k - 1], rsem.at[k - 1], lax.rem(me + k, n))
                for k in range(1, n)
            ]

    def start(self):
        for copy in self.copies:
            copy.start()

    def relay(self):
        if self.square:
            for copy, passed in zip(self.copies, self.passed):
                copy.wait_recv()
                passed.start()

    def wait(self):
        if self.square:
            for copy in self.copies:
                copy.wait_send()
            for copy in self.copies[2:]:
                copy.wait_recv()
            wait_all(self.passed)
        else:
            wait_all(self.copies)


class Scatter:
    def __init__(self, n, w, part_ref, slots, come, go, ssem, rsem):
        me = lax.axis_index("tensor")
        self.n, self.w, self.part, self.slots, self.come, self.go = n, w, part_ref, slots, come, go
        self.square = n == 4
        cols = lambda owner, at, size: part_ref.at[:, pl.ds(pl.multiple_of(owner * w + at, LANE), size)]
        if self.square:
            x, y = beside(me)
            far = 3 - me
            half = w // 2
            self.half, self.x, self.y = half, x, y
            to = lambda i, src, dst, peer: send(src, dst, ssem.at[i], rsem.at[i], peer)
            low, high = slice(0, half), slice(half, w)
            self.first = [
                to(0, cols(far, 0, half), come.at[0], x), to(1, cols(far, half, half), come.at[1], y)
            ]
            self.second = [
                to(2, cols(x, 0, half), slots.at[0, :, low], x),
                to(3, cols(y, half, half), slots.at[1, :, high], y),
            ]
            self.third = [
                to(4, go.at[0], slots.at[0, :, high], x), to(5, go.at[1], slots.at[1, :, low], y)
            ]
            self.order = [(far, 0), (far, 1), (x, 0), (y, 1), (x, 1), (y, 0), (me, 0), (me, 1)]
        else:
            self.first = [
                send(cols(lax.rem(me + k, n), 0, w), slots.at[k - 1], ssem.at[k - 1], rsem.at[k - 1],
                     lax.rem(me + k, n))
                for k in range(1, n)
            ]
            self.second = self.third = []

    def start(self):
        for copy in self.first + self.second:
            copy.start()

    def relay(self):
        if self.square:
            half = self.half
            for i, (owner, at) in enumerate(((self.x, half), (self.y, 0))):
                self.first[1 - i].wait_recv()

                def add(cols, i=i, owner=owner, at=at):
                    wide = pl.ds(pl.multiple_of(owner * self.w + at + cols.start, LANE), LANE)
                    self.go[i, :, cols] = (
                        self.part[:, wide].astype(F32) + self.come[1 - i, :, cols].astype(F32)
                    ).astype(BF)

                chunks(half, add)
                self.third[i].start()

    def wait(self):
        if self.square:
            for copy in self.first:
                copy.wait_send()
            wait_all(self.second + self.third)
        else:
            wait_all(self.first)

    def total(self, cols, wide):
        total = self.part[:, wide].astype(F32)
        for k in range(self.slots.shape[0]):
            total = total + self.slots[k, :, cols].astype(F32)
        return total


def scatter_room(n, rows, w):
    count, half = (2, w // 2) if n == 4 else (n - 1, LANE)
    return [
        pltpu.VMEM((count, rows, w), BF), pltpu.VMEM((2, rows, half), BF), pltpu.VMEM((2, rows, half), BF),
        sems(6 if n == 4 else n - 1), sems(6 if n == 4 else n - 1),
    ]


def gather_sems(n):
    return [sems(6 if n == 4 else n - 1)] * 2


def stream(count, fetch, compute):
    fetch(0, 0).start()

    def step(i, carry):
        slot = lax.rem(i, 2)

        @pl.when(i + 1 < count)
        def _():
            fetch(i + 1, 1 - slot).start()

        fetch(i, slot).wait()
        compute(i, slot)
        return carry

    lax.fori_loop(0, count, step, 0)


def wait_all(copies):
    for copy in copies:
        copy.wait()


def row_stats(n, rows, w, all_ref, acc, mean_ref, inv_ref):
    acc[...] = jnp.zeros_like(acc)

    def add(cols):
        total = all_ref[0, :, cols].astype(F32)
        for k in range(1, n):
            total = total + all_ref[k, :, cols].astype(F32)
        acc[...] += total

    chunks(w, add)
    mean_ref[...] = spread(jnp.sum(acc[...], axis=1, keepdims=True) * (1.0 / D), rows)
    acc[...] = jnp.zeros_like(acc)

    def square(cols):
        mean = mean_ref[...]
        total = jnp.zeros_like(mean)
        for k in range(n):
            center = all_ref[k, :, cols].astype(F32) - mean
            total = total + center * center
        acc[...] += total

    chunks(w, square)
    var = jnp.sum(acc[...], axis=1, keepdims=True) * (1.0 / D)
    inv_ref[...] = spread(lax.rsqrt(var + EPS), rows)


def write_act(n, w, all_ref, mean_ref, inv_ref, gain_ref, bias_ref, act_ref):
    def act(cols):
        for k in range(n):
            wide = pl.ds(pl.multiple_of(k * w + cols.start, LANE), LANE)
            center = all_ref[k, :, cols].astype(F32) - mean_ref[...]
            act_ref[:, wide] = (
                center * inv_ref[...] * gain_ref[:, wide] + bias_ref[:, wide]
            ).astype(BF)

    chunks(w, act)


def part_rows(w_ref, out_ref, ibuf, obuf, isem, osem, also):
    size = ibuf.shape[1]
    count = w_ref.shape[0] // size

    def rows_of(i):
        return pl.ds(pl.multiple_of(i * size, size), size)

    def fetch(i, slot):
        return pltpu.make_async_copy(w_ref.at[rows_of(i)], ibuf.at[slot], isem.at[slot])

    def put(i, slot):
        return pltpu.make_async_copy(obuf.at[slot], out_ref.at[:, rows_of(i)], osem.at[slot])

    fetch(0, 0).start()

    def step(i, carry):
        slot = lax.rem(i, 2)
        also(i)

        @pl.when(i + 1 < count)
        def _():
            fetch(i + 1, 1 - slot).start()

        fetch(i, slot).wait()

        @pl.when(i >= 2)
        def _():
            put(i - 2, slot).wait()

        obuf[slot] = jnp.swapaxes(ibuf[slot], 0, 1)
        put(i, slot).start()
        return carry

    lax.fori_loop(0, count, step, 0)
    for i in (count - 2, count - 1):
        put(i, i % 2).wait()


def first_norm_kernel(
    n, x_ref, gain_ref, bias_ref, w_ref, act_ref, mean_ref, inv_ref, parted_ref,
    all_ref, acc, ssem, rsem, ibuf, obuf, isem, osem,
):
    rows, w = x_ref.shape
    me = lax.axis_index("tensor")
    greet(n)
    dest = lambda owner, at, size: all_ref.at[owner, :, pl.ds(at, size)]
    gather = Gather(n, x_ref, dest, ssem, rsem)
    gather.start()
    all_ref[me] = x_ref[...]
    part_rows(w_ref, parted_ref, ibuf, obuf, isem, osem, lambda i: pl.when(i == 12)(gather.relay))
    gather.wait()
    row_stats(n, rows, w, all_ref, acc, mean_ref, inv_ref)
    write_act(n, w, all_ref, mean_ref, inv_ref, gain_ref, bias_ref, act_ref)


def second_norm_kernel(
    n, m, pieces, part_ref, x_ref, scale_ref, gain_ref, bias_ref, mlp_ref, cot_ref, act_one_ref, mixed_ref,
    w_down_ref, attn_ref, res_ref, act_ref, mean_ref, inv_ref, hgrad_ref, kcot_ref, kact_ref, *refs,
):
    hops = m // 2 - 1
    rights, lefts, refs = refs[:hops], refs[hops:2 * hops], refs[2 * hops:]
    (slots, come, go, ssem, rsem, own_ref, all_ref, acc, ssem2, rsem2, hsem,
     css, crs, cls, ass, ars, als, bgrad, wbuf, wsem) = refs
    rows, w = x_ref.shape
    me = lax.axis_index("tensor")
    greet(n, m)
    scatter = Scatter(n, w, part_ref, slots, come, go, ssem, rsem)
    scatter.start()
    line = [
        Hop(k, m, rights[k - 2] if k > 1 else mixed_ref, lefts[k - 2] if k > 1 else mixed_ref,
            rights[k - 1], lefts[k - 1], hsem.at[k - 1])
        for k in range(1, hops + 1)
    ]
    line[0].start()

    def scaled(cols):
        bgrad[:, cols] = (mlp_ref[:, cols] * cot_ref[:, cols].astype(F32)).astype(BF)

    chunks(n * w, scaled)
    side = Exchange(m, pieces, bgrad, kcot_ref, css, crs, cls)
    side.start()
    tile = wbuf.shape[1]
    count = hgrad_ref.shape[1] // tile

    def fetch(i, slot):
        return pltpu.make_async_copy(
            w_down_ref.at[pl.ds(pl.multiple_of(i * tile, tile), tile), :], wbuf.at[slot], wsem.at[slot]
        )

    def compute(i, slot):
        hgrad_ref[:, pl.ds(pl.multiple_of(i * tile, tile), tile)] = lax.dot_general(
            bgrad[...], wbuf[slot], COLS, preferred_element_type=F32
        )

        @pl.when(i == count // 2)
        def _():
            scatter.relay()

    stream(count, fetch, compute)
    line[0].wait()
    if hops > 1:
        line[1].start()
    other = Exchange(m, pieces, act_one_ref, kact_ref, ass, ars, als)
    other.start()
    scatter.wait()

    def add(cols):
        wide = pl.ds(pl.multiple_of(me * w + cols.start, LANE), LANE)
        total = scatter.total(cols, wide)
        attn_ref[:, cols] = total
        res = x_ref[:, cols].astype(F32) + scale_ref[:, wide] * total
        res_ref[:, cols] = res
        own_ref[:, cols] = res.astype(BF)

    chunks(w, add)
    dest = lambda owner, at, size: all_ref.at[owner, :, pl.ds(at, size)]
    gather = Gather(n, own_ref, dest, ssem2, rsem2)
    gather.start()
    all_ref[me] = own_ref[...]
    gather.relay()
    for k in range(1, hops - 1):
        line[k].wait()
        line[k + 1].start()
    gather.wait()
    row_stats(n, rows, w, all_ref, acc, mean_ref, inv_ref)
    write_act(n, w, all_ref, mean_ref, inv_ref, gain_ref, bias_ref, act_ref)
    line[-1].wait()
    side.wait()
    other.wait()


def norm_back(n, w, load_total, grad_ref, base_ref, mean_ref, inv_ref, gain_ref,
              sums, acc, acc2, stat_own, stats, ssem, rsem, out):
    rows = grad_ref.shape[0]
    me = lax.axis_index("tensor")
    acc[...] = jnp.zeros_like(acc)
    acc2[...] = jnp.zeros_like(acc2)

    def first(cols):
        wide = pl.ds(pl.multiple_of(me * w + cols.start, LANE), LANE)
        total = load_total(cols, wide)
        grad_ref[:, cols] = total
        normed = (base_ref[:, cols].astype(F32) - mean_ref[...]) * inv_ref[...]
        sums[0:1, cols] = jnp.sum(total * normed, axis=0, keepdims=True)
        sums[1:2, cols] = jnp.sum(total, axis=0, keepdims=True)
        scaled = total * gain_ref[:, wide]
        acc[...] += scaled
        acc2[...] += scaled * normed

    chunks(w, first)
    ones = jnp.ones((8, LANE), F32)
    high = lax.Precision.HIGHEST
    plain = lax.dot_general(ones, acc[...], COLS, precision=high, preferred_element_type=F32)
    cross = lax.dot_general(ones, acc2[...], COLS, precision=high, preferred_element_type=F32)
    line = lax.broadcasted_iota(jnp.int32, (8, rows), 0)
    stat_own[...] = jnp.where(line < 4, plain, cross)
    copies = [
        send(stat_own, stats.at[me], ssem.at[k - 1], rsem.at[k - 1], lax.rem(me + k, n))
        for k in range(1, n)
    ]
    for copy in copies:
        copy.start()
    wait_all(copies)
    both = stat_own[...]
    for k in range(1, n):
        both = both + stats[lax.rem(me + k, n)]
    both = both * (1.0 / D)
    pick = lax.broadcasted_iota(jnp.int32, (8, LANE), 0)
    acc[...] = lax.dot_general(
        both, (pick == 0).astype(F32), ROWS, precision=high, preferred_element_type=F32
    )
    acc2[...] = lax.dot_general(
        both, (pick == 4).astype(F32), ROWS, precision=high, preferred_element_type=F32
    )

    def second(cols):
        wide = pl.ds(pl.multiple_of(me * w + cols.start, LANE), LANE)
        normed = (base_ref[:, cols].astype(F32) - mean_ref[...]) * inv_ref[...]
        scaled = grad_ref[:, cols] * gain_ref[:, wide]
        out(cols, wide, inv_ref[...] * (scaled - acc[...] - normed * acc2[...]))

    chunks(w, second)


def second_back_kernel(
    n, m, gate_ref, up_ref, cot_ref, res_ref, attn_ref, mean_ref, inv_ref, gain_ref, scale_ref,
    right_ref, left_ref, gu_ref, w_ref, rgrad_ref, agrad_ref, sums_ref, gu_right, gu_left, *refs,
):
    hops = m // 2 - 1
    rights = (right_ref,) + refs[:hops - 1]
    lefts = (left_ref,) + refs[hops - 1:2 * hops - 2]
    (part_ref, slots, come, go, ssem, rsem, grad_ref, own_ref, acc, acc2, stat_own, stats,
     ssem2, rsem2, ssem3, rsem3, lsem, hsem, gsem, wbuf, wsem) = refs[2 * hops - 2:]
    w = cot_ref.shape[1]
    me = lax.axis_index("tensor")
    greet(n, m)
    line = [
        Hop(k, m, rights[k - 2], lefts[k - 2], rights[k - 1], lefts[k - 1], hsem.at[k - 2])
        for k in range(2, hops + 1)
    ]
    line[0].start()
    first = End(m, gu_ref, 0, gu_right, gu_left, gsem)
    first.start()
    scatter = Scatter(n, w, part_ref, slots, come, go, ssem, rsem)
    tile = wbuf.shape[2]
    count = D // tile

    def spot(i):
        if not scatter.square:
            return pl.ds(pl.multiple_of(i * tile, LANE), tile)
        at = 0
        for k, (owner, half) in enumerate(scatter.order):
            at = at + jnp.where(i == k, owner * w + half * tile, 0)
        return pl.ds(pl.multiple_of(at, LANE), tile)

    def fetch(i, slot):
        return pltpu.make_async_copy(w_ref.at[:, spot(i), :], wbuf.at[slot], wsem.at[slot])

    def compute(i, slot):
        part_ref[:, spot(i)] = (
            lax.dot_general(gate_ref[...], wbuf[slot, 0], COLS, preferred_element_type=F32)
            + lax.dot_general(up_ref[...], wbuf[slot, 1], COLS, preferred_element_type=F32)
        ).astype(BF)
        if scatter.square:
            for k, copy in enumerate(scatter.first + scatter.second):
                pl.when(i == k)(copy.start)
            pl.when(i == 5)(scatter.relay)

    stream(count, fetch, compute)
    if not scatter.square:
        scatter.start()
    scatter.wait()
    sums_ref[...] = jnp.zeros_like(sums_ref)

    def out(cols, wide, back):
        res_grad = cot_ref[:, cols].astype(F32) + back
        rgrad_ref[:, cols] = res_grad
        sums_ref[2:3, cols] = jnp.sum(res_grad * attn_ref[:, cols], axis=0, keepdims=True)
        own_ref[:, cols] = (scale_ref[:, wide] * res_grad).astype(BF)

    norm_back(n, w, scatter.total, grad_ref, res_ref, mean_ref, inv_ref, gain_ref,
              sums_ref, acc, acc2, stat_own, stats, ssem2, rsem2, out)
    dest = lambda owner, at, size: agrad_ref.at[:, pl.ds(pl.multiple_of(owner * w + at, LANE), size)]
    gather = Gather(n, own_ref, dest, ssem3, rsem3)
    gather.start()
    local = pltpu.make_async_copy(own_ref, dest(me, 0, w), lsem)
    local.start()
    gather.relay()
    for k in range(len(line)):
        line[k].wait()
        if k + 1 < len(line):
            line[k + 1].start()
    local.wait()
    gather.wait()
    first.wait()


def first_back_kernel(
    n, grad_in, x_ref, mean_ref, inv_ref, gain_ref, small_ref,
    part_ref, cot_ref, scale_ref,
    igrad_ref, sums, out_ref,
    slots, come, go, ssem, rsem, grad_ref, acc, acc2, stat_own, stats, ssem2, rsem2,
):
    w = x_ref.shape[1]
    greet(n)
    scatter = Scatter(n, w, part_ref, slots, come, go, ssem, rsem)
    scatter.start()
    sums[...] = small_ref[...]
    scatter.relay()

    def load_total(cols, wide):
        return grad_in[:, cols].astype(F32)

    def out(cols, wide, back):
        igrad_ref[:, cols] = back

    norm_back(n, w, load_total, grad_ref, x_ref, mean_ref, inv_ref, gain_ref,
              sums, acc, acc2, stat_own, stats, ssem2, rsem2, out)
    scatter.wait()
    me = lax.axis_index("tensor")

    def add(cols):
        wide = pl.ds(pl.multiple_of(me * w + cols.start, LANE), LANE)
        total = scatter.total(cols, wide)
        out_ref[:, cols] = scale_ref[:, wide] * total
        sums[5:6, cols] = jnp.sum(cot_ref[:, cols].astype(F32) * total, axis=0, keepdims=True)

    chunks(w, add)


def mate_of(you):
    return you + 1 - 2 * lax.rem(you, 2)


def pair_grad_kernel(
    m, act_ref, gate_ref, up_ref, hidden_ref, out_ref, right_ref, left_ref,
    acts, mates, gates, ups, flip, obuf, asem, arem, gsem, grem, lsem, hsem, osem,
):
    line = m // 2
    you = lax.axis_index("dp")
    core, mate = lax.rem(you, 2), mate_of(you)
    width = acts.shape[-1]
    tile = 512
    greet(1, m)
    hop = Hop(1, m, hidden_ref, hidden_ref, right_ref, left_ref, hsem)
    copies = [
        send_dp(gate_ref, gates, gsem.at[0], grem.at[0], mate),
        send_dp(up_ref, ups, gsem.at[1], grem.at[1], mate),
    ]
    locals_ = []
    for k in range(line):
        theirs = pl.ds(pl.multiple_of((2 * k + 1 - core) * width, LANE), width)
        ours = pl.ds(pl.multiple_of((2 * k + core) * width, LANE), width)
        copies.append(send_dp(act_ref.at[:, theirs], mates.at[k], asem.at[k], arem.at[k], mate))
        locals_.append(pltpu.make_async_copy(act_ref.at[:, ours], acts.at[k], lsem.at[k]))
    for copy in locals_ + copies:
        copy.start()
    hop.start()
    for copy in locals_:
        copy.wait()
    for k in range(line):
        flip[0, k] = acts[k].T
    for copy in copies:
        copy.wait()
    for k in range(line):
        flip[1, k] = mates[k].T
    def put(k):
        return pltpu.make_async_copy(obuf.at[k % 2], out_ref.at[k], osem.at[k % 2])

    for k in range(line):
        if k >= 2:
            put(k - 2).wait()
        for j, (near, far) in enumerate(((gate_ref, gates), (up_ref, ups))):

            def step(i, carry, k=k, j=j, near=near, far=far):
                cols = pl.ds(pl.multiple_of(i * tile, tile), tile)
                obuf[k % 2, j, :, cols] = (
                    jnp.dot(flip[0, k], near[:, cols], preferred_element_type=F32)
                    + jnp.dot(flip[1, k], far[:, cols], preferred_element_type=F32)
                ).astype(BF)
                return carry

            lax.fori_loop(0, gate_ref.shape[1] // tile, step, 0)
        put(k).start()
    for k in range(max(line - 2, 0), line):
        put(k).wait()
    hop.wait()


class SmallSums:
    def __init__(self, n, m, sums, out, parts, total, dss, drs, tss, trs):
        self.out, self.sums, self.parts, self.total = out, sums, parts, total
        me, you = lax.axis_index("tensor"), lax.axis_index("dp")
        w = sums.shape[1]
        self.m, self.you = m, you
        self.mine = pl.ds(pl.multiple_of(me * w, w), w)
        self.dp = [
            send_dp(sums, parts.at[you], dss.at[k - 1], drs.at[k - 1], lax.rem(you + k, m))
            for k in range(1, m)
        ]
        self.tensor = [
            send(total, out.at[:, self.mine], tss.at[k - 1], trs.at[k - 1], lax.rem(me + k, n))
            for k in range(1, n)
        ]

    def start(self):
        for copy in self.dp:
            copy.start()

    def finish(self):
        self.parts[self.you] = self.sums[...]
        wait_all(self.dp)
        total = self.parts[0]
        for k in range(1, self.m):
            total = total + self.parts[k]
        self.total[...] = total
        for copy in self.tensor:
            copy.start()
        self.out[:, self.mine] = total
        wait_all(self.tensor)


def small_sums_kernel(n, m, sums, out_ref, parts, total, *room):
    greet(n, m)
    small = SmallSums(n, m, sums, out_ref, parts, total, *room)
    small.start()
    small.finish()


def gathered_grad_kernel(m, turned, first, last, *refs):
    hops = m // 2 - 1
    you = lax.axis_index("dp")
    core, mate, z = lax.rem(you, 2), mate_of(you), you // 2
    todo = []
    refs = list(refs)
    for k in range(first, last + 1):
        if k == 0:
            todo.append((None, refs.pop(0), z))
        else:
            todo.append((z >= k, refs.pop(0), z - k))
            todo.append((z <= hops - k, refs.pop(0), z + k))
    side_ref = refs.pop(0)
    out_ref, blocks, flip, lsem, ssem, rsem = refs
    greet(1, m)
    copies = []
    for at, (cond, src, chip) in enumerate(todo):
        near = pltpu.make_async_copy(src, blocks.at[at, core], lsem.at[at])
        far = send_dp(src, blocks.at[at, core], ssem.at[at], rsem.at[at], mate)
        copies.append((cond, near, far))

    def when(cond, body):
        body() if cond is None else pl.when(cond)(body)

    def go(near, far):
        near.start()
        far.start()

    def done(near, far):
        near.wait()
        far.wait()

    def turn(at, chip):
        for c in range(2):
            flip[at, c] = side_ref[2 * chip + c].T

    for cond, near, far in copies:
        when(cond, functools.partial(go, near, far))
    for at, (cond, _, chip) in enumerate(todo):
        when(cond, functools.partial(turn, at, chip))
    for cond, near, far in copies:
        when(cond, functools.partial(done, near, far))
    tile = 512
    parts, width = out_ref.shape[0], blocks.shape[-1]
    if first:
        out_ref[...] = jnp.zeros_like(out_ref)
    for at, (cond, _, chip) in enumerate(todo):
        for j in range(parts):

            def step(i, carry, at=at, j=j):
                cols = pl.ds(pl.multiple_of(i * tile, tile), tile)
                total = jnp.dot(
                    flip[at, 0], blocks[at, 0, j, :, cols], preferred_element_type=F32
                ) + jnp.dot(flip[at, 1], blocks[at, 1, j, :, cols], preferred_element_type=F32)
                if turned:
                    if first or at:
                        out_ref[j, cols, :] += total.T
                    else:
                        out_ref[j, cols, :] = total.T
                elif first or at:
                    out_ref[j, :, cols] += total
                else:
                    out_ref[j, :, cols] = total
                return carry

            def run(step=step):
                lax.fori_loop(0, width // tile, step, 0)

            when(cond, run)


def qkv_kernel(act_ref, w_ref, cos_ref, sin_ref, out_ref):
    raw = jnp.dot(act_ref[...], w_ref[...], preferred_element_type=F32)
    part = pl.program_id(0)

    @pl.when(part < 2)
    def _():
        for h in range(raw.shape[1] // HD):
            cols = slice(h * HD, (h + 1) * HD)
            t = raw[:, cols]
            out_ref[:, cols] = (
                t * cos_ref[...] + pltpu.roll(t, HD // 2, 1) * sin_ref[...]
            ).astype(BF)

    @pl.when(part == 2)
    def _():
        out_ref[...] = raw.astype(BF)


def qkv_matmul(act, w_j, cos2, sin2):
    rows = act.shape[0]
    inner = w_j.shape[2]
    tile = min(512, inner)
    return pl.pallas_call(
        qkv_kernel,
        grid=(3, inner // tile),
        out_shape=jax.ShapeDtypeStruct((3, rows, inner), BF),
        in_specs=[
            pl.BlockSpec((rows, D), lambda j, i: (0, 0)),
            pl.BlockSpec((None, D, tile), lambda j, i: (j, 0, i)),
            pl.BlockSpec((rows, HD), lambda j, i: (0, 0)),
            pl.BlockSpec((rows, HD), lambda j, i: (0, 0)),
        ],
        out_specs=pl.BlockSpec((None, rows, tile), lambda j, i: (j, 0, i)),
        compiler_params=pltpu.CompilerParams(vmem_limit_bytes=40 << 20),
        cost_estimate=pl.CostEstimate(
            flops=2 * rows * D * 3 * inner, bytes_accessed=6 * D * inner, transcendentals=0
        ),
    )(act, w_j, cos2, sin2)


def attention_probs(q, k, same):
    scores = lax.dot_general(k, q, COLS, preferred_element_type=F32) * (HD ** (-0.5))
    scores = jnp.where(same, scores, -jnp.inf)
    top = jnp.max(scores, axis=0, keepdims=True)
    weight = jnp.exp(scores - top)
    return weight / jnp.sum(weight, axis=0, keepdims=True)


def same_image(rows):
    one = lax.broadcasted_iota(jnp.int32, (rows, rows), 0)
    two = lax.broadcasted_iota(jnp.int32, (rows, rows), 1)
    image = lambda i: sum((i >= SEQ * k).astype(jnp.int32) for k in range(1, rows // SEQ))
    return image(one) == image(two)


def attention_kernel(qkv_ref, w_ref, mixed_ref, part_ref):
    rows, inner = mixed_ref.shape

    def head(h, carry):
        cols = pl.ds(pl.multiple_of(h * HD, HD), HD)
        probs = attention_probs(qkv_ref[0, :, cols], qkv_ref[1, :, cols], same_image(rows))
        value = qkv_ref[2, :, cols].astype(F32).T.astype(BF)
        mixed = jnp.dot(value, probs.astype(BF), preferred_element_type=F32)
        mixed_ref[:, cols] = mixed.T.astype(BF)
        return carry

    lax.fori_loop(0, inner // HD, head, 0)

    def tile(i, carry):
        cols = pl.ds(pl.multiple_of(i * 512, 512), 512)
        part_ref[:, cols] = jnp.dot(
            mixed_ref[...], w_ref[:, cols], preferred_element_type=F32
        ).astype(BF)
        return carry

    lax.fori_loop(0, D // 512, tile, 0)


def attention_back_kernel(
    m, pieces, agrad_ref, w_ref, qkv_ref, cos_ref, sin_ref, full_ref, gu_ref,
    out_ref, kattn_ref, gu_right, gu_left, mgrad, ass, ars, als, gsem,
):
    rows, inner = mgrad.shape
    greet(1, m)
    rest = End(m, gu_ref, gu_ref.shape[2] - gu_right.shape[1], gu_right, gu_left, gsem)
    rest.start()
    side = Exchange(m, pieces, full_ref, kattn_ref, ass, ars, als)
    side.start()
    step = min(256, inner)

    def tile(i, carry):
        cols = pl.ds(pl.multiple_of(i * step, step), step)
        mgrad[:, cols] = lax.dot_general(
            agrad_ref[...], w_ref[cols, :], COLS, preferred_element_type=F32
        ).astype(BF)
        return carry

    lax.fori_loop(0, inner // step, tile, 0)

    def back(t):
        return t * cos_ref[...] - pltpu.roll(t, HD // 2, 1) * sin_ref[...]

    def head(h, carry):
        cols = pl.ds(pl.multiple_of(h * HD, HD), HD)
        q, k, v = qkv_ref[0, :, cols], qkv_ref[1, :, cols], qkv_ref[2, :, cols]
        grad = mgrad[:, cols]
        probs = attention_probs(q, k, same_image(rows))
        prob_grad = lax.dot_general(v, grad, COLS, preferred_element_type=F32)
        delta = jnp.sum(probs * prob_grad, axis=0, keepdims=True)
        score_grad = (probs * (prob_grad - delta)).astype(BF)
        scale = HD ** (-0.5)
        flipped = k.astype(F32).T.astype(BF)
        q_grad = jnp.dot(flipped, score_grad, preferred_element_type=F32).T * scale
        k_grad = jnp.dot(score_grad, q, preferred_element_type=F32) * scale
        out_ref[0, :, cols] = back(q_grad).astype(BF)
        out_ref[1, :, cols] = back(k_grad).astype(BF)
        out_ref[2, :, cols] = jnp.dot(
            probs.astype(BF), grad, preferred_element_type=F32
        ).astype(BF)
        return carry

    lax.fori_loop(0, inner // HD, head, 0)
    side.wait()
    rest.wait()


def gate_kernel(act_ref, w_ref, hgrad_ref, hidden_ref, gate_ref, up_ref):
    gate = jnp.dot(act_ref[...], w_ref[0], preferred_element_type=F32)
    up = jnp.dot(act_ref[...], w_ref[1], preferred_element_type=F32)
    sig = jax.nn.sigmoid(gate)
    grad = hgrad_ref[...]
    hidden_ref[...] = (gate * sig * up).astype(BF)
    gate_ref[...] = (grad * up * sig * (1.0 + gate * (1.0 - sig))).astype(BF)
    up_ref[...] = (grad * gate * sig).astype(BF)


def gate_matmul(act, w_j, hidden_grad):
    rows, width = hidden_grad.shape
    tile = min(256, width)
    block = pl.BlockSpec((rows, tile), lambda i: (0, i))
    return pl.pallas_call(
        gate_kernel,
        grid=(width // tile,),
        out_shape=[jax.ShapeDtypeStruct((rows, width), BF)] * 3,
        in_specs=[
            pl.BlockSpec((rows, D), lambda i: (0, 0)),
            pl.BlockSpec((2, D, tile), lambda i: (0, 0, i)),
            block,
        ],
        out_specs=[block] * 3,
        compiler_params=pltpu.CompilerParams(vmem_limit_bytes=48 << 20),
    )(act, w_j, hidden_grad)


def back_kernel(g_ref, w_ref, out_ref):
    total = None
    for j in range(g_ref.shape[0]):
        term = lax.dot_general(g_ref[j], w_ref[j], COLS, preferred_element_type=F32)
        total = term if total is None else total + term
    out_ref[...] = total.astype(BF)


def back_matmul(grads, w_j):
    parts, rows, inner = grads.shape
    tile = 512
    return pl.pallas_call(
        back_kernel,
        grid=(D // tile,),
        out_shape=jax.ShapeDtypeStruct((rows, D), BF),
        in_specs=[
            pl.BlockSpec((parts, rows, inner), lambda i: (0, 0, 0)),
            pl.BlockSpec((parts, tile, inner), lambda i: (0, i, 0)),
        ],
        out_specs=pl.BlockSpec((rows, tile), lambda i: (0, i)),
        compiler_params=pltpu.CompilerParams(vmem_limit_bytes=40 << 20),
        cost_estimate=pl.CostEstimate(
            flops=rows * D * parts * inner * 100 // 500,
            bytes_accessed=800_000,
            transcendentals=0,
        ),
    )(grads, w_j)


def vm():
    return pl.BlockSpec(memory_space=pltpu.VMEM)


def hb():
    return pl.BlockSpec(memory_space=pltpu.HBM)


def sems(*shape):
    return pltpu.SemaphoreType.DMA(shape)


def call(kernel, ident, outs, scratch, args, micros=30):
    shapes = [jax.ShapeDtypeStruct(o[0], o[1]) for o in outs]
    return list(pl.pallas_call(
        kernel,
        out_shape=shapes,
        in_specs=[hb() if a[1] else vm() for a in args],
        out_specs=[hb() if len(o) > 2 else vm() for o in outs],
        scratch_shapes=scratch,
        compiler_params=pltpu.CompilerParams(
            collective_id=ident, has_side_effects=True, vmem_limit_bytes=56 << 20
        ),
        cost_estimate=pl.CostEstimate(
            flops=micros * 100_000_000, bytes_accessed=800_000, transcendentals=0
        ),
    )(*[a[0] for a in args]))


def join_kernel(one, two, three, out_ref):
    total = one[...].astype(F32) + two[...].astype(F32) + three[...].astype(F32)
    out_ref[...] = jnp.swapaxes(total, 0, 1)


def join(one, two, three):
    _, rows, width = one.shape
    size = 64
    block = pl.BlockSpec((2, size, width), lambda i: (0, i, 0))
    return pl.pallas_call(
        join_kernel,
        grid=(rows // size,),
        out_shape=jax.ShapeDtypeStruct((rows, 2, width), F32),
        in_specs=[block] * 3,
        out_specs=pl.BlockSpec((size, 2, width), lambda i: (i, 0, 0)),
        compiler_params=pltpu.CompilerParams(vmem_limit_bytes=32 << 20),
    )(one, two, three)


class LineReduce:
    def __init__(self, part, right, left, m):
        self.part, self.line, self.t = part, m // 2, 2
        self.z = lax.axis_index("dp") // 2
        self.right = jnp.where(self.z >= 1, right.astype(F32), 0.0)
        self.left = jnp.where(self.z <= self.line - 2, left.astype(F32), 0.0)

    def take(self, i):
        i = jnp.clip(i, 0, self.line - 1)
        return lax.dynamic_index_in_dim(self.part, i, 0, keepdims=False).astype(F32)

    def step(self, after):
        line, t = self.line, self.t
        right = (self.take(self.z + line - t) + self.right).astype(BF)
        left = (self.take(self.z - line + t) + self.left).astype(BF)
        right, left = lax.optimization_barrier((right, left) + tuple(after))[:2]
        self.given = right, left
        self.right = lax.ppermute(
            right, "dp", [(2 * i + c, 2 * i + 2 + c) for i in range(t) for c in range(2)]
        ).astype(F32)
        self.left = lax.ppermute(
            left, "dp",
            [(2 * i + c, 2 * i - 2 + c) for i in range(line - t, line) for c in range(2)],
        ).astype(F32)
        self.t += 1

    def finish(self, after):
        while self.t < self.line:
            self.step(after)
        own = lax.dynamic_index_in_dim(self.part, self.z, 0, keepdims=False)
        return join(own, self.right.astype(BF), self.left.astype(BF))


def line_gather(own, m, meanwhile):
    line = m // 2
    right = left = own
    rights, lefts = [], []
    for k in range(1, line):
        right = lax.ppermute(right, "dp", [(i, i + 2) for i in range(2 * (k - 1), m - 2)])
        left = lax.ppermute(left, "dp", [(i, i - 2) for i in range(2, m - 2 * (k - 1))])
        if k in meanwhile and k < line - 1:
            right, left = lax.optimization_barrier((right, left) + meanwhile[k](right, left))[:2]
        rights.append(right)
        lefts.append(left)
    return rights, lefts


def local(
    tokens_in, ln1_gain, ln1_bias, w_qkv, w_out, scale_attn, ln2_gain, ln2_bias, w_gu, w_down,
    scale_mlp, out_cotangent, *, n, m,
):
    rows, w = tokens_in.shape
    images = rows // SEQ
    inner = w_qkv.shape[2]
    heads = inner // HD
    hidden_width = w_gu.shape[2]
    scale = HD ** (-0.5)
    line = m // 2
    hops = line - 1
    shard = D // m
    pieces = min(n, shard // LANE)
    cosines, sines = rope_tables()
    cos2 = jnp.tile(jnp.concatenate([cosines, cosines], axis=1), (images, 1))
    sin2 = jnp.tile(jnp.concatenate([-sines, sines], axis=1), (images, 1))
    wide = (rows, n * w)
    own = (rows, w)
    lanes = (rows, LANE)
    row = lambda v: v.reshape(1, D)
    V = lambda *a: [(x, False) for x in a]
    H = lambda *a: [(x, True) for x in a]

    w_j = jnp.transpose(w_qkv, (1, 0, 2))

    act_one, mean_one, inv_one, gu_j = call(
        functools.partial(first_norm_kernel, n), 1,
        [(wide, BF), (lanes, F32), (lanes, F32), ((2, D, hidden_width), BF, True)],
        [pltpu.VMEM((n,) + own, BF), pltpu.VMEM(lanes, F32)] + gather_sems(n)
        + [pltpu.VMEM((2, 128, 2, hidden_width), BF), pltpu.VMEM((2, 2, 128, hidden_width), BF),
           sems(2), sems(2)],
        V(tokens_in, row(ln1_gain), row(ln1_bias)) + H(w_gu), 50,
    )
    cot_late, act_one = lax.optimization_barrier((out_cotangent, act_one))
    cot_all = lax.all_gather(cot_late, "tensor", axis=1, tiled=True)
    qkv = qkv_matmul(act_one, w_j, cos2, sin2)
    mixed, attn_part = pl.pallas_call(
        attention_kernel,
        out_shape=[jax.ShapeDtypeStruct((rows, inner), BF), jax.ShapeDtypeStruct(wide, BF)],
        in_specs=[vm()] * 2,
        out_specs=[vm()] * 2,
        compiler_params=pltpu.CompilerParams(vmem_limit_bytes=48 << 20),
    )(qkv, w_out)
    tile = min(512, hidden_width)
    outs = call(
        functools.partial(second_norm_kernel, n, m, pieces), 2,
        [(own, F32), (own, F32), (wide, BF), (lanes, F32), (lanes, F32), ((rows, hidden_width), F32)]
        + [((m, rows, LANE), BF, True)] * 2 + [((rows, inner), BF, True)] * (2 * hops),
        scatter_room(n, rows, w)
        + [pltpu.VMEM(own, BF), pltpu.VMEM((n,) + own, BF), pltpu.VMEM(lanes, F32)]
        + gather_sems(n) + [sems(hops, 4)]
        + [sems(m - 1), sems(m - 1), pltpu.SemaphoreType.DMA] * 2
        + [pltpu.VMEM(wide, BF), pltpu.VMEM((2, tile, D), BF), sems(2)],
        V(attn_part, tokens_in, row(scale_attn), row(ln2_gain), row(ln2_bias), row(scale_mlp), cot_all)
        + H(act_one, mixed, w_down), 80,
    )
    attn_sum, residual, act_two, mean_two, inv_two, hidden_grad, kcot, kact = outs[:8]
    mixed_right, mixed_left = outs[8:8 + hops], outs[8 + hops:]
    side = lambda k: lax.all_gather(k, "tensor", axis=2, tiled=True)[:, :, :shard]
    side_act = side(kact)

    hidden, gate_grad, up_grad = gate_matmul(act_two, gu_j, hidden_grad)
    block = (rows, hidden_width)
    gu_part, hidden_r, hidden_l = call(
        functools.partial(pair_grad_kernel, m), 3,
        [((line, 2, shard, hidden_width), BF, True), (block, BF, True), (block, BF, True)],
        [pltpu.VMEM((line, rows, shard), BF), pltpu.VMEM((line, rows, shard), BF),
         pltpu.VMEM(block, BF), pltpu.VMEM(block, BF), pltpu.VMEM((2, line, shard, rows), BF),
         pltpu.VMEM((2, 2, shard, hidden_width), BF),
         sems(line), sems(line), sems(2), sems(2), sems(line), sems(4), sems(2)],
        H(act_two) + V(gate_grad, up_grad) + H(hidden), 40,
    )
    cut = shard * 7 // 8
    tile = w // 2 if n == 4 else min(512, w)
    outs = call(
        functools.partial(second_back_kernel, n, m), 4,
        [(own, F32), (wide, BF), ((8, w), F32)] + [((2, cut, hidden_width), BF, True)] * 2
        + [(block, BF, True)] * (2 * hops - 2),
        [pltpu.VMEM(wide, BF)] + scatter_room(n, rows, w)
        + [pltpu.VMEM(own, F32), pltpu.VMEM(own, BF),
         pltpu.VMEM(lanes, F32), pltpu.VMEM(lanes, F32), pltpu.VMEM((8, rows), F32),
         pltpu.VMEM((n, 8, rows), F32)] + [sems(n - 1)] * 2 + gather_sems(n)
        + [pltpu.SemaphoreType.DMA, sems(hops - 1, 4), sems(4)]
        + [pltpu.VMEM((2, 2, tile, hidden_width), BF), sems(2)],
        V(gate_grad, up_grad, out_cotangent, residual, attn_sum, mean_two, inv_two, row(ln2_gain), row(scale_attn))
        + H(hidden_r, hidden_l, gu_part, gu_j), 80,
    )
    res_grad, attn_grad, sums_two, gu_right, gu_left = outs[:5]
    hidden_right = [hidden_r] + outs[5:4 + hops]
    hidden_left = [hidden_l] + outs[4 + hops:]
    raw_grad, kattn, gu_right_b, gu_left_b = call(
        functools.partial(attention_back_kernel, m, pieces), 5,
        [((3, rows, inner), BF), ((m, rows, LANE), BF, True)]
        + [((2, shard - cut, hidden_width), BF, True)] * 2,
        [pltpu.VMEM((rows, inner), BF), sems(m - 1), sems(m - 1), pltpu.SemaphoreType.DMA, sems(4)],
        V(attn_grad, w_out, qkv, cos2, sin2) + H(attn_grad, gu_part), 25,
    )
    gu_line = LineReduce(
        gu_part,
        jnp.concatenate([gu_right, gu_right_b], axis=1),
        jnp.concatenate([gu_left, gu_left_b], axis=1),
        m,
    )
    kcot, raw_grad = lax.optimization_barrier((kcot, raw_grad))
    side_cot, side_attn = side(kcot), side(kattn)
    def gathered(ident, mine, rights, lefts, sides, turned, first=0, last=hops):
        parts, _, width = mine.shape
        shape = (parts, width, shard) if turned else (parts, shard, width)
        blocks = []
        for k in range(first, last + 1):
            blocks += [rights[k - 1], lefts[k - 1]] if k else [mine]
        count = len(blocks)
        (out,) = call(
            functools.partial(gathered_grad_kernel, m, turned, first, last), ident, [(shape, F32)],
            [pltpu.VMEM((count, 2) + mine.shape, BF), pltpu.VMEM((count, 2, shard, rows), BF),
             sems(count), sems(count), sems(count)],
            H(*blocks) + V(sides), 30,
        )
        return out

    lead = lambda arrays: [a[None] for a in arrays]
    done = {}

    def after_one(right, left):
        part = back_matmul(raw_grad, w_j)
        done["grad"] = lax.psum_scatter(part, "tensor", scatter_dimension=1, tiled=True)
        return (part,)

    def after_two(right, left):
        gu_line.step((right, left))
        late = lax.optimization_barrier((side_cot, side_attn) + gu_line.given)
        done["attn"] = late[1]
        done["down"] = gathered(
            6, hidden[None], lead(hidden_right), lead(hidden_left), late[0], True
        )[0]
        return ()

    raw_right, raw_left = line_gather(raw_grad, m, {1: after_one, 2: after_two})
    act_one_grad, down_sum = done["grad"], done["down"]
    proj_sum = gathered(7, mixed[None], lead(mixed_right), lead(mixed_left), done["attn"], True)[0]
    branch_part = jnp.dot(hidden, w_down, preferred_element_type=F32).astype(BF)
    qkv_part = gathered(8, raw_grad, raw_right, raw_left, side_act, False, 0, hops - 1)
    gu_sum = gu_line.finish((raw_right[-1], raw_left[-1], down_sum, proj_sum, qkv_part))

    small = jnp.concatenate([jnp.zeros((2, w), F32), sums_two[0:3], jnp.zeros((3, w), F32)], axis=0)
    input_grad, sums, layer_out = call(
        functools.partial(first_back_kernel, n), 9,
        [(own, F32), ((8, w), F32), (own, F32)],
        scatter_room(n, rows, w)
        + [pltpu.VMEM(own, F32),
           pltpu.VMEM(lanes, F32), pltpu.VMEM(lanes, F32), pltpu.VMEM((8, rows), F32),
           pltpu.VMEM((n, 8, rows), F32)] + [sems(n - 1)] * 2,
        V(act_one_grad, tokens_in, mean_one, inv_one, row(ln1_gain), small,
          branch_part, out_cotangent, row(scale_mlp)), 20,
    )
    input_grad = res_grad + input_grad
    layer_out = residual + layer_out
    qkv_sum = qkv_part + gathered(
        10, raw_grad, raw_right, raw_left, side_act, False, hops, hops
    )
    qkv_sum, input_grad, layer_out, sums = lax.optimization_barrier(
        (qkv_sum, input_grad, layer_out, sums)
    )
    (small_sums,) = call(
        functools.partial(small_sums_kernel, n, m), 11, [((8, n * w), F32)],
        [pltpu.VMEM((m, 8, w), F32), pltpu.VMEM((8, w), F32)] + [sems(m - 1)] * 2 + [sems(n - 1)] * 2,
        V(sums), 10,
    )
    return (
        layer_out,
        input_grad,
        small_sums[0],
        small_sums[1],
        jnp.transpose(qkv_sum, (1, 0, 2)),
        proj_sum,
        small_sums[4],
        small_sums[2],
        small_sums[3],
        gu_sum,
        down_sum,
        small_sums[5],
    )


def solution(mesh):
    placed = (
        P("dp", "tensor"),
        P(),
        P(),
        P(None, None, "tensor"),
        P("tensor", None),
        P(),
        P(),
        P(),
        P(None, None, "tensor"),
        P("tensor", None),
        P(),
        P("dp", "tensor"),
    )
    return jax.shard_map(
        functools.partial(local, n=mesh.shape["tensor"], m=mesh.shape["dp"]),
        mesh=mesh,
        in_specs=placed,
        out_specs=(
            P("dp", "tensor"),
            P("dp", "tensor"),
            P(),
            P(),
            P("dp", None, "tensor"),
            P("tensor", "dp"),
            P(),
            P(),
            P(),
            P("dp", None, "tensor"),
            P("tensor", "dp"),
            P(),
        ),
        check_vma=False,
    )
```

```python
import functools
import math

import jax
import jax.numpy as jnp
from jax import lax
from jax.experimental import pallas as pl
from jax.experimental.pallas import tpu as pltpu
from jax.sharding import PartitionSpec as P

D = 4096
HD = 128
GRID = 14
EXTRA = 5
PATCH = 196
SEQ = 201
EPS = 1e-06
LANE = 128
BF = jnp.bfloat16
F32 = jnp.float32
MESH = pl.DeviceIdType.MESH
ROWS = (((0,), (0,)), ((), ()))
COLS = (((1,), (1,)), ((), ()))


def rope_tables():
    quarter = HD // 4
    theta = (
        2.0
        * math.pi
        * jnp.exp(jnp.arange(quarter, dtype=jnp.float32) * (-4.0 * math.log(100.0) / HD))
    )
    places = jnp.arange(PATCH, dtype=jnp.int32)
    row_pos = ((places // GRID).astype(jnp.float32) + 0.5) * (2.0 / GRID) - 1.0
    col_pos = ((places % GRID).astype(jnp.float32) + 0.5) * (2.0 / GRID) - 1.0
    angles = jnp.concatenate(
        [row_pos[:, None] * theta[None, :], col_pos[:, None] * theta[None, :]], axis=1
    )
    angles = jnp.concatenate([jnp.zeros((EXTRA, HD // 2), jnp.float32), angles], axis=0)
    return (jnp.cos(angles), jnp.sin(angles))


def rotate(vectors, cosines, sines):
    halfway = HD // 2
    leading = vectors[..., :halfway]
    trailing = vectors[..., halfway:]
    cos_b = cosines[:, None, :]
    sin_b = sines[:, None, :]
    return jnp.concatenate(
        [leading * cos_b - trailing * sin_b, leading * sin_b + trailing * cos_b], axis=-1
    )


def greet(n, m=1):
    me = lax.axis_index("tensor")
    you = lax.axis_index("dp")
    barrier = pltpu.get_barrier_semaphore()
    for k in range(1, n):
        pl.semaphore_signal(
            barrier, inc=1, device_id={"tensor": lax.rem(me + k, n)}, device_id_type=MESH
        )
    for k in range(1, m):
        pl.semaphore_signal(
            barrier, inc=1, device_id={"dp": lax.rem(you + k, m)}, device_id_type=MESH
        )
    pl.semaphore_wait(barrier, n + m - 2)


def send(src, dst, send_sem, recv_sem, peer):
    return pltpu.make_async_remote_copy(
        src_ref=src,
        dst_ref=dst,
        send_sem=send_sem,
        recv_sem=recv_sem,
        device_id={"tensor": peer},
        device_id_type=MESH,
    )


def send_dp(src, dst, send_sem, recv_sem, peer):
    return pltpu.make_async_remote_copy(
        src_ref=src,
        dst_ref=dst,
        send_sem=send_sem,
        recv_sem=recv_sem,
        device_id={"dp": peer},
        device_id_type=MESH,
    )


class Hop:
    def __init__(self, k, m, right_src, left_src, right_dst, left_dst, sem):
        you = lax.axis_index("dp")
        z, last = you // 2, m // 2 - 1
        right = send_dp(right_src, right_dst, sem.at[0], sem.at[1], lax.rem(you + 2, m))
        left = send_dp(left_src, left_dst, sem.at[2], sem.at[3], lax.rem(you + m - 2, m))
        self.steps = [
            (right, (z >= k - 1) & (z < last), z >= k),
            (left, (z <= last - k + 1) & (z > 0), z <= last - k),
        ]

    def start(self):
        for copy, sends, _ in self.steps:
            pl.when(sends)(copy.start)

    def wait(self):
        for copy, sends, gets in self.steps:
            pl.when(sends)(copy.wait_send)
            pl.when(gets)(copy.wait_recv)


class End:
    def __init__(self, m, part_ref, at, right_dst, left_dst, sem):
        you = lax.axis_index("dp")
        z, last = you // 2, m // 2 - 1
        some = pl.ds(at, right_dst.shape[1])
        right = send_dp(
            part_ref.at[last, :, some], right_dst, sem.at[0], sem.at[1], lax.rem(you + 2, m)
        )
        left = send_dp(
            part_ref.at[0, :, some], left_dst, sem.at[2], sem.at[3], lax.rem(you + m - 2, m)
        )
        self.steps = [(right, z == 0, z == 1), (left, z == last, z == last - 1)]

    start = Hop.start
    wait = Hop.wait


class Exchange:
    def __init__(self, m, pieces, full_ref, out_ref, ssem, rsem, lsem):
        you = lax.axis_index("dp")
        piece = lax.rem(lax.axis_index("tensor"), pieces)
        self.copies = []
        for k in range(m):
            peer = lax.rem(you + k, m)
            cols = pl.ds(pl.multiple_of((peer * pieces + piece) * LANE, LANE), LANE)
            if k:
                copy = send_dp(
                    full_ref.at[:, cols], out_ref.at[you], ssem.at[k - 1], rsem.at[k - 1], peer
                )
            else:
                copy = pltpu.make_async_copy(full_ref.at[:, cols], out_ref.at[you], lsem)
            self.copies.append(copy)

    def start(self):
        for copy in self.copies:
            copy.start()

    def wait(self):
        for copy in self.copies:
            copy.wait()


def chunks(width, body):
    def step(j, carry):
        body(pl.ds(pl.multiple_of(j * LANE, LANE), LANE))
        return carry

    lax.fori_loop(0, width // LANE, step, 0)


def spread(column, rows):
    return jnp.broadcast_to(column, (rows, LANE))


def beside(me):
    return me + 1 - 2 * lax.rem(me, 2), me + 2 - 4 * (me // 2)


class Gather:
    def __init__(self, n, own_ref, dest, ssem, rsem):
        me = lax.axis_index("tensor")
        w = own_ref.shape[1]
        self.square = n == 4
        if self.square:
            x, y = beside(me)
            half = w // 2
            part = lambda i: own_ref.at[:, i * half:(i + 1) * half]
            to = lambda i, src, owner, at, peer: send(
                src, dest(owner, at * half, half), ssem.at[i], rsem.at[i], peer
            )
            self.copies = [
                to(0, part(0), me, 0, x), to(1, part(1), me, 1, y),
                to(2, part(1), me, 1, x), to(3, part(0), me, 0, y),
            ]
            self.passed = [
                to(4, dest(x, 0, half), x, 0, y), to(5, dest(y, half, half), y, 1, x)
            ]
        else:
            self.copies = [
                send(own_ref, dest(me, 0, w), ssem.at[k - 1], rsem.at[k - 1], lax.rem(me + k, n))
                for k in range(1, n)
            ]

    def start(self):
        for copy in self.copies:
            copy.start()

    def relay(self):
        if self.square:
            for copy, passed in zip(self.copies, self.passed):
                copy.wait_recv()
                passed.start()

    def wait(self):
        if self.square:
            for copy in self.copies:
                copy.wait_send()
            for copy in self.copies[2:]:
                copy.wait_recv()
            wait_all(self.passed)
        else:
            wait_all(self.copies)


class Scatter:
    def __init__(self, n, w, part_ref, slots, come, go, ssem, rsem):
        me = lax.axis_index("tensor")
        self.n, self.w, self.part, self.slots, self.come, self.go = n, w, part_ref, slots, come, go
        self.square = n == 4
        cols = lambda owner, at, size: part_ref.at[:, pl.ds(pl.multiple_of(owner * w + at, LANE), size)]
        if self.square:
            x, y = beside(me)
            far = 3 - me
            half = w // 2
            self.half, self.x, self.y = half, x, y
            to = lambda i, src, dst, peer: send(src, dst, ssem.at[i], rsem.at[i], peer)
            low, high = slice(0, half), slice(half, w)
            self.first = [
                to(0, cols(far, 0, half), come.at[0], x), to(1, cols(far, half, half), come.at[1], y)
            ]
            self.second = [
                to(2, cols(x, 0, half), slots.at[0, :, low], x),
                to(3, cols(y, half, half), slots.at[1, :, high], y),
            ]
            self.third = [
                to(4, go.at[0], slots.at[0, :, high], x), to(5, go.at[1], slots.at[1, :, low], y)
            ]
            self.order = [(far, 0), (far, 1), (x, 0), (y, 1), (x, 1), (y, 0), (me, 0), (me, 1)]
        else:
            self.first = [
                send(cols(lax.rem(me + k, n), 0, w), slots.at[k - 1], ssem.at[k - 1], rsem.at[k - 1],
                     lax.rem(me + k, n))
                for k in range(1, n)
            ]
            self.second = self.third = []

    def start(self):
        for copy in self.first + self.second:
            copy.start()

    def relay(self):
        if self.square:
            half = self.half
            for i, (owner, at) in enumerate(((self.x, half), (self.y, 0))):
                self.first[1 - i].wait_recv()

                def add(cols, i=i, owner=owner, at=at):
                    wide = pl.ds(pl.multiple_of(owner * self.w + at + cols.start, LANE), LANE)
                    self.go[i, :, cols] = (
                        self.part[:, wide].astype(F32) + self.come[1 - i, :, cols].astype(F32)
                    ).astype(BF)

                chunks(half, add)
                self.third[i].start()

    def wait(self):
        if self.square:
            for copy in self.first:
                copy.wait_send()
            wait_all(self.second + self.third)
        else:
            wait_all(self.first)

    def total(self, cols, wide):
        total = self.part[:, wide].astype(F32)
        for k in range(self.slots.shape[0]):
            total = total + self.slots[k, :, cols].astype(F32)
        return total


def scatter_room(n, rows, w):
    count, half = (2, w // 2) if n == 4 else (n - 1, LANE)
    return [
        pltpu.VMEM((count, rows, w), BF), pltpu.VMEM((2, rows, half), BF), pltpu.VMEM((2, rows, half), BF),
        sems(6 if n == 4 else n - 1), sems(6 if n == 4 else n - 1),
    ]


def gather_sems(n):
    return [sems(6 if n == 4 else n - 1)] * 2


def stream(count, fetch, compute):
    fetch(0, 0).start()

    def step(i, carry):
        slot = lax.rem(i, 2)

        @pl.when(i + 1 < count)
        def _():
            fetch(i + 1, 1 - slot).start()

        fetch(i, slot).wait()
        compute(i, slot)
        return carry

    lax.fori_loop(0, count, step, 0)


def wait_all(copies):
    for copy in copies:
        copy.wait()


def row_stats(n, rows, w, all_ref, acc, mean_ref, inv_ref):
    acc[...] = jnp.zeros_like(acc)

    def add(cols):
        total = all_ref[0, :, cols].astype(F32)
        for k in range(1, n):
            total = total + all_ref[k, :, cols].astype(F32)
        acc[...] += total

    chunks(w, add)
    mean_ref[...] = spread(jnp.sum(acc[...], axis=1, keepdims=True) * (1.0 / D), rows)
    acc[...] = jnp.zeros_like(acc)

    def square(cols):
        mean = mean_ref[...]
        total = jnp.zeros_like(mean)
        for k in range(n):
            center = all_ref[k, :, cols].astype(F32) - mean
            total = total + center * center
        acc[...] += total

    chunks(w, square)
    var = jnp.sum(acc[...], axis=1, keepdims=True) * (1.0 / D)
    inv_ref[...] = spread(lax.rsqrt(var + EPS), rows)


def write_act(n, w, all_ref, mean_ref, inv_ref, gain_ref, bias_ref, act_ref):
    def act(cols):
        for k in range(n):
            wide = pl.ds(pl.multiple_of(k * w + cols.start, LANE), LANE)
            center = all_ref[k, :, cols].astype(F32) - mean_ref[...]
            act_ref[:, wide] = (
                center * inv_ref[...] * gain_ref[:, wide] + bias_ref[:, wide]
            ).astype(BF)

    chunks(w, act)


def part_rows(w_ref, out_ref, ibuf, obuf, isem, osem, also):
    size = ibuf.shape[1]
    count = w_ref.shape[0] // size

    def rows_of(i):
        return pl.ds(pl.multiple_of(i * size, size), size)

    def fetch(i, slot):
        return pltpu.make_async_copy(w_ref.at[rows_of(i)], ibuf.at[slot], isem.at[slot])

    def put(i, slot):
        return pltpu.make_async_copy(obuf.at[slot], out_ref.at[:, rows_of(i)], osem.at[slot])

    fetch(0, 0).start()

    def step(i, carry):
        slot = lax.rem(i, 2)
        also(i)

        @pl.when(i + 1 < count)
        def _():
            fetch(i + 1, 1 - slot).start()

        fetch(i, slot).wait()

        @pl.when(i >= 2)
        def _():
            put(i - 2, slot).wait()

        obuf[slot] = jnp.swapaxes(ibuf[slot], 0, 1)
        put(i, slot).start()
        return carry

    lax.fori_loop(0, count, step, 0)
    for i in (count - 2, count - 1):
        put(i, i % 2).wait()


def first_norm_kernel(
    n, x_ref, gain_ref, bias_ref, early_ref, w_ref, act_ref, mean_ref, inv_ref, parted_ref, cots_ref,
    all_ref, acc, ssem, rsem, ibuf, obuf, isem, osem, csem, crem,
):
    rows, w = x_ref.shape
    me = lax.axis_index("tensor")
    greet(n)
    dest = lambda owner, at, size: all_ref.at[owner, :, pl.ds(at, size)]
    gather = Gather(n, x_ref, dest, ssem, rsem)
    gather.start()
    all_ref[me] = x_ref[...]
    into = lambda owner, at, size: cots_ref.at[owner, :, pl.ds(at, size)]
    early = Gather(n, early_ref, into, csem, crem)

    def between(i):
        @pl.when(i == 6)
        def _():
            gather.relay()
            early.start()

        pl.when(i == 13)(early.relay)

    cots_ref[me] = early_ref[...]
    part_rows(w_ref, parted_ref, ibuf, obuf, isem, osem, between)
    gather.wait()
    row_stats(n, rows, w, all_ref, acc, mean_ref, inv_ref)
    write_act(n, w, all_ref, mean_ref, inv_ref, gain_ref, bias_ref, act_ref)
    early.wait()


def second_norm_kernel(
    n, m, pieces, part_ref, x_ref, scale_ref, gain_ref, bias_ref, mlp_ref, cot_ref, cots_ref, mixed_ref,
    w_down_ref, attn_ref, res_ref, act_ref, mean_ref, inv_ref, hgrad_ref, kcot_ref, *refs,
):
    hops = m // 2 - 1
    rights, lefts, refs = refs[:hops], refs[hops:2 * hops], refs[2 * hops:]
    (slots, come, go, ssem, rsem, own_ref, all_ref, acc, ssem2, rsem2, hsem,
     css, crs, cls, bgrad, wbuf, wsem) = refs
    rows, w = x_ref.shape
    me = lax.axis_index("tensor")
    greet(n, m)
    scatter = Scatter(n, w, part_ref, slots, come, go, ssem, rsem)
    scatter.start()
    line = [
        Hop(k, m, rights[k - 2] if k > 1 else mixed_ref, lefts[k - 2] if k > 1 else mixed_ref,
            rights[k - 1], lefts[k - 1], hsem.at[k - 1])
        for k in range(1, hops + 1)
    ]
    line[0].start()

    ahead = cots_ref.shape[2]
    for owner in range(n):

        def early(cols, owner=owner):
            wide = pl.ds(pl.multiple_of(owner * w + cols.start, LANE), LANE)
            bgrad[:, wide] = (mlp_ref[:, wide] * cots_ref[owner, :, cols].astype(F32)).astype(BF)

        def late(cols, owner=owner):
            wide = pl.ds(pl.multiple_of(owner * w + ahead + cols.start, LANE), LANE)
            from_ = pl.ds(pl.multiple_of(owner * (w - ahead) + cols.start, LANE), LANE)
            bgrad[:, wide] = (mlp_ref[:, wide] * cot_ref[:, from_].astype(F32)).astype(BF)

        chunks(ahead, early)
        chunks(w - ahead, late)
    side = Exchange(m, pieces, bgrad, kcot_ref, css, crs, cls)
    side.start()
    tile = wbuf.shape[1]
    count = hgrad_ref.shape[1] // tile

    def fetch(i, slot):
        return pltpu.make_async_copy(
            w_down_ref.at[pl.ds(pl.multiple_of(i * tile, tile), tile), :], wbuf.at[slot], wsem.at[slot]
        )

    def compute(i, slot):
        hgrad_ref[:, pl.ds(pl.multiple_of(i * tile, tile), tile)] = lax.dot_general(
            bgrad[...], wbuf[slot], COLS, preferred_element_type=F32
        )

        @pl.when(i == count // 2)
        def _():
            scatter.relay()

    stream(count, fetch, compute)
    line[0].wait()
    if hops > 1:
        line[1].start()
    scatter.wait()

    def add(cols):
        wide = pl.ds(pl.multiple_of(me * w + cols.start, LANE), LANE)
        total = scatter.total(cols, wide)
        attn_ref[:, cols] = total
        res = x_ref[:, cols].astype(F32) + scale_ref[:, wide] * total
        res_ref[:, cols] = res
        own_ref[:, cols] = res.astype(BF)

    chunks(w, add)
    dest = lambda owner, at, size: all_ref.at[owner, :, pl.ds(at, size)]
    gather = Gather(n, own_ref, dest, ssem2, rsem2)
    gather.start()
    all_ref[me] = own_ref[...]
    gather.relay()
    for k in range(1, hops - 1):
        line[k].wait()
        line[k + 1].start()
    gather.wait()
    row_stats(n, rows, w, all_ref, acc, mean_ref, inv_ref)
    write_act(n, w, all_ref, mean_ref, inv_ref, gain_ref, bias_ref, act_ref)
    line[-1].wait()
    side.wait()


def norm_back(n, w, load_total, grad_ref, base_ref, mean_ref, inv_ref, gain_ref,
              sums, acc, acc2, stat_own, stats, ssem, rsem, out):
    rows = grad_ref.shape[0]
    me = lax.axis_index("tensor")
    acc[...] = jnp.zeros_like(acc)
    acc2[...] = jnp.zeros_like(acc2)

    def first(cols):
        wide = pl.ds(pl.multiple_of(me * w + cols.start, LANE), LANE)
        total = load_total(cols, wide)
        grad_ref[:, cols] = total
        normed = (base_ref[:, cols].astype(F32) - mean_ref[...]) * inv_ref[...]
        sums[0:1, cols] = jnp.sum(total * normed, axis=0, keepdims=True)
        sums[1:2, cols] = jnp.sum(total, axis=0, keepdims=True)
        scaled = total * gain_ref[:, wide]
        acc[...] += scaled
        acc2[...] += scaled * normed

    chunks(w, first)
    ones = jnp.ones((8, LANE), F32)
    high = lax.Precision.HIGHEST
    plain = lax.dot_general(ones, acc[...], COLS, precision=high, preferred_element_type=F32)
    cross = lax.dot_general(ones, acc2[...], COLS, precision=high, preferred_element_type=F32)
    line = lax.broadcasted_iota(jnp.int32, (8, rows), 0)
    stat_own[...] = jnp.where(line < 4, plain, cross)
    copies = [
        send(stat_own, stats.at[me], ssem.at[k - 1], rsem.at[k - 1], lax.rem(me + k, n))
        for k in range(1, n)
    ]
    for copy in copies:
        copy.start()
    wait_all(copies)
    both = stat_own[...]
    for k in range(1, n):
        both = both + stats[lax.rem(me + k, n)]
    both = both * (1.0 / D)
    pick = lax.broadcasted_iota(jnp.int32, (8, LANE), 0)
    acc[...] = lax.dot_general(
        both, (pick == 0).astype(F32), ROWS, precision=high, preferred_element_type=F32
    )
    acc2[...] = lax.dot_general(
        both, (pick == 4).astype(F32), ROWS, precision=high, preferred_element_type=F32
    )

    def second(cols):
        wide = pl.ds(pl.multiple_of(me * w + cols.start, LANE), LANE)
        normed = (base_ref[:, cols].astype(F32) - mean_ref[...]) * inv_ref[...]
        scaled = grad_ref[:, cols] * gain_ref[:, wide]
        out(cols, wide, inv_ref[...] * (scaled - acc[...] - normed * acc2[...]))

    chunks(w, second)


def second_back_kernel(
    n, m, gate_ref, up_ref, cot_ref, res_ref, attn_ref, mean_ref, inv_ref, gain_ref, scale_ref,
    right_ref, left_ref, gu_ref, w_ref, rgrad_ref, agrad_ref, sums_ref, gu_right, gu_left, *refs,
):
    hops = m // 2 - 1
    rights = (right_ref,) + refs[:hops - 1]
    lefts = (left_ref,) + refs[hops - 1:2 * hops - 2]
    (part_ref, slots, come, go, ssem, rsem, grad_ref, own_ref, acc, acc2, stat_own, stats,
     ssem2, rsem2, ssem3, rsem3, lsem, hsem, gsem, wbuf, wsem) = refs[2 * hops - 2:]
    w = cot_ref.shape[1]
    me = lax.axis_index("tensor")
    greet(n, m)
    line = [
        Hop(k, m, rights[k - 2], lefts[k - 2], rights[k - 1], lefts[k - 1], hsem.at[k - 2])
        for k in range(2, hops + 1)
    ]
    line[0].start()
    first = End(m, gu_ref, 0, gu_right, gu_left, gsem)
    first.start()
    scatter = Scatter(n, w, part_ref, slots, come, go, ssem, rsem)
    tile = wbuf.shape[2]
    count = D // tile

    def spot(i):
        if not scatter.square:
            return pl.ds(pl.multiple_of(i * tile, LANE), tile)
        at = 0
        for k, (owner, half) in enumerate(scatter.order):
            at = at + jnp.where(i == k, owner * w + half * tile, 0)
        return pl.ds(pl.multiple_of(at, LANE), tile)

    def fetch(i, slot):
        return pltpu.make_async_copy(w_ref.at[:, spot(i), :], wbuf.at[slot], wsem.at[slot])

    def compute(i, slot):
        part_ref[:, spot(i)] = (
            lax.dot_general(gate_ref[...], wbuf[slot, 0], COLS, preferred_element_type=F32)
            + lax.dot_general(up_ref[...], wbuf[slot, 1], COLS, preferred_element_type=F32)
        ).astype(BF)
        if scatter.square:
            for k, copy in enumerate(scatter.first + scatter.second):
                pl.when(i == k)(copy.start)
            pl.when(i == 5)(scatter.relay)

    stream(count, fetch, compute)
    if not scatter.square:
        scatter.start()
    scatter.wait()
    sums_ref[...] = jnp.zeros_like(sums_ref)

    def out(cols, wide, back):
        res_grad = cot_ref[:, cols].astype(F32) + back
        rgrad_ref[:, cols] = res_grad
        sums_ref[2:3, cols] = jnp.sum(res_grad * attn_ref[:, cols], axis=0, keepdims=True)
        own_ref[:, cols] = (scale_ref[:, wide] * res_grad).astype(BF)

    norm_back(n, w, scatter.total, grad_ref, res_ref, mean_ref, inv_ref, gain_ref,
              sums_ref, acc, acc2, stat_own, stats, ssem2, rsem2, out)
    dest = lambda owner, at, size: agrad_ref.at[:, pl.ds(pl.multiple_of(owner * w + at, LANE), size)]
    gather = Gather(n, own_ref, dest, ssem3, rsem3)
    gather.start()
    local = pltpu.make_async_copy(own_ref, dest(me, 0, w), lsem)
    local.start()
    gather.relay()
    for k in range(len(line)):
        line[k].wait()
        if k + 1 < len(line):
            line[k + 1].start()
    local.wait()
    gather.wait()
    first.wait()


def first_back_kernel(
    n, grad_in, x_ref, mean_ref, inv_ref, gain_ref, small_ref,
    part_ref, cot_ref, scale_ref,
    igrad_ref, sums, out_ref,
    slots, come, go, ssem, rsem, grad_ref, acc, acc2, stat_own, stats, ssem2, rsem2,
):
    w = x_ref.shape[1]
    greet(n)
    scatter = Scatter(n, w, part_ref, slots, come, go, ssem, rsem)
    scatter.start()
    sums[...] = small_ref[...]
    scatter.relay()

    def load_total(cols, wide):
        return grad_in[:, cols].astype(F32)

    def out(cols, wide, back):
        igrad_ref[:, cols] = back

    norm_back(n, w, load_total, grad_ref, x_ref, mean_ref, inv_ref, gain_ref,
              sums, acc, acc2, stat_own, stats, ssem2, rsem2, out)
    scatter.wait()
    me = lax.axis_index("tensor")

    def add(cols):
        wide = pl.ds(pl.multiple_of(me * w + cols.start, LANE), LANE)
        total = scatter.total(cols, wide)
        out_ref[:, cols] = scale_ref[:, wide] * total
        sums[5:6, cols] = jnp.sum(cot_ref[:, cols].astype(F32) * total, axis=0, keepdims=True)

    chunks(w, add)


def mate_of(you):
    return you + 1 - 2 * lax.rem(you, 2)


def pair_grad_kernel(
    m, act_ref, gate_ref, up_ref, hidden_ref, out_ref, right_ref, left_ref,
    acts, mates, gates, ups, flip, obuf, asem, arem, gsem, grem, lsem, hsem, osem,
):
    line = m // 2
    you = lax.axis_index("dp")
    core, mate = lax.rem(you, 2), mate_of(you)
    width = acts.shape[-1]
    tile = 512
    greet(1, m)
    hop = Hop(1, m, hidden_ref, hidden_ref, right_ref, left_ref, hsem)
    copies = [
        send_dp(gate_ref, gates, gsem.at[0], grem.at[0], mate),
        send_dp(up_ref, ups, gsem.at[1], grem.at[1], mate),
    ]
    locals_ = []
    for k in range(line):
        theirs = pl.ds(pl.multiple_of((2 * k + 1 - core) * width, LANE), width)
        ours = pl.ds(pl.multiple_of((2 * k + core) * width, LANE), width)
        copies.append(send_dp(act_ref.at[:, theirs], mates.at[k], asem.at[k], arem.at[k], mate))
        locals_.append(pltpu.make_async_copy(act_ref.at[:, ours], acts.at[k], lsem.at[k]))
    for copy in locals_ + copies:
        copy.start()
    hop.start()
    for copy in locals_:
        copy.wait()
    for k in range(line):
        flip[0, k] = acts[k].T
    for copy in copies:
        copy.wait()
    for k in range(line):
        flip[1, k] = mates[k].T
    def put(k):
        return pltpu.make_async_copy(obuf.at[k % 2], out_ref.at[k], osem.at[k % 2])

    for k in range(line):
        if k >= 2:
            put(k - 2).wait()
        for j, (near, far) in enumerate(((gate_ref, gates), (up_ref, ups))):

            def step(i, carry, k=k, j=j, near=near, far=far):
                cols = pl.ds(pl.multiple_of(i * tile, tile), tile)
                obuf[k % 2, j, :, cols] = (
                    jnp.dot(flip[0, k], near[:, cols], preferred_element_type=F32)
                    + jnp.dot(flip[1, k], far[:, cols], preferred_element_type=F32)
                ).astype(BF)
                return carry

            lax.fori_loop(0, gate_ref.shape[1] // tile, step, 0)
        put(k).start()
    for k in range(max(line - 2, 0), line):
        put(k).wait()
    hop.wait()


class SmallSums:
    def __init__(self, n, m, sums, out, parts, total, dss, drs, tss, trs):
        self.out, self.sums, self.parts, self.total = out, sums, parts, total
        me, you = lax.axis_index("tensor"), lax.axis_index("dp")
        w = sums.shape[1]
        self.m, self.you = m, you
        self.mine = pl.ds(pl.multiple_of(me * w, w), w)
        self.dp = [
            send_dp(sums, parts.at[you], dss.at[k - 1], drs.at[k - 1], lax.rem(you + k, m))
            for k in range(1, m)
        ]
        self.tensor = [
            send(total, out.at[:, self.mine], tss.at[k - 1], trs.at[k - 1], lax.rem(me + k, n))
            for k in range(1, n)
        ]

    def start(self):
        for copy in self.dp:
            copy.start()

    def finish(self):
        self.parts[self.you] = self.sums[...]
        wait_all(self.dp)
        total = self.parts[0]
        for k in range(1, self.m):
            total = total + self.parts[k]
        self.total[...] = total
        for copy in self.tensor:
            copy.start()
        self.out[:, self.mine] = total
        wait_all(self.tensor)


def small_sums_kernel(n, m, sums, out_ref, parts, total, *room):
    greet(n, m)
    small = SmallSums(n, m, sums, out_ref, parts, total, *room)
    small.start()
    small.finish()


def gathered_grad_kernel(m, turned, first, last, *refs):
    hops = m // 2 - 1
    you = lax.axis_index("dp")
    core, mate, z = lax.rem(you, 2), mate_of(you), you // 2
    todo = []
    refs = list(refs)
    for k in range(first, last + 1):
        if k == 0:
            todo.append((None, refs.pop(0), z))
        else:
            todo.append((z >= k, refs.pop(0), z - k))
            todo.append((z <= hops - k, refs.pop(0), z + k))
    side_ref = refs.pop(0)
    out_ref, blocks, flip, lsem, ssem, rsem = refs
    greet(1, m)
    copies = []
    for at, (cond, src, chip) in enumerate(todo):
        near = pltpu.make_async_copy(src, blocks.at[at, core], lsem.at[at])
        far = send_dp(src, blocks.at[at, core], ssem.at[at], rsem.at[at], mate)
        copies.append((cond, near, far))

    def when(cond, body):
        body() if cond is None else pl.when(cond)(body)

    def go(near, far):
        near.start()
        far.start()

    def done(near, far):
        near.wait()
        far.wait()

    def turn(at, chip):
        for c in range(2):
            flip[at, c] = side_ref[2 * chip + c].T

    for cond, near, far in copies:
        when(cond, functools.partial(go, near, far))
    for at, (cond, _, chip) in enumerate(todo):
        when(cond, functools.partial(turn, at, chip))
    for cond, near, far in copies:
        when(cond, functools.partial(done, near, far))
    tile = 512
    parts, width = out_ref.shape[0], blocks.shape[-1]
    if first:
        out_ref[...] = jnp.zeros_like(out_ref)
    for at, (cond, _, chip) in enumerate(todo):
        for j in range(parts):

            def step(i, carry, at=at, j=j):
                cols = pl.ds(pl.multiple_of(i * tile, tile), tile)
                total = jnp.dot(
                    flip[at, 0], blocks[at, 0, j, :, cols], preferred_element_type=F32
                ) + jnp.dot(flip[at, 1], blocks[at, 1, j, :, cols], preferred_element_type=F32)
                if turned:
                    if first or at:
                        out_ref[j, cols, :] += total.T
                    else:
                        out_ref[j, cols, :] = total.T
                elif first or at:
                    out_ref[j, :, cols] += total
                else:
                    out_ref[j, :, cols] = total
                return carry

            def run(step=step):
                lax.fori_loop(0, width // tile, step, 0)

            when(cond, run)


def qkv_kernel(act_ref, w_ref, cos_ref, sin_ref, out_ref):
    raw = jnp.dot(act_ref[...], w_ref[...], preferred_element_type=F32)
    part = pl.program_id(0)

    @pl.when(part < 2)
    def _():
        for h in range(raw.shape[1] // HD):
            cols = slice(h * HD, (h + 1) * HD)
            t = raw[:, cols]
            out_ref[:, cols] = (
                t * cos_ref[...] + pltpu.roll(t, HD // 2, 1) * sin_ref[...]
            ).astype(BF)

    @pl.when(part == 2)
    def _():
        out_ref[...] = raw.astype(BF)


def qkv_matmul(act, w_j, cos2, sin2):
    rows = act.shape[0]
    inner = w_j.shape[2]
    tile = min(512, inner)
    return pl.pallas_call(
        qkv_kernel,
        grid=(3, inner // tile),
        out_shape=jax.ShapeDtypeStruct((3, rows, inner), BF),
        in_specs=[
            pl.BlockSpec((rows, D), lambda j, i: (0, 0)),
            pl.BlockSpec((None, D, tile), lambda j, i: (j, 0, i)),
            pl.BlockSpec((rows, HD), lambda j, i: (0, 0)),
            pl.BlockSpec((rows, HD), lambda j, i: (0, 0)),
        ],
        out_specs=pl.BlockSpec((None, rows, tile), lambda j, i: (j, 0, i)),
        compiler_params=pltpu.CompilerParams(vmem_limit_bytes=40 << 20),
        cost_estimate=pl.CostEstimate(
            flops=2 * rows * D * 3 * inner, bytes_accessed=6 * D * inner, transcendentals=0
        ),
    )(act, w_j, cos2, sin2)


def attention_probs(q, k, same):
    scores = lax.dot_general(k, q, COLS, preferred_element_type=F32) * (HD ** (-0.5))
    scores = jnp.where(same, scores, -jnp.inf)
    top = jnp.max(scores, axis=0, keepdims=True)
    weight = jnp.exp(scores - top)
    return weight / jnp.sum(weight, axis=0, keepdims=True)


def same_image(rows):
    one = lax.broadcasted_iota(jnp.int32, (rows, rows), 0)
    two = lax.broadcasted_iota(jnp.int32, (rows, rows), 1)
    image = lambda i: sum((i >= SEQ * k).astype(jnp.int32) for k in range(1, rows // SEQ))
    return image(one) == image(two)


def attention_kernel(qkv_ref, w_ref, mixed_ref, part_ref):
    rows, inner = mixed_ref.shape

    def head(h, carry):
        cols = pl.ds(pl.multiple_of(h * HD, HD), HD)
        probs = attention_probs(qkv_ref[0, :, cols], qkv_ref[1, :, cols], same_image(rows))
        value = qkv_ref[2, :, cols].astype(F32).T.astype(BF)
        mixed = jnp.dot(value, probs.astype(BF), preferred_element_type=F32)
        mixed_ref[:, cols] = mixed.T.astype(BF)
        return carry

    lax.fori_loop(0, inner // HD, head, 0)

    def tile(i, carry):
        cols = pl.ds(pl.multiple_of(i * 512, 512), 512)
        part_ref[:, cols] = jnp.dot(
            mixed_ref[...], w_ref[:, cols], preferred_element_type=F32
        ).astype(BF)
        return carry

    lax.fori_loop(0, D // 512, tile, 0)


def attention_back_kernel(
    m, pieces, agrad_ref, w_ref, qkv_ref, cos_ref, sin_ref, full_ref, gu_ref,
    out_ref, kattn_ref, gu_right, gu_left, mgrad, ass, ars, als, gsem,
):
    rows, inner = mgrad.shape
    greet(1, m)
    rest = End(m, gu_ref, gu_ref.shape[2] - gu_right.shape[1], gu_right, gu_left, gsem)
    rest.start()
    side = Exchange(m, pieces, full_ref, kattn_ref, ass, ars, als)
    side.start()
    step = min(256, inner)

    def tile(i, carry):
        cols = pl.ds(pl.multiple_of(i * step, step), step)
        mgrad[:, cols] = lax.dot_general(
            agrad_ref[...], w_ref[cols, :], COLS, preferred_element_type=F32
        ).astype(BF)
        return carry

    lax.fori_loop(0, inner // step, tile, 0)

    def back(t):
        return t * cos_ref[...] - pltpu.roll(t, HD // 2, 1) * sin_ref[...]

    def head(h, carry):
        cols = pl.ds(pl.multiple_of(h * HD, HD), HD)
        q, k, v = qkv_ref[0, :, cols], qkv_ref[1, :, cols], qkv_ref[2, :, cols]
        grad = mgrad[:, cols]
        probs = attention_probs(q, k, same_image(rows))
        prob_grad = lax.dot_general(v, grad, COLS, preferred_element_type=F32)
        delta = jnp.sum(probs * prob_grad, axis=0, keepdims=True)
        score_grad = (probs * (prob_grad - delta)).astype(BF)
        scale = HD ** (-0.5)
        flipped = k.astype(F32).T.astype(BF)
        q_grad = jnp.dot(flipped, score_grad, preferred_element_type=F32).T * scale
        k_grad = jnp.dot(score_grad, q, preferred_element_type=F32) * scale
        out_ref[0, :, cols] = back(q_grad).astype(BF)
        out_ref[1, :, cols] = back(k_grad).astype(BF)
        out_ref[2, :, cols] = jnp.dot(
            probs.astype(BF), grad, preferred_element_type=F32
        ).astype(BF)
        return carry

    lax.fori_loop(0, inner // HD, head, 0)
    side.wait()
    rest.wait()


def gate_kernel(
    m, pieces, act_ref, w_ref, hgrad_ref, full_ref, hidden_ref, gate_ref, up_ref, kact_ref, ass, ars, als
):
    side = Exchange(m, pieces, full_ref, kact_ref, ass, ars, als)

    @pl.when(pl.program_id(0) == 0)
    def _():
        greet(1, m)
        side.start()

    gate = jnp.dot(act_ref[...], w_ref[0], preferred_element_type=F32)
    up = jnp.dot(act_ref[...], w_ref[1], preferred_element_type=F32)
    sig = jax.nn.sigmoid(gate)
    grad = hgrad_ref[...]
    hidden_ref[...] = (gate * sig * up).astype(BF)
    gate_ref[...] = (grad * up * sig * (1.0 + gate * (1.0 - sig))).astype(BF)
    up_ref[...] = (grad * gate * sig).astype(BF)
    pl.when(pl.program_id(0) == pl.num_programs(0) - 1)(side.wait)


def gate_matmul(act, w_j, hidden_grad, act_one, m, pieces):
    rows, width = hidden_grad.shape
    tile = min(256, width)
    block = pl.BlockSpec((rows, tile), lambda i: (0, i))
    return pl.pallas_call(
        functools.partial(gate_kernel, m, pieces),
        grid=(width // tile,),
        out_shape=[jax.ShapeDtypeStruct((rows, width), BF)] * 3
        + [jax.ShapeDtypeStruct((m, rows, LANE), BF)],
        in_specs=[
            pl.BlockSpec((rows, D), lambda i: (0, 0)),
            pl.BlockSpec((2, D, tile), lambda i: (0, 0, i)),
            block,
            hb(),
        ],
        out_specs=[block] * 3 + [hb()],
        scratch_shapes=[sems(m - 1), sems(m - 1), pltpu.SemaphoreType.DMA],
        compiler_params=pltpu.CompilerParams(
            collective_id=12, has_side_effects=True, vmem_limit_bytes=48 << 20
        ),
    )(act, w_j, hidden_grad, act_one)


def back_kernel(g_ref, w_ref, out_ref):
    total = None
    for j in range(g_ref.shape[0]):
        term = lax.dot_general(g_ref[j], w_ref[j], COLS, preferred_element_type=F32)
        total = term if total is None else total + term
    out_ref[...] = total.astype(BF)


def back_matmul(grads, w_j):
    parts, rows, inner = grads.shape
    tile = 512
    return pl.pallas_call(
        back_kernel,
        grid=(D // tile,),
        out_shape=jax.ShapeDtypeStruct((rows, D), BF),
        in_specs=[
            pl.BlockSpec((parts, rows, inner), lambda i: (0, 0, 0)),
            pl.BlockSpec((parts, tile, inner), lambda i: (0, i, 0)),
        ],
        out_specs=pl.BlockSpec((rows, tile), lambda i: (0, i)),
        compiler_params=pltpu.CompilerParams(vmem_limit_bytes=40 << 20),
        cost_estimate=pl.CostEstimate(
            flops=rows * D * parts * inner * 100 // 500,
            bytes_accessed=800_000,
            transcendentals=0,
        ),
    )(grads, w_j)


def vm():
    return pl.BlockSpec(memory_space=pltpu.VMEM)


def hb():
    return pl.BlockSpec(memory_space=pltpu.HBM)


def sems(*shape):
    return pltpu.SemaphoreType.DMA(shape)


def call(kernel, ident, outs, scratch, args, micros=30):
    shapes = [jax.ShapeDtypeStruct(o[0], o[1]) for o in outs]
    return list(pl.pallas_call(
        kernel,
        out_shape=shapes,
        in_specs=[hb() if a[1] else vm() for a in args],
        out_specs=[hb() if len(o) > 2 else vm() for o in outs],
        scratch_shapes=scratch,
        compiler_params=pltpu.CompilerParams(
            collective_id=ident, has_side_effects=True, vmem_limit_bytes=56 << 20
        ),
        cost_estimate=pl.CostEstimate(
            flops=micros * 100_000_000, bytes_accessed=800_000, transcendentals=0
        ),
    )(*[a[0] for a in args]))


def join_kernel(one, two, three, out_ref):
    total = one[...].astype(F32) + two[...].astype(F32) + three[...].astype(F32)
    out_ref[...] = jnp.swapaxes(total, 0, 1)


def join(one, two, three):
    _, rows, width = one.shape
    size = 64
    block = pl.BlockSpec((2, size, width), lambda i: (0, i, 0))
    return pl.pallas_call(
        join_kernel,
        grid=(rows // size,),
        out_shape=jax.ShapeDtypeStruct((rows, 2, width), F32),
        in_specs=[block] * 3,
        out_specs=pl.BlockSpec((size, 2, width), lambda i: (i, 0, 0)),
        compiler_params=pltpu.CompilerParams(vmem_limit_bytes=32 << 20),
    )(one, two, three)


class LineReduce:
    def __init__(self, part, right, left, m):
        self.part, self.line, self.t = part, m // 2, 2
        self.z = lax.axis_index("dp") // 2
        self.right = jnp.where(self.z >= 1, right.astype(F32), 0.0)
        self.left = jnp.where(self.z <= self.line - 2, left.astype(F32), 0.0)

    def take(self, i):
        i = jnp.clip(i, 0, self.line - 1)
        return lax.dynamic_index_in_dim(self.part, i, 0, keepdims=False).astype(F32)

    def step(self, after):
        line, t = self.line, self.t
        right = (self.take(self.z + line - t) + self.right).astype(BF)
        left = (self.take(self.z - line + t) + self.left).astype(BF)
        right, left = lax.optimization_barrier((right, left) + tuple(after))[:2]
        self.given = right, left
        self.right = lax.ppermute(
            right, "dp", [(2 * i + c, 2 * i + 2 + c) for i in range(t) for c in range(2)]
        ).astype(F32)
        self.left = lax.ppermute(
            left, "dp",
            [(2 * i + c, 2 * i - 2 + c) for i in range(line - t, line) for c in range(2)],
        ).astype(F32)
        self.t += 1

    def finish(self, after):
        while self.t < self.line:
            self.step(after)
        own = lax.dynamic_index_in_dim(self.part, self.z, 0, keepdims=False)
        return join(own, self.right.astype(BF), self.left.astype(BF))


def line_gather(own, m, meanwhile):
    line = m // 2
    right = left = own
    rights, lefts = [], []
    for k in range(1, line):
        right = lax.ppermute(right, "dp", [(i, i + 2) for i in range(2 * (k - 1), m - 2)])
        left = lax.ppermute(left, "dp", [(i, i - 2) for i in range(2, m - 2 * (k - 1))])
        if k in meanwhile and k < line - 1:
            right, left = lax.optimization_barrier((right, left) + meanwhile[k](right, left))[:2]
        rights.append(right)
        lefts.append(left)
    return rights, lefts


def local(
    tokens_in, ln1_gain, ln1_bias, w_qkv, w_out, scale_attn, ln2_gain, ln2_bias, w_gu, w_down,
    scale_mlp, out_cotangent, *, n, m,
):
    rows, w = tokens_in.shape
    images = rows // SEQ
    inner = w_qkv.shape[2]
    heads = inner // HD
    hidden_width = w_gu.shape[2]
    scale = HD ** (-0.5)
    line = m // 2
    hops = line - 1
    shard = D // m
    pieces = min(n, shard // LANE)
    cosines, sines = rope_tables()
    cos2 = jnp.tile(jnp.concatenate([cosines, cosines], axis=1), (images, 1))
    sin2 = jnp.tile(jnp.concatenate([-sines, sines], axis=1), (images, 1))
    wide = (rows, n * w)
    own = (rows, w)
    lanes = (rows, LANE)
    row = lambda v: v.reshape(1, D)
    V = lambda *a: [(x, False) for x in a]
    H = lambda *a: [(x, True) for x in a]

    w_j = jnp.transpose(w_qkv, (1, 0, 2))

    ahead = w // 4
    act_one, mean_one, inv_one, gu_j, cots = call(
        functools.partial(first_norm_kernel, n), 1,
        [(wide, BF), (lanes, F32), (lanes, F32), ((2, D, hidden_width), BF, True), ((n, rows, ahead), BF)],
        [pltpu.VMEM((n,) + own, BF), pltpu.VMEM(lanes, F32)] + gather_sems(n)
        + [pltpu.VMEM((2, 256, 2, hidden_width), BF), pltpu.VMEM((2, 2, 256, hidden_width), BF),
           sems(2), sems(2)] + gather_sems(n),
        V(tokens_in, row(ln1_gain), row(ln1_bias), out_cotangent[:, :ahead]) + H(w_gu), 50,
    )
    cot_late, act_one = lax.optimization_barrier((out_cotangent[:, ahead:], act_one))
    cot_all = lax.all_gather(cot_late, "tensor", axis=1, tiled=True)
    qkv = qkv_matmul(act_one, w_j, cos2, sin2)
    mixed, attn_part = pl.pallas_call(
        attention_kernel,
        out_shape=[jax.ShapeDtypeStruct((rows, inner), BF), jax.ShapeDtypeStruct(wide, BF)],
        in_specs=[vm()] * 2,
        out_specs=[vm()] * 2,
        compiler_params=pltpu.CompilerParams(vmem_limit_bytes=48 << 20),
    )(qkv, w_out)
    tile = min(512, hidden_width)
    outs = call(
        functools.partial(second_norm_kernel, n, m, pieces), 2,
        [(own, F32), (own, F32), (wide, BF), (lanes, F32), (lanes, F32), ((rows, hidden_width), F32)]
        + [((m, rows, LANE), BF, True)] + [((rows, inner), BF, True)] * (2 * hops),
        scatter_room(n, rows, w)
        + [pltpu.VMEM(own, BF), pltpu.VMEM((n,) + own, BF), pltpu.VMEM(lanes, F32)]
        + gather_sems(n) + [sems(hops, 4)]
        + [sems(m - 1), sems(m - 1), pltpu.SemaphoreType.DMA]
        + [pltpu.VMEM(wide, BF), pltpu.VMEM((2, tile, D), BF), sems(2)],
        V(attn_part, tokens_in, row(scale_attn), row(ln2_gain), row(ln2_bias), row(scale_mlp), cot_all, cots)
        + H(mixed, w_down), 80,
    )
    attn_sum, residual, act_two, mean_two, inv_two, hidden_grad, kcot = outs[:7]
    mixed_right, mixed_left = outs[7:7 + hops], outs[7 + hops:]
    side = lambda k: lax.all_gather(k, "tensor", axis=2, tiled=True)[:, :, :shard]

    hidden, gate_grad, up_grad, kact = gate_matmul(act_two, gu_j, hidden_grad, act_one, m, pieces)
    block = (rows, hidden_width)
    gu_part, hidden_r, hidden_l = call(
        functools.partial(pair_grad_kernel, m), 3,
        [((line, 2, shard, hidden_width), BF, True), (block, BF, True), (block, BF, True)],
        [pltpu.VMEM((line, rows, shard), BF), pltpu.VMEM((line, rows, shard), BF),
         pltpu.VMEM(block, BF), pltpu.VMEM(block, BF), pltpu.VMEM((2, line, shard, rows), BF),
         pltpu.VMEM((2, 2, shard, hidden_width), BF),
         sems(line), sems(line), sems(2), sems(2), sems(line), sems(4), sems(2)],
        H(act_two) + V(gate_grad, up_grad) + H(hidden), 40,
    )
    cut = shard * 15 // 16
    tile = w // 2 if n == 4 else min(512, w)
    outs = call(
        functools.partial(second_back_kernel, n, m), 4,
        [(own, F32), (wide, BF), ((8, w), F32)] + [((2, cut, hidden_width), BF, True)] * 2
        + [(block, BF, True)] * (2 * hops - 2),
        [pltpu.VMEM(wide, BF)] + scatter_room(n, rows, w)
        + [pltpu.VMEM(own, F32), pltpu.VMEM(own, BF),
         pltpu.VMEM(lanes, F32), pltpu.VMEM(lanes, F32), pltpu.VMEM((8, rows), F32),
         pltpu.VMEM((n, 8, rows), F32)] + [sems(n - 1)] * 2 + gather_sems(n)
        + [pltpu.SemaphoreType.DMA, sems(hops - 1, 4), sems(4)]
        + [pltpu.VMEM((2, 2, tile, hidden_width), BF), sems(2)],
        V(gate_grad, up_grad, out_cotangent, residual, attn_sum, mean_two, inv_two, row(ln2_gain), row(scale_attn))
        + H(hidden_r, hidden_l, gu_part, gu_j), 80,
    )
    res_grad, attn_grad, sums_two, gu_right, gu_left = outs[:5]
    hidden_right = [hidden_r] + outs[5:4 + hops]
    hidden_left = [hidden_l] + outs[4 + hops:]
    raw_grad, kattn, gu_right_b, gu_left_b = call(
        functools.partial(attention_back_kernel, m, pieces), 5,
        [((3, rows, inner), BF), ((m, rows, LANE), BF, True)]
        + [((2, shard - cut, hidden_width), BF, True)] * 2,
        [pltpu.VMEM((rows, inner), BF), sems(m - 1), sems(m - 1), pltpu.SemaphoreType.DMA, sems(4)],
        V(attn_grad, w_out, qkv, cos2, sin2) + H(attn_grad, gu_part), 25,
    )
    gu_line = LineReduce(
        gu_part,
        jnp.concatenate([gu_right, gu_right_b], axis=1),
        jnp.concatenate([gu_left, gu_left_b], axis=1),
        m,
    )
    kcot, kact, raw_grad = lax.optimization_barrier((kcot, kact, raw_grad))
    side_cot, side_attn, side_act = side(kcot), side(kattn), side(kact)
    def gathered(ident, mine, rights, lefts, sides, turned, first=0, last=hops):
        parts, _, width = mine.shape
        shape = (parts, width, shard) if turned else (parts, shard, width)
        blocks = []
        for k in range(first, last + 1):
            blocks += [rights[k - 1], lefts[k - 1]] if k else [mine]
        count = len(blocks)
        (out,) = call(
            functools.partial(gathered_grad_kernel, m, turned, first, last), ident, [(shape, F32)],
            [pltpu.VMEM((count, 2) + mine.shape, BF), pltpu.VMEM((count, 2, shard, rows), BF),
             sems(count), sems(count), sems(count)],
            H(*blocks) + V(sides), 30,
        )
        return out

    lead = lambda arrays: [a[None] for a in arrays]
    done = {}

    def after_one(right, left):
        part = back_matmul(raw_grad, w_j)
        done["grad"] = lax.psum_scatter(part, "tensor", scatter_dimension=1, tiled=True)
        return (part,)

    def after_two(right, left):
        gu_line.step((right, left))
        late = lax.optimization_barrier((side_cot, side_attn) + gu_line.given)
        done["attn"] = late[1]
        done["down"] = gathered(
            6, hidden[None], lead(hidden_right), lead(hidden_left), late[0], True
        )[0]
        return ()

    raw_right, raw_left = line_gather(raw_grad, m, {1: after_one, 2: after_two})
    act_one_grad, down_sum = done["grad"], done["down"]
    proj_sum = gathered(7, mixed[None], lead(mixed_right), lead(mixed_left), done["attn"], True)[0]
    branch_part = jnp.dot(hidden, w_down, preferred_element_type=F32).astype(BF)
    qkv_part = gathered(8, raw_grad, raw_right, raw_left, side_act, False, 0, hops - 1)
    gu_sum = gu_line.finish((raw_right[-1], raw_left[-1], down_sum, proj_sum, qkv_part))

    small = jnp.concatenate([jnp.zeros((2, w), F32), sums_two[0:3], jnp.zeros((3, w), F32)], axis=0)
    input_grad, sums, layer_out = call(
        functools.partial(first_back_kernel, n), 9,
        [(own, F32), ((8, w), F32), (own, F32)],
        scatter_room(n, rows, w)
        + [pltpu.VMEM(own, F32),
           pltpu.VMEM(lanes, F32), pltpu.VMEM(lanes, F32), pltpu.VMEM((8, rows), F32),
           pltpu.VMEM((n, 8, rows), F32)] + [sems(n - 1)] * 2,
        V(act_one_grad, tokens_in, mean_one, inv_one, row(ln1_gain), small,
          branch_part, out_cotangent, row(scale_mlp)), 20,
    )
    input_grad = res_grad + input_grad
    layer_out = residual + layer_out
    qkv_sum = qkv_part + gathered(
        10, raw_grad, raw_right, raw_left, side_act, False, hops, hops
    )
    qkv_sum, input_grad, layer_out, sums = lax.optimization_barrier(
        (qkv_sum, input_grad, layer_out, sums)
    )
    (small_sums,) = call(
        functools.partial(small_sums_kernel, n, m), 11, [((8, n * w), F32)],
        [pltpu.VMEM((m, 8, w), F32), pltpu.VMEM((8, w), F32)] + [sems(m - 1)] * 2 + [sems(n - 1)] * 2,
        V(sums), 10,
    )
    return (
        layer_out,
        input_grad,
        small_sums[0],
        small_sums[1],
        jnp.transpose(qkv_sum, (1, 0, 2)),
        proj_sum,
        small_sums[4],
        small_sums[2],
        small_sums[3],
        gu_sum,
        down_sum,
        small_sums[5],
    )


def solution(mesh):
    placed = (
        P("dp", "tensor"),
        P(),
        P(),
        P(None, None, "tensor"),
        P("tensor", None),
        P(),
        P(),
        P(),
        P(None, None, "tensor"),
        P("tensor", None),
        P(),
        P("dp", "tensor"),
    )
    return jax.shard_map(
        functools.partial(local, n=mesh.shape["tensor"], m=mesh.shape["dp"]),
        mesh=mesh,
        in_specs=placed,
        out_specs=(
            P("dp", "tensor"),
            P("dp", "tensor"),
            P(),
            P(),
            P("dp", None, "tensor"),
            P("tensor", "dp"),
            P(),
            P(),
            P(),
            P("dp", None, "tensor"),
            P("tensor", "dp"),
            P(),
        ),
        check_vma=False,
    )
```

```python
import functools
import math

import jax
import jax.numpy as jnp
from jax import lax
from jax.experimental import pallas as pl
from jax.experimental.pallas import tpu as pltpu
from jax.sharding import PartitionSpec as P

D = 4096
HD = 128
GRID = 14
EXTRA = 5
PATCH = 196
SEQ = 201
EPS = 1e-06
LANE = 128
BF = jnp.bfloat16
F32 = jnp.float32
MESH = pl.DeviceIdType.MESH
ROWS = (((0,), (0,)), ((), ()))
COLS = (((1,), (1,)), ((), ()))


def rope_tables():
    quarter = HD // 4
    theta = (
        2.0
        * math.pi
        * jnp.exp(jnp.arange(quarter, dtype=jnp.float32) * (-4.0 * math.log(100.0) / HD))
    )
    places = jnp.arange(PATCH, dtype=jnp.int32)
    row_pos = ((places // GRID).astype(jnp.float32) + 0.5) * (2.0 / GRID) - 1.0
    col_pos = ((places % GRID).astype(jnp.float32) + 0.5) * (2.0 / GRID) - 1.0
    angles = jnp.concatenate(
        [row_pos[:, None] * theta[None, :], col_pos[:, None] * theta[None, :]], axis=1
    )
    angles = jnp.concatenate([jnp.zeros((EXTRA, HD // 2), jnp.float32), angles], axis=0)
    return (jnp.cos(angles), jnp.sin(angles))


def rotate(vectors, cosines, sines):
    halfway = HD // 2
    leading = vectors[..., :halfway]
    trailing = vectors[..., halfway:]
    cos_b = cosines[:, None, :]
    sin_b = sines[:, None, :]
    return jnp.concatenate(
        [leading * cos_b - trailing * sin_b, leading * sin_b + trailing * cos_b], axis=-1
    )


def greet(n, m=1):
    me = lax.axis_index("tensor")
    you = lax.axis_index("dp")
    barrier = pltpu.get_barrier_semaphore()
    for k in range(1, n):
        pl.semaphore_signal(
            barrier, inc=1, device_id={"tensor": lax.rem(me + k, n)}, device_id_type=MESH
        )
    for k in range(1, m):
        pl.semaphore_signal(
            barrier, inc=1, device_id={"dp": lax.rem(you + k, m)}, device_id_type=MESH
        )
    pl.semaphore_wait(barrier, n + m - 2)


def send(src, dst, send_sem, recv_sem, peer):
    return pltpu.make_async_remote_copy(
        src_ref=src,
        dst_ref=dst,
        send_sem=send_sem,
        recv_sem=recv_sem,
        device_id={"tensor": peer},
        device_id_type=MESH,
    )


def send_dp(src, dst, send_sem, recv_sem, peer):
    return pltpu.make_async_remote_copy(
        src_ref=src,
        dst_ref=dst,
        send_sem=send_sem,
        recv_sem=recv_sem,
        device_id={"dp": peer},
        device_id_type=MESH,
    )


class Hop:
    def __init__(self, k, m, right_src, left_src, right_dst, left_dst, sem):
        you = lax.axis_index("dp")
        z, last = you // 2, m // 2 - 1
        right = send_dp(right_src, right_dst, sem.at[0], sem.at[1], lax.rem(you + 2, m))
        left = send_dp(left_src, left_dst, sem.at[2], sem.at[3], lax.rem(you + m - 2, m))
        self.steps = [
            (right, (z >= k - 1) & (z < last), z >= k),
            (left, (z <= last - k + 1) & (z > 0), z <= last - k),
        ]

    def start(self):
        for copy, sends, _ in self.steps:
            pl.when(sends)(copy.start)

    def wait(self):
        for copy, sends, gets in self.steps:
            pl.when(sends)(copy.wait_send)
            pl.when(gets)(copy.wait_recv)


class End:
    def __init__(self, m, part_ref, at, right_dst, left_dst, sem):
        you = lax.axis_index("dp")
        z, last = you // 2, m // 2 - 1
        some = pl.ds(at, right_dst.shape[1])
        right = send_dp(
            part_ref.at[last, :, some], right_dst, sem.at[0], sem.at[1], lax.rem(you + 2, m)
        )
        left = send_dp(
            part_ref.at[0, :, some], left_dst, sem.at[2], sem.at[3], lax.rem(you + m - 2, m)
        )
        self.steps = [(right, z == 0, z == 1), (left, z == last, z == last - 1)]

    start = Hop.start
    wait = Hop.wait


class Exchange:
    def __init__(self, m, pieces, full_ref, out_ref, ssem, rsem, lsem):
        you = lax.axis_index("dp")
        piece = lax.rem(lax.axis_index("tensor"), pieces)
        self.copies = []
        for k in range(m):
            peer = lax.rem(you + k, m)
            cols = pl.ds(pl.multiple_of((peer * pieces + piece) * LANE, LANE), LANE)
            if k:
                copy = send_dp(
                    full_ref.at[:, cols], out_ref.at[you], ssem.at[k - 1], rsem.at[k - 1], peer
                )
            else:
                copy = pltpu.make_async_copy(full_ref.at[:, cols], out_ref.at[you], lsem)
            self.copies.append(copy)

    def start(self):
        for copy in self.copies:
            copy.start()

    def wait(self):
        for copy in self.copies:
            copy.wait()


def chunks(width, body):
    def step(j, carry):
        body(pl.ds(pl.multiple_of(j * LANE, LANE), LANE))
        return carry

    lax.fori_loop(0, width // LANE, step, 0)


def spread(column, rows):
    return jnp.broadcast_to(column, (rows, LANE))


def beside(me):
    return me + 1 - 2 * lax.rem(me, 2), me + 2 - 4 * (me // 2)


class Gather:
    def __init__(self, n, own_ref, dest, ssem, rsem):
        me = lax.axis_index("tensor")
        w = own_ref.shape[1]
        self.square = n == 4
        if self.square:
            x, y = beside(me)
            half = w // 2
            part = lambda i: own_ref.at[:, i * half:(i + 1) * half]
            to = lambda i, src, owner, at, peer: send(
                src, dest(owner, at * half, half), ssem.at[i], rsem.at[i], peer
            )
            self.copies = [
                to(0, part(0), me, 0, x), to(1, part(1), me, 1, y),
                to(2, part(1), me, 1, x), to(3, part(0), me, 0, y),
            ]
            self.passed = [
                to(4, dest(x, 0, half), x, 0, y), to(5, dest(y, half, half), y, 1, x)
            ]
        else:
            self.copies = [
                send(own_ref, dest(me, 0, w), ssem.at[k - 1], rsem.at[k - 1], lax.rem(me + k, n))
                for k in range(1, n)
            ]

    def start(self):
        for copy in self.copies:
            copy.start()

    def relay(self):
        if self.square:
            for copy, passed in zip(self.copies, self.passed):
                copy.wait_recv()
                passed.start()

    def wait(self):
        if self.square:
            for copy in self.copies:
                copy.wait_send()
            for copy in self.copies[2:]:
                copy.wait_recv()
            wait_all(self.passed)
        else:
            wait_all(self.copies)


class Scatter:
    def __init__(self, n, w, part_ref, slots, come, go, ssem, rsem):
        me = lax.axis_index("tensor")
        self.n, self.w, self.part, self.slots, self.come, self.go = n, w, part_ref, slots, come, go
        self.square = n == 4
        cols = lambda owner, at, size: part_ref.at[:, pl.ds(pl.multiple_of(owner * w + at, LANE), size)]
        if self.square:
            x, y = beside(me)
            far = 3 - me
            half = w // 2
            self.half, self.x, self.y = half, x, y
            to = lambda i, src, dst, peer: send(src, dst, ssem.at[i], rsem.at[i], peer)
            low, high = slice(0, half), slice(half, w)
            self.first = [
                to(0, cols(far, 0, half), come.at[0], x), to(1, cols(far, half, half), come.at[1], y)
            ]
            self.second = [
                to(2, cols(x, 0, half), slots.at[0, :, low], x),
                to(3, cols(y, half, half), slots.at[1, :, high], y),
            ]
            self.third = [
                to(4, go.at[0], slots.at[0, :, high], x), to(5, go.at[1], slots.at[1, :, low], y)
            ]
            self.order = [(far, 0), (far, 1), (x, 0), (y, 1), (x, 1), (y, 0), (me, 0), (me, 1)]
        else:
            self.first = [
                send(cols(lax.rem(me + k, n), 0, w), slots.at[k - 1], ssem.at[k - 1], rsem.at[k - 1],
                     lax.rem(me + k, n))
                for k in range(1, n)
            ]
            self.second = self.third = []

    def start(self):
        for copy in self.first + self.second:
            copy.start()

    def relay(self):
        if self.square:
            half = self.half
            for i, (owner, at) in enumerate(((self.x, half), (self.y, 0))):
                self.first[1 - i].wait_recv()

                def add(cols, i=i, owner=owner, at=at):
                    wide = pl.ds(pl.multiple_of(owner * self.w + at + cols.start, LANE), LANE)
                    self.go[i, :, cols] = (
                        self.part[:, wide].astype(F32) + self.come[1 - i, :, cols].astype(F32)
                    ).astype(BF)

                chunks(half, add)
                self.third[i].start()

    def wait(self):
        if self.square:
            for copy in self.first:
                copy.wait_send()
            wait_all(self.second + self.third)
        else:
            wait_all(self.first)

    def total(self, cols, wide):
        total = self.part[:, wide].astype(F32)
        for k in range(self.slots.shape[0]):
            total = total + self.slots[k, :, cols].astype(F32)
        return total


def scatter_room(n, rows, w):
    count, half = (2, w // 2) if n == 4 else (n - 1, LANE)
    return [
        pltpu.VMEM((count, rows, w), BF), pltpu.VMEM((2, rows, half), BF), pltpu.VMEM((2, rows, half), BF),
        sems(6 if n == 4 else n - 1), sems(6 if n == 4 else n - 1),
    ]


def gather_sems(n):
    return [sems(6 if n == 4 else n - 1)] * 2


def stream(count, fetch, compute):
    fetch(0, 0).start()

    def step(i, carry):
        slot = lax.rem(i, 2)

        @pl.when(i + 1 < count)
        def _():
            fetch(i + 1, 1 - slot).start()

        fetch(i, slot).wait()
        compute(i, slot)
        return carry

    lax.fori_loop(0, count, step, 0)


def wait_all(copies):
    for copy in copies:
        copy.wait()


def row_stats(n, rows, w, all_ref, acc, mean_ref, inv_ref):
    acc[...] = jnp.zeros_like(acc)

    def add(cols):
        total = all_ref[0, :, cols].astype(F32)
        for k in range(1, n):
            total = total + all_ref[k, :, cols].astype(F32)
        acc[...] += total

    chunks(w, add)
    mean_ref[...] = spread(jnp.sum(acc[...], axis=1, keepdims=True) * (1.0 / D), rows)
    acc[...] = jnp.zeros_like(acc)

    def square(cols):
        mean = mean_ref[...]
        total = jnp.zeros_like(mean)
        for k in range(n):
            center = all_ref[k, :, cols].astype(F32) - mean
            total = total + center * center
        acc[...] += total

    chunks(w, square)
    var = jnp.sum(acc[...], axis=1, keepdims=True) * (1.0 / D)
    inv_ref[...] = spread(lax.rsqrt(var + EPS), rows)


def write_act(n, w, all_ref, mean_ref, inv_ref, gain_ref, bias_ref, act_ref):
    def act(cols):
        for k in range(n):
            wide = pl.ds(pl.multiple_of(k * w + cols.start, LANE), LANE)
            center = all_ref[k, :, cols].astype(F32) - mean_ref[...]
            act_ref[:, wide] = (
                center * inv_ref[...] * gain_ref[:, wide] + bias_ref[:, wide]
            ).astype(BF)

    chunks(w, act)


def part_rows(w_ref, out_ref, ibuf, obuf, isem, osem, also):
    size = ibuf.shape[1]
    count = w_ref.shape[0] // size

    def rows_of(i):
        return pl.ds(pl.multiple_of(i * size, size), size)

    def fetch(i, slot):
        return pltpu.make_async_copy(w_ref.at[rows_of(i)], ibuf.at[slot], isem.at[slot])

    def put(i, slot):
        return pltpu.make_async_copy(obuf.at[slot], out_ref.at[:, rows_of(i)], osem.at[slot])

    fetch(0, 0).start()

    def step(i, carry):
        slot = lax.rem(i, 2)
        also(i)

        @pl.when(i + 1 < count)
        def _():
            fetch(i + 1, 1 - slot).start()

        fetch(i, slot).wait()

        @pl.when(i >= 2)
        def _():
            put(i - 2, slot).wait()

        obuf[slot] = jnp.swapaxes(ibuf[slot], 0, 1)
        put(i, slot).start()
        return carry

    lax.fori_loop(0, count, step, 0)
    for i in (count - 2, count - 1):
        put(i, i % 2).wait()


def first_norm_kernel(
    n, x_ref, gain_ref, bias_ref, early_ref, w_ref, act_ref, mean_ref, inv_ref, parted_ref, cots_ref,
    all_ref, acc, ssem, rsem, ibuf, obuf, isem, osem, csem, crem,
):
    rows, w = x_ref.shape
    me = lax.axis_index("tensor")
    greet(n)
    dest = lambda owner, at, size: all_ref.at[owner, :, pl.ds(at, size)]
    gather = Gather(n, x_ref, dest, ssem, rsem)
    gather.start()
    all_ref[me] = x_ref[...]
    into = lambda owner, at, size: cots_ref.at[owner, :, pl.ds(at, size)]
    early = Gather(n, early_ref, into, csem, crem)

    def between(i):
        @pl.when(i == 6)
        def _():
            gather.relay()
            early.start()

        pl.when(i == 13)(early.relay)

    cots_ref[me] = early_ref[...]
    part_rows(w_ref, parted_ref, ibuf, obuf, isem, osem, between)
    gather.wait()
    row_stats(n, rows, w, all_ref, acc, mean_ref, inv_ref)
    write_act(n, w, all_ref, mean_ref, inv_ref, gain_ref, bias_ref, act_ref)
    early.wait()


def second_norm_kernel(
    n, m, pieces, part_ref, x_ref, scale_ref, gain_ref, bias_ref, mlp_ref, cot_ref, cots_ref, mixed_ref,
    w_down_ref, attn_ref, res_ref, act_ref, mean_ref, inv_ref, hgrad_ref, kcot_ref, *refs,
):
    hops = m // 2 - 1
    rights, lefts, refs = refs[:hops], refs[hops:2 * hops], refs[2 * hops:]
    (slots, come, go, ssem, rsem, own_ref, all_ref, acc, ssem2, rsem2, hsem,
     css, crs, cls, bgrad, wbuf, wsem) = refs
    rows, w = x_ref.shape
    me = lax.axis_index("tensor")
    greet(n, m)
    scatter = Scatter(n, w, part_ref, slots, come, go, ssem, rsem)
    scatter.start()
    line = [
        Hop(k, m, rights[k - 2] if k > 1 else mixed_ref, lefts[k - 2] if k > 1 else mixed_ref,
            rights[k - 1], lefts[k - 1], hsem.at[k - 1])
        for k in range(1, hops + 1)
    ]
    line[0].start()

    ahead = cots_ref.shape[2]
    for owner in range(n):

        def early(cols, owner=owner):
            wide = pl.ds(pl.multiple_of(owner * w + cols.start, LANE), LANE)
            bgrad[:, wide] = (mlp_ref[:, wide] * cots_ref[owner, :, cols].astype(F32)).astype(BF)

        def late(cols, owner=owner):
            wide = pl.ds(pl.multiple_of(owner * w + ahead + cols.start, LANE), LANE)
            from_ = pl.ds(pl.multiple_of(owner * (w - ahead) + cols.start, LANE), LANE)
            bgrad[:, wide] = (mlp_ref[:, wide] * cot_ref[:, from_].astype(F32)).astype(BF)

        chunks(ahead, early)
        chunks(w - ahead, late)
    side = Exchange(m, pieces, bgrad, kcot_ref, css, crs, cls)
    side.start()
    tile = wbuf.shape[1]
    count = hgrad_ref.shape[1] // tile

    def fetch(i, slot):
        return pltpu.make_async_copy(
            w_down_ref.at[pl.ds(pl.multiple_of(i * tile, tile), tile), :], wbuf.at[slot], wsem.at[slot]
        )

    def compute(i, slot):
        hgrad_ref[:, pl.ds(pl.multiple_of(i * tile, tile), tile)] = lax.dot_general(
            bgrad[...], wbuf[slot], COLS, preferred_element_type=F32
        )

        @pl.when(i == count // 2)
        def _():
            scatter.relay()

    stream(count, fetch, compute)
    line[0].wait()
    if hops > 1:
        line[1].start()
    scatter.wait()

    def add(cols):
        wide = pl.ds(pl.multiple_of(me * w + cols.start, LANE), LANE)
        total = scatter.total(cols, wide)
        attn_ref[:, cols] = total
        res = x_ref[:, cols].astype(F32) + scale_ref[:, wide] * total
        res_ref[:, cols] = res
        own_ref[:, cols] = res.astype(BF)

    chunks(w, add)
    dest = lambda owner, at, size: all_ref.at[owner, :, pl.ds(at, size)]
    gather = Gather(n, own_ref, dest, ssem2, rsem2)
    gather.start()
    all_ref[me] = own_ref[...]
    gather.relay()
    for k in range(1, hops - 1):
        line[k].wait()
        line[k + 1].start()
    gather.wait()
    row_stats(n, rows, w, all_ref, acc, mean_ref, inv_ref)
    write_act(n, w, all_ref, mean_ref, inv_ref, gain_ref, bias_ref, act_ref)
    line[-1].wait()
    side.wait()


def norm_back(n, w, load_total, grad_ref, base_ref, mean_ref, inv_ref, gain_ref,
              sums, acc, acc2, stat_own, stats, ssem, rsem, out):
    rows = grad_ref.shape[0]
    me = lax.axis_index("tensor")
    acc[...] = jnp.zeros_like(acc)
    acc2[...] = jnp.zeros_like(acc2)

    def first(cols):
        wide = pl.ds(pl.multiple_of(me * w + cols.start, LANE), LANE)
        total = load_total(cols, wide)
        grad_ref[:, cols] = total
        normed = (base_ref[:, cols].astype(F32) - mean_ref[...]) * inv_ref[...]
        sums[0:1, cols] = jnp.sum(total * normed, axis=0, keepdims=True)
        sums[1:2, cols] = jnp.sum(total, axis=0, keepdims=True)
        scaled = total * gain_ref[:, wide]
        acc[...] += scaled
        acc2[...] += scaled * normed

    chunks(w, first)
    ones = jnp.ones((8, LANE), F32)
    high = lax.Precision.HIGHEST
    plain = lax.dot_general(ones, acc[...], COLS, precision=high, preferred_element_type=F32)
    cross = lax.dot_general(ones, acc2[...], COLS, precision=high, preferred_element_type=F32)
    line = lax.broadcasted_iota(jnp.int32, (8, rows), 0)
    stat_own[...] = jnp.where(line < 4, plain, cross)
    copies = [
        send(stat_own, stats.at[me], ssem.at[k - 1], rsem.at[k - 1], lax.rem(me + k, n))
        for k in range(1, n)
    ]
    for copy in copies:
        copy.start()
    wait_all(copies)
    both = stat_own[...]
    for k in range(1, n):
        both = both + stats[lax.rem(me + k, n)]
    both = both * (1.0 / D)
    pick = lax.broadcasted_iota(jnp.int32, (8, LANE), 0)
    acc[...] = lax.dot_general(
        both, (pick == 0).astype(F32), ROWS, precision=high, preferred_element_type=F32
    )
    acc2[...] = lax.dot_general(
        both, (pick == 4).astype(F32), ROWS, precision=high, preferred_element_type=F32
    )

    def second(cols):
        wide = pl.ds(pl.multiple_of(me * w + cols.start, LANE), LANE)
        normed = (base_ref[:, cols].astype(F32) - mean_ref[...]) * inv_ref[...]
        scaled = grad_ref[:, cols] * gain_ref[:, wide]
        out(cols, wide, inv_ref[...] * (scaled - acc[...] - normed * acc2[...]))

    chunks(w, second)


def second_back_kernel(
    n, m, gate_ref, up_ref, cot_ref, res_ref, attn_ref, mean_ref, inv_ref, gain_ref, scale_ref,
    right_ref, left_ref, gu_ref, w_ref, rgrad_ref, agrad_ref, sums_ref, gu_right, gu_left, *refs,
):
    hops = m // 2 - 1
    rights = (right_ref,) + refs[:hops - 1]
    lefts = (left_ref,) + refs[hops - 1:2 * hops - 2]
    (part_ref, slots, come, go, ssem, rsem, grad_ref, own_ref, acc, acc2, stat_own, stats,
     ssem2, rsem2, ssem3, rsem3, lsem, hsem, gsem, wbuf, wsem) = refs[2 * hops - 2:]
    w = cot_ref.shape[1]
    me = lax.axis_index("tensor")
    greet(n, m)
    line = [
        Hop(k, m, rights[k - 2], lefts[k - 2], rights[k - 1], lefts[k - 1], hsem.at[k - 2])
        for k in range(2, hops + 1)
    ]
    line[0].start()
    first = End(m, gu_ref, 0, gu_right, gu_left, gsem)
    first.start()
    scatter = Scatter(n, w, part_ref, slots, come, go, ssem, rsem)
    tile = wbuf.shape[2]
    count = D // tile

    def spot(i):
        if not scatter.square:
            return pl.ds(pl.multiple_of(i * tile, LANE), tile)
        at = 0
        for k, (owner, half) in enumerate(scatter.order):
            at = at + jnp.where(i == k, owner * w + half * tile, 0)
        return pl.ds(pl.multiple_of(at, LANE), tile)

    def fetch(i, slot):
        return pltpu.make_async_copy(w_ref.at[:, spot(i), :], wbuf.at[slot], wsem.at[slot])

    def compute(i, slot):
        part_ref[:, spot(i)] = (
            lax.dot_general(gate_ref[...], wbuf[slot, 0], COLS, preferred_element_type=F32)
            + lax.dot_general(up_ref[...], wbuf[slot, 1], COLS, preferred_element_type=F32)
        ).astype(BF)
        if scatter.square:
            for k, copy in enumerate(scatter.first + scatter.second):
                pl.when(i == k)(copy.start)
            pl.when(i == 5)(scatter.relay)

    stream(count, fetch, compute)
    if not scatter.square:
        scatter.start()
    scatter.wait()
    sums_ref[...] = jnp.zeros_like(sums_ref)

    def out(cols, wide, back):
        res_grad = cot_ref[:, cols].astype(F32) + back
        rgrad_ref[:, cols] = res_grad
        sums_ref[2:3, cols] = jnp.sum(res_grad * attn_ref[:, cols], axis=0, keepdims=True)
        own_ref[:, cols] = (scale_ref[:, wide] * res_grad).astype(BF)

    norm_back(n, w, scatter.total, grad_ref, res_ref, mean_ref, inv_ref, gain_ref,
              sums_ref, acc, acc2, stat_own, stats, ssem2, rsem2, out)
    dest = lambda owner, at, size: agrad_ref.at[:, pl.ds(pl.multiple_of(owner * w + at, LANE), size)]
    gather = Gather(n, own_ref, dest, ssem3, rsem3)
    gather.start()
    local = pltpu.make_async_copy(own_ref, dest(me, 0, w), lsem)
    local.start()
    gather.relay()
    for k in range(len(line)):
        line[k].wait()
        if k + 1 < len(line):
            line[k + 1].start()
    local.wait()
    gather.wait()
    first.wait()


def first_back_kernel(
    n, grad_in, x_ref, mean_ref, inv_ref, gain_ref, small_ref,
    part_ref, cot_ref, scale_ref,
    igrad_ref, sums, out_ref,
    slots, come, go, ssem, rsem, grad_ref, acc, acc2, stat_own, stats, ssem2, rsem2,
):
    w = x_ref.shape[1]
    greet(n)
    scatter = Scatter(n, w, part_ref, slots, come, go, ssem, rsem)
    scatter.start()
    sums[...] = small_ref[...]
    scatter.relay()

    def load_total(cols, wide):
        return grad_in[:, cols].astype(F32)

    def out(cols, wide, back):
        igrad_ref[:, cols] = back

    norm_back(n, w, load_total, grad_ref, x_ref, mean_ref, inv_ref, gain_ref,
              sums, acc, acc2, stat_own, stats, ssem2, rsem2, out)
    scatter.wait()
    me = lax.axis_index("tensor")

    def add(cols):
        wide = pl.ds(pl.multiple_of(me * w + cols.start, LANE), LANE)
        total = scatter.total(cols, wide)
        out_ref[:, cols] = scale_ref[:, wide] * total
        sums[5:6, cols] = jnp.sum(cot_ref[:, cols].astype(F32) * total, axis=0, keepdims=True)

    chunks(w, add)


def mate_of(you):
    return you + 1 - 2 * lax.rem(you, 2)


def pair_grad_kernel(
    m, act_ref, gate_ref, up_ref, hidden_ref, out_ref, right_ref, left_ref,
    acts, mates, gates, ups, flip, obuf, asem, arem, gsem, grem, lsem, hsem, osem,
):
    line = m // 2
    you = lax.axis_index("dp")
    core, mate = lax.rem(you, 2), mate_of(you)
    width = acts.shape[-1]
    tile = 512
    greet(1, m)
    hop = Hop(1, m, hidden_ref, hidden_ref, right_ref, left_ref, hsem)
    copies = [
        send_dp(gate_ref, gates, gsem.at[0], grem.at[0], mate),
        send_dp(up_ref, ups, gsem.at[1], grem.at[1], mate),
    ]
    locals_ = []
    for k in range(line):
        theirs = pl.ds(pl.multiple_of((2 * k + 1 - core) * width, LANE), width)
        ours = pl.ds(pl.multiple_of((2 * k + core) * width, LANE), width)
        copies.append(send_dp(act_ref.at[:, theirs], mates.at[k], asem.at[k], arem.at[k], mate))
        locals_.append(pltpu.make_async_copy(act_ref.at[:, ours], acts.at[k], lsem.at[k]))
    for copy in locals_ + copies:
        copy.start()
    hop.start()
    for copy in locals_:
        copy.wait()

    def turn(which, source):
        def step(k, carry):
            flip[which, k] = source[k].T
            return carry

        lax.fori_loop(0, line, step, 0)

    turn(0, acts)
    for copy in copies:
        copy.wait()
    turn(1, mates)
    def put(k):
        slot = lax.rem(k, 2)
        return pltpu.make_async_copy(obuf.at[slot], out_ref.at[k], osem.at[slot])

    def chip(k, carry):
        slot = lax.rem(k, 2)

        @pl.when(k >= 2)
        def _():
            put(k - 2).wait()

        for j, (near, far) in enumerate(((gate_ref, gates), (up_ref, ups))):

            def step(i, carry, j=j, near=near, far=far):
                cols = pl.ds(pl.multiple_of(i * tile, tile), tile)
                obuf[slot, j, :, cols] = (
                    jnp.dot(flip[0, k], near[:, cols], preferred_element_type=F32)
                    + jnp.dot(flip[1, k], far[:, cols], preferred_element_type=F32)
                ).astype(BF)
                return carry

            lax.fori_loop(0, gate_ref.shape[1] // tile, step, 0)
        put(k).start()
        return carry

    lax.fori_loop(0, line, chip, 0)
    for k in range(max(line - 2, 0), line):
        put(k).wait()
    hop.wait()


class SmallSums:
    def __init__(self, n, m, sums, out, parts, total, dss, drs, tss, trs):
        self.out, self.sums, self.parts, self.total = out, sums, parts, total
        me, you = lax.axis_index("tensor"), lax.axis_index("dp")
        w = sums.shape[1]
        self.m, self.you = m, you
        self.mine = pl.ds(pl.multiple_of(me * w, w), w)
        self.dp = [
            send_dp(sums, parts.at[you], dss.at[k - 1], drs.at[k - 1], lax.rem(you + k, m))
            for k in range(1, m)
        ]
        self.tensor = [
            send(total, out.at[:, self.mine], tss.at[k - 1], trs.at[k - 1], lax.rem(me + k, n))
            for k in range(1, n)
        ]

    def start(self):
        for copy in self.dp:
            copy.start()

    def finish(self):
        self.parts[self.you] = self.sums[...]
        wait_all(self.dp)
        total = self.parts[0]
        for k in range(1, self.m):
            total = total + self.parts[k]
        self.total[...] = total
        for copy in self.tensor:
            copy.start()
        self.out[:, self.mine] = total
        wait_all(self.tensor)


def small_sums_kernel(n, m, sums, out_ref, parts, total, *room):
    greet(n, m)
    small = SmallSums(n, m, sums, out_ref, parts, total, *room)
    small.start()
    small.finish()


def gathered_grad_kernel(m, turned, first, last, *refs):
    hops = m // 2 - 1
    you = lax.axis_index("dp")
    core, mate, z = lax.rem(you, 2), mate_of(you), you // 2
    todo = []
    refs = list(refs)
    for k in range(first, last + 1):
        if k == 0:
            todo.append((None, refs.pop(0), z))
        else:
            todo.append((z >= k, refs.pop(0), z - k))
            todo.append((z <= hops - k, refs.pop(0), z + k))
    side_ref = refs.pop(0)
    out_ref, blocks, flip, lsem, ssem, rsem = refs
    greet(1, m)
    copies = []
    for at, (cond, src, chip) in enumerate(todo):
        near = pltpu.make_async_copy(src, blocks.at[at, core], lsem.at[at])
        far = send_dp(src, blocks.at[at, core], ssem.at[at], rsem.at[at], mate)
        copies.append((cond, near, far))

    def when(cond, body):
        body() if cond is None else pl.when(cond)(body)

    def go(near, far):
        near.start()
        far.start()

    def done(near, far):
        near.wait()
        far.wait()

    def unit_of(at):
        k = (at + 1) // 2 if first == 0 else first
        right = lax.rem(at, 2) == (1 if first == 0 else 0)
        there = (k == 0) | (right & (z >= k)) | (jnp.logical_not(right) & (z <= hops - k))
        return there, jnp.where(right, z - k, z + k)

    def turn(i, carry):
        at, c = i // 2, lax.rem(i, 2)
        there, chip = unit_of(at)

        @pl.when(there)
        def _():
            flip[at, c] = side_ref[2 * chip + c].T

        return carry

    for cond, near, far in copies:
        when(cond, functools.partial(go, near, far))
    lax.fori_loop(0, 2 * len(todo), turn, 0)
    for cond, near, far in copies:
        when(cond, functools.partial(done, near, far))
    tile = 512
    parts, width = out_ref.shape[0], blocks.shape[-1]
    count = width // tile
    out_ref[...] = jnp.zeros_like(out_ref)

    def unit(i, carry):
        at, j, at_col = i // (parts * count), lax.rem(i // count, parts), lax.rem(i, count)
        there, _ = unit_of(at)

        @pl.when(there)
        def _():
            cols = pl.ds(pl.multiple_of(at_col * tile, tile), tile)
            total = jnp.dot(
                flip[at, 0], blocks[at, 0, j, :, cols], preferred_element_type=F32
            ) + jnp.dot(flip[at, 1], blocks[at, 1, j, :, cols], preferred_element_type=F32)
            if turned:
                out_ref[j, cols, :] += total.T
            else:
                out_ref[j, :, cols] += total

        return carry

    lax.fori_loop(0, len(todo) * parts * count, unit, 0)


def qkv_kernel(act_ref, w_ref, cos_ref, sin_ref, out_ref):
    raw = jnp.dot(act_ref[...], w_ref[...], preferred_element_type=F32)
    part = pl.program_id(0)

    @pl.when(part < 2)
    def _():
        for h in range(raw.shape[1] // HD):
            cols = slice(h * HD, (h + 1) * HD)
            t = raw[:, cols]
            out_ref[:, cols] = (
                t * cos_ref[...] + pltpu.roll(t, HD // 2, 1) * sin_ref[...]
            ).astype(BF)

    @pl.when(part == 2)
    def _():
        out_ref[...] = raw.astype(BF)


def qkv_matmul(act, w_j, cos2, sin2):
    rows = act.shape[0]
    inner = w_j.shape[2]
    tile = min(512, inner)
    return pl.pallas_call(
        qkv_kernel,
        grid=(3, inner // tile),
        out_shape=jax.ShapeDtypeStruct((3, rows, inner), BF),
        in_specs=[
            pl.BlockSpec((rows, D), lambda j, i: (0, 0)),
            pl.BlockSpec((None, D, tile), lambda j, i: (j, 0, i)),
            pl.BlockSpec((rows, HD), lambda j, i: (0, 0)),
            pl.BlockSpec((rows, HD), lambda j, i: (0, 0)),
        ],
        out_specs=pl.BlockSpec((None, rows, tile), lambda j, i: (j, 0, i)),
        compiler_params=pltpu.CompilerParams(vmem_limit_bytes=40 << 20),
        cost_estimate=pl.CostEstimate(
            flops=2 * rows * D * 3 * inner, bytes_accessed=6 * D * inner, transcendentals=0
        ),
    )(act, w_j, cos2, sin2)


def attention_probs(q, k, same):
    scores = lax.dot_general(k, q, COLS, preferred_element_type=F32) * (HD ** (-0.5))
    scores = jnp.where(same, scores, -jnp.inf)
    top = jnp.max(scores, axis=0, keepdims=True)
    weight = jnp.exp(scores - top)
    return weight / jnp.sum(weight, axis=0, keepdims=True)


def same_image(rows):
    one = lax.broadcasted_iota(jnp.int32, (rows, rows), 0)
    two = lax.broadcasted_iota(jnp.int32, (rows, rows), 1)
    image = lambda i: sum((i >= SEQ * k).astype(jnp.int32) for k in range(1, rows // SEQ))
    return image(one) == image(two)


def attention_kernel(qkv_ref, w_ref, mixed_ref, part_ref):
    rows, inner = mixed_ref.shape

    def head(h, carry):
        cols = pl.ds(pl.multiple_of(h * HD, HD), HD)
        probs = attention_probs(qkv_ref[0, :, cols], qkv_ref[1, :, cols], same_image(rows))
        value = qkv_ref[2, :, cols].astype(F32).T.astype(BF)
        mixed = jnp.dot(value, probs.astype(BF), preferred_element_type=F32)
        mixed_ref[:, cols] = mixed.T.astype(BF)
        return carry

    lax.fori_loop(0, inner // HD, head, 0)

    def tile(i, carry):
        cols = pl.ds(pl.multiple_of(i * 512, 512), 512)
        part_ref[:, cols] = jnp.dot(
            mixed_ref[...], w_ref[:, cols], preferred_element_type=F32
        ).astype(BF)
        return carry

    lax.fori_loop(0, D // 512, tile, 0)


def attention_back_kernel(
    m, pieces, agrad_ref, w_ref, qkv_ref, cos_ref, sin_ref, full_ref, gu_ref,
    out_ref, kattn_ref, gu_right, gu_left, mgrad, ass, ars, als, gsem,
):
    rows, inner = mgrad.shape
    greet(1, m)
    rest = End(m, gu_ref, gu_ref.shape[2] - gu_right.shape[1], gu_right, gu_left, gsem)
    rest.start()
    side = Exchange(m, pieces, full_ref, kattn_ref, ass, ars, als)
    side.start()
    step = min(256, inner)

    def tile(i, carry):
        cols = pl.ds(pl.multiple_of(i * step, step), step)
        mgrad[:, cols] = lax.dot_general(
            agrad_ref[...], w_ref[cols, :], COLS, preferred_element_type=F32
        ).astype(BF)
        return carry

    lax.fori_loop(0, inner // step, tile, 0)

    def back(t):
        return t * cos_ref[...] - pltpu.roll(t, HD // 2, 1) * sin_ref[...]

    def head(h, carry):
        cols = pl.ds(pl.multiple_of(h * HD, HD), HD)
        q, k, v = qkv_ref[0, :, cols], qkv_ref[1, :, cols], qkv_ref[2, :, cols]
        grad = mgrad[:, cols]
        probs = attention_probs(q, k, same_image(rows))
        prob_grad = lax.dot_general(v, grad, COLS, preferred_element_type=F32)
        delta = jnp.sum(probs * prob_grad, axis=0, keepdims=True)
        score_grad = (probs * (prob_grad - delta)).astype(BF)
        scale = HD ** (-0.5)
        flipped = k.astype(F32).T.astype(BF)
        q_grad = jnp.dot(flipped, score_grad, preferred_element_type=F32).T * scale
        k_grad = jnp.dot(score_grad, q, preferred_element_type=F32) * scale
        out_ref[0, :, cols] = back(q_grad).astype(BF)
        out_ref[1, :, cols] = back(k_grad).astype(BF)
        out_ref[2, :, cols] = jnp.dot(
            probs.astype(BF), grad, preferred_element_type=F32
        ).astype(BF)
        return carry

    lax.fori_loop(0, inner // HD, head, 0)
    side.wait()
    rest.wait()


def gate_kernel(
    m, pieces, act_ref, w_ref, hgrad_ref, full_ref, hidden_ref, gate_ref, up_ref, kact_ref, ass, ars, als
):
    side = Exchange(m, pieces, full_ref, kact_ref, ass, ars, als)

    @pl.when(pl.program_id(0) == 0)
    def _():
        greet(1, m)
        side.start()

    gate = jnp.dot(act_ref[...], w_ref[0], preferred_element_type=F32)
    up = jnp.dot(act_ref[...], w_ref[1], preferred_element_type=F32)
    sig = jax.nn.sigmoid(gate)
    grad = hgrad_ref[...]
    hidden_ref[...] = (gate * sig * up).astype(BF)
    gate_ref[...] = (grad * up * sig * (1.0 + gate * (1.0 - sig))).astype(BF)
    up_ref[...] = (grad * gate * sig).astype(BF)
    pl.when(pl.program_id(0) == pl.num_programs(0) - 1)(side.wait)


def gate_matmul(act, w_j, hidden_grad, act_one, m, pieces):
    rows, width = hidden_grad.shape
    tile = min(256, width)
    block = pl.BlockSpec((rows, tile), lambda i: (0, i))
    return pl.pallas_call(
        functools.partial(gate_kernel, m, pieces),
        grid=(width // tile,),
        out_shape=[jax.ShapeDtypeStruct((rows, width), BF)] * 3
        + [jax.ShapeDtypeStruct((m, rows, LANE), BF)],
        in_specs=[
            pl.BlockSpec((rows, D), lambda i: (0, 0)),
            pl.BlockSpec((2, D, tile), lambda i: (0, 0, i)),
            block,
            hb(),
        ],
        out_specs=[block] * 3 + [hb()],
        scratch_shapes=[sems(m - 1), sems(m - 1), pltpu.SemaphoreType.DMA],
        compiler_params=pltpu.CompilerParams(
            collective_id=12, has_side_effects=True, vmem_limit_bytes=48 << 20
        ),
    )(act, w_j, hidden_grad, act_one)


def back_kernel(g_ref, w_ref, out_ref):
    total = None
    for j in range(g_ref.shape[0]):
        term = lax.dot_general(g_ref[j], w_ref[j], COLS, preferred_element_type=F32)
        total = term if total is None else total + term
    out_ref[...] = total.astype(BF)


def back_matmul(grads, w_j):
    parts, rows, inner = grads.shape
    tile = 512
    return pl.pallas_call(
        back_kernel,
        grid=(D // tile,),
        out_shape=jax.ShapeDtypeStruct((rows, D), BF),
        in_specs=[
            pl.BlockSpec((parts, rows, inner), lambda i: (0, 0, 0)),
            pl.BlockSpec((parts, tile, inner), lambda i: (0, i, 0)),
        ],
        out_specs=pl.BlockSpec((rows, tile), lambda i: (0, i)),
        compiler_params=pltpu.CompilerParams(vmem_limit_bytes=40 << 20),
        cost_estimate=pl.CostEstimate(
            flops=rows * D * parts * inner * 100 // 500,
            bytes_accessed=800_000,
            transcendentals=0,
        ),
    )(grads, w_j)


def vm():
    return pl.BlockSpec(memory_space=pltpu.VMEM)


def hb():
    return pl.BlockSpec(memory_space=pltpu.HBM)


def sems(*shape):
    return pltpu.SemaphoreType.DMA(shape)


def call(kernel, ident, outs, scratch, args, micros=30):
    shapes = [jax.ShapeDtypeStruct(o[0], o[1]) for o in outs]
    return list(pl.pallas_call(
        kernel,
        out_shape=shapes,
        in_specs=[hb() if a[1] else vm() for a in args],
        out_specs=[hb() if len(o) > 2 else vm() for o in outs],
        scratch_shapes=scratch,
        compiler_params=pltpu.CompilerParams(
            collective_id=ident, has_side_effects=True, vmem_limit_bytes=56 << 20
        ),
        cost_estimate=pl.CostEstimate(
            flops=micros * 100_000_000, bytes_accessed=800_000, transcendentals=0
        ),
    )(*[a[0] for a in args]))


def join_kernel(one, two, three, out_ref):
    total = one[...].astype(F32) + two[...].astype(F32) + three[...].astype(F32)
    out_ref[...] = jnp.swapaxes(total, 0, 1)


def join(one, two, three):
    _, rows, width = one.shape
    size = 64
    block = pl.BlockSpec((2, size, width), lambda i: (0, i, 0))
    return pl.pallas_call(
        join_kernel,
        grid=(rows // size,),
        out_shape=jax.ShapeDtypeStruct((rows, 2, width), F32),
        in_specs=[block] * 3,
        out_specs=pl.BlockSpec((size, 2, width), lambda i: (i, 0, 0)),
        compiler_params=pltpu.CompilerParams(vmem_limit_bytes=32 << 20),
    )(one, two, three)


class LineReduce:
    def __init__(self, part, right, left, m):
        self.part, self.line, self.t = part, m // 2, 2
        self.z = lax.axis_index("dp") // 2
        self.right = jnp.where(self.z >= 1, right.astype(F32), 0.0)
        self.left = jnp.where(self.z <= self.line - 2, left.astype(F32), 0.0)

    def take(self, i):
        i = jnp.clip(i, 0, self.line - 1)
        return lax.dynamic_index_in_dim(self.part, i, 0, keepdims=False).astype(F32)

    def step(self, after):
        line, t = self.line, self.t
        right = (self.take(self.z + line - t) + self.right).astype(BF)
        left = (self.take(self.z - line + t) + self.left).astype(BF)
        right, left = lax.optimization_barrier((right, left) + tuple(after))[:2]
        self.given = right, left
        self.right = lax.ppermute(
            right, "dp", [(2 * i + c, 2 * i + 2 + c) for i in range(t) for c in range(2)]
        ).astype(F32)
        self.left = lax.ppermute(
            left, "dp",
            [(2 * i + c, 2 * i - 2 + c) for i in range(line - t, line) for c in range(2)],
        ).astype(F32)
        self.t += 1

    def finish(self, after):
        while self.t < self.line:
            self.step(after)
        own = lax.dynamic_index_in_dim(self.part, self.z, 0, keepdims=False)
        return join(own, self.right.astype(BF), self.left.astype(BF))


def line_gather(own, m, meanwhile):
    line = m // 2
    right = left = own
    rights, lefts = [], []
    for k in range(1, line):
        right = lax.ppermute(right, "dp", [(i, i + 2) for i in range(2 * (k - 1), m - 2)])
        left = lax.ppermute(left, "dp", [(i, i - 2) for i in range(2, m - 2 * (k - 1))])
        if k in meanwhile and k < line - 1:
            right, left = lax.optimization_barrier((right, left) + meanwhile[k](right, left))[:2]
        rights.append(right)
        lefts.append(left)
    return rights, lefts


def local(
    tokens_in, ln1_gain, ln1_bias, w_qkv, w_out, scale_attn, ln2_gain, ln2_bias, w_gu, w_down,
    scale_mlp, out_cotangent, *, n, m,
):
    rows, w = tokens_in.shape
    images = rows // SEQ
    inner = w_qkv.shape[2]
    heads = inner // HD
    hidden_width = w_gu.shape[2]
    scale = HD ** (-0.5)
    line = m // 2
    hops = line - 1
    shard = D // m
    pieces = min(n, shard // LANE)
    cosines, sines = rope_tables()
    cos2 = jnp.tile(jnp.concatenate([cosines, cosines], axis=1), (images, 1))
    sin2 = jnp.tile(jnp.concatenate([-sines, sines], axis=1), (images, 1))
    wide = (rows, n * w)
    own = (rows, w)
    lanes = (rows, LANE)
    row = lambda v: v.reshape(1, D)
    V = lambda *a: [(x, False) for x in a]
    H = lambda *a: [(x, True) for x in a]

    w_j = jnp.transpose(w_qkv, (1, 0, 2))

    ahead = w // 4
    act_one, mean_one, inv_one, gu_j, cots = call(
        functools.partial(first_norm_kernel, n), 1,
        [(wide, BF), (lanes, F32), (lanes, F32), ((2, D, hidden_width), BF, True), ((n, rows, ahead), BF)],
        [pltpu.VMEM((n,) + own, BF), pltpu.VMEM(lanes, F32)] + gather_sems(n)
        + [pltpu.VMEM((2, 256, 2, hidden_width), BF), pltpu.VMEM((2, 2, 256, hidden_width), BF),
           sems(2), sems(2)] + gather_sems(n),
        V(tokens_in, row(ln1_gain), row(ln1_bias), out_cotangent[:, :ahead]) + H(w_gu), 50,
    )
    cot_late, act_one = lax.optimization_barrier((out_cotangent[:, ahead:], act_one))
    cot_all = lax.all_gather(cot_late, "tensor", axis=1, tiled=True)
    qkv = qkv_matmul(act_one, w_j, cos2, sin2)
    mixed, attn_part = pl.pallas_call(
        attention_kernel,
        out_shape=[jax.ShapeDtypeStruct((rows, inner), BF), jax.ShapeDtypeStruct(wide, BF)],
        in_specs=[vm()] * 2,
        out_specs=[vm()] * 2,
        compiler_params=pltpu.CompilerParams(vmem_limit_bytes=48 << 20),
    )(qkv, w_out)
    tile = min(512, hidden_width)
    outs = call(
        functools.partial(second_norm_kernel, n, m, pieces), 2,
        [(own, F32), (own, F32), (wide, BF), (lanes, F32), (lanes, F32), ((rows, hidden_width), F32)]
        + [((m, rows, LANE), BF, True)] + [((rows, inner), BF, True)] * (2 * hops),
        scatter_room(n, rows, w)
        + [pltpu.VMEM(own, BF), pltpu.VMEM((n,) + own, BF), pltpu.VMEM(lanes, F32)]
        + gather_sems(n) + [sems(hops, 4)]
        + [sems(m - 1), sems(m - 1), pltpu.SemaphoreType.DMA]
        + [pltpu.VMEM(wide, BF), pltpu.VMEM((2, tile, D), BF), sems(2)],
        V(attn_part, tokens_in, row(scale_attn), row(ln2_gain), row(ln2_bias), row(scale_mlp), cot_all, cots)
        + H(mixed, w_down), 80,
    )
    attn_sum, residual, act_two, mean_two, inv_two, hidden_grad, kcot = outs[:7]
    mixed_right, mixed_left = outs[7:7 + hops], outs[7 + hops:]
    side = lambda k: lax.all_gather(k, "tensor", axis=2, tiled=True)[:, :, :shard]

    hidden, gate_grad, up_grad, kact = gate_matmul(act_two, gu_j, hidden_grad, act_one, m, pieces)
    block = (rows, hidden_width)
    gu_part, hidden_r, hidden_l = call(
        functools.partial(pair_grad_kernel, m), 3,
        [((line, 2, shard, hidden_width), BF, True), (block, BF, True), (block, BF, True)],
        [pltpu.VMEM((line, rows, shard), BF), pltpu.VMEM((line, rows, shard), BF),
         pltpu.VMEM(block, BF), pltpu.VMEM(block, BF), pltpu.VMEM((2, line, shard, rows), BF),
         pltpu.VMEM((2, 2, shard, hidden_width), BF),
         sems(line), sems(line), sems(2), sems(2), sems(line), sems(4), sems(2)],
        H(act_two) + V(gate_grad, up_grad) + H(hidden), 40,
    )
    cut = shard * 15 // 16
    tile = w // 2 if n == 4 else min(512, w)
    outs = call(
        functools.partial(second_back_kernel, n, m), 4,
        [(own, F32), (wide, BF), ((8, w), F32)] + [((2, cut, hidden_width), BF, True)] * 2
        + [(block, BF, True)] * (2 * hops - 2),
        [pltpu.VMEM(wide, BF)] + scatter_room(n, rows, w)
        + [pltpu.VMEM(own, F32), pltpu.VMEM(own, BF),
         pltpu.VMEM(lanes, F32), pltpu.VMEM(lanes, F32), pltpu.VMEM((8, rows), F32),
         pltpu.VMEM((n, 8, rows), F32)] + [sems(n - 1)] * 2 + gather_sems(n)
        + [pltpu.SemaphoreType.DMA, sems(hops - 1, 4), sems(4)]
        + [pltpu.VMEM((2, 2, tile, hidden_width), BF), sems(2)],
        V(gate_grad, up_grad, out_cotangent, residual, attn_sum, mean_two, inv_two, row(ln2_gain), row(scale_attn))
        + H(hidden_r, hidden_l, gu_part, gu_j), 80,
    )
    res_grad, attn_grad, sums_two, gu_right, gu_left = outs[:5]
    hidden_right = [hidden_r] + outs[5:4 + hops]
    hidden_left = [hidden_l] + outs[4 + hops:]
    raw_grad, kattn, gu_right_b, gu_left_b = call(
        functools.partial(attention_back_kernel, m, pieces), 5,
        [((3, rows, inner), BF), ((m, rows, LANE), BF, True)]
        + [((2, shard - cut, hidden_width), BF, True)] * 2,
        [pltpu.VMEM((rows, inner), BF), sems(m - 1), sems(m - 1), pltpu.SemaphoreType.DMA, sems(4)],
        V(attn_grad, w_out, qkv, cos2, sin2) + H(attn_grad, gu_part), 25,
    )
    gu_line = LineReduce(
        gu_part,
        jnp.concatenate([gu_right, gu_right_b], axis=1),
        jnp.concatenate([gu_left, gu_left_b], axis=1),
        m,
    )
    kcot, kact, raw_grad = lax.optimization_barrier((kcot, kact, raw_grad))
    side_cot, side_attn, side_act = side(kcot), side(kattn), side(kact)
    def gathered(ident, mine, rights, lefts, sides, turned, first=0, last=hops):
        parts, _, width = mine.shape
        shape = (parts, width, shard) if turned else (parts, shard, width)
        blocks = []
        for k in range(first, last + 1):
            blocks += [rights[k - 1], lefts[k - 1]] if k else [mine]
        count = len(blocks)
        (out,) = call(
            functools.partial(gathered_grad_kernel, m, turned, first, last), ident, [(shape, F32)],
            [pltpu.VMEM((count, 2) + mine.shape, BF), pltpu.VMEM((count, 2, shard, rows), BF),
             sems(count), sems(count), sems(count)],
            H(*blocks) + V(sides), 30,
        )
        return out

    lead = lambda arrays: [a[None] for a in arrays]
    done = {}

    def after_one(right, left):
        part = back_matmul(raw_grad, w_j)
        done["grad"] = lax.psum_scatter(part, "tensor", scatter_dimension=1, tiled=True)
        return (part,)

    def after_two(right, left):
        gu_line.step((right, left))
        late = lax.optimization_barrier((side_cot, side_attn) + gu_line.given)
        done["attn"] = late[1]
        done["down"] = gathered(
            6, hidden[None], lead(hidden_right), lead(hidden_left), late[0], True
        )[0]
        return ()

    raw_right, raw_left = line_gather(raw_grad, m, {1: after_one, 2: after_two})
    act_one_grad, down_sum = done["grad"], done["down"]
    proj_sum = gathered(7, mixed[None], lead(mixed_right), lead(mixed_left), done["attn"], True)[0]
    branch_part = jnp.dot(hidden, w_down, preferred_element_type=F32).astype(BF)
    qkv_part = gathered(8, raw_grad, raw_right, raw_left, side_act, False, 0, hops - 1)
    gu_sum = gu_line.finish((raw_right[-1], raw_left[-1], down_sum, proj_sum, qkv_part))

    small = jnp.concatenate([jnp.zeros((2, w), F32), sums_two[0:3], jnp.zeros((3, w), F32)], axis=0)
    input_grad, sums, layer_out = call(
        functools.partial(first_back_kernel, n), 9,
        [(own, F32), ((8, w), F32), (own, F32)],
        scatter_room(n, rows, w)
        + [pltpu.VMEM(own, F32),
           pltpu.VMEM(lanes, F32), pltpu.VMEM(lanes, F32), pltpu.VMEM((8, rows), F32),
           pltpu.VMEM((n, 8, rows), F32)] + [sems(n - 1)] * 2,
        V(act_one_grad, tokens_in, mean_one, inv_one, row(ln1_gain), small,
          branch_part, out_cotangent, row(scale_mlp)), 20,
    )
    input_grad = res_grad + input_grad
    layer_out = residual + layer_out
    qkv_sum = qkv_part + gathered(
        10, raw_grad, raw_right, raw_left, side_act, False, hops, hops
    )
    qkv_sum, input_grad, layer_out, sums = lax.optimization_barrier(
        (qkv_sum, input_grad, layer_out, sums)
    )
    (small_sums,) = call(
        functools.partial(small_sums_kernel, n, m), 11, [((8, n * w), F32)],
        [pltpu.VMEM((m, 8, w), F32), pltpu.VMEM((8, w), F32)] + [sems(m - 1)] * 2 + [sems(n - 1)] * 2,
        V(sums), 10,
    )
    return (
        layer_out,
        input_grad,
        small_sums[0],
        small_sums[1],
        jnp.transpose(qkv_sum, (1, 0, 2)),
        proj_sum,
        small_sums[4],
        small_sums[2],
        small_sums[3],
        gu_sum,
        down_sum,
        small_sums[5],
    )


def solution(mesh):
    placed = (
        P("dp", "tensor"),
        P(),
        P(),
        P(None, None, "tensor"),
        P("tensor", None),
        P(),
        P(),
        P(),
        P(None, None, "tensor"),
        P("tensor", None),
        P(),
        P("dp", "tensor"),
    )
    return jax.shard_map(
        functools.partial(local, n=mesh.shape["tensor"], m=mesh.shape["dp"]),
        mesh=mesh,
        in_specs=placed,
        out_specs=(
            P("dp", "tensor"),
            P("dp", "tensor"),
            P(),
            P(),
            P("dp", None, "tensor"),
            P("tensor", "dp"),
            P(),
            P(),
            P(),
            P("dp", None, "tensor"),
            P("tensor", "dp"),
            P(),
        ),
        check_vma=False,
    )
```

```python
import functools
import math

import jax
import jax.numpy as jnp
from jax import lax
from jax.experimental import pallas as pl
from jax.experimental.pallas import tpu as pltpu
from jax.sharding import PartitionSpec as P

D = 4096
HD = 128
GRID = 14
EXTRA = 5
PATCH = 196
SEQ = 201
EPS = 1e-06
LANE = 128
BF = jnp.bfloat16
F32 = jnp.float32
MESH = pl.DeviceIdType.MESH
ROWS = (((0,), (0,)), ((), ()))
COLS = (((1,), (1,)), ((), ()))


def rope_tables():
    quarter = HD // 4
    theta = (
        2.0
        * math.pi
        * jnp.exp(jnp.arange(quarter, dtype=jnp.float32) * (-4.0 * math.log(100.0) / HD))
    )
    places = jnp.arange(PATCH, dtype=jnp.int32)
    row_pos = ((places // GRID).astype(jnp.float32) + 0.5) * (2.0 / GRID) - 1.0
    col_pos = ((places % GRID).astype(jnp.float32) + 0.5) * (2.0 / GRID) - 1.0
    angles = jnp.concatenate(
        [row_pos[:, None] * theta[None, :], col_pos[:, None] * theta[None, :]], axis=1
    )
    angles = jnp.concatenate([jnp.zeros((EXTRA, HD // 2), jnp.float32), angles], axis=0)
    return (jnp.cos(angles), jnp.sin(angles))


def rotate(vectors, cosines, sines):
    halfway = HD // 2
    leading = vectors[..., :halfway]
    trailing = vectors[..., halfway:]
    cos_b = cosines[:, None, :]
    sin_b = sines[:, None, :]
    return jnp.concatenate(
        [leading * cos_b - trailing * sin_b, leading * sin_b + trailing * cos_b], axis=-1
    )


def greet(n, m=1):
    me = lax.axis_index("tensor")
    you = lax.axis_index("dp")
    barrier = pltpu.get_barrier_semaphore()
    for k in range(1, n):
        pl.semaphore_signal(
            barrier, inc=1, device_id={"tensor": lax.rem(me + k, n)}, device_id_type=MESH
        )
    for k in range(1, m):
        pl.semaphore_signal(
            barrier, inc=1, device_id={"dp": lax.rem(you + k, m)}, device_id_type=MESH
        )
    pl.semaphore_wait(barrier, n + m - 2)


def send(src, dst, send_sem, recv_sem, peer):
    return pltpu.make_async_remote_copy(
        src_ref=src,
        dst_ref=dst,
        send_sem=send_sem,
        recv_sem=recv_sem,
        device_id={"tensor": peer},
        device_id_type=MESH,
    )


def send_dp(src, dst, send_sem, recv_sem, peer):
    return pltpu.make_async_remote_copy(
        src_ref=src,
        dst_ref=dst,
        send_sem=send_sem,
        recv_sem=recv_sem,
        device_id={"dp": peer},
        device_id_type=MESH,
    )


class Hop:
    def __init__(self, k, m, right_src, left_src, right_dst, left_dst, sem):
        you = lax.axis_index("dp")
        z, last = you // 2, m // 2 - 1
        right = send_dp(right_src, right_dst, sem.at[0], sem.at[1], lax.rem(you + 2, m))
        left = send_dp(left_src, left_dst, sem.at[2], sem.at[3], lax.rem(you + m - 2, m))
        self.steps = [
            (right, (z >= k - 1) & (z < last), z >= k),
            (left, (z <= last - k + 1) & (z > 0), z <= last - k),
        ]

    def start(self):
        for copy, sends, _ in self.steps:
            pl.when(sends)(copy.start)

    def wait(self):
        for copy, sends, gets in self.steps:
            pl.when(sends)(copy.wait_send)
            pl.when(gets)(copy.wait_recv)


class End:
    def __init__(self, m, part_ref, at, right_dst, left_dst, sem):
        you = lax.axis_index("dp")
        z, last = you // 2, m // 2 - 1
        some = pl.ds(at, right_dst.shape[1])
        right = send_dp(
            part_ref.at[last, :, some], right_dst, sem.at[0], sem.at[1], lax.rem(you + 2, m)
        )
        left = send_dp(
            part_ref.at[0, :, some], left_dst, sem.at[2], sem.at[3], lax.rem(you + m - 2, m)
        )
        self.steps = [(right, z == 0, z == 1), (left, z == last, z == last - 1)]

    start = Hop.start
    wait = Hop.wait


class Exchange:
    def __init__(self, m, pieces, full_ref, out_ref, ssem, rsem, lsem):
        you = lax.axis_index("dp")
        piece = lax.rem(lax.axis_index("tensor"), pieces)
        self.copies = []
        for k in range(m):
            peer = lax.rem(you + k, m)
            cols = pl.ds(pl.multiple_of((peer * pieces + piece) * LANE, LANE), LANE)
            if k:
                copy = send_dp(
                    full_ref.at[:, cols], out_ref.at[you], ssem.at[k - 1], rsem.at[k - 1], peer
                )
            else:
                copy = pltpu.make_async_copy(full_ref.at[:, cols], out_ref.at[you], lsem)
            self.copies.append(copy)

    def start(self):
        for copy in self.copies:
            copy.start()

    def wait(self):
        for copy in self.copies:
            copy.wait()


def chunks(width, body):
    def step(j, carry):
        body(pl.ds(pl.multiple_of(j * LANE, LANE), LANE))
        return carry

    lax.fori_loop(0, width // LANE, step, 0)


def spread(column, rows):
    return jnp.broadcast_to(column, (rows, LANE))


def beside(me):
    return me + 1 - 2 * lax.rem(me, 2), me + 2 - 4 * (me // 2)


class Gather:
    def __init__(self, n, own_ref, dest, ssem, rsem):
        me = lax.axis_index("tensor")
        w = own_ref.shape[1]
        self.square = n == 4
        if self.square:
            x, y = beside(me)
            half = w // 2
            part = lambda i: own_ref.at[:, i * half:(i + 1) * half]
            to = lambda i, src, owner, at, peer: send(
                src, dest(owner, at * half, half), ssem.at[i], rsem.at[i], peer
            )
            self.copies = [
                to(0, part(0), me, 0, x), to(1, part(1), me, 1, y),
                to(2, part(1), me, 1, x), to(3, part(0), me, 0, y),
            ]
            self.passed = [
                to(4, dest(x, 0, half), x, 0, y), to(5, dest(y, half, half), y, 1, x)
            ]
        else:
            self.copies = [
                send(own_ref, dest(me, 0, w), ssem.at[k - 1], rsem.at[k - 1], lax.rem(me + k, n))
                for k in range(1, n)
            ]

    def start(self):
        for copy in self.copies:
            copy.start()

    def relay(self):
        if self.square:
            for copy, passed in zip(self.copies, self.passed):
                copy.wait_recv()
                passed.start()

    def wait(self):
        if self.square:
            for copy in self.copies:
                copy.wait_send()
            for copy in self.copies[2:]:
                copy.wait_recv()
            wait_all(self.passed)
        else:
            wait_all(self.copies)


class Scatter:
    def __init__(self, n, w, part_ref, slots, come, go, ssem, rsem):
        me = lax.axis_index("tensor")
        self.n, self.w, self.part, self.slots, self.come, self.go = n, w, part_ref, slots, come, go
        self.square = n == 4
        cols = lambda owner, at, size: part_ref.at[:, pl.ds(pl.multiple_of(owner * w + at, LANE), size)]
        if self.square:
            x, y = beside(me)
            far = 3 - me
            half = w // 2
            self.half, self.x, self.y = half, x, y
            to = lambda i, src, dst, peer: send(src, dst, ssem.at[i], rsem.at[i], peer)
            low, high = slice(0, half), slice(half, w)
            self.first = [
                to(0, cols(far, 0, half), come.at[0], x), to(1, cols(far, half, half), come.at[1], y)
            ]
            self.second = [
                to(2, cols(x, 0, half), slots.at[0, :, low], x),
                to(3, cols(y, half, half), slots.at[1, :, high], y),
            ]
            self.third = [
                to(4, go.at[0], slots.at[0, :, high], x), to(5, go.at[1], slots.at[1, :, low], y)
            ]
            self.order = [(far, 0), (far, 1), (x, 0), (y, 1), (x, 1), (y, 0), (me, 0), (me, 1)]
        else:
            self.first = [
                send(cols(lax.rem(me + k, n), 0, w), slots.at[k - 1], ssem.at[k - 1], rsem.at[k - 1],
                     lax.rem(me + k, n))
                for k in range(1, n)
            ]
            self.second = self.third = []

    def start(self):
        for copy in self.first + self.second:
            copy.start()

    def relay(self):
        if self.square:
            half = self.half
            for i, (owner, at) in enumerate(((self.x, half), (self.y, 0))):
                self.first[1 - i].wait_recv()

                def add(cols, i=i, owner=owner, at=at):
                    wide = pl.ds(pl.multiple_of(owner * self.w + at + cols.start, LANE), LANE)
                    self.go[i, :, cols] = (
                        self.part[:, wide].astype(F32) + self.come[1 - i, :, cols].astype(F32)
                    ).astype(BF)

                chunks(half, add)
                self.third[i].start()

    def wait(self):
        if self.square:
            for copy in self.first:
                copy.wait_send()
            wait_all(self.second + self.third)
        else:
            wait_all(self.first)

    def total(self, cols, wide):
        total = self.part[:, wide].astype(F32)
        for k in range(self.slots.shape[0]):
            total = total + self.slots[k, :, cols].astype(F32)
        return total


def scatter_room(n, rows, w):
    count, half = (2, w // 2) if n == 4 else (n - 1, LANE)
    return [
        pltpu.VMEM((count, rows, w), BF), pltpu.VMEM((2, rows, half), BF), pltpu.VMEM((2, rows, half), BF),
        sems(6 if n == 4 else n - 1), sems(6 if n == 4 else n - 1),
    ]


def gather_sems(n):
    return [sems(6 if n == 4 else n - 1)] * 2


def stream(count, fetch, compute):
    fetch(0, 0).start()

    def step(i, carry):
        slot = lax.rem(i, 2)

        @pl.when(i + 1 < count)
        def _():
            fetch(i + 1, 1 - slot).start()

        fetch(i, slot).wait()
        compute(i, slot)
        return carry

    lax.fori_loop(0, count, step, 0)


def wait_all(copies):
    for copy in copies:
        copy.wait()


def row_stats(n, rows, w, all_ref, acc, mean_ref, inv_ref):
    acc[...] = jnp.zeros_like(acc)

    def add(cols):
        total = all_ref[0, :, cols].astype(F32)
        for k in range(1, n):
            total = total + all_ref[k, :, cols].astype(F32)
        acc[...] += total

    chunks(w, add)
    mean_ref[...] = spread(jnp.sum(acc[...], axis=1, keepdims=True) * (1.0 / D), rows)
    acc[...] = jnp.zeros_like(acc)

    def square(cols):
        mean = mean_ref[...]
        total = jnp.zeros_like(mean)
        for k in range(n):
            center = all_ref[k, :, cols].astype(F32) - mean
            total = total + center * center
        acc[...] += total

    chunks(w, square)
    var = jnp.sum(acc[...], axis=1, keepdims=True) * (1.0 / D)
    inv_ref[...] = spread(lax.rsqrt(var + EPS), rows)


def write_act(n, w, all_ref, mean_ref, inv_ref, gain_ref, bias_ref, act_ref):
    def act(cols):
        for k in range(n):
            wide = pl.ds(pl.multiple_of(k * w + cols.start, LANE), LANE)
            center = all_ref[k, :, cols].astype(F32) - mean_ref[...]
            act_ref[:, wide] = (
                center * inv_ref[...] * gain_ref[:, wide] + bias_ref[:, wide]
            ).astype(BF)

    chunks(w, act)


def part_rows(w_ref, out_ref, ibuf, obuf, isem, osem, also):
    size = ibuf.shape[1]
    count = w_ref.shape[0] // size

    def rows_of(i):
        return pl.ds(pl.multiple_of(i * size, size), size)

    def fetch(i, slot):
        return pltpu.make_async_copy(w_ref.at[rows_of(i)], ibuf.at[slot], isem.at[slot])

    def put(i, slot):
        return pltpu.make_async_copy(obuf.at[slot], out_ref.at[:, rows_of(i)], osem.at[slot])

    fetch(0, 0).start()

    def step(i, carry):
        slot = lax.rem(i, 2)
        also(i)

        @pl.when(i + 1 < count)
        def _():
            fetch(i + 1, 1 - slot).start()

        fetch(i, slot).wait()

        @pl.when(i >= 2)
        def _():
            put(i - 2, slot).wait()

        obuf[slot] = jnp.swapaxes(ibuf[slot], 0, 1)
        put(i, slot).start()
        return carry

    lax.fori_loop(0, count, step, 0)
    for i in (count - 2, count - 1):
        put(i, i % 2).wait()


def first_norm_kernel(
    n, x_ref, gain_ref, bias_ref, cot_ref, w_ref, act_ref, mean_ref, inv_ref, parted_ref, cots_ref,
    all_ref, acc, ssem, rsem, ibuf, obuf, isem, osem, csem, crem,
):
    rows, w = x_ref.shape
    me = lax.axis_index("tensor")
    greet(n)
    dest = lambda owner, at, size: all_ref.at[owner, :, pl.ds(at, size)]
    gather = Gather(n, x_ref, dest, ssem, rsem)
    gather.start()
    all_ref[me] = x_ref[...]
    early_ref = cot_ref.at[:, :cots_ref.shape[2]]
    into = lambda owner, at, size: cots_ref.at[owner, :, pl.ds(at, size)]
    early = Gather(n, early_ref, into, csem, crem)

    def between(i):
        @pl.when(i == 6)
        def _():
            gather.relay()
            early.start()

        pl.when(i == 13)(early.relay)

    cots_ref[me] = early_ref[...]
    part_rows(w_ref, parted_ref, ibuf, obuf, isem, osem, between)
    gather.wait()
    row_stats(n, rows, w, all_ref, acc, mean_ref, inv_ref)
    write_act(n, w, all_ref, mean_ref, inv_ref, gain_ref, bias_ref, act_ref)
    early.wait()


def second_norm_kernel(
    n, m, pieces, part_ref, x_ref, scale_ref, gain_ref, bias_ref, mlp_ref, cot_ref, cots_ref, mixed_ref,
    w_down_ref, attn_ref, res_ref, act_ref, mean_ref, inv_ref, hgrad_ref, kcot_ref, *refs,
):
    hops = m // 2 - 1
    rights, lefts, refs = refs[:hops], refs[hops:2 * hops], refs[2 * hops:]
    (slots, come, go, ssem, rsem, own_ref, all_ref, acc, ssem2, rsem2, hsem,
     css, crs, cls, bgrad, wbuf, wsem) = refs
    rows, w = x_ref.shape
    me = lax.axis_index("tensor")
    greet(n, m)
    scatter = Scatter(n, w, part_ref, slots, come, go, ssem, rsem)
    scatter.start()
    line = [
        Hop(k, m, rights[k - 2] if k > 1 else mixed_ref, lefts[k - 2] if k > 1 else mixed_ref,
            rights[k - 1], lefts[k - 1], hsem.at[k - 1])
        for k in range(1, hops + 1)
    ]
    line[0].start()

    ahead = cots_ref.shape[2]
    for owner in range(n):

        def early(cols, owner=owner):
            wide = pl.ds(pl.multiple_of(owner * w + cols.start, LANE), LANE)
            bgrad[:, wide] = (mlp_ref[:, wide] * cots_ref[owner, :, cols].astype(F32)).astype(BF)

        def late(cols, owner=owner):
            wide = pl.ds(pl.multiple_of(owner * w + ahead + cols.start, LANE), LANE)
            from_ = pl.ds(pl.multiple_of(owner * (w - ahead) + cols.start, LANE), LANE)
            bgrad[:, wide] = (mlp_ref[:, wide] * cot_ref[:, from_].astype(F32)).astype(BF)

        chunks(ahead, early)
        chunks(w - ahead, late)
    side = Exchange(m, pieces, bgrad, kcot_ref, css, crs, cls)
    side.start()
    tile = wbuf.shape[1]
    count = hgrad_ref.shape[1] // tile

    def fetch(i, slot):
        return pltpu.make_async_copy(
            w_down_ref.at[pl.ds(pl.multiple_of(i * tile, tile), tile), :], wbuf.at[slot], wsem.at[slot]
        )

    def compute(i, slot):
        hgrad_ref[:, pl.ds(pl.multiple_of(i * tile, tile), tile)] = lax.dot_general(
            bgrad[...], wbuf[slot], COLS, preferred_element_type=F32
        )

        @pl.when(i == count // 2)
        def _():
            scatter.relay()

    stream(count, fetch, compute)
    line[0].wait()
    if hops > 1:
        line[1].start()
    scatter.wait()

    def add(cols):
        wide = pl.ds(pl.multiple_of(me * w + cols.start, LANE), LANE)
        total = scatter.total(cols, wide)
        attn_ref[:, cols] = total
        res = x_ref[:, cols].astype(F32) + scale_ref[:, wide] * total
        res_ref[:, cols] = res
        own_ref[:, cols] = res.astype(BF)

    chunks(w, add)
    dest = lambda owner, at, size: all_ref.at[owner, :, pl.ds(at, size)]
    gather = Gather(n, own_ref, dest, ssem2, rsem2)
    gather.start()
    all_ref[me] = own_ref[...]
    gather.relay()
    for k in range(1, hops - 1):
        line[k].wait()
        line[k + 1].start()
    gather.wait()
    row_stats(n, rows, w, all_ref, acc, mean_ref, inv_ref)
    write_act(n, w, all_ref, mean_ref, inv_ref, gain_ref, bias_ref, act_ref)
    line[-1].wait()
    side.wait()


def norm_back(n, w, load_total, grad_ref, base_ref, mean_ref, inv_ref, gain_ref,
              sums, acc, acc2, stat_own, stats, ssem, rsem, out):
    rows = grad_ref.shape[0]
    me = lax.axis_index("tensor")
    acc[...] = jnp.zeros_like(acc)
    acc2[...] = jnp.zeros_like(acc2)

    def first(cols):
        wide = pl.ds(pl.multiple_of(me * w + cols.start, LANE), LANE)
        total = load_total(cols, wide)
        grad_ref[:, cols] = total
        normed = (base_ref[:, cols].astype(F32) - mean_ref[...]) * inv_ref[...]
        sums[0:1, cols] = jnp.sum(total * normed, axis=0, keepdims=True)
        sums[1:2, cols] = jnp.sum(total, axis=0, keepdims=True)
        scaled = total * gain_ref[:, wide]
        acc[...] += scaled
        acc2[...] += scaled * normed

    chunks(w, first)
    ones = jnp.ones((8, LANE), F32)
    high = lax.Precision.HIGHEST
    plain = lax.dot_general(ones, acc[...], COLS, precision=high, preferred_element_type=F32)
    cross = lax.dot_general(ones, acc2[...], COLS, precision=high, preferred_element_type=F32)
    line = lax.broadcasted_iota(jnp.int32, (8, rows), 0)
    stat_own[...] = jnp.where(line < 4, plain, cross)
    copies = [
        send(stat_own, stats.at[me], ssem.at[k - 1], rsem.at[k - 1], lax.rem(me + k, n))
        for k in range(1, n)
    ]
    for copy in copies:
        copy.start()
    wait_all(copies)
    both = stat_own[...]
    for k in range(1, n):
        both = both + stats[lax.rem(me + k, n)]
    both = both * (1.0 / D)
    pick = lax.broadcasted_iota(jnp.int32, (8, LANE), 0)
    acc[...] = lax.dot_general(
        both, (pick == 0).astype(F32), ROWS, precision=high, preferred_element_type=F32
    )
    acc2[...] = lax.dot_general(
        both, (pick == 4).astype(F32), ROWS, precision=high, preferred_element_type=F32
    )

    def second(cols):
        wide = pl.ds(pl.multiple_of(me * w + cols.start, LANE), LANE)
        normed = (base_ref[:, cols].astype(F32) - mean_ref[...]) * inv_ref[...]
        scaled = grad_ref[:, cols] * gain_ref[:, wide]
        out(cols, wide, inv_ref[...] * (scaled - acc[...] - normed * acc2[...]))

    chunks(w, second)


def second_back_kernel(
    n, m, gate_ref, up_ref, cot_ref, res_ref, attn_ref, mean_ref, inv_ref, gain_ref, scale_ref,
    right_ref, left_ref, gu_ref, w_ref, rgrad_ref, agrad_ref, sums_ref, gu_right, gu_left, *refs,
):
    hops = m // 2 - 1
    rights = (right_ref,) + refs[:hops - 1]
    lefts = (left_ref,) + refs[hops - 1:2 * hops - 2]
    (part_ref, slots, come, go, ssem, rsem, grad_ref, own_ref, acc, acc2, stat_own, stats,
     ssem2, rsem2, ssem3, rsem3, lsem, hsem, gsem, wbuf, wsem) = refs[2 * hops - 2:]
    w = cot_ref.shape[1]
    me = lax.axis_index("tensor")
    greet(n, m)
    line = [
        Hop(k, m, rights[k - 2], lefts[k - 2], rights[k - 1], lefts[k - 1], hsem.at[k - 2])
        for k in range(2, hops + 1)
    ]
    line[0].start()
    first = End(m, gu_ref, 0, gu_right, gu_left, gsem)
    first.start()
    scatter = Scatter(n, w, part_ref, slots, come, go, ssem, rsem)
    tile = wbuf.shape[2]
    count = D // tile

    def spot(i):
        if not scatter.square:
            return pl.ds(pl.multiple_of(i * tile, LANE), tile)
        at = 0
        for k, (owner, half) in enumerate(scatter.order):
            at = at + jnp.where(i == k, owner * w + half * tile, 0)
        return pl.ds(pl.multiple_of(at, LANE), tile)

    def fetch(i, slot):
        return pltpu.make_async_copy(w_ref.at[:, spot(i), :], wbuf.at[slot], wsem.at[slot])

    def compute(i, slot):
        part_ref[:, spot(i)] = (
            lax.dot_general(gate_ref[...], wbuf[slot, 0], COLS, preferred_element_type=F32)
            + lax.dot_general(up_ref[...], wbuf[slot, 1], COLS, preferred_element_type=F32)
        ).astype(BF)
        if scatter.square:
            for k, copy in enumerate(scatter.first + scatter.second):
                pl.when(i == k)(copy.start)
            pl.when(i == 5)(scatter.relay)

    stream(count, fetch, compute)
    if not scatter.square:
        scatter.start()
    scatter.wait()
    sums_ref[...] = jnp.zeros_like(sums_ref)

    def out(cols, wide, back):
        res_grad = cot_ref[:, cols].astype(F32) + back
        rgrad_ref[:, cols] = res_grad
        sums_ref[2:3, cols] = jnp.sum(res_grad * attn_ref[:, cols], axis=0, keepdims=True)
        own_ref[:, cols] = (scale_ref[:, wide] * res_grad).astype(BF)

    norm_back(n, w, scatter.total, grad_ref, res_ref, mean_ref, inv_ref, gain_ref,
              sums_ref, acc, acc2, stat_own, stats, ssem2, rsem2, out)
    dest = lambda owner, at, size: agrad_ref.at[:, pl.ds(pl.multiple_of(owner * w + at, LANE), size)]
    gather = Gather(n, own_ref, dest, ssem3, rsem3)
    gather.start()
    local = pltpu.make_async_copy(own_ref, dest(me, 0, w), lsem)
    local.start()
    gather.relay()
    for k in range(len(line)):
        line[k].wait()
        if k + 1 < len(line):
            line[k + 1].start()
    local.wait()
    gather.wait()
    first.wait()


def first_back_kernel(
    n, grad_in, x_ref, mean_ref, inv_ref, gain_ref, small_ref,
    part_ref, cot_ref, scale_ref,
    igrad_ref, sums, out_ref,
    slots, come, go, ssem, rsem, grad_ref, acc, acc2, stat_own, stats, ssem2, rsem2,
):
    w = x_ref.shape[1]
    greet(n)
    scatter = Scatter(n, w, part_ref, slots, come, go, ssem, rsem)
    scatter.start()
    sums[...] = small_ref[...]
    scatter.relay()

    def load_total(cols, wide):
        return grad_in[:, cols].astype(F32)

    def out(cols, wide, back):
        igrad_ref[:, cols] = back

    norm_back(n, w, load_total, grad_ref, x_ref, mean_ref, inv_ref, gain_ref,
              sums, acc, acc2, stat_own, stats, ssem2, rsem2, out)
    scatter.wait()
    me = lax.axis_index("tensor")

    def add(cols):
        wide = pl.ds(pl.multiple_of(me * w + cols.start, LANE), LANE)
        total = scatter.total(cols, wide)
        out_ref[:, cols] = scale_ref[:, wide] * total
        sums[5:6, cols] = jnp.sum(cot_ref[:, cols].astype(F32) * total, axis=0, keepdims=True)

    chunks(w, add)


def mate_of(you):
    return you + 1 - 2 * lax.rem(you, 2)


def pair_grad_kernel(
    m, act_ref, gate_ref, up_ref, hidden_ref, out_ref, right_ref, left_ref,
    acts, mates, gates, ups, flip, obuf, asem, arem, gsem, grem, lsem, hsem, osem,
):
    line = m // 2
    you = lax.axis_index("dp")
    core, mate = lax.rem(you, 2), mate_of(you)
    width = acts.shape[-1]
    tile = 512
    greet(1, m)
    hop = Hop(1, m, hidden_ref, hidden_ref, right_ref, left_ref, hsem)
    copies = [
        send_dp(gate_ref, gates, gsem.at[0], grem.at[0], mate),
        send_dp(up_ref, ups, gsem.at[1], grem.at[1], mate),
    ]
    locals_ = []
    for k in range(line):
        theirs = pl.ds(pl.multiple_of((2 * k + 1 - core) * width, LANE), width)
        ours = pl.ds(pl.multiple_of((2 * k + core) * width, LANE), width)
        copies.append(send_dp(act_ref.at[:, theirs], mates.at[k], asem.at[k], arem.at[k], mate))
        locals_.append(pltpu.make_async_copy(act_ref.at[:, ours], acts.at[k], lsem.at[k]))
    for copy in locals_ + copies:
        copy.start()
    hop.start()
    for copy in locals_:
        copy.wait()

    def turn(which, source):
        def step(k, carry):
            flip[which, k] = source[k].T
            return carry

        lax.fori_loop(0, line, step, 0)

    turn(0, acts)
    for copy in copies:
        copy.wait()
    turn(1, mates)
    def put(k):
        slot = lax.rem(k, 2)
        return pltpu.make_async_copy(obuf.at[slot], out_ref.at[k], osem.at[slot])

    def chip(k, carry):
        slot = lax.rem(k, 2)

        @pl.when(k >= 2)
        def _():
            put(k - 2).wait()

        for j, (near, far) in enumerate(((gate_ref, gates), (up_ref, ups))):

            def step(i, carry, j=j, near=near, far=far):
                cols = pl.ds(pl.multiple_of(i * tile, tile), tile)
                obuf[slot, j, :, cols] = (
                    jnp.dot(flip[0, k], near[:, cols], preferred_element_type=F32)
                    + jnp.dot(flip[1, k], far[:, cols], preferred_element_type=F32)
                ).astype(BF)
                return carry

            lax.fori_loop(0, gate_ref.shape[1] // tile, step, 0)
        put(k).start()
        return carry

    lax.fori_loop(0, line, chip, 0)
    for k in range(max(line - 2, 0), line):
        put(k).wait()
    hop.wait()


class SmallSums:
    def __init__(self, n, m, sums, out, parts, total, dss, drs, tss, trs):
        self.out, self.sums, self.parts, self.total = out, sums, parts, total
        me, you = lax.axis_index("tensor"), lax.axis_index("dp")
        w = sums.shape[1]
        self.m, self.you = m, you
        self.mine = pl.ds(pl.multiple_of(me * w, w), w)
        self.dp = [
            send_dp(sums, parts.at[you], dss.at[k - 1], drs.at[k - 1], lax.rem(you + k, m))
            for k in range(1, m)
        ]
        self.tensor = [
            send(total, out.at[:, self.mine], tss.at[k - 1], trs.at[k - 1], lax.rem(me + k, n))
            for k in range(1, n)
        ]

    def start(self):
        for copy in self.dp:
            copy.start()

    def finish(self):
        self.parts[self.you] = self.sums[...]
        wait_all(self.dp)
        total = self.parts[0]
        for k in range(1, self.m):
            total = total + self.parts[k]
        self.total[...] = total
        for copy in self.tensor:
            copy.start()
        self.out[:, self.mine] = total
        wait_all(self.tensor)


def small_sums_kernel(n, m, sums, out_ref, parts, total, *room):
    greet(n, m)
    small = SmallSums(n, m, sums, out_ref, parts, total, *room)
    small.start()
    small.finish()


def gathered_grad_kernel(m, turned, first, last, *refs):
    hops = m // 2 - 1
    you = lax.axis_index("dp")
    core, mate, z = lax.rem(you, 2), mate_of(you), you // 2
    todo = []
    refs = list(refs)
    for k in range(first, last + 1):
        if k == 0:
            todo.append((None, refs.pop(0), z))
        else:
            todo.append((z >= k, refs.pop(0), z - k))
            todo.append((z <= hops - k, refs.pop(0), z + k))
    side_ref = refs.pop(0)
    out_ref, blocks, flip, lsem, ssem, rsem = refs
    greet(1, m)
    copies = []
    for at, (cond, src, chip) in enumerate(todo):
        near = pltpu.make_async_copy(src, blocks.at[at, core], lsem.at[at])
        far = send_dp(src, blocks.at[at, core], ssem.at[at], rsem.at[at], mate)
        copies.append((cond, near, far))

    def when(cond, body):
        body() if cond is None else pl.when(cond)(body)

    def go(near, far):
        near.start()
        far.start()

    def done(near, far):
        near.wait()
        far.wait()

    def unit_of(at):
        k = (at + 1) // 2 if first == 0 else first
        right = lax.rem(at, 2) == (1 if first == 0 else 0)
        there = (k == 0) | (right & (z >= k)) | (jnp.logical_not(right) & (z <= hops - k))
        return there, jnp.where(right, z - k, z + k)

    def turn(i, carry):
        at, c = i // 2, lax.rem(i, 2)
        there, chip = unit_of(at)

        @pl.when(there)
        def _():
            flip[at, c] = side_ref[2 * chip + c].T

        return carry

    for cond, near, far in copies:
        when(cond, functools.partial(go, near, far))
    lax.fori_loop(0, 2 * len(todo), turn, 0)
    for cond, near, far in copies:
        when(cond, functools.partial(done, near, far))
    tile = 512
    parts, width = out_ref.shape[0], blocks.shape[-1]
    count = width // tile
    out_ref[...] = jnp.zeros_like(out_ref)

    def unit(i, carry):
        at, j, at_col = i // (parts * count), lax.rem(i // count, parts), lax.rem(i, count)
        there, _ = unit_of(at)

        @pl.when(there)
        def _():
            cols = pl.ds(pl.multiple_of(at_col * tile, tile), tile)
            total = jnp.dot(
                flip[at, 0], blocks[at, 0, j, :, cols], preferred_element_type=F32
            ) + jnp.dot(flip[at, 1], blocks[at, 1, j, :, cols], preferred_element_type=F32)
            if turned:
                out_ref[j, cols, :] += total.T
            else:
                out_ref[j, :, cols] += total

        return carry

    lax.fori_loop(0, len(todo) * parts * count, unit, 0)


def qkv_kernel(act_ref, w_ref, cos_ref, sin_ref, out_ref):
    raw = jnp.dot(act_ref[...], w_ref[...], preferred_element_type=F32)
    part = pl.program_id(0)

    @pl.when(part < 2)
    def _():
        for h in range(raw.shape[1] // HD):
            cols = slice(h * HD, (h + 1) * HD)
            t = raw[:, cols]
            out_ref[:, cols] = (
                t * cos_ref[...] + pltpu.roll(t, HD // 2, 1) * sin_ref[...]
            ).astype(BF)

    @pl.when(part == 2)
    def _():
        out_ref[...] = raw.astype(BF)


def qkv_matmul(act, w_j, cos2, sin2):
    rows = act.shape[0]
    inner = w_j.shape[2]
    tile = min(512, inner)
    return pl.pallas_call(
        qkv_kernel,
        grid=(3, inner // tile),
        out_shape=jax.ShapeDtypeStruct((3, rows, inner), BF),
        in_specs=[
            pl.BlockSpec((rows, D), lambda j, i: (0, 0)),
            pl.BlockSpec((None, D, tile), lambda j, i: (j, 0, i)),
            pl.BlockSpec((rows, HD), lambda j, i: (0, 0)),
            pl.BlockSpec((rows, HD), lambda j, i: (0, 0)),
        ],
        out_specs=pl.BlockSpec((None, rows, tile), lambda j, i: (j, 0, i)),
        compiler_params=pltpu.CompilerParams(vmem_limit_bytes=40 << 20),
        cost_estimate=pl.CostEstimate(
            flops=2 * rows * D * 3 * inner, bytes_accessed=6 * D * inner, transcendentals=0
        ),
    )(act, w_j, cos2, sin2)


def attention_probs(q, k, same):
    scores = lax.dot_general(k, q, COLS, preferred_element_type=F32) * (HD ** (-0.5))
    scores = jnp.where(same, scores, -jnp.inf)
    top = jnp.max(scores, axis=0, keepdims=True)
    weight = jnp.exp(scores - top)
    return weight / jnp.sum(weight, axis=0, keepdims=True)


def same_image(rows):
    one = lax.broadcasted_iota(jnp.int32, (rows, rows), 0)
    two = lax.broadcasted_iota(jnp.int32, (rows, rows), 1)
    image = lambda i: sum((i >= SEQ * k).astype(jnp.int32) for k in range(1, rows // SEQ))
    return image(one) == image(two)


def attention_kernel(qkv_ref, w_hbm, mixed_ref, part_ref, w_ref, wsem):
    rows, inner = mixed_ref.shape
    weights = pltpu.make_async_copy(w_hbm, w_ref, wsem)
    weights.start()

    def head(h, carry):
        cols = pl.ds(pl.multiple_of(h * HD, HD), HD)
        probs = attention_probs(qkv_ref[0, :, cols], qkv_ref[1, :, cols], same_image(rows))
        value = qkv_ref[2, :, cols].astype(F32).T.astype(BF)
        mixed = jnp.dot(value, probs.astype(BF), preferred_element_type=F32)
        mixed_ref[:, cols] = mixed.T.astype(BF)
        return carry

    lax.fori_loop(0, inner // HD, head, 0)
    weights.wait()

    def tile(i, carry):
        cols = pl.ds(pl.multiple_of(i * 512, 512), 512)
        part_ref[:, cols] = jnp.dot(
            mixed_ref[...], w_ref[:, cols], preferred_element_type=F32
        ).astype(BF)
        return carry

    lax.fori_loop(0, D // 512, tile, 0)


def attention_back_kernel(
    m, pieces, agrad_ref, qkv_ref, cos_ref, sin_ref, full_ref, gu_ref, w_ref,
    out_ref, kattn_ref, gu_right, gu_left, mgrad, ass, ars, als, gsem, wbuf, wsem,
):
    rows, inner = mgrad.shape
    greet(1, m)
    rest = End(m, gu_ref, gu_ref.shape[2] - gu_right.shape[1], gu_right, gu_left, gsem)
    rest.start()
    side = Exchange(m, pieces, full_ref, kattn_ref, ass, ars, als)
    side.start()
    step = min(256, inner)

    def fetch(i, slot):
        some = pl.ds(pl.multiple_of(i * step, step), step)
        return pltpu.make_async_copy(w_ref.at[some, :], wbuf.at[slot], wsem.at[slot])

    def tile(i, slot):
        cols = pl.ds(pl.multiple_of(i * step, step), step)
        mgrad[:, cols] = lax.dot_general(
            agrad_ref[...], wbuf[slot], COLS, preferred_element_type=F32
        ).astype(BF)

    stream(inner // step, fetch, tile)

    def back(t):
        return t * cos_ref[...] - pltpu.roll(t, HD // 2, 1) * sin_ref[...]

    def head(h, carry):
        cols = pl.ds(pl.multiple_of(h * HD, HD), HD)
        q, k, v = qkv_ref[0, :, cols], qkv_ref[1, :, cols], qkv_ref[2, :, cols]
        grad = mgrad[:, cols]
        probs = attention_probs(q, k, same_image(rows))
        prob_grad = lax.dot_general(v, grad, COLS, preferred_element_type=F32)
        delta = jnp.sum(probs * prob_grad, axis=0, keepdims=True)
        score_grad = (probs * (prob_grad - delta)).astype(BF)
        scale = HD ** (-0.5)
        flipped = k.astype(F32).T.astype(BF)
        q_grad = jnp.dot(flipped, score_grad, preferred_element_type=F32).T * scale
        k_grad = jnp.dot(score_grad, q, preferred_element_type=F32) * scale
        out_ref[0, :, cols] = back(q_grad).astype(BF)
        out_ref[1, :, cols] = back(k_grad).astype(BF)
        out_ref[2, :, cols] = jnp.dot(
            probs.astype(BF), grad, preferred_element_type=F32
        ).astype(BF)
        return carry

    lax.fori_loop(0, inner // HD, head, 0)
    side.wait()
    rest.wait()


def gate_kernel(
    m, pieces, act_ref, w_ref, hgrad_ref, full_ref, hidden_ref, gate_ref, up_ref, kact_ref, ass, ars, als
):
    side = Exchange(m, pieces, full_ref, kact_ref, ass, ars, als)

    @pl.when(pl.program_id(0) == 0)
    def _():
        greet(1, m)
        side.start()

    gate = jnp.dot(act_ref[...], w_ref[0], preferred_element_type=F32)
    up = jnp.dot(act_ref[...], w_ref[1], preferred_element_type=F32)
    sig = jax.nn.sigmoid(gate)
    grad = hgrad_ref[...]
    hidden_ref[...] = (gate * sig * up).astype(BF)
    gate_ref[...] = (grad * up * sig * (1.0 + gate * (1.0 - sig))).astype(BF)
    up_ref[...] = (grad * gate * sig).astype(BF)
    pl.when(pl.program_id(0) == pl.num_programs(0) - 1)(side.wait)


def gate_matmul(act, w_j, hidden_grad, act_one, m, pieces):
    rows, width = hidden_grad.shape
    tile = min(256, width)
    block = pl.BlockSpec((rows, tile), lambda i: (0, i))
    return pl.pallas_call(
        functools.partial(gate_kernel, m, pieces),
        grid=(width // tile,),
        out_shape=[jax.ShapeDtypeStruct((rows, width), BF)] * 3
        + [jax.ShapeDtypeStruct((m, rows, LANE), BF)],
        in_specs=[
            pl.BlockSpec((rows, D), lambda i: (0, 0)),
            pl.BlockSpec((2, D, tile), lambda i: (0, 0, i)),
            block,
            hb(),
        ],
        out_specs=[block] * 3 + [hb()],
        scratch_shapes=[sems(m - 1), sems(m - 1), pltpu.SemaphoreType.DMA],
        compiler_params=pltpu.CompilerParams(
            collective_id=12, has_side_effects=True, vmem_limit_bytes=48 << 20
        ),
    )(act, w_j, hidden_grad, act_one)


def back_kernel(g_ref, w_ref, out_ref):
    total = None
    for j in range(g_ref.shape[0]):
        term = lax.dot_general(g_ref[j], w_ref[j], COLS, preferred_element_type=F32)
        total = term if total is None else total + term
    out_ref[...] = total.astype(BF)


def back_matmul(grads, w_j):
    parts, rows, inner = grads.shape
    tile = 512
    return pl.pallas_call(
        back_kernel,
        grid=(D // tile,),
        out_shape=jax.ShapeDtypeStruct((rows, D), BF),
        in_specs=[
            pl.BlockSpec((parts, rows, inner), lambda i: (0, 0, 0)),
            pl.BlockSpec((parts, tile, inner), lambda i: (0, i, 0)),
        ],
        out_specs=pl.BlockSpec((rows, tile), lambda i: (0, i)),
        compiler_params=pltpu.CompilerParams(vmem_limit_bytes=40 << 20),
        cost_estimate=pl.CostEstimate(
            flops=rows * D * parts * inner * 100 // 500,
            bytes_accessed=800_000,
            transcendentals=0,
        ),
    )(grads, w_j)


def vm():
    return pl.BlockSpec(memory_space=pltpu.VMEM)


def hb():
    return pl.BlockSpec(memory_space=pltpu.HBM)


def sems(*shape):
    return pltpu.SemaphoreType.DMA(shape)


def call(kernel, ident, outs, scratch, args, micros=30):
    shapes = [jax.ShapeDtypeStruct(o[0], o[1]) for o in outs]
    return list(pl.pallas_call(
        kernel,
        out_shape=shapes,
        in_specs=[hb() if a[1] else vm() for a in args],
        out_specs=[hb() if len(o) > 2 else vm() for o in outs],
        scratch_shapes=scratch,
        compiler_params=pltpu.CompilerParams(
            collective_id=ident, has_side_effects=True, vmem_limit_bytes=56 << 20
        ),
        cost_estimate=pl.CostEstimate(
            flops=micros * 100_000_000, bytes_accessed=800_000, transcendentals=0
        ),
    )(*[a[0] for a in args]))


def join_kernel(one, two, three, out_ref):
    total = one[...].astype(F32) + two[...].astype(F32) + three[...].astype(F32)
    out_ref[...] = jnp.swapaxes(total, 0, 1)


def join(one, two, three):
    _, rows, width = one.shape
    size = 64
    block = pl.BlockSpec((2, size, width), lambda i: (0, i, 0))
    return pl.pallas_call(
        join_kernel,
        grid=(rows // size,),
        out_shape=jax.ShapeDtypeStruct((rows, 2, width), F32),
        in_specs=[block] * 3,
        out_specs=pl.BlockSpec((size, 2, width), lambda i: (i, 0, 0)),
        compiler_params=pltpu.CompilerParams(vmem_limit_bytes=32 << 20),
    )(one, two, three)


class LineReduce:
    def __init__(self, part, right, left, m):
        self.part, self.line, self.t = part, m // 2, 2
        self.z = lax.axis_index("dp") // 2
        self.right = jnp.where(self.z >= 1, right.astype(F32), 0.0)
        self.left = jnp.where(self.z <= self.line - 2, left.astype(F32), 0.0)

    def take(self, i):
        i = jnp.clip(i, 0, self.line - 1)
        return lax.dynamic_index_in_dim(self.part, i, 0, keepdims=False).astype(F32)

    def step(self, after):
        line, t = self.line, self.t
        right = (self.take(self.z + line - t) + self.right).astype(BF)
        left = (self.take(self.z - line + t) + self.left).astype(BF)
        right, left = lax.optimization_barrier((right, left) + tuple(after))[:2]
        self.given = right, left
        self.right = lax.ppermute(
            right, "dp", [(2 * i + c, 2 * i + 2 + c) for i in range(t) for c in range(2)]
        ).astype(F32)
        self.left = lax.ppermute(
            left, "dp",
            [(2 * i + c, 2 * i - 2 + c) for i in range(line - t, line) for c in range(2)],
        ).astype(F32)
        self.t += 1

    def finish(self, after):
        while self.t < self.line:
            self.step(after)
        own = lax.dynamic_index_in_dim(self.part, self.z, 0, keepdims=False)
        return join(own, self.right.astype(BF), self.left.astype(BF))


def line_gather(own, m, meanwhile):
    line = m // 2
    right = left = own
    rights, lefts = [], []
    for k in range(1, line):
        right = lax.ppermute(right, "dp", [(i, i + 2) for i in range(2 * (k - 1), m - 2)])
        left = lax.ppermute(left, "dp", [(i, i - 2) for i in range(2, m - 2 * (k - 1))])
        if k in meanwhile and k < line - 1:
            right, left = lax.optimization_barrier((right, left) + meanwhile[k](right, left))[:2]
        rights.append(right)
        lefts.append(left)
    return rights, lefts


def local(
    tokens_in, ln1_gain, ln1_bias, w_qkv, w_out, scale_attn, ln2_gain, ln2_bias, w_gu, w_down,
    scale_mlp, out_cotangent, *, n, m,
):
    rows, w = tokens_in.shape
    images = rows // SEQ
    inner = w_qkv.shape[2]
    heads = inner // HD
    hidden_width = w_gu.shape[2]
    scale = HD ** (-0.5)
    line = m // 2
    hops = line - 1
    shard = D // m
    pieces = min(n, shard // LANE)
    cosines, sines = rope_tables()
    cos2 = jnp.tile(jnp.concatenate([cosines, cosines], axis=1), (images, 1))
    sin2 = jnp.tile(jnp.concatenate([-sines, sines], axis=1), (images, 1))
    wide = (rows, n * w)
    own = (rows, w)
    lanes = (rows, LANE)
    row = lambda v: v.reshape(1, D)
    V = lambda *a: [(x, False) for x in a]
    H = lambda *a: [(x, True) for x in a]

    w_j = jnp.transpose(w_qkv, (1, 0, 2))

    ahead = w // 4
    act_one, mean_one, inv_one, gu_j, cots = call(
        functools.partial(first_norm_kernel, n), 1,
        [(wide, BF), (lanes, F32), (lanes, F32), ((2, D, hidden_width), BF, True), ((n, rows, ahead), BF)],
        [pltpu.VMEM((n,) + own, BF), pltpu.VMEM(lanes, F32)] + gather_sems(n)
        + [pltpu.VMEM((2, 256, 2, hidden_width), BF), pltpu.VMEM((2, 2, 256, hidden_width), BF),
           sems(2), sems(2)] + gather_sems(n),
        V(tokens_in, row(ln1_gain), row(ln1_bias), out_cotangent) + H(w_gu), 50,
    )
    cot_late, act_one = lax.optimization_barrier((out_cotangent[:, ahead:], act_one))
    cot_all = lax.all_gather(cot_late, "tensor", axis=1, tiled=True)
    qkv = qkv_matmul(act_one, w_j, cos2, sin2)
    mixed, attn_part = pl.pallas_call(
        attention_kernel,
        out_shape=[jax.ShapeDtypeStruct((rows, inner), BF), jax.ShapeDtypeStruct(wide, BF)],
        in_specs=[vm(), hb()],
        out_specs=[vm()] * 2,
        scratch_shapes=[pltpu.VMEM(w_out.shape, BF), pltpu.SemaphoreType.DMA],
        compiler_params=pltpu.CompilerParams(vmem_limit_bytes=48 << 20),
    )(qkv, w_out)
    tile = min(512, hidden_width)
    outs = call(
        functools.partial(second_norm_kernel, n, m, pieces), 2,
        [(own, F32), (own, F32), (wide, BF), (lanes, F32), (lanes, F32), ((rows, hidden_width), F32)]
        + [((m, rows, LANE), BF, True)] + [((rows, inner), BF, True)] * (2 * hops),
        scatter_room(n, rows, w)
        + [pltpu.VMEM(own, BF), pltpu.VMEM((n,) + own, BF), pltpu.VMEM(lanes, F32)]
        + gather_sems(n) + [sems(hops, 4)]
        + [sems(m - 1), sems(m - 1), pltpu.SemaphoreType.DMA]
        + [pltpu.VMEM(wide, BF), pltpu.VMEM((2, tile, D), BF), sems(2)],
        V(attn_part, tokens_in, row(scale_attn), row(ln2_gain), row(ln2_bias), row(scale_mlp), cot_all, cots)
        + H(mixed, w_down), 80,
    )
    attn_sum, residual, act_two, mean_two, inv_two, hidden_grad, kcot = outs[:7]
    mixed_right, mixed_left = outs[7:7 + hops], outs[7 + hops:]
    side = lambda k: lax.all_gather(k, "tensor", axis=2, tiled=True)[:, :, :shard]

    hidden, gate_grad, up_grad, kact = gate_matmul(act_two, gu_j, hidden_grad, act_one, m, pieces)
    block = (rows, hidden_width)
    gu_part, hidden_r, hidden_l = call(
        functools.partial(pair_grad_kernel, m), 3,
        [((line, 2, shard, hidden_width), BF, True), (block, BF, True), (block, BF, True)],
        [pltpu.VMEM((line, rows, shard), BF), pltpu.VMEM((line, rows, shard), BF),
         pltpu.VMEM(block, BF), pltpu.VMEM(block, BF), pltpu.VMEM((2, line, shard, rows), BF),
         pltpu.VMEM((2, 2, shard, hidden_width), BF),
         sems(line), sems(line), sems(2), sems(2), sems(line), sems(4), sems(2)],
        H(act_two) + V(gate_grad, up_grad) + H(hidden), 40,
    )
    cut = shard * 15 // 16
    tile = w // 2 if n == 4 else min(512, w)
    outs = call(
        functools.partial(second_back_kernel, n, m), 4,
        [(own, F32), (wide, BF), ((8, w), F32)] + [((2, cut, hidden_width), BF, True)] * 2
        + [(block, BF, True)] * (2 * hops - 2),
        [pltpu.VMEM(wide, BF)] + scatter_room(n, rows, w)
        + [pltpu.VMEM(own, F32), pltpu.VMEM(own, BF),
         pltpu.VMEM(lanes, F32), pltpu.VMEM(lanes, F32), pltpu.VMEM((8, rows), F32),
         pltpu.VMEM((n, 8, rows), F32)] + [sems(n - 1)] * 2 + gather_sems(n)
        + [pltpu.SemaphoreType.DMA, sems(hops - 1, 4), sems(4)]
        + [pltpu.VMEM((2, 2, tile, hidden_width), BF), sems(2)],
        V(gate_grad, up_grad, out_cotangent, residual, attn_sum, mean_two, inv_two, row(ln2_gain), row(scale_attn))
        + H(hidden_r, hidden_l, gu_part, gu_j), 80,
    )
    res_grad, attn_grad, sums_two, gu_right, gu_left = outs[:5]
    hidden_right = [hidden_r] + outs[5:4 + hops]
    hidden_left = [hidden_l] + outs[4 + hops:]
    raw_grad, kattn, gu_right_b, gu_left_b = call(
        functools.partial(attention_back_kernel, m, pieces), 5,
        [((3, rows, inner), BF), ((m, rows, LANE), BF, True)]
        + [((2, shard - cut, hidden_width), BF, True)] * 2,
        [pltpu.VMEM((rows, inner), BF), sems(m - 1), sems(m - 1), pltpu.SemaphoreType.DMA, sems(4),
         pltpu.VMEM((2, min(256, inner), D), BF), sems(2)],
        V(attn_grad, qkv, cos2, sin2) + H(attn_grad, gu_part, w_out), 25,
    )
    gu_line = LineReduce(
        gu_part,
        jnp.concatenate([gu_right, gu_right_b], axis=1),
        jnp.concatenate([gu_left, gu_left_b], axis=1),
        m,
    )
    kcot, kact, raw_grad = lax.optimization_barrier((kcot, kact, raw_grad))
    side_cot, side_attn, side_act = side(kcot), side(kattn), side(kact)
    def gathered(ident, mine, rights, lefts, sides, turned, first=0, last=hops):
        parts, _, width = mine.shape
        shape = (parts, width, shard) if turned else (parts, shard, width)
        blocks = []
        for k in range(first, last + 1):
            blocks += [rights[k - 1], lefts[k - 1]] if k else [mine]
        count = len(blocks)
        (out,) = call(
            functools.partial(gathered_grad_kernel, m, turned, first, last), ident, [(shape, F32)],
            [pltpu.VMEM((count, 2) + mine.shape, BF), pltpu.VMEM((count, 2, shard, rows), BF),
             sems(count), sems(count), sems(count)],
            H(*blocks) + V(sides), 30,
        )
        return out

    lead = lambda arrays: [a[None] for a in arrays]
    done = {}

    def after_one(right, left):
        part = back_matmul(raw_grad, w_j)
        done["grad"] = lax.psum_scatter(part, "tensor", scatter_dimension=1, tiled=True)
        done["attn"], done["hidden"] = lax.optimization_barrier(
            (side_attn, hidden, part, right, left)
        )[:2]
        return (part,)

    def after_two(right, left):
        done["proj"] = gathered(
            7, mixed[None], lead(mixed_right), lead(mixed_left), done["attn"], True
        )[0]
        done["part"] = jnp.dot(done["hidden"], w_down, preferred_element_type=F32).astype(BF)
        gu_line.step((right, left, done["proj"], done["part"]))
        late = lax.optimization_barrier((side_cot,) + gu_line.given)
        done["down"] = gathered(
            6, hidden[None], lead(hidden_right), lead(hidden_left), late[0], True
        )[0]
        return ()

    raw_right, raw_left = line_gather(raw_grad, m, {1: after_one, 2: after_two})
    act_one_grad, down_sum = done["grad"], done["down"]
    proj_sum = done["proj"]
    branch_part = done["part"]
    qkv_part = gathered(8, raw_grad, raw_right, raw_left, side_act, False, 0, hops - 1)
    gu_sum = gu_line.finish((raw_right[-1], raw_left[-1], down_sum, proj_sum, qkv_part))

    small = jnp.concatenate([jnp.zeros((2, w), F32), sums_two[0:3], jnp.zeros((3, w), F32)], axis=0)
    input_grad, sums, layer_out = call(
        functools.partial(first_back_kernel, n), 9,
        [(own, F32), ((8, w), F32), (own, F32)],
        scatter_room(n, rows, w)
        + [pltpu.VMEM(own, F32),
           pltpu.VMEM(lanes, F32), pltpu.VMEM(lanes, F32), pltpu.VMEM((8, rows), F32),
           pltpu.VMEM((n, 8, rows), F32)] + [sems(n - 1)] * 2,
        V(act_one_grad, tokens_in, mean_one, inv_one, row(ln1_gain), small,
          branch_part, out_cotangent, row(scale_mlp)), 20,
    )
    input_grad = res_grad + input_grad
    layer_out = residual + layer_out
    qkv_sum = qkv_part + gathered(
        10, raw_grad, raw_right, raw_left, side_act, False, hops, hops
    )
    qkv_sum, input_grad, layer_out, sums = lax.optimization_barrier(
        (qkv_sum, input_grad, layer_out, sums)
    )
    (small_sums,) = call(
        functools.partial(small_sums_kernel, n, m), 11, [((8, n * w), F32)],
        [pltpu.VMEM((m, 8, w), F32), pltpu.VMEM((8, w), F32)] + [sems(m - 1)] * 2 + [sems(n - 1)] * 2,
        V(sums), 10,
    )
    return (
        layer_out,
        input_grad,
        small_sums[0],
        small_sums[1],
        jnp.transpose(qkv_sum, (1, 0, 2)),
        proj_sum,
        small_sums[4],
        small_sums[2],
        small_sums[3],
        gu_sum,
        down_sum,
        small_sums[5],
    )


def solution(mesh):
    placed = (
        P("dp", "tensor"),
        P(),
        P(),
        P(None, None, "tensor"),
        P("tensor", None),
        P(),
        P(),
        P(),
        P(None, None, "tensor"),
        P("tensor", None),
        P(),
        P("dp", "tensor"),
    )
    return jax.shard_map(
        functools.partial(local, n=mesh.shape["tensor"], m=mesh.shape["dp"]),
        mesh=mesh,
        in_specs=placed,
        out_specs=(
            P("dp", "tensor"),
            P("dp", "tensor"),
            P(),
            P(),
            P("dp", None, "tensor"),
            P("tensor", "dp"),
            P(),
            P(),
            P(),
            P("dp", None, "tensor"),
            P("tensor", "dp"),
            P(),
        ),
        check_vma=False,
    )
```

```python
import functools
import math

import jax
import jax.numpy as jnp
from jax import lax
from jax.experimental import pallas as pl
from jax.experimental.pallas import tpu as pltpu
from jax.sharding import PartitionSpec as P

D = 4096
HD = 128
GRID = 14
EXTRA = 5
PATCH = 196
SEQ = 201
EPS = 1e-06
LANE = 128
BF = jnp.bfloat16
F32 = jnp.float32
MESH = pl.DeviceIdType.MESH
ROWS = (((0,), (0,)), ((), ()))
COLS = (((1,), (1,)), ((), ()))


def rope_tables():
    quarter = HD // 4
    theta = (
        2.0
        * math.pi
        * jnp.exp(jnp.arange(quarter, dtype=jnp.float32) * (-4.0 * math.log(100.0) / HD))
    )
    places = jnp.arange(PATCH, dtype=jnp.int32)
    row_pos = ((places // GRID).astype(jnp.float32) + 0.5) * (2.0 / GRID) - 1.0
    col_pos = ((places % GRID).astype(jnp.float32) + 0.5) * (2.0 / GRID) - 1.0
    angles = jnp.concatenate(
        [row_pos[:, None] * theta[None, :], col_pos[:, None] * theta[None, :]], axis=1
    )
    angles = jnp.concatenate([jnp.zeros((EXTRA, HD // 2), jnp.float32), angles], axis=0)
    return (jnp.cos(angles), jnp.sin(angles))


def rotate(vectors, cosines, sines):
    halfway = HD // 2
    leading = vectors[..., :halfway]
    trailing = vectors[..., halfway:]
    cos_b = cosines[:, None, :]
    sin_b = sines[:, None, :]
    return jnp.concatenate(
        [leading * cos_b - trailing * sin_b, leading * sin_b + trailing * cos_b], axis=-1
    )


def greet(n, m=1):
    me = lax.axis_index("tensor")
    you = lax.axis_index("dp")
    barrier = pltpu.get_barrier_semaphore()
    for k in range(1, n):
        pl.semaphore_signal(
            barrier, inc=1, device_id={"tensor": lax.rem(me + k, n)}, device_id_type=MESH
        )
    for k in range(1, m):
        pl.semaphore_signal(
            barrier, inc=1, device_id={"dp": lax.rem(you + k, m)}, device_id_type=MESH
        )
    pl.semaphore_wait(barrier, n + m - 2)


def send(src, dst, send_sem, recv_sem, peer):
    return pltpu.make_async_remote_copy(
        src_ref=src,
        dst_ref=dst,
        send_sem=send_sem,
        recv_sem=recv_sem,
        device_id={"tensor": peer},
        device_id_type=MESH,
    )


def send_dp(src, dst, send_sem, recv_sem, peer):
    return pltpu.make_async_remote_copy(
        src_ref=src,
        dst_ref=dst,
        send_sem=send_sem,
        recv_sem=recv_sem,
        device_id={"dp": peer},
        device_id_type=MESH,
    )


class Hop:
    def __init__(self, k, m, right_src, left_src, right_dst, left_dst, sem):
        you = lax.axis_index("dp")
        z, last = you // 2, m // 2 - 1
        right = send_dp(right_src, right_dst, sem.at[0], sem.at[1], lax.rem(you + 2, m))
        left = send_dp(left_src, left_dst, sem.at[2], sem.at[3], lax.rem(you + m - 2, m))
        self.steps = [
            (right, (z >= k - 1) & (z < last), z >= k),
            (left, (z <= last - k + 1) & (z > 0), z <= last - k),
        ]

    def start(self):
        for copy, sends, _ in self.steps:
            pl.when(sends)(copy.start)

    def wait(self):
        for copy, sends, gets in self.steps:
            pl.when(sends)(copy.wait_send)
            pl.when(gets)(copy.wait_recv)


class End:
    def __init__(self, m, part_ref, at, right_dst, left_dst, sem):
        you = lax.axis_index("dp")
        z, last = you // 2, m // 2 - 1
        some = pl.ds(at, right_dst.shape[1])
        right = send_dp(
            part_ref.at[last, :, some], right_dst, sem.at[0], sem.at[1], lax.rem(you + 2, m)
        )
        left = send_dp(
            part_ref.at[0, :, some], left_dst, sem.at[2], sem.at[3], lax.rem(you + m - 2, m)
        )
        self.steps = [(right, z == 0, z == 1), (left, z == last, z == last - 1)]

    start = Hop.start
    wait = Hop.wait


class Exchange:
    def __init__(self, m, pieces, full_ref, out_ref, ssem, rsem, lsem):
        you = lax.axis_index("dp")
        piece = lax.rem(lax.axis_index("tensor"), pieces)
        self.copies = []
        for k in range(m):
            peer = lax.rem(you + k, m)
            cols = pl.ds(pl.multiple_of((peer * pieces + piece) * LANE, LANE), LANE)
            if k:
                copy = send_dp(
                    full_ref.at[:, cols], out_ref.at[you], ssem.at[k - 1], rsem.at[k - 1], peer
                )
            else:
                copy = pltpu.make_async_copy(full_ref.at[:, cols], out_ref.at[you], lsem)
            self.copies.append(copy)

    def start(self):
        for copy in self.copies:
            copy.start()

    def wait(self):
        for copy in self.copies:
            copy.wait()


def chunks(width, body):
    def step(j, carry):
        body(pl.ds(pl.multiple_of(j * LANE, LANE), LANE))
        return carry

    lax.fori_loop(0, width // LANE, step, 0)


def spread(column, rows):
    return jnp.broadcast_to(column, (rows, LANE))


def beside(me):
    return me + 1 - 2 * lax.rem(me, 2), me + 2 - 4 * (me // 2)


class Gather:
    def __init__(self, n, own_ref, dest, ssem, rsem):
        me = lax.axis_index("tensor")
        w = own_ref.shape[1]
        self.square = n == 4
        if self.square:
            x, y = beside(me)
            half = w // 2
            part = lambda i: own_ref.at[:, i * half:(i + 1) * half]
            to = lambda i, src, owner, at, peer: send(
                src, dest(owner, at * half, half), ssem.at[i], rsem.at[i], peer
            )
            self.copies = [
                to(0, part(0), me, 0, x), to(1, part(1), me, 1, y),
                to(2, part(1), me, 1, x), to(3, part(0), me, 0, y),
            ]
            self.passed = [
                to(4, dest(x, 0, half), x, 0, y), to(5, dest(y, half, half), y, 1, x)
            ]
        else:
            self.copies = [
                send(own_ref, dest(me, 0, w), ssem.at[k - 1], rsem.at[k - 1], lax.rem(me + k, n))
                for k in range(1, n)
            ]

    def start(self):
        for copy in self.copies:
            copy.start()

    def relay(self):
        if self.square:
            for copy, passed in zip(self.copies, self.passed):
                copy.wait_recv()
                passed.start()

    def wait(self):
        if self.square:
            for copy in self.copies:
                copy.wait_send()
            for copy in self.copies[2:]:
                copy.wait_recv()
            wait_all(self.passed)
        else:
            wait_all(self.copies)


class Scatter:
    def __init__(self, n, w, part_ref, slots, come, go, ssem, rsem):
        me = lax.axis_index("tensor")
        self.n, self.w, self.part, self.slots, self.come, self.go = n, w, part_ref, slots, come, go
        self.square = n == 4
        cols = lambda owner, at, size: part_ref.at[:, pl.ds(pl.multiple_of(owner * w + at, LANE), size)]
        if self.square:
            x, y = beside(me)
            far = 3 - me
            half = w // 2
            self.half, self.x, self.y = half, x, y
            to = lambda i, src, dst, peer: send(src, dst, ssem.at[i], rsem.at[i], peer)
            low, high = slice(0, half), slice(half, w)
            self.first = [
                to(0, cols(far, 0, half), come.at[0], x), to(1, cols(far, half, half), come.at[1], y)
            ]
            self.second = [
                to(2, cols(x, 0, half), slots.at[0, :, low], x),
                to(3, cols(y, half, half), slots.at[1, :, high], y),
            ]
            self.third = [
                to(4, go.at[0], slots.at[0, :, high], x), to(5, go.at[1], slots.at[1, :, low], y)
            ]
            self.order = [(far, 0), (far, 1), (x, 0), (y, 1), (x, 1), (y, 0), (me, 0), (me, 1)]
        else:
            self.first = [
                send(cols(lax.rem(me + k, n), 0, w), slots.at[k - 1], ssem.at[k - 1], rsem.at[k - 1],
                     lax.rem(me + k, n))
                for k in range(1, n)
            ]
            self.second = self.third = []

    def start(self):
        for copy in self.first + self.second:
            copy.start()

    def relay(self):
        if self.square:
            half = self.half
            for i, (owner, at) in enumerate(((self.x, half), (self.y, 0))):
                self.first[1 - i].wait_recv()

                def add(cols, i=i, owner=owner, at=at):
                    wide = pl.ds(pl.multiple_of(owner * self.w + at + cols.start, LANE), LANE)
                    self.go[i, :, cols] = (
                        self.part[:, wide].astype(F32) + self.come[1 - i, :, cols].astype(F32)
                    ).astype(BF)

                chunks(half, add)
                self.third[i].start()

    def wait(self):
        if self.square:
            for copy in self.first:
                copy.wait_send()
            wait_all(self.second + self.third)
        else:
            wait_all(self.first)

    def total(self, cols, wide):
        total = self.part[:, wide].astype(F32)
        for k in range(self.slots.shape[0]):
            total = total + self.slots[k, :, cols].astype(F32)
        return total


def scatter_room(n, rows, w):
    count, half = (2, w // 2) if n == 4 else (n - 1, LANE)
    return [
        pltpu.VMEM((count, rows, w), BF), pltpu.VMEM((2, rows, half), BF), pltpu.VMEM((2, rows, half), BF),
        sems(6 if n == 4 else n - 1), sems(6 if n == 4 else n - 1),
    ]


def gather_sems(n):
    return [sems(6 if n == 4 else n - 1)] * 2


def stream(count, fetch, compute):
    fetch(0, 0).start()

    def step(i, carry):
        slot = lax.rem(i, 2)

        @pl.when(i + 1 < count)
        def _():
            fetch(i + 1, 1 - slot).start()

        fetch(i, slot).wait()
        compute(i, slot)
        return carry

    lax.fori_loop(0, count, step, 0)


def wait_all(copies):
    for copy in copies:
        copy.wait()


def row_stats(n, rows, w, all_ref, acc, mean_ref, inv_ref):
    acc[...] = jnp.zeros_like(acc)

    def add(cols):
        total = all_ref[0, :, cols].astype(F32)
        for k in range(1, n):
            total = total + all_ref[k, :, cols].astype(F32)
        acc[...] += total

    chunks(w, add)
    mean_ref[...] = spread(jnp.sum(acc[...], axis=1, keepdims=True) * (1.0 / D), rows)
    acc[...] = jnp.zeros_like(acc)

    def square(cols):
        mean = mean_ref[...]
        total = jnp.zeros_like(mean)
        for k in range(n):
            center = all_ref[k, :, cols].astype(F32) - mean
            total = total + center * center
        acc[...] += total

    chunks(w, square)
    var = jnp.sum(acc[...], axis=1, keepdims=True) * (1.0 / D)
    inv_ref[...] = spread(lax.rsqrt(var + EPS), rows)


def write_act(n, w, all_ref, mean_ref, inv_ref, gain_ref, bias_ref, act_ref):
    def act(cols):
        for k in range(n):
            wide = pl.ds(pl.multiple_of(k * w + cols.start, LANE), LANE)
            center = all_ref[k, :, cols].astype(F32) - mean_ref[...]
            act_ref[:, wide] = (
                center * inv_ref[...] * gain_ref[:, wide] + bias_ref[:, wide]
            ).astype(BF)

    chunks(w, act)


def part_rows(w_ref, out_ref, ibuf, obuf, isem, osem, also):
    size = ibuf.shape[1]
    count = w_ref.shape[0] // size

    def rows_of(i):
        return pl.ds(pl.multiple_of(i * size, size), size)

    def fetch(i, slot):
        return pltpu.make_async_copy(w_ref.at[rows_of(i)], ibuf.at[slot], isem.at[slot])

    def put(i, slot):
        return pltpu.make_async_copy(obuf.at[slot], out_ref.at[:, rows_of(i)], osem.at[slot])

    fetch(0, 0).start()

    def step(i, carry):
        slot = lax.rem(i, 2)
        also(i)

        @pl.when(i + 1 < count)
        def _():
            fetch(i + 1, 1 - slot).start()

        fetch(i, slot).wait()

        @pl.when(i >= 2)
        def _():
            put(i - 2, slot).wait()

        obuf[slot] = jnp.swapaxes(ibuf[slot], 0, 1)
        put(i, slot).start()
        return carry

    lax.fori_loop(0, count, step, 0)
    for i in (count - 2, count - 1):
        put(i, i % 2).wait()


def first_norm_kernel(
    n, x_ref, gain_ref, bias_ref, cot_ref, w_ref, act_ref, mean_ref, inv_ref, parted_ref, cots_ref, late_ref,
    all_ref, acc, ssem, rsem, ibuf, obuf, isem, osem, csem, crem,
):
    rows, w = x_ref.shape
    me = lax.axis_index("tensor")
    greet(n)
    dest = lambda owner, at, size: all_ref.at[owner, :, pl.ds(at, size)]
    gather = Gather(n, x_ref, dest, ssem, rsem)
    gather.start()
    all_ref[me] = x_ref[...]
    early_ref = cot_ref.at[:, :cots_ref.shape[2]]
    into = lambda owner, at, size: cots_ref.at[owner, :, pl.ds(at, size)]
    early = Gather(n, early_ref, into, csem, crem)

    def between(i):
        @pl.when(i == 6)
        def _():
            gather.relay()
            early.start()

    cots_ref[me] = early_ref[...]
    late_ref[...] = cot_ref[:, cots_ref.shape[2]:]
    part_rows(w_ref, parted_ref, ibuf, obuf, isem, osem, between)
    gather.wait()
    row_stats(n, rows, w, all_ref, acc, mean_ref, inv_ref)
    early.relay()
    write_act(n, w, all_ref, mean_ref, inv_ref, gain_ref, bias_ref, act_ref)
    early.wait()


def second_norm_kernel(
    n, m, pieces, part_ref, x_ref, scale_ref, gain_ref, bias_ref, mlp_ref, cot_ref, cots_ref, mixed_ref,
    w_down_ref, attn_ref, res_ref, act_ref, mean_ref, inv_ref, hgrad_ref, kcot_ref, *refs,
):
    hops = m // 2 - 1
    rights, lefts, refs = refs[:hops], refs[hops:2 * hops], refs[2 * hops:]
    (slots, come, go, ssem, rsem, own_ref, all_ref, acc, ssem2, rsem2, hsem,
     css, crs, cls, bgrad, wbuf, wsem) = refs
    rows, w = x_ref.shape
    me = lax.axis_index("tensor")
    greet(n, m)
    scatter = Scatter(n, w, part_ref, slots, come, go, ssem, rsem)
    scatter.start()
    line = [
        Hop(k, m, rights[k - 2] if k > 1 else mixed_ref, lefts[k - 2] if k > 1 else mixed_ref,
            rights[k - 1], lefts[k - 1], hsem.at[k - 1])
        for k in range(1, hops + 1)
    ]
    line[0].start()

    ahead = cots_ref.shape[2]
    for owner in range(n):

        def early(cols, owner=owner):
            wide = pl.ds(pl.multiple_of(owner * w + cols.start, LANE), LANE)
            bgrad[:, wide] = (mlp_ref[:, wide] * cots_ref[owner, :, cols].astype(F32)).astype(BF)

        def late(cols, owner=owner):
            wide = pl.ds(pl.multiple_of(owner * w + ahead + cols.start, LANE), LANE)
            from_ = pl.ds(pl.multiple_of(owner * (w - ahead) + cols.start, LANE), LANE)
            bgrad[:, wide] = (mlp_ref[:, wide] * cot_ref[:, from_].astype(F32)).astype(BF)

        chunks(ahead, early)
        chunks(w - ahead, late)
    side = Exchange(m, pieces, bgrad, kcot_ref, css, crs, cls)
    side.start()
    tile = wbuf.shape[1]
    count = hgrad_ref.shape[1] // tile

    def fetch(i, slot):
        return pltpu.make_async_copy(
            w_down_ref.at[pl.ds(pl.multiple_of(i * tile, tile), tile), :], wbuf.at[slot], wsem.at[slot]
        )

    def compute(i, slot):
        hgrad_ref[:, pl.ds(pl.multiple_of(i * tile, tile), tile)] = lax.dot_general(
            bgrad[...], wbuf[slot], COLS, preferred_element_type=F32
        )

        @pl.when(i == count // 2)
        def _():
            scatter.relay()

    stream(count, fetch, compute)
    line[0].wait()
    if hops > 1:
        line[1].start()
    scatter.wait()

    def add(cols):
        wide = pl.ds(pl.multiple_of(me * w + cols.start, LANE), LANE)
        total = scatter.total(cols, wide)
        attn_ref[:, cols] = total
        res = x_ref[:, cols].astype(F32) + scale_ref[:, wide] * total
        res_ref[:, cols] = res
        own_ref[:, cols] = res.astype(BF)

    chunks(w, add)
    dest = lambda owner, at, size: all_ref.at[owner, :, pl.ds(at, size)]
    gather = Gather(n, own_ref, dest, ssem2, rsem2)
    gather.start()
    all_ref[me] = own_ref[...]
    gather.relay()
    for k in range(1, hops - 1):
        line[k].wait()
        line[k + 1].start()
    gather.wait()
    row_stats(n, rows, w, all_ref, acc, mean_ref, inv_ref)
    write_act(n, w, all_ref, mean_ref, inv_ref, gain_ref, bias_ref, act_ref)
    line[-1].wait()
    side.wait()


def norm_back(n, w, load_total, grad_ref, base_ref, mean_ref, inv_ref, gain_ref,
              sums, acc, acc2, stat_own, stats, ssem, rsem, out):
    rows = grad_ref.shape[0]
    me = lax.axis_index("tensor")
    acc[...] = jnp.zeros_like(acc)
    acc2[...] = jnp.zeros_like(acc2)

    def first(cols):
        wide = pl.ds(pl.multiple_of(me * w + cols.start, LANE), LANE)
        total = load_total(cols, wide)
        grad_ref[:, cols] = total
        normed = (base_ref[:, cols].astype(F32) - mean_ref[...]) * inv_ref[...]
        sums[0:1, cols] = jnp.sum(total * normed, axis=0, keepdims=True)
        sums[1:2, cols] = jnp.sum(total, axis=0, keepdims=True)
        scaled = total * gain_ref[:, wide]
        acc[...] += scaled
        acc2[...] += scaled * normed

    chunks(w, first)
    ones = jnp.ones((8, LANE), F32)
    high = lax.Precision.HIGHEST
    plain = lax.dot_general(ones, acc[...], COLS, precision=high, preferred_element_type=F32)
    cross = lax.dot_general(ones, acc2[...], COLS, precision=high, preferred_element_type=F32)
    line = lax.broadcasted_iota(jnp.int32, (8, rows), 0)
    stat_own[...] = jnp.where(line < 4, plain, cross)
    copies = [
        send(stat_own, stats.at[me], ssem.at[k - 1], rsem.at[k - 1], lax.rem(me + k, n))
        for k in range(1, n)
    ]
    for copy in copies:
        copy.start()
    wait_all(copies)
    both = stat_own[...]
    for k in range(1, n):
        both = both + stats[lax.rem(me + k, n)]
    both = both * (1.0 / D)
    pick = lax.broadcasted_iota(jnp.int32, (8, LANE), 0)
    acc[...] = lax.dot_general(
        both, (pick == 0).astype(F32), ROWS, precision=high, preferred_element_type=F32
    )
    acc2[...] = lax.dot_general(
        both, (pick == 4).astype(F32), ROWS, precision=high, preferred_element_type=F32
    )

    def second(cols):
        wide = pl.ds(pl.multiple_of(me * w + cols.start, LANE), LANE)
        normed = (base_ref[:, cols].astype(F32) - mean_ref[...]) * inv_ref[...]
        scaled = grad_ref[:, cols] * gain_ref[:, wide]
        out(cols, wide, inv_ref[...] * (scaled - acc[...] - normed * acc2[...]))

    chunks(w, second)


def second_back_kernel(
    n, m, gate_ref, up_ref, cot_ref, res_ref, attn_ref, mean_ref, inv_ref, gain_ref, scale_ref,
    right_ref, left_ref, gu_ref, w_ref, rgrad_ref, agrad_ref, sums_ref, gu_right, gu_left, *refs,
):
    hops = m // 2 - 1
    rights = (right_ref,) + refs[:hops - 1]
    lefts = (left_ref,) + refs[hops - 1:2 * hops - 2]
    (part_ref, slots, come, go, ssem, rsem, grad_ref, own_ref, acc, acc2, stat_own, stats,
     ssem2, rsem2, ssem3, rsem3, lsem, hsem, gsem, wbuf, wsem) = refs[2 * hops - 2:]
    w = cot_ref.shape[1]
    me = lax.axis_index("tensor")
    greet(n, m)
    line = [
        Hop(k, m, rights[k - 2], lefts[k - 2], rights[k - 1], lefts[k - 1], hsem.at[k - 2])
        for k in range(2, hops + 1)
    ]
    line[0].start()
    first = End(m, gu_ref, 0, gu_right, gu_left, gsem)
    first.start()
    scatter = Scatter(n, w, part_ref, slots, come, go, ssem, rsem)
    tile = wbuf.shape[2]
    count = D // tile

    def spot(i):
        if not scatter.square:
            return pl.ds(pl.multiple_of(i * tile, LANE), tile)
        at = 0
        for k, (owner, half) in enumerate(scatter.order):
            at = at + jnp.where(i == k, owner * w + half * tile, 0)
        return pl.ds(pl.multiple_of(at, LANE), tile)

    def fetch(i, slot):
        return pltpu.make_async_copy(w_ref.at[:, spot(i), :], wbuf.at[slot], wsem.at[slot])

    def compute(i, slot):
        part_ref[:, spot(i)] = (
            lax.dot_general(gate_ref[...], wbuf[slot, 0], COLS, preferred_element_type=F32)
            + lax.dot_general(up_ref[...], wbuf[slot, 1], COLS, preferred_element_type=F32)
        ).astype(BF)
        if scatter.square:
            for k, copy in enumerate(scatter.first + scatter.second):
                pl.when(i == k)(copy.start)
            pl.when(i == 5)(scatter.relay)

    stream(count, fetch, compute)
    if not scatter.square:
        scatter.start()
    scatter.wait()
    sums_ref[...] = jnp.zeros_like(sums_ref)

    def out(cols, wide, back):
        res_grad = cot_ref[:, cols].astype(F32) + back
        rgrad_ref[:, cols] = res_grad
        sums_ref[2:3, cols] = jnp.sum(res_grad * attn_ref[:, cols], axis=0, keepdims=True)
        own_ref[:, cols] = (scale_ref[:, wide] * res_grad).astype(BF)

    norm_back(n, w, scatter.total, grad_ref, res_ref, mean_ref, inv_ref, gain_ref,
              sums_ref, acc, acc2, stat_own, stats, ssem2, rsem2, out)
    dest = lambda owner, at, size: agrad_ref.at[:, pl.ds(pl.multiple_of(owner * w + at, LANE), size)]
    gather = Gather(n, own_ref, dest, ssem3, rsem3)
    gather.start()
    local = pltpu.make_async_copy(own_ref, dest(me, 0, w), lsem)
    local.start()
    gather.relay()
    for k in range(len(line)):
        line[k].wait()
        if k + 1 < len(line):
            line[k + 1].start()
    local.wait()
    gather.wait()
    first.wait()


def first_back_kernel(
    n, grad_in, x_ref, mean_ref, inv_ref, gain_ref, small_ref,
    part_ref, cot_ref, scale_ref,
    igrad_ref, sums, out_ref,
    slots, come, go, ssem, rsem, grad_ref, acc, acc2, stat_own, stats, ssem2, rsem2,
):
    w = x_ref.shape[1]
    greet(n)
    scatter = Scatter(n, w, part_ref, slots, come, go, ssem, rsem)
    scatter.start()
    sums[...] = small_ref[...]
    scatter.relay()

    def load_total(cols, wide):
        return grad_in[:, cols].astype(F32)

    def out(cols, wide, back):
        igrad_ref[:, cols] = back

    norm_back(n, w, load_total, grad_ref, x_ref, mean_ref, inv_ref, gain_ref,
              sums, acc, acc2, stat_own, stats, ssem2, rsem2, out)
    scatter.wait()
    me = lax.axis_index("tensor")

    def add(cols):
        wide = pl.ds(pl.multiple_of(me * w + cols.start, LANE), LANE)
        total = scatter.total(cols, wide)
        out_ref[:, cols] = scale_ref[:, wide] * total
        sums[5:6, cols] = jnp.sum(cot_ref[:, cols].astype(F32) * total, axis=0, keepdims=True)

    chunks(w, add)


def mate_of(you):
    return you + 1 - 2 * lax.rem(you, 2)


def pair_grad_kernel(
    m, act_ref, gate_ref, up_ref, hidden_ref, out_ref, right_ref, left_ref,
    acts, mates, gates, ups, flip, obuf, asem, arem, gsem, grem, lsem, hsem, osem,
):
    line = m // 2
    you = lax.axis_index("dp")
    core, mate = lax.rem(you, 2), mate_of(you)
    width = acts.shape[-1]
    tile = 512
    greet(1, m)
    hop = Hop(1, m, hidden_ref, hidden_ref, right_ref, left_ref, hsem)
    copies = [
        send_dp(gate_ref, gates, gsem.at[0], grem.at[0], mate),
        send_dp(up_ref, ups, gsem.at[1], grem.at[1], mate),
    ]
    locals_ = []
    for k in range(line):
        theirs = pl.ds(pl.multiple_of((2 * k + 1 - core) * width, LANE), width)
        ours = pl.ds(pl.multiple_of((2 * k + core) * width, LANE), width)
        copies.append(send_dp(act_ref.at[:, theirs], mates.at[k], asem.at[k], arem.at[k], mate))
        locals_.append(pltpu.make_async_copy(act_ref.at[:, ours], acts.at[k], lsem.at[k]))
    for copy in locals_ + copies:
        copy.start()
    hop.start()
    for copy in locals_:
        copy.wait()

    def turn(which, source):
        def step(k, carry):
            flip[which, k] = source[k].T
            return carry

        lax.fori_loop(0, line, step, 0)

    turn(0, acts)
    for copy in copies:
        copy.wait()
    turn(1, mates)
    def put(k):
        slot = lax.rem(k, 2)
        return pltpu.make_async_copy(obuf.at[slot], out_ref.at[k], osem.at[slot])

    def chip(k, carry):
        slot = lax.rem(k, 2)

        @pl.when(k >= 2)
        def _():
            put(k - 2).wait()

        for j, (near, far) in enumerate(((gate_ref, gates), (up_ref, ups))):

            def step(i, carry, j=j, near=near, far=far):
                cols = pl.ds(pl.multiple_of(i * tile, tile), tile)
                obuf[slot, j, :, cols] = (
                    jnp.dot(flip[0, k], near[:, cols], preferred_element_type=F32)
                    + jnp.dot(flip[1, k], far[:, cols], preferred_element_type=F32)
                ).astype(BF)
                return carry

            lax.fori_loop(0, gate_ref.shape[1] // tile, step, 0)
        put(k).start()
        return carry

    lax.fori_loop(0, line, chip, 0)
    for k in range(max(line - 2, 0), line):
        put(k).wait()
    hop.wait()


class SmallSums:
    def __init__(self, n, m, sums, out, parts, total, dss, drs, tss, trs):
        self.out, self.sums, self.parts, self.total = out, sums, parts, total
        me, you = lax.axis_index("tensor"), lax.axis_index("dp")
        w = sums.shape[1]
        self.m, self.you = m, you
        self.mine = pl.ds(pl.multiple_of(me * w, w), w)
        self.dp = [
            send_dp(sums, parts.at[you], dss.at[k - 1], drs.at[k - 1], lax.rem(you + k, m))
            for k in range(1, m)
        ]
        self.tensor = [
            send(total, out.at[:, self.mine], tss.at[k - 1], trs.at[k - 1], lax.rem(me + k, n))
            for k in range(1, n)
        ]

    def start(self):
        for copy in self.dp:
            copy.start()

    def finish(self):
        self.parts[self.you] = self.sums[...]
        wait_all(self.dp)
        total = self.parts[0]
        for k in range(1, self.m):
            total = total + self.parts[k]
        self.total[...] = total
        for copy in self.tensor:
            copy.start()
        self.out[:, self.mine] = total
        wait_all(self.tensor)


def small_sums_kernel(n, m, sums, out_ref, parts, total, *room):
    greet(n, m)
    small = SmallSums(n, m, sums, out_ref, parts, total, *room)
    small.start()
    small.finish()


def gathered_grad_kernel(m, turned, first, last, *refs):
    hops = m // 2 - 1
    you = lax.axis_index("dp")
    core, mate, z = lax.rem(you, 2), mate_of(you), you // 2
    todo = []
    refs = list(refs)
    for k in range(first, last + 1):
        if k == 0:
            todo.append((None, refs.pop(0), z))
        else:
            todo.append((z >= k, refs.pop(0), z - k))
            todo.append((z <= hops - k, refs.pop(0), z + k))
    side_ref = refs.pop(0)
    out_ref, blocks, flip, lsem, ssem, rsem = refs
    greet(1, m)
    copies = []
    for at, (cond, src, chip) in enumerate(todo):
        near = pltpu.make_async_copy(src, blocks.at[at, core], lsem.at[at])
        far = send_dp(src, blocks.at[at, core], ssem.at[at], rsem.at[at], mate)
        copies.append((cond, near, far))

    def when(cond, body):
        body() if cond is None else pl.when(cond)(body)

    def go(near, far):
        near.start()
        far.start()

    def done(near, far):
        near.wait()
        far.wait()

    def unit_of(at):
        k = (at + 1) // 2 if first == 0 else first
        right = lax.rem(at, 2) == (1 if first == 0 else 0)
        there = (k == 0) | (right & (z >= k)) | (jnp.logical_not(right) & (z <= hops - k))
        return there, jnp.where(right, z - k, z + k)

    def turn(i, carry):
        at, c = i // 2, lax.rem(i, 2)
        there, chip = unit_of(at)

        @pl.when(there)
        def _():
            flip[at, c] = side_ref[2 * chip + c].T

        return carry

    for cond, near, far in copies:
        when(cond, functools.partial(go, near, far))
    lax.fori_loop(0, 2 * len(todo), turn, 0)
    for cond, near, far in copies:
        when(cond, functools.partial(done, near, far))
    tile = 512
    parts, width = out_ref.shape[0], blocks.shape[-1]
    count = width // tile
    out_ref[...] = jnp.zeros_like(out_ref)

    def unit(i, carry):
        at, j, at_col = i // (parts * count), lax.rem(i // count, parts), lax.rem(i, count)
        there, _ = unit_of(at)

        @pl.when(there)
        def _():
            cols = pl.ds(pl.multiple_of(at_col * tile, tile), tile)
            total = jnp.dot(
                flip[at, 0], blocks[at, 0, j, :, cols], preferred_element_type=F32
            ) + jnp.dot(flip[at, 1], blocks[at, 1, j, :, cols], preferred_element_type=F32)
            if turned:
                out_ref[j, cols, :] += total.T
            else:
                out_ref[j, :, cols] += total

        return carry

    lax.fori_loop(0, len(todo) * parts * count, unit, 0)


def qkv_kernel(act_ref, w_ref, cos_ref, sin_ref, out_ref):
    raw = jnp.dot(act_ref[...], w_ref[...], preferred_element_type=F32)
    part = pl.program_id(0)

    @pl.when(part < 2)
    def _():
        for h in range(raw.shape[1] // HD):
            cols = slice(h * HD, (h + 1) * HD)
            t = raw[:, cols]
            out_ref[:, cols] = (
                t * cos_ref[...] + pltpu.roll(t, HD // 2, 1) * sin_ref[...]
            ).astype(BF)

    @pl.when(part == 2)
    def _():
        out_ref[...] = raw.astype(BF)


def qkv_matmul(act, w_j, cos2, sin2):
    rows = act.shape[0]
    inner = w_j.shape[2]
    tile = min(512, inner)
    return pl.pallas_call(
        qkv_kernel,
        grid=(3, inner // tile),
        out_shape=jax.ShapeDtypeStruct((3, rows, inner), BF),
        in_specs=[
            pl.BlockSpec((rows, D), lambda j, i: (0, 0)),
            pl.BlockSpec((None, D, tile), lambda j, i: (j, 0, i)),
            pl.BlockSpec((rows, HD), lambda j, i: (0, 0)),
            pl.BlockSpec((rows, HD), lambda j, i: (0, 0)),
        ],
        out_specs=pl.BlockSpec((None, rows, tile), lambda j, i: (j, 0, i)),
        compiler_params=pltpu.CompilerParams(vmem_limit_bytes=40 << 20),
        cost_estimate=pl.CostEstimate(
            flops=2 * rows * D * 3 * inner, bytes_accessed=6 * D * inner, transcendentals=0
        ),
    )(act, w_j, cos2, sin2)


def attention_probs(q, k, same):
    scores = lax.dot_general(k, q, COLS, preferred_element_type=F32) * (HD ** (-0.5))
    scores = jnp.where(same, scores, -jnp.inf)
    top = jnp.max(scores, axis=0, keepdims=True)
    weight = jnp.exp(scores - top)
    return weight / jnp.sum(weight, axis=0, keepdims=True)


def same_image(rows):
    one = lax.broadcasted_iota(jnp.int32, (rows, rows), 0)
    two = lax.broadcasted_iota(jnp.int32, (rows, rows), 1)
    image = lambda i: sum((i >= SEQ * k).astype(jnp.int32) for k in range(1, rows // SEQ))
    return image(one) == image(two)


def attention_kernel(qkv_ref, w_hbm, mixed_ref, part_ref, w_ref, wsem):
    rows, inner = mixed_ref.shape
    weights = pltpu.make_async_copy(w_hbm, w_ref, wsem)
    weights.start()

    def head(h, carry):
        cols = pl.ds(pl.multiple_of(h * HD, HD), HD)
        probs = attention_probs(qkv_ref[0, :, cols], qkv_ref[1, :, cols], same_image(rows))
        value = qkv_ref[2, :, cols].astype(F32).T.astype(BF)
        mixed = jnp.dot(value, probs.astype(BF), preferred_element_type=F32)
        mixed_ref[:, cols] = mixed.T.astype(BF)
        return carry

    lax.fori_loop(0, inner // HD, head, 0)
    weights.wait()

    def tile(i, carry):
        cols = pl.ds(pl.multiple_of(i * 512, 512), 512)
        part_ref[:, cols] = jnp.dot(
            mixed_ref[...], w_ref[:, cols], preferred_element_type=F32
        ).astype(BF)
        return carry

    lax.fori_loop(0, D // 512, tile, 0)


def attention_back_kernel(
    m, pieces, agrad_ref, qkv_ref, cos_ref, sin_ref, full_ref, w_ref,
    out_ref, kattn_ref, mgrad, ass, ars, als, wbuf, wsem,
):
    rows, inner = mgrad.shape
    greet(1, m)
    side = Exchange(m, pieces, full_ref, kattn_ref, ass, ars, als)
    side.start()
    step = min(256, inner)

    def fetch(i, slot):
        some = pl.ds(pl.multiple_of(i * step, step), step)
        return pltpu.make_async_copy(w_ref.at[some, :], wbuf.at[slot], wsem.at[slot])

    def tile(i, slot):
        cols = pl.ds(pl.multiple_of(i * step, step), step)
        mgrad[:, cols] = lax.dot_general(
            agrad_ref[...], wbuf[slot], COLS, preferred_element_type=F32
        ).astype(BF)

    stream(inner // step, fetch, tile)

    def back(t):
        return t * cos_ref[...] - pltpu.roll(t, HD // 2, 1) * sin_ref[...]

    def head(h, carry):
        cols = pl.ds(pl.multiple_of(h * HD, HD), HD)
        q, k, v = qkv_ref[0, :, cols], qkv_ref[1, :, cols], qkv_ref[2, :, cols]
        grad = mgrad[:, cols]
        probs = attention_probs(q, k, same_image(rows))
        prob_grad = lax.dot_general(v, grad, COLS, preferred_element_type=F32)
        delta = jnp.sum(probs * prob_grad, axis=0, keepdims=True)
        score_grad = (probs * (prob_grad - delta)).astype(BF)
        scale = HD ** (-0.5)
        flipped = k.astype(F32).T.astype(BF)
        q_grad = jnp.dot(flipped, score_grad, preferred_element_type=F32).T * scale
        k_grad = jnp.dot(score_grad, q, preferred_element_type=F32) * scale
        out_ref[0, :, cols] = back(q_grad).astype(BF)
        out_ref[1, :, cols] = back(k_grad).astype(BF)
        out_ref[2, :, cols] = jnp.dot(
            probs.astype(BF), grad, preferred_element_type=F32
        ).astype(BF)
        return carry

    lax.fori_loop(0, inner // HD, head, 0)
    side.wait()


def gate_kernel(
    m, pieces, act_ref, w_ref, hgrad_ref, full_ref, hidden_ref, gate_ref, up_ref, kact_ref, ass, ars, als
):
    side = Exchange(m, pieces, full_ref, kact_ref, ass, ars, als)

    @pl.when(pl.program_id(0) == 0)
    def _():
        greet(1, m)
        side.start()

    gate = jnp.dot(act_ref[...], w_ref[0], preferred_element_type=F32)
    up = jnp.dot(act_ref[...], w_ref[1], preferred_element_type=F32)
    sig = jax.nn.sigmoid(gate)
    grad = hgrad_ref[...]
    hidden_ref[...] = (gate * sig * up).astype(BF)
    gate_ref[...] = (grad * up * sig * (1.0 + gate * (1.0 - sig))).astype(BF)
    up_ref[...] = (grad * gate * sig).astype(BF)
    pl.when(pl.program_id(0) == pl.num_programs(0) - 1)(side.wait)


def gate_matmul(act, w_j, hidden_grad, act_one, m, pieces):
    rows, width = hidden_grad.shape
    tile = min(256, width)
    block = pl.BlockSpec((rows, tile), lambda i: (0, i))
    return pl.pallas_call(
        functools.partial(gate_kernel, m, pieces),
        grid=(width // tile,),
        out_shape=[jax.ShapeDtypeStruct((rows, width), BF)] * 3
        + [jax.ShapeDtypeStruct((m, rows, LANE), BF)],
        in_specs=[
            pl.BlockSpec((rows, D), lambda i: (0, 0)),
            pl.BlockSpec((2, D, tile), lambda i: (0, 0, i)),
            block,
            hb(),
        ],
        out_specs=[block] * 3 + [hb()],
        scratch_shapes=[sems(m - 1), sems(m - 1), pltpu.SemaphoreType.DMA],
        compiler_params=pltpu.CompilerParams(
            collective_id=12, has_side_effects=True, vmem_limit_bytes=48 << 20
        ),
    )(act, w_j, hidden_grad, act_one)


def back_kernel(g_ref, w_ref, out_ref):
    total = None
    for j in range(g_ref.shape[0]):
        term = lax.dot_general(g_ref[j], w_ref[j], COLS, preferred_element_type=F32)
        total = term if total is None else total + term
    out_ref[...] = total.astype(BF)


def back_matmul(grads, w_j):
    parts, rows, inner = grads.shape
    tile = 512
    return pl.pallas_call(
        back_kernel,
        grid=(D // tile,),
        out_shape=jax.ShapeDtypeStruct((rows, D), BF),
        in_specs=[
            pl.BlockSpec((parts, rows, inner), lambda i: (0, 0, 0)),
            pl.BlockSpec((parts, tile, inner), lambda i: (0, i, 0)),
        ],
        out_specs=pl.BlockSpec((rows, tile), lambda i: (0, i)),
        compiler_params=pltpu.CompilerParams(vmem_limit_bytes=40 << 20),
        cost_estimate=pl.CostEstimate(
            flops=rows * D * parts * inner * 100 // 500,
            bytes_accessed=800_000,
            transcendentals=0,
        ),
    )(grads, w_j)


def vm():
    return pl.BlockSpec(memory_space=pltpu.VMEM)


def hb():
    return pl.BlockSpec(memory_space=pltpu.HBM)


def sems(*shape):
    return pltpu.SemaphoreType.DMA(shape)


def call(kernel, ident, outs, scratch, args, micros=30):
    shapes = [jax.ShapeDtypeStruct(o[0], o[1]) for o in outs]
    return list(pl.pallas_call(
        kernel,
        out_shape=shapes,
        in_specs=[hb() if a[1] else vm() for a in args],
        out_specs=[hb() if len(o) > 2 else vm() for o in outs],
        scratch_shapes=scratch,
        compiler_params=pltpu.CompilerParams(
            collective_id=ident, has_side_effects=True, vmem_limit_bytes=56 << 20
        ),
        cost_estimate=pl.CostEstimate(
            flops=micros * 100_000_000, bytes_accessed=800_000, transcendentals=0
        ),
    )(*[a[0] for a in args]))


def join_kernel(one, two, three, out_ref):
    total = one[...].astype(F32) + two[...].astype(F32) + three[...].astype(F32)
    out_ref[...] = jnp.swapaxes(total, 0, 1)


def join(one, two, three):
    _, rows, width = one.shape
    size = 64
    block = pl.BlockSpec((2, size, width), lambda i: (0, i, 0))
    return pl.pallas_call(
        join_kernel,
        grid=(rows // size,),
        out_shape=jax.ShapeDtypeStruct((rows, 2, width), F32),
        in_specs=[block] * 3,
        out_specs=pl.BlockSpec((size, 2, width), lambda i: (i, 0, 0)),
        compiler_params=pltpu.CompilerParams(vmem_limit_bytes=32 << 20),
    )(one, two, three)


class LineReduce:
    def __init__(self, part, right, left, m):
        self.part, self.line, self.t = part, m // 2, 2
        self.z = lax.axis_index("dp") // 2
        right, left = (jnp.concatenate(pieces, axis=1).astype(F32) for pieces in (right, left))
        self.right = jnp.where(self.z >= 1, right, 0.0)
        self.left = jnp.where(self.z <= self.line - 2, left, 0.0)

    def take(self, i):
        i = jnp.clip(i, 0, self.line - 1)
        return lax.dynamic_index_in_dim(self.part, i, 0, keepdims=False).astype(F32)

    def step(self, after):
        line, t = self.line, self.t
        right = (self.take(self.z + line - t) + self.right).astype(BF)
        left = (self.take(self.z - line + t) + self.left).astype(BF)
        right, left = lax.optimization_barrier((right, left) + tuple(after))[:2]
        self.given = right, left
        self.right = lax.ppermute(
            right, "dp", [(2 * i + c, 2 * i + 2 + c) for i in range(t) for c in range(2)]
        ).astype(F32)
        self.left = lax.ppermute(
            left, "dp",
            [(2 * i + c, 2 * i - 2 + c) for i in range(line - t, line) for c in range(2)],
        ).astype(F32)
        self.t += 1

    def finish(self, after):
        while self.t < self.line:
            self.step(after)
        own = lax.dynamic_index_in_dim(self.part, self.z, 0, keepdims=False)
        return join(own, self.right.astype(BF), self.left.astype(BF))


def line_gather(own, m, meanwhile):
    line = m // 2
    right = left = own
    rights, lefts = [], []
    for k in range(1, line):
        right = lax.ppermute(right, "dp", [(i, i + 2) for i in range(2 * (k - 1), m - 2)])
        left = lax.ppermute(left, "dp", [(i, i - 2) for i in range(2, m - 2 * (k - 1))])
        if k in meanwhile and k < line - 1:
            right, left = lax.optimization_barrier((right, left) + meanwhile[k](right, left))[:2]
        rights.append(right)
        lefts.append(left)
    return rights, lefts


def local(
    tokens_in, ln1_gain, ln1_bias, w_qkv, w_out, scale_attn, ln2_gain, ln2_bias, w_gu, w_down,
    scale_mlp, out_cotangent, *, n, m,
):
    rows, w = tokens_in.shape
    images = rows // SEQ
    inner = w_qkv.shape[2]
    heads = inner // HD
    hidden_width = w_gu.shape[2]
    scale = HD ** (-0.5)
    line = m // 2
    hops = line - 1
    shard = D // m
    pieces = min(n, shard // LANE)
    cosines, sines = rope_tables()
    cos2 = jnp.tile(jnp.concatenate([cosines, cosines], axis=1), (images, 1))
    sin2 = jnp.tile(jnp.concatenate([-sines, sines], axis=1), (images, 1))
    wide = (rows, n * w)
    own = (rows, w)
    lanes = (rows, LANE)
    row = lambda v: v.reshape(1, D)
    V = lambda *a: [(x, False) for x in a]
    H = lambda *a: [(x, True) for x in a]

    w_j = jnp.transpose(w_qkv, (1, 0, 2))

    ahead = w // 2
    act_one, mean_one, inv_one, gu_j, cots, cot_late = call(
        functools.partial(first_norm_kernel, n), 1,
        [(wide, BF), (lanes, F32), (lanes, F32), ((2, D, hidden_width), BF, True), ((n, rows, ahead), BF),
         ((rows, w - ahead), BF)],
        [pltpu.VMEM((n,) + own, BF), pltpu.VMEM(lanes, F32)] + gather_sems(n)
        + [pltpu.VMEM((2, 256, 2, hidden_width), BF), pltpu.VMEM((2, 2, 256, hidden_width), BF),
           sems(2), sems(2)] + gather_sems(n),
        V(tokens_in, row(ln1_gain), row(ln1_bias), out_cotangent) + H(w_gu), 50,
    )
    cot_all = lax.all_gather(cot_late, "tensor", axis=1, tiled=True)
    qkv = qkv_matmul(act_one, w_j, cos2, sin2)
    mixed, attn_part = pl.pallas_call(
        attention_kernel,
        out_shape=[jax.ShapeDtypeStruct((rows, inner), BF), jax.ShapeDtypeStruct(wide, BF)],
        in_specs=[vm(), hb()],
        out_specs=[vm()] * 2,
        scratch_shapes=[pltpu.VMEM(w_out.shape, BF), pltpu.SemaphoreType.DMA],
        compiler_params=pltpu.CompilerParams(vmem_limit_bytes=48 << 20),
    )(qkv, w_out)
    tile = min(512, hidden_width)
    outs = call(
        functools.partial(second_norm_kernel, n, m, pieces), 2,
        [(own, F32), (own, F32), (wide, BF), (lanes, F32), (lanes, F32), ((rows, hidden_width), F32)]
        + [((m, rows, LANE), BF, True)] + [((rows, inner), BF, True)] * (2 * hops),
        scatter_room(n, rows, w)
        + [pltpu.VMEM(own, BF), pltpu.VMEM((n,) + own, BF), pltpu.VMEM(lanes, F32)]
        + gather_sems(n) + [sems(hops, 4)]
        + [sems(m - 1), sems(m - 1), pltpu.SemaphoreType.DMA]
        + [pltpu.VMEM(wide, BF), pltpu.VMEM((2, tile, D), BF), sems(2)],
        V(attn_part, tokens_in, row(scale_attn), row(ln2_gain), row(ln2_bias), row(scale_mlp), cot_all, cots)
        + H(mixed, w_down), 80,
    )
    attn_sum, residual, act_two, mean_two, inv_two, hidden_grad, kcot = outs[:7]
    mixed_right, mixed_left = outs[7:7 + hops], outs[7 + hops:]
    side = lambda k: lax.all_gather(k, "tensor", axis=2, tiled=True)[:, :, :shard]

    hidden, gate_grad, up_grad, kact = gate_matmul(act_two, gu_j, hidden_grad, act_one, m, pieces)
    block = (rows, hidden_width)
    gu_part, hidden_r, hidden_l = call(
        functools.partial(pair_grad_kernel, m), 3,
        [((line, 2, shard, hidden_width), BF, True), (block, BF, True), (block, BF, True)],
        [pltpu.VMEM((line, rows, shard), BF), pltpu.VMEM((line, rows, shard), BF),
         pltpu.VMEM(block, BF), pltpu.VMEM(block, BF), pltpu.VMEM((2, line, shard, rows), BF),
         pltpu.VMEM((2, 2, shard, hidden_width), BF),
         sems(line), sems(line), sems(2), sems(2), sems(line), sems(4), sems(2)],
        H(act_two) + V(gate_grad, up_grad) + H(hidden), 40,
    )
    cut = shard * 5 // 8
    tile = w // 2 if n == 4 else min(512, w)
    outs = call(
        functools.partial(second_back_kernel, n, m), 4,
        [(own, F32), (wide, BF), ((8, w), F32)] + [((2, cut, hidden_width), BF, True)] * 2
        + [(block, BF, True)] * (2 * hops - 2),
        [pltpu.VMEM(wide, BF)] + scatter_room(n, rows, w)
        + [pltpu.VMEM(own, F32), pltpu.VMEM(own, BF),
         pltpu.VMEM(lanes, F32), pltpu.VMEM(lanes, F32), pltpu.VMEM((8, rows), F32),
         pltpu.VMEM((n, 8, rows), F32)] + [sems(n - 1)] * 2 + gather_sems(n)
        + [pltpu.SemaphoreType.DMA, sems(hops - 1, 4), sems(4)]
        + [pltpu.VMEM((2, 2, tile, hidden_width), BF), sems(2)],
        V(gate_grad, up_grad, out_cotangent, residual, attn_sum, mean_two, inv_two, row(ln2_gain), row(scale_attn))
        + H(hidden_r, hidden_l, gu_part, gu_j), 80,
    )
    res_grad, attn_grad, sums_two, gu_right, gu_left = outs[:5]
    hidden_right = [hidden_r] + outs[5:4 + hops]
    hidden_left = [hidden_l] + outs[4 + hops:]
    raw_grad, kattn = call(
        functools.partial(attention_back_kernel, m, pieces), 5,
        [((3, rows, inner), BF), ((m, rows, LANE), BF, True)],
        [pltpu.VMEM((rows, inner), BF), sems(m - 1), sems(m - 1), pltpu.SemaphoreType.DMA,
         pltpu.VMEM((2, min(256, inner), D), BF), sems(2)],
        V(attn_grad, qkv, cos2, sin2) + H(attn_grad, w_out), 25,
    )
    kcot, kact, raw_grad = lax.optimization_barrier((kcot, kact, raw_grad))
    side_cot, side_attn, side_act = side(kcot), side(kattn), side(kact)
    def gathered(ident, mine, rights, lefts, sides, turned, first=0, last=hops):
        parts, _, width = mine.shape
        shape = (parts, width, shard) if turned else (parts, shard, width)
        blocks = []
        for k in range(first, last + 1):
            blocks += [rights[k - 1], lefts[k - 1]] if k else [mine]
        count = len(blocks)
        (out,) = call(
            functools.partial(gathered_grad_kernel, m, turned, first, last), ident, [(shape, F32)],
            [pltpu.VMEM((count, 2) + mine.shape, BF), pltpu.VMEM((count, 2, shard, rows), BF),
             sems(count), sems(count), sems(count)],
            H(*blocks) + V(sides), 30,
        )
        return out

    lead = lambda arrays: [a[None] for a in arrays]
    done = {}

    def after_one(right, left):
        part = back_matmul(raw_grad, w_j)
        done["grad"] = lax.psum_scatter(part, "tensor", scatter_dimension=1, tiled=True)
        done["attn"], done["hidden"] = lax.optimization_barrier(
            (side_attn, hidden, part, right, left)
        )[:2]
        ends = lax.optimization_barrier(
            (gu_part[line - 1, :, cut:], gu_part[0, :, cut:], right, left, part)
        )
        done["rest"] = (
            lax.ppermute(ends[0], "dp", [(c, 2 + c) for c in range(2)]),
            lax.ppermute(ends[1], "dp", [(m - 2 + c, m - 4 + c) for c in range(2)]),
        )
        return (part,)

    def after_two(right, left):
        done["proj"] = gathered(
            7, mixed[None], lead(mixed_right), lead(mixed_left), done["attn"], False
        )[0].T
        done["part"] = jnp.dot(done["hidden"], w_down, preferred_element_type=F32).astype(BF)
        rest = lax.optimization_barrier(done["rest"] + (done["proj"], done["part"]))
        gu_line = LineReduce(gu_part, (gu_right, rest[0]), (gu_left, rest[1]), m)
        gu_line.step((right, left))
        done["gu"] = gu_line
        late = lax.optimization_barrier((side_cot,) + gu_line.given)
        done["down"] = gathered(
            6, hidden[None], lead(hidden_right), lead(hidden_left), late[0], False
        )[0].T
        return ()

    raw_right, raw_left = line_gather(raw_grad, m, {1: after_one, 2: after_two})
    act_one_grad, down_sum = done["grad"], done["down"]
    proj_sum = done["proj"]
    branch_part = done["part"]
    qkv_part = gathered(8, raw_grad, raw_right, raw_left, side_act, False, 0, hops - 1)
    gu_sum = done["gu"].finish((raw_right[-1], raw_left[-1], down_sum, proj_sum, qkv_part))

    small = jnp.concatenate([jnp.zeros((2, w), F32), sums_two[0:3], jnp.zeros((3, w), F32)], axis=0)
    input_grad, sums, layer_out = call(
        functools.partial(first_back_kernel, n), 9,
        [(own, F32), ((8, w), F32), (own, F32)],
        scatter_room(n, rows, w)
        + [pltpu.VMEM(own, F32),
           pltpu.VMEM(lanes, F32), pltpu.VMEM(lanes, F32), pltpu.VMEM((8, rows), F32),
           pltpu.VMEM((n, 8, rows), F32)] + [sems(n - 1)] * 2,
        V(act_one_grad, tokens_in, mean_one, inv_one, row(ln1_gain), small,
          branch_part, out_cotangent, row(scale_mlp)), 20,
    )
    input_grad = res_grad + input_grad
    layer_out = residual + layer_out
    qkv_sum = qkv_part + gathered(
        10, raw_grad, raw_right, raw_left, side_act, False, hops, hops
    )
    qkv_sum, input_grad, layer_out, down_sum, proj_sum, sums = lax.optimization_barrier(
        (qkv_sum, input_grad, layer_out, down_sum, proj_sum, sums)
    )
    (small_sums,) = call(
        functools.partial(small_sums_kernel, n, m), 11, [((8, n * w), F32)],
        [pltpu.VMEM((m, 8, w), F32), pltpu.VMEM((8, w), F32)] + [sems(m - 1)] * 2 + [sems(n - 1)] * 2,
        V(sums), 10,
    )
    return (
        layer_out,
        input_grad,
        small_sums[0],
        small_sums[1],
        jnp.transpose(qkv_sum, (1, 0, 2)),
        proj_sum,
        small_sums[4],
        small_sums[2],
        small_sums[3],
        gu_sum,
        down_sum,
        small_sums[5],
    )


def solution(mesh):
    placed = (
        P("dp", "tensor"),
        P(),
        P(),
        P(None, None, "tensor"),
        P("tensor", None),
        P(),
        P(),
        P(),
        P(None, None, "tensor"),
        P("tensor", None),
        P(),
        P("dp", "tensor"),
    )
    return jax.shard_map(
        functools.partial(local, n=mesh.shape["tensor"], m=mesh.shape["dp"]),
        mesh=mesh,
        in_specs=placed,
        out_specs=(
            P("dp", "tensor"),
            P("dp", "tensor"),
            P(),
            P(),
            P("dp", None, "tensor"),
            P("tensor", "dp"),
            P(),
            P(),
            P(),
            P("dp", None, "tensor"),
            P("tensor", "dp"),
            P(),
        ),
        check_vma=False,
    )
```

```python
import functools
import math

import jax
import jax.numpy as jnp
from jax import lax
from jax.experimental import pallas as pl
from jax.experimental.pallas import tpu as pltpu
from jax.sharding import PartitionSpec as P

D = 4096
HD = 128
GRID = 14
EXTRA = 5
PATCH = 196
SEQ = 201
EPS = 1e-06
LANE = 128
BF = jnp.bfloat16
F32 = jnp.float32
MESH = pl.DeviceIdType.MESH
ROWS = (((0,), (0,)), ((), ()))
COLS = (((1,), (1,)), ((), ()))


def rope_tables():
    quarter = HD // 4
    theta = (
        2.0
        * math.pi
        * jnp.exp(jnp.arange(quarter, dtype=jnp.float32) * (-4.0 * math.log(100.0) / HD))
    )
    places = jnp.arange(PATCH, dtype=jnp.int32)
    row_pos = ((places // GRID).astype(jnp.float32) + 0.5) * (2.0 / GRID) - 1.0
    col_pos = ((places % GRID).astype(jnp.float32) + 0.5) * (2.0 / GRID) - 1.0
    angles = jnp.concatenate(
        [row_pos[:, None] * theta[None, :], col_pos[:, None] * theta[None, :]], axis=1
    )
    angles = jnp.concatenate([jnp.zeros((EXTRA, HD // 2), jnp.float32), angles], axis=0)
    return (jnp.cos(angles), jnp.sin(angles))


def rotate(vectors, cosines, sines):
    halfway = HD // 2
    leading = vectors[..., :halfway]
    trailing = vectors[..., halfway:]
    cos_b = cosines[:, None, :]
    sin_b = sines[:, None, :]
    return jnp.concatenate(
        [leading * cos_b - trailing * sin_b, leading * sin_b + trailing * cos_b], axis=-1
    )


def greet(n, m=1):
    me = lax.axis_index("tensor")
    you = lax.axis_index("dp")
    barrier = pltpu.get_barrier_semaphore()
    for k in range(1, n):
        pl.semaphore_signal(
            barrier, inc=1, device_id={"tensor": lax.rem(me + k, n)}, device_id_type=MESH
        )
    for k in range(1, m):
        pl.semaphore_signal(
            barrier, inc=1, device_id={"dp": lax.rem(you + k, m)}, device_id_type=MESH
        )
    pl.semaphore_wait(barrier, n + m - 2)


def send(src, dst, send_sem, recv_sem, peer):
    return pltpu.make_async_remote_copy(
        src_ref=src,
        dst_ref=dst,
        send_sem=send_sem,
        recv_sem=recv_sem,
        device_id={"tensor": peer},
        device_id_type=MESH,
    )


def send_dp(src, dst, send_sem, recv_sem, peer):
    return pltpu.make_async_remote_copy(
        src_ref=src,
        dst_ref=dst,
        send_sem=send_sem,
        recv_sem=recv_sem,
        device_id={"dp": peer},
        device_id_type=MESH,
    )


class Hop:
    def __init__(self, k, m, right_src, left_src, right_dst, left_dst, sem):
        you = lax.axis_index("dp")
        z, last = you // 2, m // 2 - 1
        right = send_dp(right_src, right_dst, sem.at[0], sem.at[1], lax.rem(you + 2, m))
        left = send_dp(left_src, left_dst, sem.at[2], sem.at[3], lax.rem(you + m - 2, m))
        self.steps = [
            (right, (z >= k - 1) & (z < last), z >= k),
            (left, (z <= last - k + 1) & (z > 0), z <= last - k),
        ]

    def start(self):
        for copy, sends, _ in self.steps:
            pl.when(sends)(copy.start)

    def wait(self):
        for copy, sends, gets in self.steps:
            pl.when(sends)(copy.wait_send)
            pl.when(gets)(copy.wait_recv)


class End:
    def __init__(self, m, part_ref, at, right_dst, left_dst, sem):
        you = lax.axis_index("dp")
        z, last = you // 2, m // 2 - 1
        some = pl.ds(at, right_dst.shape[1])
        right = send_dp(
            part_ref.at[last, :, some], right_dst, sem.at[0], sem.at[1], lax.rem(you + 2, m)
        )
        left = send_dp(
            part_ref.at[0, :, some], left_dst, sem.at[2], sem.at[3], lax.rem(you + m - 2, m)
        )
        self.steps = [(right, z == 0, z == 1), (left, z == last, z == last - 1)]

    start = Hop.start
    wait = Hop.wait


class Exchange:
    def __init__(self, m, pieces, full_ref, out_ref, ssem, rsem, lsem):
        you = lax.axis_index("dp")
        piece = lax.rem(lax.axis_index("tensor"), pieces)
        self.copies = []
        for k in range(m):
            peer = lax.rem(you + k, m)
            cols = pl.ds(pl.multiple_of((peer * pieces + piece) * LANE, LANE), LANE)
            if k:
                copy = send_dp(
                    full_ref.at[:, cols], out_ref.at[you], ssem.at[k - 1], rsem.at[k - 1], peer
                )
            else:
                copy = pltpu.make_async_copy(full_ref.at[:, cols], out_ref.at[you], lsem)
            self.copies.append(copy)

    def start(self):
        for copy in self.copies:
            copy.start()

    def wait(self):
        for copy in self.copies:
            copy.wait()


def chunks(width, body):
    def step(j, carry):
        body(pl.ds(pl.multiple_of(j * LANE, LANE), LANE))
        return carry

    lax.fori_loop(0, width // LANE, step, 0)


def spread(column, rows):
    return jnp.broadcast_to(column, (rows, LANE))


def beside(me):
    return me + 1 - 2 * lax.rem(me, 2), me + 2 - 4 * (me // 2)


class Gather:
    def __init__(self, n, own_ref, dest, ssem, rsem):
        me = lax.axis_index("tensor")
        w = own_ref.shape[1]
        self.square = n == 4
        if self.square:
            x, y = beside(me)
            half = w // 2
            part = lambda i: own_ref.at[:, i * half:(i + 1) * half]
            to = lambda i, src, owner, at, peer: send(
                src, dest(owner, at * half, half), ssem.at[i], rsem.at[i], peer
            )
            self.copies = [
                to(0, part(0), me, 0, x), to(1, part(1), me, 1, y),
                to(2, part(1), me, 1, x), to(3, part(0), me, 0, y),
            ]
            self.passed = [
                to(4, dest(x, 0, half), x, 0, y), to(5, dest(y, half, half), y, 1, x)
            ]
        else:
            self.copies = [
                send(own_ref, dest(me, 0, w), ssem.at[k - 1], rsem.at[k - 1], lax.rem(me + k, n))
                for k in range(1, n)
            ]

    def start(self):
        for copy in self.copies:
            copy.start()

    def relay(self):
        if self.square:
            for copy, passed in zip(self.copies, self.passed):
                copy.wait_recv()
                passed.start()

    def wait(self):
        if self.square:
            for copy in self.copies:
                copy.wait_send()
            for copy in self.copies[2:]:
                copy.wait_recv()
            wait_all(self.passed)
        else:
            wait_all(self.copies)


class Scatter:
    def __init__(self, n, w, part_ref, slots, come, go, ssem, rsem):
        me = lax.axis_index("tensor")
        self.n, self.w, self.part, self.slots, self.come, self.go = n, w, part_ref, slots, come, go
        self.square = n == 4
        cols = lambda owner, at, size: part_ref.at[:, pl.ds(pl.multiple_of(owner * w + at, LANE), size)]
        if self.square:
            x, y = beside(me)
            far = 3 - me
            half = w // 2
            self.half, self.x, self.y = half, x, y
            to = lambda i, src, dst, peer: send(src, dst, ssem.at[i], rsem.at[i], peer)
            low, high = slice(0, half), slice(half, w)
            self.first = [
                to(0, cols(far, 0, half), come.at[0], x), to(1, cols(far, half, half), come.at[1], y)
            ]
            self.second = [
                to(2, cols(x, 0, half), slots.at[0, :, low], x),
                to(3, cols(y, half, half), slots.at[1, :, high], y),
            ]
            self.third = [
                to(4, go.at[0], slots.at[0, :, high], x), to(5, go.at[1], slots.at[1, :, low], y)
            ]
            self.order = [(far, 0), (far, 1), (x, 0), (y, 1), (x, 1), (y, 0), (me, 0), (me, 1)]
        else:
            self.first = [
                send(cols(lax.rem(me + k, n), 0, w), slots.at[k - 1], ssem.at[k - 1], rsem.at[k - 1],
                     lax.rem(me + k, n))
                for k in range(1, n)
            ]
            self.second = self.third = []

    def start(self):
        for copy in self.first + self.second:
            copy.start()

    def relay(self):
        if self.square:
            half = self.half
            for i, (owner, at) in enumerate(((self.x, half), (self.y, 0))):
                self.first[1 - i].wait_recv()

                def add(cols, i=i, owner=owner, at=at):
                    wide = pl.ds(pl.multiple_of(owner * self.w + at + cols.start, LANE), LANE)
                    self.go[i, :, cols] = (
                        self.part[:, wide].astype(F32) + self.come[1 - i, :, cols].astype(F32)
                    ).astype(BF)

                chunks(half, add)
                self.third[i].start()

    def wait(self):
        if self.square:
            for copy in self.first:
                copy.wait_send()
            wait_all(self.second + self.third)
        else:
            wait_all(self.first)

    def total(self, cols, wide):
        total = self.part[:, wide].astype(F32)
        for k in range(self.slots.shape[0]):
            total = total + self.slots[k, :, cols].astype(F32)
        return total


def scatter_room(n, rows, w):
    count, half = (2, w // 2) if n == 4 else (n - 1, LANE)
    return [
        pltpu.VMEM((count, rows, w), BF), pltpu.VMEM((2, rows, half), BF), pltpu.VMEM((2, rows, half), BF),
        sems(6 if n == 4 else n - 1), sems(6 if n == 4 else n - 1),
    ]


def gather_sems(n):
    return [sems(6 if n == 4 else n - 1)] * 2


def stream(count, fetch, compute):
    fetch(0, 0).start()

    def step(i, carry):
        slot = lax.rem(i, 2)

        @pl.when(i + 1 < count)
        def _():
            fetch(i + 1, 1 - slot).start()

        fetch(i, slot).wait()
        compute(i, slot)
        return carry

    lax.fori_loop(0, count, step, 0)


def wait_all(copies):
    for copy in copies:
        copy.wait()


def row_stats(n, rows, w, all_ref, acc, mean_ref, inv_ref):
    acc[...] = jnp.zeros_like(acc)

    def add(cols):
        total = all_ref[0, :, cols].astype(F32)
        for k in range(1, n):
            total = total + all_ref[k, :, cols].astype(F32)
        acc[...] += total

    chunks(w, add)
    mean_ref[...] = spread(jnp.sum(acc[...], axis=1, keepdims=True) * (1.0 / D), rows)
    acc[...] = jnp.zeros_like(acc)

    def square(cols):
        mean = mean_ref[...]
        total = jnp.zeros_like(mean)
        for k in range(n):
            center = all_ref[k, :, cols].astype(F32) - mean
            total = total + center * center
        acc[...] += total

    chunks(w, square)
    var = jnp.sum(acc[...], axis=1, keepdims=True) * (1.0 / D)
    inv_ref[...] = spread(lax.rsqrt(var + EPS), rows)


def write_act(n, w, all_ref, mean_ref, inv_ref, gain_ref, bias_ref, act_ref):
    def act(cols):
        for k in range(n):
            wide = pl.ds(pl.multiple_of(k * w + cols.start, LANE), LANE)
            center = all_ref[k, :, cols].astype(F32) - mean_ref[...]
            act_ref[:, wide] = (
                center * inv_ref[...] * gain_ref[:, wide] + bias_ref[:, wide]
            ).astype(BF)

    chunks(w, act)


def part_rows(w_ref, out_ref, ibuf, obuf, isem, osem, also):
    size = ibuf.shape[1]
    count = w_ref.shape[0] // size

    def rows_of(i):
        return pl.ds(pl.multiple_of(i * size, size), size)

    def fetch(i, slot):
        return pltpu.make_async_copy(w_ref.at[rows_of(i)], ibuf.at[slot], isem.at[slot])

    def put(i, slot):
        return pltpu.make_async_copy(obuf.at[slot], out_ref.at[:, rows_of(i)], osem.at[slot])

    fetch(0, 0).start()

    def step(i, carry):
        slot = lax.rem(i, 2)
        also(i)

        @pl.when(i + 1 < count)
        def _():
            fetch(i + 1, 1 - slot).start()

        fetch(i, slot).wait()

        @pl.when(i >= 2)
        def _():
            put(i - 2, slot).wait()

        obuf[slot] = jnp.swapaxes(ibuf[slot], 0, 1)
        put(i, slot).start()
        return carry

    lax.fori_loop(0, count, step, 0)
    for i in (count - 2, count - 1):
        put(i, i % 2).wait()


def first_norm_kernel(
    n, x_ref, gain_ref, bias_ref, cot_ref, w_ref, act_ref, mean_ref, inv_ref, parted_ref, cots_ref, late_ref,
    all_ref, acc, ssem, rsem, ibuf, obuf, isem, osem, csem, crem,
):
    rows, w = x_ref.shape
    me = lax.axis_index("tensor")
    greet(n)
    dest = lambda owner, at, size: all_ref.at[owner, :, pl.ds(at, size)]
    gather = Gather(n, x_ref, dest, ssem, rsem)
    gather.start()
    all_ref[me] = x_ref[...]
    early_ref = cot_ref.at[:, :cots_ref.shape[2]]
    into = lambda owner, at, size: cots_ref.at[owner, :, pl.ds(at, size)]
    early = Gather(n, early_ref, into, csem, crem)

    def between(i):
        @pl.when(i == 6)
        def _():
            gather.relay()
            early.start()

    cots_ref[me] = early_ref[...]
    late_ref[...] = cot_ref[:, cots_ref.shape[2]:]
    part_rows(w_ref, parted_ref, ibuf, obuf, isem, osem, between)
    gather.wait()
    row_stats(n, rows, w, all_ref, acc, mean_ref, inv_ref)
    early.relay()
    write_act(n, w, all_ref, mean_ref, inv_ref, gain_ref, bias_ref, act_ref)
    early.wait()


def second_norm_kernel(
    n, m, pieces, part_ref, x_ref, scale_ref, gain_ref, bias_ref, mlp_ref, cot_ref, cots_ref, mixed_ref,
    w_down_ref, attn_ref, res_ref, act_ref, mean_ref, inv_ref, hgrad_ref, kcot_ref, *refs,
):
    hops = m // 2 - 1
    rights, lefts, refs = refs[:hops], refs[hops:2 * hops], refs[2 * hops:]
    (slots, come, go, ssem, rsem, own_ref, all_ref, acc, ssem2, rsem2, hsem,
     css, crs, cls, bgrad, wbuf, wsem) = refs
    rows, w = x_ref.shape
    me = lax.axis_index("tensor")
    greet(n, m)
    scatter = Scatter(n, w, part_ref, slots, come, go, ssem, rsem)
    scatter.start()
    line = [
        Hop(k, m, rights[k - 2] if k > 1 else mixed_ref, lefts[k - 2] if k > 1 else mixed_ref,
            rights[k - 1], lefts[k - 1], hsem.at[k - 1])
        for k in range(1, hops + 1)
    ]
    line[0].start()

    ahead = cots_ref.shape[2]
    for owner in range(n):

        def early(cols, owner=owner):
            wide = pl.ds(pl.multiple_of(owner * w + cols.start, LANE), LANE)
            bgrad[:, wide] = (mlp_ref[:, wide] * cots_ref[owner, :, cols].astype(F32)).astype(BF)

        def late(cols, owner=owner):
            wide = pl.ds(pl.multiple_of(owner * w + ahead + cols.start, LANE), LANE)
            from_ = pl.ds(pl.multiple_of(owner * (w - ahead) + cols.start, LANE), LANE)
            bgrad[:, wide] = (mlp_ref[:, wide] * cot_ref[:, from_].astype(F32)).astype(BF)

        chunks(ahead, early)
        chunks(w - ahead, late)
    side = Exchange(m, pieces, bgrad, kcot_ref, css, crs, cls)
    side.start()
    tile = wbuf.shape[1]
    count = hgrad_ref.shape[1] // tile

    def fetch(i, slot):
        return pltpu.make_async_copy(
            w_down_ref.at[pl.ds(pl.multiple_of(i * tile, tile), tile), :], wbuf.at[slot], wsem.at[slot]
        )

    def compute(i, slot):
        hgrad_ref[:, pl.ds(pl.multiple_of(i * tile, tile), tile)] = lax.dot_general(
            bgrad[...], wbuf[slot], COLS, preferred_element_type=F32
        )

        @pl.when(i == count // 2)
        def _():
            scatter.relay()

    stream(count, fetch, compute)
    line[0].wait()
    if hops > 1:
        line[1].start()
    scatter.wait()

    def add(cols):
        wide = pl.ds(pl.multiple_of(me * w + cols.start, LANE), LANE)
        total = scatter.total(cols, wide)
        attn_ref[:, cols] = total
        res = x_ref[:, cols].astype(F32) + scale_ref[:, wide] * total
        res_ref[:, cols] = res
        own_ref[:, cols] = res.astype(BF)

    chunks(w, add)
    dest = lambda owner, at, size: all_ref.at[owner, :, pl.ds(at, size)]
    gather = Gather(n, own_ref, dest, ssem2, rsem2)
    gather.start()
    all_ref[me] = own_ref[...]
    gather.relay()
    for k in range(1, hops - 1):
        line[k].wait()
        line[k + 1].start()
    gather.wait()
    row_stats(n, rows, w, all_ref, acc, mean_ref, inv_ref)
    write_act(n, w, all_ref, mean_ref, inv_ref, gain_ref, bias_ref, act_ref)
    line[-1].wait()
    side.wait()


def norm_back(n, w, load_total, grad_ref, base_ref, mean_ref, inv_ref, gain_ref,
              sums, acc, acc2, stat_own, stats, ssem, rsem, out):
    rows = grad_ref.shape[0]
    me = lax.axis_index("tensor")
    acc[...] = jnp.zeros_like(acc)
    acc2[...] = jnp.zeros_like(acc2)

    def first(cols):
        wide = pl.ds(pl.multiple_of(me * w + cols.start, LANE), LANE)
        total = load_total(cols, wide)
        grad_ref[:, cols] = total
        normed = (base_ref[:, cols].astype(F32) - mean_ref[...]) * inv_ref[...]
        sums[0:1, cols] = jnp.sum(total * normed, axis=0, keepdims=True)
        sums[1:2, cols] = jnp.sum(total, axis=0, keepdims=True)
        scaled = total * gain_ref[:, wide]
        acc[...] += scaled
        acc2[...] += scaled * normed

    chunks(w, first)
    ones = jnp.ones((8, LANE), F32)
    high = lax.Precision.HIGHEST
    plain = lax.dot_general(ones, acc[...], COLS, precision=high, preferred_element_type=F32)
    cross = lax.dot_general(ones, acc2[...], COLS, precision=high, preferred_element_type=F32)
    line = lax.broadcasted_iota(jnp.int32, (8, rows), 0)
    stat_own[...] = jnp.where(line < 4, plain, cross)
    copies = [
        send(stat_own, stats.at[me], ssem.at[k - 1], rsem.at[k - 1], lax.rem(me + k, n))
        for k in range(1, n)
    ]
    for copy in copies:
        copy.start()
    wait_all(copies)
    both = stat_own[...]
    for k in range(1, n):
        both = both + stats[lax.rem(me + k, n)]
    both = both * (1.0 / D)
    pick = lax.broadcasted_iota(jnp.int32, (8, LANE), 0)
    acc[...] = lax.dot_general(
        both, (pick == 0).astype(F32), ROWS, precision=high, preferred_element_type=F32
    )
    acc2[...] = lax.dot_general(
        both, (pick == 4).astype(F32), ROWS, precision=high, preferred_element_type=F32
    )

    def second(cols):
        wide = pl.ds(pl.multiple_of(me * w + cols.start, LANE), LANE)
        normed = (base_ref[:, cols].astype(F32) - mean_ref[...]) * inv_ref[...]
        scaled = grad_ref[:, cols] * gain_ref[:, wide]
        out(cols, wide, inv_ref[...] * (scaled - acc[...] - normed * acc2[...]))

    chunks(w, second)


def second_back_kernel(
    n, m, gate_ref, up_ref, cot_ref, res_ref, attn_ref, mean_ref, inv_ref, gain_ref, scale_ref,
    right_ref, left_ref, gu_ref, w_ref, rgrad_ref, agrad_ref, sums_ref, gu_right, gu_left, *refs,
):
    hops = m // 2 - 1
    rights = (right_ref,) + refs[:hops - 1]
    lefts = (left_ref,) + refs[hops - 1:2 * hops - 2]
    (part_ref, slots, come, go, ssem, rsem, grad_ref, own_ref, acc, acc2, stat_own, stats,
     ssem2, rsem2, ssem3, rsem3, lsem, hsem, gsem, wbuf, wsem) = refs[2 * hops - 2:]
    w = cot_ref.shape[1]
    me = lax.axis_index("tensor")
    greet(n, m)
    line = [
        Hop(k, m, rights[k - 2], lefts[k - 2], rights[k - 1], lefts[k - 1], hsem.at[k - 2])
        for k in range(2, hops + 1)
    ]
    line[0].start()
    first = End(m, gu_ref, 0, gu_right, gu_left, gsem)
    first.start()
    scatter = Scatter(n, w, part_ref, slots, come, go, ssem, rsem)
    tile = wbuf.shape[2]
    count = D // tile

    def spot(i):
        if not scatter.square:
            return pl.ds(pl.multiple_of(i * tile, LANE), tile)
        at = 0
        for k, (owner, half) in enumerate(scatter.order):
            at = at + jnp.where(i == k, owner * w + half * tile, 0)
        return pl.ds(pl.multiple_of(at, LANE), tile)

    def fetch(i, slot):
        return pltpu.make_async_copy(w_ref.at[:, spot(i), :], wbuf.at[slot], wsem.at[slot])

    def compute(i, slot):
        part_ref[:, spot(i)] = (
            lax.dot_general(gate_ref[...], wbuf[slot, 0], COLS, preferred_element_type=F32)
            + lax.dot_general(up_ref[...], wbuf[slot, 1], COLS, preferred_element_type=F32)
        ).astype(BF)
        if scatter.square:
            for k, copy in enumerate(scatter.first + scatter.second):
                pl.when(i == k)(copy.start)
            pl.when(i == 5)(scatter.relay)

    stream(count, fetch, compute)
    if not scatter.square:
        scatter.start()
    scatter.wait()
    line[0].wait()
    for hop in line[1:2]:
        hop.start()
    sums_ref[...] = jnp.zeros_like(sums_ref)

    def out(cols, wide, back):
        res_grad = cot_ref[:, cols].astype(F32) + back
        rgrad_ref[:, cols] = res_grad
        sums_ref[2:3, cols] = jnp.sum(res_grad * attn_ref[:, cols], axis=0, keepdims=True)
        own_ref[:, cols] = (scale_ref[:, wide] * res_grad).astype(BF)

    norm_back(n, w, scatter.total, grad_ref, res_ref, mean_ref, inv_ref, gain_ref,
              sums_ref, acc, acc2, stat_own, stats, ssem2, rsem2, out)
    dest = lambda owner, at, size: agrad_ref.at[:, pl.ds(pl.multiple_of(owner * w + at, LANE), size)]
    gather = Gather(n, own_ref, dest, ssem3, rsem3)
    gather.start()
    local = pltpu.make_async_copy(own_ref, dest(me, 0, w), lsem)
    local.start()
    gather.relay()
    for k in range(1, len(line)):
        line[k].wait()
        if k + 1 < len(line):
            line[k + 1].start()
    local.wait()
    gather.wait()
    first.wait()


def first_back_kernel(
    n, grad_in, x_ref, mean_ref, inv_ref, gain_ref, small_ref,
    part_ref, cot_ref, scale_ref,
    igrad_ref, sums, out_ref,
    slots, come, go, ssem, rsem, grad_ref, acc, acc2, stat_own, stats, ssem2, rsem2,
):
    w = x_ref.shape[1]
    greet(n)
    scatter = Scatter(n, w, part_ref, slots, come, go, ssem, rsem)
    scatter.start()
    sums[...] = small_ref[...]
    scatter.relay()

    def load_total(cols, wide):
        return grad_in[:, cols].astype(F32)

    def out(cols, wide, back):
        igrad_ref[:, cols] = back

    norm_back(n, w, load_total, grad_ref, x_ref, mean_ref, inv_ref, gain_ref,
              sums, acc, acc2, stat_own, stats, ssem2, rsem2, out)
    scatter.wait()
    me = lax.axis_index("tensor")

    def add(cols):
        wide = pl.ds(pl.multiple_of(me * w + cols.start, LANE), LANE)
        total = scatter.total(cols, wide)
        out_ref[:, cols] = scale_ref[:, wide] * total
        sums[5:6, cols] = jnp.sum(cot_ref[:, cols].astype(F32) * total, axis=0, keepdims=True)

    chunks(w, add)


def mate_of(you):
    return you + 1 - 2 * lax.rem(you, 2)


def pair_grad_kernel(
    m, act_ref, gate_ref, up_ref, hidden_ref, out_ref, right_ref, left_ref,
    acts, mates, gates, ups, flip, obuf, asem, arem, gsem, grem, lsem, hsem, osem,
):
    line = m // 2
    you = lax.axis_index("dp")
    core, mate = lax.rem(you, 2), mate_of(you)
    width = acts.shape[-1]
    tile = 512
    greet(1, m)
    hop = Hop(1, m, hidden_ref, hidden_ref, right_ref, left_ref, hsem)
    copies = [
        send_dp(gate_ref, gates, gsem.at[0], grem.at[0], mate),
        send_dp(up_ref, ups, gsem.at[1], grem.at[1], mate),
    ]
    locals_ = []
    for k in range(line):
        theirs = pl.ds(pl.multiple_of((2 * k + 1 - core) * width, LANE), width)
        ours = pl.ds(pl.multiple_of((2 * k + core) * width, LANE), width)
        copies.append(send_dp(act_ref.at[:, theirs], mates.at[k], asem.at[k], arem.at[k], mate))
        locals_.append(pltpu.make_async_copy(act_ref.at[:, ours], acts.at[k], lsem.at[k]))
    for copy in locals_ + copies:
        copy.start()
    hop.start()
    for copy in locals_:
        copy.wait()

    def turn(which, source):
        def step(k, carry):
            flip[which, k] = source[k].T
            return carry

        lax.fori_loop(0, line, step, 0)

    turn(0, acts)
    for copy in copies:
        copy.wait()
    turn(1, mates)
    def put(k):
        slot = lax.rem(k, 2)
        return pltpu.make_async_copy(obuf.at[slot], out_ref.at[k], osem.at[slot])

    def chip(k, carry):
        slot = lax.rem(k, 2)

        @pl.when(k >= 2)
        def _():
            put(k - 2).wait()

        for j, (near, far) in enumerate(((gate_ref, gates), (up_ref, ups))):

            def step(i, carry, j=j, near=near, far=far):
                cols = pl.ds(pl.multiple_of(i * tile, tile), tile)
                obuf[slot, j, :, cols] = (
                    jnp.dot(flip[0, k], near[:, cols], preferred_element_type=F32)
                    + jnp.dot(flip[1, k], far[:, cols], preferred_element_type=F32)
                ).astype(BF)
                return carry

            lax.fori_loop(0, gate_ref.shape[1] // tile, step, 0)
        put(k).start()
        return carry

    lax.fori_loop(0, line, chip, 0)
    for k in range(max(line - 2, 0), line):
        put(k).wait()
    hop.wait()


class SmallSums:
    def __init__(self, n, m, sums, out, parts, total, dss, drs, tss, trs):
        self.out, self.sums, self.parts, self.total = out, sums, parts, total
        me, you = lax.axis_index("tensor"), lax.axis_index("dp")
        w = sums.shape[1]
        self.m, self.you = m, you
        self.mine = pl.ds(pl.multiple_of(me * w, w), w)
        self.dp = [
            send_dp(sums, parts.at[you], dss.at[k - 1], drs.at[k - 1], lax.rem(you + k, m))
            for k in range(1, m)
        ]
        self.tensor = [
            send(total, out.at[:, self.mine], tss.at[k - 1], trs.at[k - 1], lax.rem(me + k, n))
            for k in range(1, n)
        ]

    def start(self):
        for copy in self.dp:
            copy.start()

    def finish(self):
        self.parts[self.you] = self.sums[...]
        wait_all(self.dp)
        total = self.parts[0]
        for k in range(1, self.m):
            total = total + self.parts[k]
        self.total[...] = total
        for copy in self.tensor:
            copy.start()
        self.out[:, self.mine] = total
        wait_all(self.tensor)


def small_sums_kernel(n, m, sums, out_ref, parts, total, *room):
    greet(n, m)
    small = SmallSums(n, m, sums, out_ref, parts, total, *room)
    small.start()
    small.finish()


def gathered_grad_kernel(m, turned, first, last, *refs):
    hops = m // 2 - 1
    you = lax.axis_index("dp")
    core, mate, z = lax.rem(you, 2), mate_of(you), you // 2
    todo = []
    refs = list(refs)
    for k in range(first, last + 1):
        if k == 0:
            todo.append((None, refs.pop(0), z))
        else:
            todo.append((z >= k, refs.pop(0), z - k))
            todo.append((z <= hops - k, refs.pop(0), z + k))
    side_ref = refs.pop(0)
    out_ref, blocks, flip, lsem, ssem, rsem = refs
    greet(1, m)
    copies = []
    for at, (cond, src, chip) in enumerate(todo):
        near = pltpu.make_async_copy(src, blocks.at[at, core], lsem.at[at])
        far = send_dp(src, blocks.at[at, core], ssem.at[at], rsem.at[at], mate)
        copies.append((cond, near, far))

    def when(cond, body):
        body() if cond is None else pl.when(cond)(body)

    def go(near, far):
        near.start()
        far.start()

    def done(near, far):
        near.wait()
        far.wait()

    def unit_of(at):
        k = (at + 1) // 2 if first == 0 else first
        right = lax.rem(at, 2) == (1 if first == 0 else 0)
        there = (k == 0) | (right & (z >= k)) | (jnp.logical_not(right) & (z <= hops - k))
        return there, jnp.where(right, z - k, z + k)

    def turn(i, carry):
        at, c = i // 2, lax.rem(i, 2)
        there, chip = unit_of(at)

        @pl.when(there)
        def _():
            flip[at, c] = side_ref[2 * chip + c].T

        return carry

    for cond, near, far in copies:
        when(cond, functools.partial(go, near, far))
    lax.fori_loop(0, 2 * len(todo), turn, 0)
    for cond, near, far in copies:
        when(cond, functools.partial(done, near, far))
    tile = 512
    parts, width = out_ref.shape[0], blocks.shape[-1]
    count = width // tile
    out_ref[...] = jnp.zeros_like(out_ref)

    def unit(i, carry):
        at, j, at_col = i // (parts * count), lax.rem(i // count, parts), lax.rem(i, count)
        there, _ = unit_of(at)

        @pl.when(there)
        def _():
            cols = pl.ds(pl.multiple_of(at_col * tile, tile), tile)
            total = jnp.dot(
                flip[at, 0], blocks[at, 0, j, :, cols], preferred_element_type=F32
            ) + jnp.dot(flip[at, 1], blocks[at, 1, j, :, cols], preferred_element_type=F32)
            if turned:
                out_ref[j, cols, :] += total.T
            else:
                out_ref[j, :, cols] += total

        return carry

    lax.fori_loop(0, len(todo) * parts * count, unit, 0)


def qkv_kernel(act_ref, w_ref, cos_ref, sin_ref, out_ref):
    raw = jnp.dot(act_ref[...], w_ref[...], preferred_element_type=F32)
    part = pl.program_id(0)

    @pl.when(part < 2)
    def _():
        for h in range(raw.shape[1] // HD):
            cols = slice(h * HD, (h + 1) * HD)
            t = raw[:, cols]
            out_ref[:, cols] = (
                t * cos_ref[...] + pltpu.roll(t, HD // 2, 1) * sin_ref[...]
            ).astype(BF)

    @pl.when(part == 2)
    def _():
        out_ref[...] = raw.astype(BF)


def qkv_matmul(act, w_j, cos2, sin2):
    rows = act.shape[0]
    inner = w_j.shape[2]
    tile = min(512, inner)
    return pl.pallas_call(
        qkv_kernel,
        grid=(3, inner // tile),
        out_shape=jax.ShapeDtypeStruct((3, rows, inner), BF),
        in_specs=[
            pl.BlockSpec((rows, D), lambda j, i: (0, 0)),
            pl.BlockSpec((None, D, tile), lambda j, i: (j, 0, i)),
            pl.BlockSpec((rows, HD), lambda j, i: (0, 0)),
            pl.BlockSpec((rows, HD), lambda j, i: (0, 0)),
        ],
        out_specs=pl.BlockSpec((None, rows, tile), lambda j, i: (j, 0, i)),
        compiler_params=pltpu.CompilerParams(vmem_limit_bytes=40 << 20),
        cost_estimate=pl.CostEstimate(
            flops=2 * rows * D * 3 * inner, bytes_accessed=6 * D * inner, transcendentals=0
        ),
    )(act, w_j, cos2, sin2)


def attention_probs(q, k, same):
    scores = lax.dot_general(k, q, COLS, preferred_element_type=F32) * (HD ** (-0.5))
    scores = jnp.where(same, scores, -jnp.inf)
    top = jnp.max(scores, axis=0, keepdims=True)
    weight = jnp.exp(scores - top)
    return weight / jnp.sum(weight, axis=0, keepdims=True)


def same_image(rows):
    one = lax.broadcasted_iota(jnp.int32, (rows, rows), 0)
    two = lax.broadcasted_iota(jnp.int32, (rows, rows), 1)
    image = lambda i: sum((i >= SEQ * k).astype(jnp.int32) for k in range(1, rows // SEQ))
    return image(one) == image(two)


def attention_kernel(qkv_ref, w_hbm, mixed_ref, part_ref, w_ref, wsem):
    rows, inner = mixed_ref.shape
    weights = pltpu.make_async_copy(w_hbm, w_ref, wsem)
    weights.start()

    def head(h, carry):
        cols = pl.ds(pl.multiple_of(h * HD, HD), HD)
        probs = attention_probs(qkv_ref[0, :, cols], qkv_ref[1, :, cols], same_image(rows))
        value = qkv_ref[2, :, cols].astype(F32).T.astype(BF)
        mixed = jnp.dot(value, probs.astype(BF), preferred_element_type=F32)
        mixed_ref[:, cols] = mixed.T.astype(BF)
        return carry

    lax.fori_loop(0, inner // HD, head, 0)
    weights.wait()

    def tile(i, carry):
        cols = pl.ds(pl.multiple_of(i * 512, 512), 512)
        part_ref[:, cols] = jnp.dot(
            mixed_ref[...], w_ref[:, cols], preferred_element_type=F32
        ).astype(BF)
        return carry

    lax.fori_loop(0, D // 512, tile, 0)


def attention_back_kernel(
    m, pieces, agrad_ref, qkv_ref, cos_ref, sin_ref, full_ref, w_ref,
    out_ref, kattn_ref, mgrad, ass, ars, als, wbuf, wsem,
):
    rows, inner = mgrad.shape
    greet(1, m)
    side = Exchange(m, pieces, full_ref, kattn_ref, ass, ars, als)
    side.start()
    step = min(256, inner)

    def fetch(i, slot):
        some = pl.ds(pl.multiple_of(i * step, step), step)
        return pltpu.make_async_copy(w_ref.at[some, :], wbuf.at[slot], wsem.at[slot])

    def tile(i, slot):
        cols = pl.ds(pl.multiple_of(i * step, step), step)
        mgrad[:, cols] = lax.dot_general(
            agrad_ref[...], wbuf[slot], COLS, preferred_element_type=F32
        ).astype(BF)

    stream(inner // step, fetch, tile)

    def back(t):
        return t * cos_ref[...] - pltpu.roll(t, HD // 2, 1) * sin_ref[...]

    def head(h, carry):
        cols = pl.ds(pl.multiple_of(h * HD, HD), HD)
        q, k, v = qkv_ref[0, :, cols], qkv_ref[1, :, cols], qkv_ref[2, :, cols]
        grad = mgrad[:, cols]
        probs = attention_probs(q, k, same_image(rows))
        prob_grad = lax.dot_general(v, grad, COLS, preferred_element_type=F32)
        delta = jnp.sum(probs * prob_grad, axis=0, keepdims=True)
        score_grad = (probs * (prob_grad - delta)).astype(BF)
        scale = HD ** (-0.5)
        flipped = k.astype(F32).T.astype(BF)
        q_grad = jnp.dot(flipped, score_grad, preferred_element_type=F32).T * scale
        k_grad = jnp.dot(score_grad, q, preferred_element_type=F32) * scale
        out_ref[0, :, cols] = back(q_grad).astype(BF)
        out_ref[1, :, cols] = back(k_grad).astype(BF)
        out_ref[2, :, cols] = jnp.dot(
            probs.astype(BF), grad, preferred_element_type=F32
        ).astype(BF)
        return carry

    lax.fori_loop(0, inner // HD, head, 0)
    side.wait()


def gate_kernel(
    m, pieces, act_ref, w_ref, hgrad_ref, full_ref, hidden_ref, gate_ref, up_ref, kact_ref, ass, ars, als
):
    side = Exchange(m, pieces, full_ref, kact_ref, ass, ars, als)

    @pl.when(pl.program_id(0) == 0)
    def _():
        greet(1, m)
        side.start()

    gate = jnp.dot(act_ref[...], w_ref[0], preferred_element_type=F32)
    up = jnp.dot(act_ref[...], w_ref[1], preferred_element_type=F32)
    sig = jax.nn.sigmoid(gate)
    grad = hgrad_ref[...]
    hidden_ref[...] = (gate * sig * up).astype(BF)
    gate_ref[...] = (grad * up * sig * (1.0 + gate * (1.0 - sig))).astype(BF)
    up_ref[...] = (grad * gate * sig).astype(BF)
    pl.when(pl.program_id(0) == pl.num_programs(0) - 1)(side.wait)


def gate_matmul(act, w_j, hidden_grad, act_one, m, pieces):
    rows, width = hidden_grad.shape
    tile = min(256, width)
    block = pl.BlockSpec((rows, tile), lambda i: (0, i))
    return pl.pallas_call(
        functools.partial(gate_kernel, m, pieces),
        grid=(width // tile,),
        out_shape=[jax.ShapeDtypeStruct((rows, width), BF)] * 3
        + [jax.ShapeDtypeStruct((m, rows, LANE), BF)],
        in_specs=[
            pl.BlockSpec((rows, D), lambda i: (0, 0)),
            pl.BlockSpec((2, D, tile), lambda i: (0, 0, i)),
            block,
            hb(),
        ],
        out_specs=[block] * 3 + [hb()],
        scratch_shapes=[sems(m - 1), sems(m - 1), pltpu.SemaphoreType.DMA],
        compiler_params=pltpu.CompilerParams(
            collective_id=12, has_side_effects=True, vmem_limit_bytes=48 << 20
        ),
    )(act, w_j, hidden_grad, act_one)


def back_kernel(g_ref, w_ref, out_ref):
    total = None
    for j in range(g_ref.shape[0]):
        term = lax.dot_general(g_ref[j], w_ref[j], COLS, preferred_element_type=F32)
        total = term if total is None else total + term
    out_ref[...] = total.astype(BF)


def back_matmul(grads, w_j):
    parts, rows, inner = grads.shape
    tile = 512
    return pl.pallas_call(
        back_kernel,
        grid=(D // tile,),
        out_shape=jax.ShapeDtypeStruct((rows, D), BF),
        in_specs=[
            pl.BlockSpec((parts, rows, inner), lambda i: (0, 0, 0)),
            pl.BlockSpec((parts, tile, inner), lambda i: (0, i, 0)),
        ],
        out_specs=pl.BlockSpec((rows, tile), lambda i: (0, i)),
        compiler_params=pltpu.CompilerParams(vmem_limit_bytes=40 << 20),
        cost_estimate=pl.CostEstimate(
            flops=rows * D * parts * inner * 100 // 500,
            bytes_accessed=800_000,
            transcendentals=0,
        ),
    )(grads, w_j)


def vm():
    return pl.BlockSpec(memory_space=pltpu.VMEM)


def hb():
    return pl.BlockSpec(memory_space=pltpu.HBM)


def sems(*shape):
    return pltpu.SemaphoreType.DMA(shape)


def call(kernel, ident, outs, scratch, args, micros=30):
    shapes = [jax.ShapeDtypeStruct(o[0], o[1]) for o in outs]
    return list(pl.pallas_call(
        kernel,
        out_shape=shapes,
        in_specs=[hb() if a[1] else vm() for a in args],
        out_specs=[hb() if len(o) > 2 else vm() for o in outs],
        scratch_shapes=scratch,
        compiler_params=pltpu.CompilerParams(
            collective_id=ident, has_side_effects=True, vmem_limit_bytes=56 << 20
        ),
        cost_estimate=pl.CostEstimate(
            flops=micros * 100_000_000, bytes_accessed=800_000, transcendentals=0
        ),
    )(*[a[0] for a in args]))


def join_kernel(one, two, three, out_ref):
    total = one[...].astype(F32) + two[...].astype(F32) + three[...].astype(F32)
    out_ref[...] = jnp.swapaxes(total, 0, 1)


def join(one, two, three):
    _, rows, width = one.shape
    size = 64
    block = pl.BlockSpec((2, size, width), lambda i: (0, i, 0))
    return pl.pallas_call(
        join_kernel,
        grid=(rows // size,),
        out_shape=jax.ShapeDtypeStruct((rows, 2, width), F32),
        in_specs=[block] * 3,
        out_specs=pl.BlockSpec((size, 2, width), lambda i: (i, 0, 0)),
        compiler_params=pltpu.CompilerParams(vmem_limit_bytes=32 << 20),
    )(one, two, three)


class LineReduce:
    def __init__(self, part, right, left, m):
        self.part, self.line, self.t = part, m // 2, 2
        self.z = lax.axis_index("dp") // 2
        right, left = (jnp.concatenate(pieces, axis=1).astype(F32) for pieces in (right, left))
        self.right = jnp.where(self.z >= 1, right, 0.0)
        self.left = jnp.where(self.z <= self.line - 2, left, 0.0)

    def take(self, i):
        i = jnp.clip(i, 0, self.line - 1)
        return lax.dynamic_index_in_dim(self.part, i, 0, keepdims=False).astype(F32)

    def step(self, after):
        line, t = self.line, self.t
        right = (self.take(self.z + line - t) + self.right).astype(BF)
        left = (self.take(self.z - line + t) + self.left).astype(BF)
        right, left = lax.optimization_barrier((right, left) + tuple(after))[:2]
        self.given = right, left
        self.right = lax.ppermute(
            right, "dp", [(2 * i + c, 2 * i + 2 + c) for i in range(t) for c in range(2)]
        ).astype(F32)
        self.left = lax.ppermute(
            left, "dp",
            [(2 * i + c, 2 * i - 2 + c) for i in range(line - t, line) for c in range(2)],
        ).astype(F32)
        self.t += 1

    def finish(self, after):
        while self.t < self.line:
            self.step(after)
        own = lax.dynamic_index_in_dim(self.part, self.z, 0, keepdims=False)
        return join(own, self.right.astype(BF), self.left.astype(BF))


def line_gather(own, m, meanwhile):
    line = m // 2
    right = left = own
    rights, lefts = [], []
    for k in range(1, line):
        right = lax.ppermute(right, "dp", [(i, i + 2) for i in range(2 * (k - 1), m - 2)])
        left = lax.ppermute(left, "dp", [(i, i - 2) for i in range(2, m - 2 * (k - 1))])
        if k in meanwhile and k < line - 1:
            right, left = lax.optimization_barrier((right, left) + meanwhile[k](right, left))[:2]
        rights.append(right)
        lefts.append(left)
    return rights, lefts


def local(
    tokens_in, ln1_gain, ln1_bias, w_qkv, w_out, scale_attn, ln2_gain, ln2_bias, w_gu, w_down,
    scale_mlp, out_cotangent, *, n, m,
):
    rows, w = tokens_in.shape
    images = rows // SEQ
    inner = w_qkv.shape[2]
    heads = inner // HD
    hidden_width = w_gu.shape[2]
    scale = HD ** (-0.5)
    line = m // 2
    hops = line - 1
    shard = D // m
    pieces = min(n, shard // LANE)
    cosines, sines = rope_tables()
    cos2 = jnp.tile(jnp.concatenate([cosines, cosines], axis=1), (images, 1))
    sin2 = jnp.tile(jnp.concatenate([-sines, sines], axis=1), (images, 1))
    wide = (rows, n * w)
    own = (rows, w)
    lanes = (rows, LANE)
    row = lambda v: v.reshape(1, D)
    V = lambda *a: [(x, False) for x in a]
    H = lambda *a: [(x, True) for x in a]

    w_j = jnp.transpose(w_qkv, (1, 0, 2))

    ahead = w // 2
    act_one, mean_one, inv_one, gu_j, cots, cot_late = call(
        functools.partial(first_norm_kernel, n), 1,
        [(wide, BF), (lanes, F32), (lanes, F32), ((2, D, hidden_width), BF, True), ((n, rows, ahead), BF),
         ((rows, w - ahead), BF)],
        [pltpu.VMEM((n,) + own, BF), pltpu.VMEM(lanes, F32)] + gather_sems(n)
        + [pltpu.VMEM((2, 256, 2, hidden_width), BF), pltpu.VMEM((2, 2, 256, hidden_width), BF),
           sems(2), sems(2)] + gather_sems(n),
        V(tokens_in, row(ln1_gain), row(ln1_bias), out_cotangent) + H(w_gu), 50,
    )
    cot_all = lax.all_gather(cot_late, "tensor", axis=1, tiled=True)
    qkv = qkv_matmul(act_one, w_j, cos2, sin2)
    mixed, attn_part = pl.pallas_call(
        attention_kernel,
        out_shape=[jax.ShapeDtypeStruct((rows, inner), BF), jax.ShapeDtypeStruct(wide, BF)],
        in_specs=[vm(), hb()],
        out_specs=[vm()] * 2,
        scratch_shapes=[pltpu.VMEM(w_out.shape, BF), pltpu.SemaphoreType.DMA],
        compiler_params=pltpu.CompilerParams(vmem_limit_bytes=48 << 20),
    )(qkv, w_out)
    tile = min(512, hidden_width)
    outs = call(
        functools.partial(second_norm_kernel, n, m, pieces), 2,
        [(own, F32), (own, F32), (wide, BF), (lanes, F32), (lanes, F32), ((rows, hidden_width), F32)]
        + [((m, rows, LANE), BF, True)] + [((rows, inner), BF, True)] * (2 * hops),
        scatter_room(n, rows, w)
        + [pltpu.VMEM(own, BF), pltpu.VMEM((n,) + own, BF), pltpu.VMEM(lanes, F32)]
        + gather_sems(n) + [sems(hops, 4)]
        + [sems(m - 1), sems(m - 1), pltpu.SemaphoreType.DMA]
        + [pltpu.VMEM(wide, BF), pltpu.VMEM((2, tile, D), BF), sems(2)],
        V(attn_part, tokens_in, row(scale_attn), row(ln2_gain), row(ln2_bias), row(scale_mlp), cot_all, cots)
        + H(mixed, w_down), 80,
    )
    attn_sum, residual, act_two, mean_two, inv_two, hidden_grad, kcot = outs[:7]
    mixed_right, mixed_left = outs[7:7 + hops], outs[7 + hops:]
    side = lambda k: lax.all_gather(k, "tensor", axis=2, tiled=True)[:, :, :shard]

    hidden, gate_grad, up_grad, kact = gate_matmul(act_two, gu_j, hidden_grad, act_one, m, pieces)
    block = (rows, hidden_width)
    gu_part, hidden_r, hidden_l = call(
        functools.partial(pair_grad_kernel, m), 3,
        [((line, 2, shard, hidden_width), BF, True), (block, BF, True), (block, BF, True)],
        [pltpu.VMEM((line, rows, shard), BF), pltpu.VMEM((line, rows, shard), BF),
         pltpu.VMEM(block, BF), pltpu.VMEM(block, BF), pltpu.VMEM((2, line, shard, rows), BF),
         pltpu.VMEM((2, 2, shard, hidden_width), BF),
         sems(line), sems(line), sems(2), sems(2), sems(line), sems(4), sems(2)],
        H(act_two) + V(gate_grad, up_grad) + H(hidden), 40,
    )
    cut = shard * 5 // 8
    tile = w // 2 if n == 4 else min(512, w)
    outs = call(
        functools.partial(second_back_kernel, n, m), 4,
        [(own, F32), (wide, BF), ((8, w), F32)] + [((2, cut, hidden_width), BF, True)] * 2
        + [(block, BF, True)] * (2 * hops - 2),
        [pltpu.VMEM(wide, BF)] + scatter_room(n, rows, w)
        + [pltpu.VMEM(own, F32), pltpu.VMEM(own, BF),
         pltpu.VMEM(lanes, F32), pltpu.VMEM(lanes, F32), pltpu.VMEM((8, rows), F32),
         pltpu.VMEM((n, 8, rows), F32)] + [sems(n - 1)] * 2 + gather_sems(n)
        + [pltpu.SemaphoreType.DMA, sems(hops - 1, 4), sems(4)]
        + [pltpu.VMEM((2, 2, tile, hidden_width), BF), sems(2)],
        V(gate_grad, up_grad, out_cotangent, residual, attn_sum, mean_two, inv_two, row(ln2_gain), row(scale_attn))
        + H(hidden_r, hidden_l, gu_part, gu_j), 80,
    )
    res_grad, attn_grad, sums_two, gu_right, gu_left = outs[:5]
    hidden_right = [hidden_r] + outs[5:4 + hops]
    hidden_left = [hidden_l] + outs[4 + hops:]
    raw_grad, kattn = call(
        functools.partial(attention_back_kernel, m, pieces), 5,
        [((3, rows, inner), BF), ((m, rows, LANE), BF, True)],
        [pltpu.VMEM((rows, inner), BF), sems(m - 1), sems(m - 1), pltpu.SemaphoreType.DMA,
         pltpu.VMEM((2, min(256, inner), D), BF), sems(2)],
        V(attn_grad, qkv, cos2, sin2) + H(attn_grad, w_out), 25,
    )
    kcot, kact, raw_grad = lax.optimization_barrier((kcot, kact, raw_grad))
    side_cot, side_attn, side_act = side(kcot), side(kattn), side(kact)
    def gathered(ident, mine, rights, lefts, sides, turned, first=0, last=hops):
        parts, _, width = mine.shape
        shape = (parts, width, shard) if turned else (parts, shard, width)
        blocks = []
        for k in range(first, last + 1):
            blocks += [rights[k - 1], lefts[k - 1]] if k else [mine]
        count = len(blocks)
        (out,) = call(
            functools.partial(gathered_grad_kernel, m, turned, first, last), ident, [(shape, F32)],
            [pltpu.VMEM((count, 2) + mine.shape, BF), pltpu.VMEM((count, 2, shard, rows), BF),
             sems(count), sems(count), sems(count)],
            H(*blocks) + V(sides), 30,
        )
        return out

    lead = lambda arrays: [a[None] for a in arrays]
    done = {}

    def after_one(right, left):
        part = back_matmul(raw_grad, w_j)
        done["grad"] = lax.psum_scatter(part, "tensor", scatter_dimension=1, tiled=True)
        done["attn"], done["hidden"] = lax.optimization_barrier(
            (side_attn, hidden, part, right, left)
        )[:2]
        ends = lax.optimization_barrier(
            (gu_part[line - 1, :, cut:], gu_part[0, :, cut:], right, left, part)
        )
        done["rest"] = (
            lax.ppermute(ends[0], "dp", [(c, 2 + c) for c in range(2)]),
            lax.ppermute(ends[1], "dp", [(m - 2 + c, m - 4 + c) for c in range(2)]),
        )
        return (part,)

    def after_two(right, left):
        done["proj"] = gathered(
            7, mixed[None], lead(mixed_right), lead(mixed_left), done["attn"], False
        )[0].T
        done["part"] = jnp.dot(done["hidden"], w_down, preferred_element_type=F32).astype(BF)
        rest = lax.optimization_barrier(done["rest"] + (done["proj"], done["part"]))
        gu_line = LineReduce(gu_part, (gu_right, rest[0]), (gu_left, rest[1]), m)
        gu_line.step((right, left))
        done["gu"] = gu_line
        late = lax.optimization_barrier((side_cot,) + gu_line.given)
        done["down"] = gathered(
            6, hidden[None], lead(hidden_right), lead(hidden_left), late[0], False
        )[0].T
        return ()

    raw_right, raw_left = line_gather(raw_grad, m, {1: after_one, 2: after_two})
    act_one_grad, down_sum = done["grad"], done["down"]
    proj_sum = done["proj"]
    branch_part = done["part"]
    qkv_part = gathered(8, raw_grad, raw_right, raw_left, side_act, False, 0, hops - 1)
    gu_sum = done["gu"].finish((raw_right[-1], raw_left[-1], down_sum, proj_sum, qkv_part))

    small = jnp.concatenate([jnp.zeros((2, w), F32), sums_two[0:3], jnp.zeros((3, w), F32)], axis=0)
    input_grad, sums, layer_out = call(
        functools.partial(first_back_kernel, n), 9,
        [(own, F32), ((8, w), F32), (own, F32)],
        scatter_room(n, rows, w)
        + [pltpu.VMEM(own, F32),
           pltpu.VMEM(lanes, F32), pltpu.VMEM(lanes, F32), pltpu.VMEM((8, rows), F32),
           pltpu.VMEM((n, 8, rows), F32)] + [sems(n - 1)] * 2,
        V(act_one_grad, tokens_in, mean_one, inv_one, row(ln1_gain), small,
          branch_part, out_cotangent, row(scale_mlp)), 20,
    )
    input_grad = res_grad + input_grad
    layer_out = residual + layer_out
    qkv_sum = qkv_part + gathered(
        10, raw_grad, raw_right, raw_left, side_act, False, hops, hops
    )
    qkv_sum, input_grad, layer_out, down_sum, proj_sum, sums = lax.optimization_barrier(
        (qkv_sum, input_grad, layer_out, down_sum, proj_sum, sums)
    )
    (small_sums,) = call(
        functools.partial(small_sums_kernel, n, m), 11, [((8, n * w), F32)],
        [pltpu.VMEM((m, 8, w), F32), pltpu.VMEM((8, w), F32)] + [sems(m - 1)] * 2 + [sems(n - 1)] * 2,
        V(sums), 10,
    )
    return (
        layer_out,
        input_grad,
        small_sums[0],
        small_sums[1],
        jnp.transpose(qkv_sum, (1, 0, 2)),
        proj_sum,
        small_sums[4],
        small_sums[2],
        small_sums[3],
        gu_sum,
        down_sum,
        small_sums[5],
    )


def solution(mesh):
    placed = (
        P("dp", "tensor"),
        P(),
        P(),
        P(None, None, "tensor"),
        P("tensor", None),
        P(),
        P(),
        P(),
        P(None, None, "tensor"),
        P("tensor", None),
        P(),
        P("dp", "tensor"),
    )
    return jax.shard_map(
        functools.partial(local, n=mesh.shape["tensor"], m=mesh.shape["dp"]),
        mesh=mesh,
        in_specs=placed,
        out_specs=(
            P("dp", "tensor"),
            P("dp", "tensor"),
            P(),
            P(),
            P("dp", None, "tensor"),
            P("tensor", "dp"),
            P(),
            P(),
            P(),
            P("dp", None, "tensor"),
            P("tensor", "dp"),
            P(),
        ),
        check_vma=False,
    )
```

```python
import functools
import math

import jax
import jax.numpy as jnp
from jax import lax
from jax.experimental import pallas as pl
from jax.experimental.pallas import tpu as pltpu
from jax.sharding import PartitionSpec as P

D = 4096
HD = 128
GRID = 14
EXTRA = 5
PATCH = 196
SEQ = 201
EPS = 1e-06
LANE = 128
BF = jnp.bfloat16
F32 = jnp.float32
MESH = pl.DeviceIdType.MESH
ROWS = (((0,), (0,)), ((), ()))
COLS = (((1,), (1,)), ((), ()))


def rope_tables():
    quarter = HD // 4
    theta = (
        2.0
        * math.pi
        * jnp.exp(jnp.arange(quarter, dtype=jnp.float32) * (-4.0 * math.log(100.0) / HD))
    )
    places = jnp.arange(PATCH, dtype=jnp.int32)
    row_pos = ((places // GRID).astype(jnp.float32) + 0.5) * (2.0 / GRID) - 1.0
    col_pos = ((places % GRID).astype(jnp.float32) + 0.5) * (2.0 / GRID) - 1.0
    angles = jnp.concatenate(
        [row_pos[:, None] * theta[None, :], col_pos[:, None] * theta[None, :]], axis=1
    )
    angles = jnp.concatenate([jnp.zeros((EXTRA, HD // 2), jnp.float32), angles], axis=0)
    return (jnp.cos(angles), jnp.sin(angles))


def rotate(vectors, cosines, sines):
    halfway = HD // 2
    leading = vectors[..., :halfway]
    trailing = vectors[..., halfway:]
    cos_b = cosines[:, None, :]
    sin_b = sines[:, None, :]
    return jnp.concatenate(
        [leading * cos_b - trailing * sin_b, leading * sin_b + trailing * cos_b], axis=-1
    )


def greet(n, m=1):
    me = lax.axis_index("tensor")
    you = lax.axis_index("dp")
    barrier = pltpu.get_barrier_semaphore()
    for k in range(1, n):
        pl.semaphore_signal(
            barrier, inc=1, device_id={"tensor": lax.rem(me + k, n)}, device_id_type=MESH
        )
    for k in range(1, m):
        pl.semaphore_signal(
            barrier, inc=1, device_id={"dp": lax.rem(you + k, m)}, device_id_type=MESH
        )
    pl.semaphore_wait(barrier, n + m - 2)


def send(src, dst, send_sem, recv_sem, peer):
    return pltpu.make_async_remote_copy(
        src_ref=src,
        dst_ref=dst,
        send_sem=send_sem,
        recv_sem=recv_sem,
        device_id={"tensor": peer},
        device_id_type=MESH,
    )


def send_dp(src, dst, send_sem, recv_sem, peer):
    return pltpu.make_async_remote_copy(
        src_ref=src,
        dst_ref=dst,
        send_sem=send_sem,
        recv_sem=recv_sem,
        device_id={"dp": peer},
        device_id_type=MESH,
    )


class Hop:
    def __init__(self, k, m, right_src, left_src, right_dst, left_dst, sem):
        you = lax.axis_index("dp")
        z, last = you // 2, m // 2 - 1
        right = send_dp(right_src, right_dst, sem.at[0], sem.at[1], lax.rem(you + 2, m))
        left = send_dp(left_src, left_dst, sem.at[2], sem.at[3], lax.rem(you + m - 2, m))
        self.steps = [
            (right, (z >= k - 1) & (z < last), z >= k),
            (left, (z <= last - k + 1) & (z > 0), z <= last - k),
        ]

    def start(self):
        for copy, sends, _ in self.steps:
            pl.when(sends)(copy.start)

    def wait(self):
        for copy, sends, gets in self.steps:
            pl.when(sends)(copy.wait_send)
            pl.when(gets)(copy.wait_recv)


class End:
    def __init__(self, m, part_ref, at, right_dst, left_dst, sem):
        you = lax.axis_index("dp")
        z, last = you // 2, m // 2 - 1
        some = pl.ds(at, right_dst.shape[1])
        right = send_dp(
            part_ref.at[last, :, some], right_dst, sem.at[0], sem.at[1], lax.rem(you + 2, m)
        )
        left = send_dp(
            part_ref.at[0, :, some], left_dst, sem.at[2], sem.at[3], lax.rem(you + m - 2, m)
        )
        self.steps = [(right, z == 0, z == 1), (left, z == last, z == last - 1)]

    start = Hop.start
    wait = Hop.wait


class Exchange:
    def __init__(self, m, pieces, full_ref, out_ref, ssem, rsem, lsem):
        you = lax.axis_index("dp")
        piece = lax.rem(lax.axis_index("tensor"), pieces)
        self.copies = []
        for k in range(m):
            peer = lax.rem(you + k, m)
            cols = pl.ds(pl.multiple_of((peer * pieces + piece) * LANE, LANE), LANE)
            if k:
                copy = send_dp(
                    full_ref.at[:, cols], out_ref.at[you], ssem.at[k - 1], rsem.at[k - 1], peer
                )
            else:
                copy = pltpu.make_async_copy(full_ref.at[:, cols], out_ref.at[you], lsem)
            self.copies.append(copy)

    def start(self):
        for copy in self.copies:
            copy.start()

    def wait(self):
        for copy in self.copies:
            copy.wait()


def chunks(width, body):
    def step(j, carry):
        body(pl.ds(pl.multiple_of(j * LANE, LANE), LANE))
        return carry

    lax.fori_loop(0, width // LANE, step, 0)


def spread(column, rows):
    return jnp.broadcast_to(column, (rows, LANE))


def beside(me):
    return me + 1 - 2 * lax.rem(me, 2), me + 2 - 4 * (me // 2)


class Gather:
    def __init__(self, n, own_ref, dest, ssem, rsem):
        me = lax.axis_index("tensor")
        w = own_ref.shape[1]
        self.square = n == 4
        if self.square:
            x, y = beside(me)
            half = w // 2
            part = lambda i: own_ref.at[:, i * half:(i + 1) * half]
            to = lambda i, src, owner, at, peer: send(
                src, dest(owner, at * half, half), ssem.at[i], rsem.at[i], peer
            )
            self.copies = [
                to(0, part(0), me, 0, x), to(1, part(1), me, 1, y),
                to(2, part(1), me, 1, x), to(3, part(0), me, 0, y),
            ]
            self.passed = [
                to(4, dest(x, 0, half), x, 0, y), to(5, dest(y, half, half), y, 1, x)
            ]
        else:
            self.copies = [
                send(own_ref, dest(me, 0, w), ssem.at[k - 1], rsem.at[k - 1], lax.rem(me + k, n))
                for k in range(1, n)
            ]

    def start(self):
        for copy in self.copies:
            copy.start()

    def relay(self):
        if self.square:
            for copy, passed in zip(self.copies, self.passed):
                copy.wait_recv()
                passed.start()

    def wait(self):
        if self.square:
            for copy in self.copies:
                copy.wait_send()
            for copy in self.copies[2:]:
                copy.wait_recv()
            wait_all(self.passed)
        else:
            wait_all(self.copies)


class Scatter:
    def __init__(self, n, w, part_ref, slots, come, go, ssem, rsem):
        me = lax.axis_index("tensor")
        self.n, self.w, self.part, self.slots, self.come, self.go = n, w, part_ref, slots, come, go
        self.square = n == 4
        cols = lambda owner, at, size: part_ref.at[:, pl.ds(pl.multiple_of(owner * w + at, LANE), size)]
        if self.square:
            x, y = beside(me)
            far = 3 - me
            half = w // 2
            self.half, self.x, self.y = half, x, y
            to = lambda i, src, dst, peer: send(src, dst, ssem.at[i], rsem.at[i], peer)
            low, high = slice(0, half), slice(half, w)
            self.first = [
                to(0, cols(far, 0, half), come.at[0], x), to(1, cols(far, half, half), come.at[1], y)
            ]
            self.second = [
                to(2, cols(x, 0, half), slots.at[0, :, low], x),
                to(3, cols(y, half, half), slots.at[1, :, high], y),
            ]
            self.third = [
                to(4, go.at[0], slots.at[0, :, high], x), to(5, go.at[1], slots.at[1, :, low], y)
            ]
            self.order = [(far, 0), (far, 1), (x, 0), (y, 1), (x, 1), (y, 0), (me, 0), (me, 1)]
        else:
            self.first = [
                send(cols(lax.rem(me + k, n), 0, w), slots.at[k - 1], ssem.at[k - 1], rsem.at[k - 1],
                     lax.rem(me + k, n))
                for k in range(1, n)
            ]
            self.second = self.third = []

    def start(self):
        for copy in self.first + self.second:
            copy.start()

    def relay(self):
        if self.square:
            half = self.half
            for i, (owner, at) in enumerate(((self.x, half), (self.y, 0))):
                self.first[1 - i].wait_recv()

                def add(cols, i=i, owner=owner, at=at):
                    wide = pl.ds(pl.multiple_of(owner * self.w + at + cols.start, LANE), LANE)
                    self.go[i, :, cols] = (
                        self.part[:, wide].astype(F32) + self.come[1 - i, :, cols].astype(F32)
                    ).astype(BF)

                chunks(half, add)
                self.third[i].start()

    def wait(self):
        if self.square:
            for copy in self.first:
                copy.wait_send()
            wait_all(self.second + self.third)
        else:
            wait_all(self.first)

    def total(self, cols, wide):
        total = self.part[:, wide].astype(F32)
        for k in range(self.slots.shape[0]):
            total = total + self.slots[k, :, cols].astype(F32)
        return total


def scatter_room(n, rows, w):
    count, half = (2, w // 2) if n == 4 else (n - 1, LANE)
    return [
        pltpu.VMEM((count, rows, w), BF), pltpu.VMEM((2, rows, half), BF), pltpu.VMEM((2, rows, half), BF),
        sems(6 if n == 4 else n - 1), sems(6 if n == 4 else n - 1),
    ]


def gather_sems(n):
    return [sems(6 if n == 4 else n - 1)] * 2


def stream(count, fetch, compute):
    fetch(0, 0).start()

    def step(i, carry):
        slot = lax.rem(i, 2)

        @pl.when(i + 1 < count)
        def _():
            fetch(i + 1, 1 - slot).start()

        fetch(i, slot).wait()
        compute(i, slot)
        return carry

    lax.fori_loop(0, count, step, 0)


def wait_all(copies):
    for copy in copies:
        copy.wait()


def row_stats(n, rows, w, all_ref, acc, mean_ref, inv_ref):
    acc[...] = jnp.zeros_like(acc)

    def add(cols):
        total = all_ref[0, :, cols].astype(F32)
        for k in range(1, n):
            total = total + all_ref[k, :, cols].astype(F32)
        acc[...] += total

    chunks(w, add)
    mean_ref[...] = spread(jnp.sum(acc[...], axis=1, keepdims=True) * (1.0 / D), rows)
    acc[...] = jnp.zeros_like(acc)

    def square(cols):
        mean = mean_ref[...]
        total = jnp.zeros_like(mean)
        for k in range(n):
            center = all_ref[k, :, cols].astype(F32) - mean
            total = total + center * center
        acc[...] += total

    chunks(w, square)
    var = jnp.sum(acc[...], axis=1, keepdims=True) * (1.0 / D)
    inv_ref[...] = spread(lax.rsqrt(var + EPS), rows)


def write_act(n, w, all_ref, mean_ref, inv_ref, gain_ref, bias_ref, act_ref):
    def act(cols):
        for k in range(n):
            wide = pl.ds(pl.multiple_of(k * w + cols.start, LANE), LANE)
            center = all_ref[k, :, cols].astype(F32) - mean_ref[...]
            act_ref[:, wide] = (
                center * inv_ref[...] * gain_ref[:, wide] + bias_ref[:, wide]
            ).astype(BF)

    chunks(w, act)


def part_rows(w_ref, out_ref, ibuf, obuf, isem, osem, also):
    size = ibuf.shape[1]
    count = w_ref.shape[0] // size

    def rows_of(i):
        return pl.ds(pl.multiple_of(i * size, size), size)

    def fetch(i, slot):
        return pltpu.make_async_copy(w_ref.at[rows_of(i)], ibuf.at[slot], isem.at[slot])

    def put(i, slot):
        return pltpu.make_async_copy(obuf.at[slot], out_ref.at[:, rows_of(i)], osem.at[slot])

    fetch(0, 0).start()

    def step(i, carry):
        slot = lax.rem(i, 2)
        also(i)

        @pl.when(i + 1 < count)
        def _():
            fetch(i + 1, 1 - slot).start()

        fetch(i, slot).wait()

        @pl.when(i >= 2)
        def _():
            put(i - 2, slot).wait()

        obuf[slot] = jnp.swapaxes(ibuf[slot], 0, 1)
        put(i, slot).start()
        return carry

    lax.fori_loop(0, count, step, 0)
    for i in (count - 2, count - 1):
        put(i, i % 2).wait()


def first_norm_kernel(
    n, x_ref, gain_ref, bias_ref, cot_ref, w_ref, act_ref, mean_ref, inv_ref, parted_ref, cots_ref, late_ref,
    all_ref, acc, ssem, rsem, ibuf, obuf, isem, osem, csem, crem,
):
    rows, w = x_ref.shape
    me = lax.axis_index("tensor")
    greet(n)
    dest = lambda owner, at, size: all_ref.at[owner, :, pl.ds(at, size)]
    gather = Gather(n, x_ref, dest, ssem, rsem)
    gather.start()
    all_ref[me] = x_ref[...]
    early_ref = cot_ref.at[:, :cots_ref.shape[2]]
    into = lambda owner, at, size: cots_ref.at[owner, :, pl.ds(at, size)]
    early = Gather(n, early_ref, into, csem, crem)

    def between(i):
        @pl.when(i == 6)
        def _():
            gather.relay()
            early.start()

    cots_ref[me] = early_ref[...]
    late_ref[...] = cot_ref[:, cots_ref.shape[2]:]
    part_rows(w_ref, parted_ref, ibuf, obuf, isem, osem, between)
    gather.wait()
    row_stats(n, rows, w, all_ref, acc, mean_ref, inv_ref)
    early.relay()
    write_act(n, w, all_ref, mean_ref, inv_ref, gain_ref, bias_ref, act_ref)
    early.wait()


def second_norm_kernel(
    n, m, pieces, part_ref, x_ref, scale_ref, gain_ref, bias_ref, mlp_ref, cot_ref, cots_ref, mixed_ref,
    w_down_ref, attn_ref, res_ref, act_ref, mean_ref, inv_ref, hgrad_ref, kcot_ref, *refs,
):
    hops = m // 2 - 1
    rights, lefts, refs = refs[:hops], refs[hops:2 * hops], refs[2 * hops:]
    (slots, come, go, ssem, rsem, own_ref, all_ref, acc, ssem2, rsem2, hsem,
     css, crs, cls, bgrad, wbuf, wsem) = refs
    rows, w = x_ref.shape
    me = lax.axis_index("tensor")
    greet(n, m)
    scatter = Scatter(n, w, part_ref, slots, come, go, ssem, rsem)
    scatter.start()
    line = [
        Hop(k, m, rights[k - 2] if k > 1 else mixed_ref, lefts[k - 2] if k > 1 else mixed_ref,
            rights[k - 1], lefts[k - 1], hsem.at[k - 1])
        for k in range(1, hops + 1)
    ]
    line[0].start()

    ahead = cots_ref.shape[2]
    for owner in range(n):

        def early(cols, owner=owner):
            wide = pl.ds(pl.multiple_of(owner * w + cols.start, LANE), LANE)
            bgrad[:, wide] = (mlp_ref[:, wide] * cots_ref[owner, :, cols].astype(F32)).astype(BF)

        def late(cols, owner=owner):
            wide = pl.ds(pl.multiple_of(owner * w + ahead + cols.start, LANE), LANE)
            from_ = pl.ds(pl.multiple_of(owner * (w - ahead) + cols.start, LANE), LANE)
            bgrad[:, wide] = (mlp_ref[:, wide] * cot_ref[:, from_].astype(F32)).astype(BF)

        chunks(ahead, early)
        chunks(w - ahead, late)
    side = Exchange(m, pieces, bgrad, kcot_ref, css, crs, cls)
    side.start()
    tile = wbuf.shape[1]
    count = hgrad_ref.shape[1] // tile

    def fetch(i, slot):
        return pltpu.make_async_copy(
            w_down_ref.at[pl.ds(pl.multiple_of(i * tile, tile), tile), :], wbuf.at[slot], wsem.at[slot]
        )

    def compute(i, slot):
        hgrad_ref[:, pl.ds(pl.multiple_of(i * tile, tile), tile)] = lax.dot_general(
            bgrad[...], wbuf[slot], COLS, preferred_element_type=F32
        )

        @pl.when(i == count // 2)
        def _():
            scatter.relay()

    stream(count, fetch, compute)
    line[0].wait()
    if hops > 1:
        line[1].start()
    scatter.wait()

    def add(cols):
        wide = pl.ds(pl.multiple_of(me * w + cols.start, LANE), LANE)
        total = scatter.total(cols, wide)
        attn_ref[:, cols] = total
        res = x_ref[:, cols].astype(F32) + scale_ref[:, wide] * total
        res_ref[:, cols] = res
        own_ref[:, cols] = res.astype(BF)

    chunks(w, add)
    dest = lambda owner, at, size: all_ref.at[owner, :, pl.ds(at, size)]
    gather = Gather(n, own_ref, dest, ssem2, rsem2)
    gather.start()
    all_ref[me] = own_ref[...]
    gather.relay()
    for k in range(1, hops - 1):
        line[k].wait()
        line[k + 1].start()
    gather.wait()
    row_stats(n, rows, w, all_ref, acc, mean_ref, inv_ref)
    write_act(n, w, all_ref, mean_ref, inv_ref, gain_ref, bias_ref, act_ref)
    line[-1].wait()
    side.wait()


def norm_back(n, w, load_total, grad_ref, base_ref, mean_ref, inv_ref, gain_ref,
              sums, acc, acc2, stat_own, stats, ssem, rsem, out):
    rows = grad_ref.shape[0]
    me = lax.axis_index("tensor")
    acc[...] = jnp.zeros_like(acc)
    acc2[...] = jnp.zeros_like(acc2)

    def first(cols):
        wide = pl.ds(pl.multiple_of(me * w + cols.start, LANE), LANE)
        total = load_total(cols, wide)
        grad_ref[:, cols] = total
        normed = (base_ref[:, cols].astype(F32) - mean_ref[...]) * inv_ref[...]
        sums[0:1, cols] = jnp.sum(total * normed, axis=0, keepdims=True)
        sums[1:2, cols] = jnp.sum(total, axis=0, keepdims=True)
        scaled = total * gain_ref[:, wide]
        acc[...] += scaled
        acc2[...] += scaled * normed

    chunks(w, first)
    ones = jnp.ones((8, LANE), F32)
    high = lax.Precision.HIGHEST
    plain = lax.dot_general(ones, acc[...], COLS, precision=high, preferred_element_type=F32)
    cross = lax.dot_general(ones, acc2[...], COLS, precision=high, preferred_element_type=F32)
    line = lax.broadcasted_iota(jnp.int32, (8, rows), 0)
    stat_own[...] = jnp.where(line < 4, plain, cross)
    copies = [
        send(stat_own, stats.at[me], ssem.at[k - 1], rsem.at[k - 1], lax.rem(me + k, n))
        for k in range(1, n)
    ]
    for copy in copies:
        copy.start()
    wait_all(copies)
    both = stat_own[...]
    for k in range(1, n):
        both = both + stats[lax.rem(me + k, n)]
    both = both * (1.0 / D)
    pick = lax.broadcasted_iota(jnp.int32, (8, LANE), 0)
    acc[...] = lax.dot_general(
        both, (pick == 0).astype(F32), ROWS, precision=high, preferred_element_type=F32
    )
    acc2[...] = lax.dot_general(
        both, (pick == 4).astype(F32), ROWS, precision=high, preferred_element_type=F32
    )

    def second(cols):
        wide = pl.ds(pl.multiple_of(me * w + cols.start, LANE), LANE)
        normed = (base_ref[:, cols].astype(F32) - mean_ref[...]) * inv_ref[...]
        scaled = grad_ref[:, cols] * gain_ref[:, wide]
        out(cols, wide, inv_ref[...] * (scaled - acc[...] - normed * acc2[...]))

    chunks(w, second)


def second_back_kernel(
    n, m, gate_ref, up_ref, cot_ref, res_ref, attn_ref, mean_ref, inv_ref, gain_ref, scale_ref,
    right_ref, left_ref, gu_ref, w_ref, rgrad_ref, agrad_ref, sums_ref, gu_right, gu_left, *refs,
):
    hops = m // 2 - 1
    rights = (right_ref,) + refs[:hops - 1]
    lefts = (left_ref,) + refs[hops - 1:2 * hops - 2]
    (part_ref, slots, come, go, ssem, rsem, grad_ref, own_ref, acc, acc2, stat_own, stats,
     ssem2, rsem2, ssem3, rsem3, lsem, hsem, gsem, wbuf, wsem) = refs[2 * hops - 2:]
    w = cot_ref.shape[1]
    me = lax.axis_index("tensor")
    greet(n, m)
    line = [
        Hop(k, m, rights[k - 2], lefts[k - 2], rights[k - 1], lefts[k - 1], hsem.at[k - 2])
        for k in range(2, hops + 1)
    ]
    line[0].start()
    first = End(m, gu_ref, 0, gu_right, gu_left, gsem)
    first.start()
    scatter = Scatter(n, w, part_ref, slots, come, go, ssem, rsem)
    tile = wbuf.shape[2]
    count = D // tile

    def spot(i):
        if not scatter.square:
            return pl.ds(pl.multiple_of(i * tile, LANE), tile)
        at = 0
        for k, (owner, half) in enumerate(scatter.order):
            at = at + jnp.where(i == k, owner * w + half * tile, 0)
        return pl.ds(pl.multiple_of(at, LANE), tile)

    def fetch(i, slot):
        return pltpu.make_async_copy(w_ref.at[:, spot(i), :], wbuf.at[slot], wsem.at[slot])

    def compute(i, slot):
        part_ref[:, spot(i)] = (
            lax.dot_general(gate_ref[...], wbuf[slot, 0], COLS, preferred_element_type=F32)
            + lax.dot_general(up_ref[...], wbuf[slot, 1], COLS, preferred_element_type=F32)
        ).astype(BF)
        if scatter.square:
            for k, copy in enumerate(scatter.first + scatter.second):
                pl.when(i == k)(copy.start)
            pl.when(i == 5)(scatter.relay)

    stream(count, fetch, compute)
    if not scatter.square:
        scatter.start()
    scatter.wait()
    line[0].wait()
    for hop in line[1:2]:
        hop.start()
    sums_ref[...] = jnp.zeros_like(sums_ref)

    def out(cols, wide, back):
        res_grad = cot_ref[:, cols].astype(F32) + back
        rgrad_ref[:, cols] = res_grad
        sums_ref[2:3, cols] = jnp.sum(res_grad * attn_ref[:, cols], axis=0, keepdims=True)
        own_ref[:, cols] = (scale_ref[:, wide] * res_grad).astype(BF)

    norm_back(n, w, scatter.total, grad_ref, res_ref, mean_ref, inv_ref, gain_ref,
              sums_ref, acc, acc2, stat_own, stats, ssem2, rsem2, out)
    dest = lambda owner, at, size: agrad_ref.at[:, pl.ds(pl.multiple_of(owner * w + at, LANE), size)]
    gather = Gather(n, own_ref, dest, ssem3, rsem3)
    gather.start()
    local = pltpu.make_async_copy(own_ref, dest(me, 0, w), lsem)
    local.start()
    gather.relay()
    for k in range(1, len(line)):
        line[k].wait()
        if k + 1 < len(line):
            line[k + 1].start()
    local.wait()
    gather.wait()
    first.wait()


def first_back_kernel(
    n, grad_in, x_ref, mean_ref, inv_ref, gain_ref, small_ref,
    part_ref, cot_ref, scale_ref,
    igrad_ref, sums, out_ref,
    slots, come, go, ssem, rsem, grad_ref, acc, acc2, stat_own, stats, ssem2, rsem2,
):
    w = x_ref.shape[1]
    greet(n)
    scatter = Scatter(n, w, part_ref, slots, come, go, ssem, rsem)
    scatter.start()
    sums[...] = small_ref[...]
    scatter.relay()

    def load_total(cols, wide):
        return grad_in[:, cols].astype(F32)

    def out(cols, wide, back):
        igrad_ref[:, cols] = back

    norm_back(n, w, load_total, grad_ref, x_ref, mean_ref, inv_ref, gain_ref,
              sums, acc, acc2, stat_own, stats, ssem2, rsem2, out)
    scatter.wait()
    me = lax.axis_index("tensor")

    def add(cols):
        wide = pl.ds(pl.multiple_of(me * w + cols.start, LANE), LANE)
        total = scatter.total(cols, wide)
        out_ref[:, cols] = scale_ref[:, wide] * total
        sums[5:6, cols] = jnp.sum(cot_ref[:, cols].astype(F32) * total, axis=0, keepdims=True)

    chunks(w, add)


def mate_of(you):
    return you + 1 - 2 * lax.rem(you, 2)


def pair_grad_kernel(
    m, act_ref, gate_ref, up_ref, hidden_ref, out_ref, right_ref, left_ref,
    acts, mates, gates, ups, flip, obuf, asem, arem, gsem, grem, lsem, hsem, osem,
):
    line = m // 2
    you = lax.axis_index("dp")
    core, mate = lax.rem(you, 2), mate_of(you)
    width = acts.shape[-1]
    tile = 512
    greet(1, m)
    hop = Hop(1, m, hidden_ref, hidden_ref, right_ref, left_ref, hsem)
    copies = [
        send_dp(gate_ref, gates, gsem.at[0], grem.at[0], mate),
        send_dp(up_ref, ups, gsem.at[1], grem.at[1], mate),
    ]
    locals_ = []
    for k in range(line):
        theirs = pl.ds(pl.multiple_of((2 * k + 1 - core) * width, LANE), width)
        ours = pl.ds(pl.multiple_of((2 * k + core) * width, LANE), width)
        copies.append(send_dp(act_ref.at[:, theirs], mates.at[k], asem.at[k], arem.at[k], mate))
        locals_.append(pltpu.make_async_copy(act_ref.at[:, ours], acts.at[k], lsem.at[k]))
    for copy in locals_ + copies:
        copy.start()
    hop.start()
    for copy in locals_:
        copy.wait()

    def turn(which, source):
        def step(k, carry):
            flip[which, k] = source[k].T
            return carry

        lax.fori_loop(0, line, step, 0)

    turn(0, acts)
    for copy in copies:
        copy.wait()
    turn(1, mates)
    def put(k):
        slot = lax.rem(k, 2)
        return pltpu.make_async_copy(obuf.at[slot], out_ref.at[k], osem.at[slot])

    def chip(k, carry):
        slot = lax.rem(k, 2)

        @pl.when(k >= 2)
        def _():
            put(k - 2).wait()

        for j, (near, far) in enumerate(((gate_ref, gates), (up_ref, ups))):

            def step(i, carry, j=j, near=near, far=far):
                cols = pl.ds(pl.multiple_of(i * tile, tile), tile)
                obuf[slot, j, :, cols] = (
                    jnp.dot(flip[0, k], near[:, cols], preferred_element_type=F32)
                    + jnp.dot(flip[1, k], far[:, cols], preferred_element_type=F32)
                ).astype(BF)
                return carry

            lax.fori_loop(0, gate_ref.shape[1] // tile, step, 0)
        put(k).start()
        return carry

    lax.fori_loop(0, line, chip, 0)
    for k in range(max(line - 2, 0), line):
        put(k).wait()
    hop.wait()


class SmallSums:
    def __init__(self, n, m, sums, out, parts, total, dss, drs, tss, trs):
        self.out, self.sums, self.parts, self.total = out, sums, parts, total
        me, you = lax.axis_index("tensor"), lax.axis_index("dp")
        w = sums.shape[1]
        self.m, self.you = m, you
        self.mine = pl.ds(pl.multiple_of(me * w, w), w)
        self.dp = [
            send_dp(sums, parts.at[you], dss.at[k - 1], drs.at[k - 1], lax.rem(you + k, m))
            for k in range(1, m)
        ]
        self.tensor = [
            send(total, out.at[:, self.mine], tss.at[k - 1], trs.at[k - 1], lax.rem(me + k, n))
            for k in range(1, n)
        ]

    def start(self):
        for copy in self.dp:
            copy.start()

    def finish(self):
        self.parts[self.you] = self.sums[...]
        wait_all(self.dp)
        total = self.parts[0]
        for k in range(1, self.m):
            total = total + self.parts[k]
        self.total[...] = total
        for copy in self.tensor:
            copy.start()
        self.out[:, self.mine] = total
        wait_all(self.tensor)


def small_sums_kernel(n, m, sums, out_ref, parts, total, *room):
    greet(n, m)
    small = SmallSums(n, m, sums, out_ref, parts, total, *room)
    small.start()
    small.finish()


def gathered_grad_kernel(m, turned, first, last, *refs):
    hops = m // 2 - 1
    you = lax.axis_index("dp")
    core, mate, z = lax.rem(you, 2), mate_of(you), you // 2
    todo = []
    refs = list(refs)
    for k in range(first, last + 1):
        if k == 0:
            todo.append((None, refs.pop(0), z))
        else:
            todo.append((z >= k, refs.pop(0), z - k))
            todo.append((z <= hops - k, refs.pop(0), z + k))
    side_ref = refs.pop(0)
    out_ref, blocks, flip, lsem, ssem, rsem = refs
    greet(1, m)
    copies = []
    for at, (cond, src, chip) in enumerate(todo):
        near = pltpu.make_async_copy(src, blocks.at[at, core], lsem.at[at])
        far = send_dp(src, blocks.at[at, core], ssem.at[at], rsem.at[at], mate)
        copies.append((cond, near, far))

    def when(cond, body):
        body() if cond is None else pl.when(cond)(body)

    def go(near, far):
        near.start()
        far.start()

    def done(near, far):
        near.wait()
        far.wait()

    def unit_of(at):
        k = (at + 1) // 2 if first == 0 else first
        right = lax.rem(at, 2) == (1 if first == 0 else 0)
        there = (k == 0) | (right & (z >= k)) | (jnp.logical_not(right) & (z <= hops - k))
        return there, jnp.where(right, z - k, z + k)

    def turn(i, carry):
        at, c = i // 2, lax.rem(i, 2)
        there, chip = unit_of(at)

        @pl.when(there)
        def _():
            flip[at, c] = side_ref[2 * chip + c].T

        return carry

    for cond, near, far in copies:
        when(cond, functools.partial(go, near, far))
    lax.fori_loop(0, 2 * len(todo), turn, 0)
    for cond, near, far in copies:
        when(cond, functools.partial(done, near, far))
    tile = 512
    parts, width = out_ref.shape[0], blocks.shape[-1]
    count = width // tile
    out_ref[...] = jnp.zeros_like(out_ref)

    def unit(i, carry):
        at, j, at_col = i // (parts * count), lax.rem(i // count, parts), lax.rem(i, count)
        there, _ = unit_of(at)

        @pl.when(there)
        def _():
            cols = pl.ds(pl.multiple_of(at_col * tile, tile), tile)
            total = jnp.dot(
                flip[at, 0], blocks[at, 0, j, :, cols], preferred_element_type=F32
            ) + jnp.dot(flip[at, 1], blocks[at, 1, j, :, cols], preferred_element_type=F32)
            if turned:
                out_ref[j, cols, :] += total.T
            else:
                out_ref[j, :, cols] += total

        return carry

    lax.fori_loop(0, len(todo) * parts * count, unit, 0)


def qkv_kernel(act_ref, w_ref, cos_ref, sin_ref, out_ref):
    raw = jnp.dot(act_ref[...], w_ref[...], preferred_element_type=F32)
    part = pl.program_id(0)

    @pl.when(part < 2)
    def _():
        for h in range(raw.shape[1] // HD):
            cols = slice(h * HD, (h + 1) * HD)
            t = raw[:, cols]
            out_ref[:, cols] = (
                t * cos_ref[...] + pltpu.roll(t, HD // 2, 1) * sin_ref[...]
            ).astype(BF)

    @pl.when(part == 2)
    def _():
        out_ref[...] = raw.astype(BF)


def qkv_matmul(act, w_j, cos2, sin2):
    rows = act.shape[0]
    inner = w_j.shape[2]
    tile = min(512, inner)
    return pl.pallas_call(
        qkv_kernel,
        grid=(3, inner // tile),
        out_shape=jax.ShapeDtypeStruct((3, rows, inner), BF),
        in_specs=[
            pl.BlockSpec((rows, D), lambda j, i: (0, 0)),
            pl.BlockSpec((None, D, tile), lambda j, i: (j, 0, i)),
            pl.BlockSpec((rows, HD), lambda j, i: (0, 0)),
            pl.BlockSpec((rows, HD), lambda j, i: (0, 0)),
        ],
        out_specs=pl.BlockSpec((None, rows, tile), lambda j, i: (j, 0, i)),
        compiler_params=pltpu.CompilerParams(vmem_limit_bytes=40 << 20),
        cost_estimate=pl.CostEstimate(
            flops=2 * rows * D * 3 * inner, bytes_accessed=6 * D * inner, transcendentals=0
        ),
    )(pltpu.with_memory_space_constraint(act, pltpu.HBM), w_j, cos2, sin2)


def attention_probs(q, k, same):
    scores = lax.dot_general(k, q, COLS, preferred_element_type=F32) * (HD ** (-0.5))
    scores = jnp.where(same, scores, -jnp.inf)
    top = jnp.max(scores, axis=0, keepdims=True)
    weight = jnp.exp(scores - top)
    return weight / jnp.sum(weight, axis=0, keepdims=True)


def same_image(rows):
    one = lax.broadcasted_iota(jnp.int32, (rows, rows), 0)
    two = lax.broadcasted_iota(jnp.int32, (rows, rows), 1)
    image = lambda i: sum((i >= SEQ * k).astype(jnp.int32) for k in range(1, rows // SEQ))
    return image(one) == image(two)


def attention_kernel(qkv_ref, w_hbm, mixed_ref, part_ref, w_ref, wsem):
    rows, inner = mixed_ref.shape
    weights = pltpu.make_async_copy(w_hbm, w_ref, wsem)
    weights.start()

    def head(h, carry):
        cols = pl.ds(pl.multiple_of(h * HD, HD), HD)
        probs = attention_probs(qkv_ref[0, :, cols], qkv_ref[1, :, cols], same_image(rows))
        value = qkv_ref[2, :, cols].astype(F32).T.astype(BF)
        mixed = jnp.dot(value, probs.astype(BF), preferred_element_type=F32)
        mixed_ref[:, cols] = mixed.T.astype(BF)
        return carry

    lax.fori_loop(0, inner // HD, head, 0)
    weights.wait()

    def tile(i, carry):
        cols = pl.ds(pl.multiple_of(i * 512, 512), 512)
        part_ref[:, cols] = jnp.dot(
            mixed_ref[...], w_ref[:, cols], preferred_element_type=F32
        ).astype(BF)
        return carry

    lax.fori_loop(0, D // 512, tile, 0)


def attention_back_kernel(
    m, pieces, agrad_ref, qkv_ref, cos_ref, sin_ref, full_ref, w_ref,
    out_ref, kattn_ref, mgrad, ass, ars, als, wbuf, wsem,
):
    rows, inner = mgrad.shape
    greet(1, m)
    side = Exchange(m, pieces, full_ref, kattn_ref, ass, ars, als)
    side.start()
    step = min(256, inner)

    def fetch(i, slot):
        some = pl.ds(pl.multiple_of(i * step, step), step)
        return pltpu.make_async_copy(w_ref.at[some, :], wbuf.at[slot], wsem.at[slot])

    def tile(i, slot):
        cols = pl.ds(pl.multiple_of(i * step, step), step)
        mgrad[:, cols] = lax.dot_general(
            agrad_ref[...], wbuf[slot], COLS, preferred_element_type=F32
        ).astype(BF)

    stream(inner // step, fetch, tile)

    def back(t):
        return t * cos_ref[...] - pltpu.roll(t, HD // 2, 1) * sin_ref[...]

    def head(h, carry):
        cols = pl.ds(pl.multiple_of(h * HD, HD), HD)
        q, k, v = qkv_ref[0, :, cols], qkv_ref[1, :, cols], qkv_ref[2, :, cols]
        grad = mgrad[:, cols]
        probs = attention_probs(q, k, same_image(rows))
        prob_grad = lax.dot_general(v, grad, COLS, preferred_element_type=F32)
        delta = jnp.sum(probs * prob_grad, axis=0, keepdims=True)
        score_grad = (probs * (prob_grad - delta)).astype(BF)
        scale = HD ** (-0.5)
        flipped = k.astype(F32).T.astype(BF)
        q_grad = jnp.dot(flipped, score_grad, preferred_element_type=F32).T * scale
        k_grad = jnp.dot(score_grad, q, preferred_element_type=F32) * scale
        out_ref[0, :, cols] = back(q_grad).astype(BF)
        out_ref[1, :, cols] = back(k_grad).astype(BF)
        out_ref[2, :, cols] = jnp.dot(
            probs.astype(BF), grad, preferred_element_type=F32
        ).astype(BF)
        return carry

    lax.fori_loop(0, inner // HD, head, 0)
    side.wait()


def gate_kernel(
    m, pieces, act_ref, w_ref, hgrad_ref, full_ref, hidden_ref, gate_ref, up_ref, kact_ref, ass, ars, als
):
    side = Exchange(m, pieces, full_ref, kact_ref, ass, ars, als)

    @pl.when(pl.program_id(0) == 0)
    def _():
        greet(1, m)
        side.start()

    gate = jnp.dot(act_ref[...], w_ref[0], preferred_element_type=F32)
    up = jnp.dot(act_ref[...], w_ref[1], preferred_element_type=F32)
    sig = jax.nn.sigmoid(gate)
    grad = hgrad_ref[...]
    hidden_ref[...] = (gate * sig * up).astype(BF)
    gate_ref[...] = (grad * up * sig * (1.0 + gate * (1.0 - sig))).astype(BF)
    up_ref[...] = (grad * gate * sig).astype(BF)
    pl.when(pl.program_id(0) == pl.num_programs(0) - 1)(side.wait)


def gate_matmul(act, w_j, hidden_grad, act_one, m, pieces):
    rows, width = hidden_grad.shape
    tile = min(256, width)
    block = pl.BlockSpec((rows, tile), lambda i: (0, i))
    return pl.pallas_call(
        functools.partial(gate_kernel, m, pieces),
        grid=(width // tile,),
        out_shape=[pltpu.HBM((rows, width), BF)] * 3 + [jax.ShapeDtypeStruct((m, rows, LANE), BF)],
        in_specs=[
            pl.BlockSpec((rows, D), lambda i: (0, 0)),
            pl.BlockSpec((2, D, tile), lambda i: (0, 0, i)),
            block,
            hb(),
        ],
        out_specs=[block] * 3 + [hb()],
        scratch_shapes=[sems(m - 1), sems(m - 1), pltpu.SemaphoreType.DMA],
        compiler_params=pltpu.CompilerParams(
            collective_id=12, has_side_effects=True, vmem_limit_bytes=48 << 20
        ),
    )(pltpu.with_memory_space_constraint(act, pltpu.HBM), w_j, hidden_grad, act_one)


def back_kernel(g_ref, w_ref, out_ref):
    total = None
    for j in range(g_ref.shape[0]):
        term = lax.dot_general(g_ref[j], w_ref[j], COLS, preferred_element_type=F32)
        total = term if total is None else total + term
    out_ref[...] = total.astype(BF)


def back_matmul(grads, w_j):
    parts, rows, inner = grads.shape
    tile = 512
    return pl.pallas_call(
        back_kernel,
        grid=(D // tile,),
        out_shape=jax.ShapeDtypeStruct((rows, D), BF),
        in_specs=[
            pl.BlockSpec((parts, rows, inner), lambda i: (0, 0, 0)),
            pl.BlockSpec((parts, tile, inner), lambda i: (0, i, 0)),
        ],
        out_specs=pl.BlockSpec((rows, tile), lambda i: (0, i)),
        compiler_params=pltpu.CompilerParams(vmem_limit_bytes=40 << 20),
        cost_estimate=pl.CostEstimate(
            flops=rows * D * parts * inner * 100 // 500,
            bytes_accessed=800_000,
            transcendentals=0,
        ),
    )(grads, w_j)


def vm():
    return pl.BlockSpec(memory_space=pltpu.VMEM)


def hb():
    return pl.BlockSpec(memory_space=pltpu.HBM)


def sems(*shape):
    return pltpu.SemaphoreType.DMA(shape)


def call(kernel, ident, outs, scratch, args, micros=30):
    shapes = [jax.ShapeDtypeStruct(o[0], o[1]) for o in outs]
    return list(pl.pallas_call(
        kernel,
        out_shape=shapes,
        in_specs=[hb() if a[1] else vm() for a in args],
        out_specs=[hb() if len(o) > 2 else vm() for o in outs],
        scratch_shapes=scratch,
        compiler_params=pltpu.CompilerParams(
            collective_id=ident, has_side_effects=True, vmem_limit_bytes=56 << 20
        ),
        cost_estimate=pl.CostEstimate(
            flops=micros * 100_000_000, bytes_accessed=800_000, transcendentals=0
        ),
    )(*[a[0] for a in args]))


def join_kernel(one, two, three, out_ref):
    total = one[...].astype(F32) + two[...].astype(F32) + three[...].astype(F32)
    out_ref[...] = jnp.swapaxes(total, 0, 1)


def join(one, two, three):
    _, rows, width = one.shape
    size = 64
    block = pl.BlockSpec((2, size, width), lambda i: (0, i, 0))
    return pl.pallas_call(
        join_kernel,
        grid=(rows // size,),
        out_shape=jax.ShapeDtypeStruct((rows, 2, width), F32),
        in_specs=[block] * 3,
        out_specs=pl.BlockSpec((size, 2, width), lambda i: (i, 0, 0)),
        compiler_params=pltpu.CompilerParams(vmem_limit_bytes=32 << 20),
    )(*[pltpu.with_memory_space_constraint(v, pltpu.HBM) for v in (one, two, three)])


class LineReduce:
    def __init__(self, part, right, left, m):
        self.part, self.line, self.t = part, m // 2, 2
        self.z = lax.axis_index("dp") // 2
        right, left = (jnp.concatenate(pieces, axis=1).astype(F32) for pieces in (right, left))
        self.right = jnp.where(self.z >= 1, right, 0.0)
        self.left = jnp.where(self.z <= self.line - 2, left, 0.0)

    def take(self, i):
        i = jnp.clip(i, 0, self.line - 1)
        return lax.dynamic_index_in_dim(self.part, i, 0, keepdims=False).astype(F32)

    def step(self, after):
        line, t = self.line, self.t
        right = (self.take(self.z + line - t) + self.right).astype(BF)
        left = (self.take(self.z - line + t) + self.left).astype(BF)
        right, left = lax.optimization_barrier((right, left) + tuple(after))[:2]
        self.given = right, left
        self.right = lax.ppermute(
            right, "dp", [(2 * i + c, 2 * i + 2 + c) for i in range(t) for c in range(2)]
        ).astype(F32)
        self.left = lax.ppermute(
            left, "dp",
            [(2 * i + c, 2 * i - 2 + c) for i in range(line - t, line) for c in range(2)],
        ).astype(F32)
        self.t += 1

    def finish(self, after):
        while self.t < self.line:
            self.step(after)
        own = lax.dynamic_index_in_dim(self.part, self.z, 0, keepdims=False)
        return join(own, self.right.astype(BF), self.left.astype(BF))


def line_gather(own, m, meanwhile):
    line = m // 2
    right = left = own
    rights, lefts = [], []
    for k in range(1, line):
        right = lax.ppermute(right, "dp", [(i, i + 2) for i in range(2 * (k - 1), m - 2)])
        left = lax.ppermute(left, "dp", [(i, i - 2) for i in range(2, m - 2 * (k - 1))])
        if k in meanwhile and k < line - 1:
            right, left = lax.optimization_barrier((right, left) + meanwhile[k](right, left))[:2]
        rights.append(right)
        lefts.append(left)
    return rights, lefts


def local(
    tokens_in, ln1_gain, ln1_bias, w_qkv, w_out, scale_attn, ln2_gain, ln2_bias, w_gu, w_down,
    scale_mlp, out_cotangent, *, n, m,
):
    rows, w = tokens_in.shape
    images = rows // SEQ
    inner = w_qkv.shape[2]
    heads = inner // HD
    hidden_width = w_gu.shape[2]
    scale = HD ** (-0.5)
    line = m // 2
    hops = line - 1
    shard = D // m
    pieces = min(n, shard // LANE)
    cosines, sines = rope_tables()
    cos2 = jnp.tile(jnp.concatenate([cosines, cosines], axis=1), (images, 1))
    sin2 = jnp.tile(jnp.concatenate([-sines, sines], axis=1), (images, 1))
    wide = (rows, n * w)
    own = (rows, w)
    lanes = (rows, LANE)
    row = lambda v: v.reshape(1, D)
    V = lambda *a: [(x, False) for x in a]
    H = lambda *a: [(x, True) for x in a]

    w_j = jnp.transpose(w_qkv, (1, 0, 2))

    ahead = w // 2
    act_one, mean_one, inv_one, gu_j, cots, cot_late = call(
        functools.partial(first_norm_kernel, n), 1,
        [(wide, BF), (lanes, F32), (lanes, F32), ((2, D, hidden_width), BF, True), ((n, rows, ahead), BF),
         ((rows, w - ahead), BF)],
        [pltpu.VMEM((n,) + own, BF), pltpu.VMEM(lanes, F32)] + gather_sems(n)
        + [pltpu.VMEM((2, 256, 2, hidden_width), BF), pltpu.VMEM((2, 2, 256, hidden_width), BF),
           sems(2), sems(2)] + gather_sems(n),
        V(tokens_in, row(ln1_gain), row(ln1_bias), out_cotangent) + H(w_gu), 50,
    )
    cot_all = lax.all_gather(cot_late, "tensor", axis=1, tiled=True)
    qkv = qkv_matmul(act_one, w_j, cos2, sin2)
    mixed, attn_part = pl.pallas_call(
        attention_kernel,
        out_shape=[jax.ShapeDtypeStruct((rows, inner), BF), jax.ShapeDtypeStruct(wide, BF)],
        in_specs=[vm(), hb()],
        out_specs=[vm()] * 2,
        scratch_shapes=[pltpu.VMEM(w_out.shape, BF), pltpu.SemaphoreType.DMA],
        compiler_params=pltpu.CompilerParams(vmem_limit_bytes=48 << 20),
    )(qkv, w_out)
    tile = min(512, hidden_width)
    outs = call(
        functools.partial(second_norm_kernel, n, m, pieces), 2,
        [(own, F32), (own, F32), (wide, BF), (lanes, F32), (lanes, F32), ((rows, hidden_width), F32)]
        + [((m, rows, LANE), BF, True)] + [((rows, inner), BF, True)] * (2 * hops),
        scatter_room(n, rows, w)
        + [pltpu.VMEM(own, BF), pltpu.VMEM((n,) + own, BF), pltpu.VMEM(lanes, F32)]
        + gather_sems(n) + [sems(hops, 4)]
        + [sems(m - 1), sems(m - 1), pltpu.SemaphoreType.DMA]
        + [pltpu.VMEM(wide, BF), pltpu.VMEM((2, tile, D), BF), sems(2)],
        V(attn_part, tokens_in, row(scale_attn), row(ln2_gain), row(ln2_bias), row(scale_mlp), cot_all, cots)
        + H(mixed, w_down), 80,
    )
    attn_sum, residual, act_two, mean_two, inv_two, hidden_grad, kcot = outs[:7]
    mixed_right, mixed_left = outs[7:7 + hops], outs[7 + hops:]
    side = lambda k: lax.all_gather(k, "tensor", axis=2, tiled=True)[:, :, :shard]

    hidden, gate_grad, up_grad, kact = gate_matmul(act_two, gu_j, hidden_grad, act_one, m, pieces)
    block = (rows, hidden_width)
    gu_part, hidden_r, hidden_l = call(
        functools.partial(pair_grad_kernel, m), 3,
        [((line, 2, shard, hidden_width), BF, True), (block, BF, True), (block, BF, True)],
        [pltpu.VMEM((line, rows, shard), BF), pltpu.VMEM((line, rows, shard), BF),
         pltpu.VMEM(block, BF), pltpu.VMEM(block, BF), pltpu.VMEM((2, line, shard, rows), BF),
         pltpu.VMEM((2, 2, shard, hidden_width), BF),
         sems(line), sems(line), sems(2), sems(2), sems(line), sems(4), sems(2)],
        H(act_two) + V(gate_grad, up_grad) + H(hidden), 40,
    )
    cut = shard * 5 // 8
    tile = w // 2 if n == 4 else min(512, w)
    outs = call(
        functools.partial(second_back_kernel, n, m), 4,
        [(own, F32), (wide, BF), ((8, w), F32)] + [((2, cut, hidden_width), BF, True)] * 2
        + [(block, BF, True)] * (2 * hops - 2),
        [pltpu.VMEM(wide, BF)] + scatter_room(n, rows, w)
        + [pltpu.VMEM(own, F32), pltpu.VMEM(own, BF),
         pltpu.VMEM(lanes, F32), pltpu.VMEM(lanes, F32), pltpu.VMEM((8, rows), F32),
         pltpu.VMEM((n, 8, rows), F32)] + [sems(n - 1)] * 2 + gather_sems(n)
        + [pltpu.SemaphoreType.DMA, sems(hops - 1, 4), sems(4)]
        + [pltpu.VMEM((2, 2, tile, hidden_width), BF), sems(2)],
        V(gate_grad, up_grad, out_cotangent, residual, attn_sum, mean_two, inv_two, row(ln2_gain), row(scale_attn))
        + H(hidden_r, hidden_l, gu_part, gu_j), 80,
    )
    res_grad, attn_grad, sums_two, gu_right, gu_left = outs[:5]
    hidden_right = [hidden_r] + outs[5:4 + hops]
    hidden_left = [hidden_l] + outs[4 + hops:]
    raw_grad, kattn = call(
        functools.partial(attention_back_kernel, m, pieces), 5,
        [((3, rows, inner), BF), ((m, rows, LANE), BF, True)],
        [pltpu.VMEM((rows, inner), BF), sems(m - 1), sems(m - 1), pltpu.SemaphoreType.DMA,
         pltpu.VMEM((2, min(256, inner), D), BF), sems(2)],
        V(attn_grad, qkv, cos2, sin2) + H(attn_grad, w_out), 25,
    )
    kcot, kact, raw_grad = lax.optimization_barrier((kcot, kact, raw_grad))
    side_cot, side_attn, side_act = side(kcot), side(kattn), side(kact)
    def gathered(ident, mine, rights, lefts, sides, turned, first=0, last=hops):
        parts, _, width = mine.shape
        shape = (parts, width, shard) if turned else (parts, shard, width)
        blocks = []
        for k in range(first, last + 1):
            blocks += [rights[k - 1], lefts[k - 1]] if k else [mine]
        count = len(blocks)
        (out,) = call(
            functools.partial(gathered_grad_kernel, m, turned, first, last), ident, [(shape, F32)],
            [pltpu.VMEM((count, 2) + mine.shape, BF), pltpu.VMEM((count, 2, shard, rows), BF),
             sems(count), sems(count), sems(count)],
            H(*blocks) + V(sides), 30,
        )
        return out

    lead = lambda arrays: [a[None] for a in arrays]
    done = {}

    def after_one(right, left):
        part = back_matmul(raw_grad, w_j)
        done["grad"] = lax.psum_scatter(part, "tensor", scatter_dimension=1, tiled=True)
        done["attn"], done["hidden"] = lax.optimization_barrier(
            (side_attn, hidden, part, right, left)
        )[:2]
        ends = lax.optimization_barrier(
            (gu_part[line - 1, :, cut:], gu_part[0, :, cut:], right, left, part)
        )
        done["rest"] = (
            lax.ppermute(ends[0], "dp", [(c, 2 + c) for c in range(2)]),
            lax.ppermute(ends[1], "dp", [(m - 2 + c, m - 4 + c) for c in range(2)]),
        )
        return (part,)

    def after_two(right, left):
        done["proj"] = gathered(
            7, mixed[None], lead(mixed_right), lead(mixed_left), done["attn"], False
        )[0].T
        done["part"] = jnp.dot(done["hidden"], w_down, preferred_element_type=F32).astype(BF)
        rest = lax.optimization_barrier(done["rest"] + (done["proj"], done["part"]))
        gu_line = LineReduce(gu_part, (gu_right, rest[0]), (gu_left, rest[1]), m)
        gu_line.step((right, left))
        done["gu"] = gu_line
        late = lax.optimization_barrier((side_cot,) + gu_line.given)
        done["down"] = gathered(
            6, hidden[None], lead(hidden_right), lead(hidden_left), late[0], False
        )[0].T
        return ()

    raw_right, raw_left = line_gather(raw_grad, m, {1: after_one, 2: after_two})
    act_one_grad, down_sum = done["grad"], done["down"]
    proj_sum = done["proj"]
    branch_part = done["part"]
    qkv_part = gathered(8, raw_grad, raw_right, raw_left, side_act, False, 0, hops - 1)
    gu_sum = done["gu"].finish((raw_right[-1], raw_left[-1], down_sum, proj_sum, qkv_part))

    small = jnp.concatenate([jnp.zeros((2, w), F32), sums_two[0:3], jnp.zeros((3, w), F32)], axis=0)
    input_grad, sums, layer_out = call(
        functools.partial(first_back_kernel, n), 9,
        [(own, F32), ((8, w), F32), (own, F32)],
        scatter_room(n, rows, w)
        + [pltpu.VMEM(own, F32),
           pltpu.VMEM(lanes, F32), pltpu.VMEM(lanes, F32), pltpu.VMEM((8, rows), F32),
           pltpu.VMEM((n, 8, rows), F32)] + [sems(n - 1)] * 2,
        V(act_one_grad, tokens_in, mean_one, inv_one, row(ln1_gain), small,
          branch_part, out_cotangent, row(scale_mlp)), 20,
    )
    input_grad = res_grad + input_grad
    layer_out = residual + layer_out
    qkv_sum = qkv_part + gathered(
        10, raw_grad, raw_right, raw_left, side_act, False, hops, hops
    )
    qkv_sum, input_grad, layer_out, down_sum, proj_sum, sums = lax.optimization_barrier(
        (qkv_sum, input_grad, layer_out, down_sum, proj_sum, sums)
    )
    (small_sums,) = call(
        functools.partial(small_sums_kernel, n, m), 11, [((8, n * w), F32)],
        [pltpu.VMEM((m, 8, w), F32), pltpu.VMEM((8, w), F32)] + [sems(m - 1)] * 2 + [sems(n - 1)] * 2,
        V(sums), 10,
    )
    return (
        layer_out,
        input_grad,
        small_sums[0],
        small_sums[1],
        jnp.transpose(qkv_sum, (1, 0, 2)),
        proj_sum,
        small_sums[4],
        small_sums[2],
        small_sums[3],
        gu_sum,
        down_sum,
        small_sums[5],
    )


def solution(mesh):
    placed = (
        P("dp", "tensor"),
        P(),
        P(),
        P(None, None, "tensor"),
        P("tensor", None),
        P(),
        P(),
        P(),
        P(None, None, "tensor"),
        P("tensor", None),
        P(),
        P("dp", "tensor"),
    )
    return jax.shard_map(
        functools.partial(local, n=mesh.shape["tensor"], m=mesh.shape["dp"]),
        mesh=mesh,
        in_specs=placed,
        out_specs=(
            P("dp", "tensor"),
            P("dp", "tensor"),
            P(),
            P(),
            P("dp", None, "tensor"),
            P("tensor", "dp"),
            P(),
            P(),
            P(),
            P("dp", None, "tensor"),
            P("tensor", "dp"),
            P(),
        ),
        check_vma=False,
    )
```

```python
import functools
import math

import jax
import jax.numpy as jnp
from jax import lax
from jax.experimental import pallas as pl
from jax.experimental.pallas import tpu as pltpu
from jax.sharding import PartitionSpec as P

D = 4096
HD = 128
GRID = 14
EXTRA = 5
PATCH = 196
SEQ = 201
EPS = 1e-06
LANE = 128
BF = jnp.bfloat16
F32 = jnp.float32
MESH = pl.DeviceIdType.MESH
ROWS = (((0,), (0,)), ((), ()))
COLS = (((1,), (1,)), ((), ()))


def rope_tables():
    quarter = HD // 4
    theta = (
        2.0
        * math.pi
        * jnp.exp(jnp.arange(quarter, dtype=jnp.float32) * (-4.0 * math.log(100.0) / HD))
    )
    places = jnp.arange(PATCH, dtype=jnp.int32)
    row_pos = ((places // GRID).astype(jnp.float32) + 0.5) * (2.0 / GRID) - 1.0
    col_pos = ((places % GRID).astype(jnp.float32) + 0.5) * (2.0 / GRID) - 1.0
    angles = jnp.concatenate(
        [row_pos[:, None] * theta[None, :], col_pos[:, None] * theta[None, :]], axis=1
    )
    angles = jnp.concatenate([jnp.zeros((EXTRA, HD // 2), jnp.float32), angles], axis=0)
    return (jnp.cos(angles), jnp.sin(angles))


def rotate(vectors, cosines, sines):
    halfway = HD // 2
    leading = vectors[..., :halfway]
    trailing = vectors[..., halfway:]
    cos_b = cosines[:, None, :]
    sin_b = sines[:, None, :]
    return jnp.concatenate(
        [leading * cos_b - trailing * sin_b, leading * sin_b + trailing * cos_b], axis=-1
    )


def greet(n, m=1):
    me = lax.axis_index("tensor")
    you = lax.axis_index("dp")
    barrier = pltpu.get_barrier_semaphore()
    for k in range(1, n):
        pl.semaphore_signal(
            barrier, inc=1, device_id={"tensor": lax.rem(me + k, n)}, device_id_type=MESH
        )
    for k in range(1, m):
        pl.semaphore_signal(
            barrier, inc=1, device_id={"dp": lax.rem(you + k, m)}, device_id_type=MESH
        )
    pl.semaphore_wait(barrier, n + m - 2)


def send(src, dst, send_sem, recv_sem, peer):
    return pltpu.make_async_remote_copy(
        src_ref=src,
        dst_ref=dst,
        send_sem=send_sem,
        recv_sem=recv_sem,
        device_id={"tensor": peer},
        device_id_type=MESH,
    )


def send_dp(src, dst, send_sem, recv_sem, peer):
    return pltpu.make_async_remote_copy(
        src_ref=src,
        dst_ref=dst,
        send_sem=send_sem,
        recv_sem=recv_sem,
        device_id={"dp": peer},
        device_id_type=MESH,
    )


class Hop:
    def __init__(self, k, m, right_src, left_src, right_dst, left_dst, sem):
        you = lax.axis_index("dp")
        z, last = you // 2, m // 2 - 1
        right = send_dp(right_src, right_dst, sem.at[0], sem.at[1], lax.rem(you + 2, m))
        left = send_dp(left_src, left_dst, sem.at[2], sem.at[3], lax.rem(you + m - 2, m))
        self.steps = [
            (right, (z >= k - 1) & (z < last), z >= k),
            (left, (z <= last - k + 1) & (z > 0), z <= last - k),
        ]

    def start(self):
        for copy, sends, _ in self.steps:
            pl.when(sends)(copy.start)

    def wait(self):
        for copy, sends, gets in self.steps:
            pl.when(sends)(copy.wait_send)
            pl.when(gets)(copy.wait_recv)


class End:
    def __init__(self, m, part_ref, at, right_dst, left_dst, sem):
        you = lax.axis_index("dp")
        z, last = you // 2, m // 2 - 1
        some = pl.ds(at, right_dst.shape[1])
        right = send_dp(
            part_ref.at[last, :, some], right_dst, sem.at[0], sem.at[1], lax.rem(you + 2, m)
        )
        left = send_dp(
            part_ref.at[0, :, some], left_dst, sem.at[2], sem.at[3], lax.rem(you + m - 2, m)
        )
        self.steps = [(right, z == 0, z == 1), (left, z == last, z == last - 1)]

    start = Hop.start
    wait = Hop.wait


class Exchange:
    def __init__(self, m, pieces, full_ref, out_ref, ssem, rsem, lsem):
        you = lax.axis_index("dp")
        piece = lax.rem(lax.axis_index("tensor"), pieces)
        self.copies = []
        for k in range(m):
            peer = lax.rem(you + k, m)
            cols = pl.ds(pl.multiple_of((peer * pieces + piece) * LANE, LANE), LANE)
            if k:
                copy = send_dp(
                    full_ref.at[:, cols], out_ref.at[you], ssem.at[k - 1], rsem.at[k - 1], peer
                )
            else:
                copy = pltpu.make_async_copy(full_ref.at[:, cols], out_ref.at[you], lsem)
            self.copies.append(copy)

    def start(self):
        for copy in self.copies:
            copy.start()

    def wait(self):
        for copy in self.copies:
            copy.wait()


def chunks(width, body):
    def step(j, carry):
        body(pl.ds(pl.multiple_of(j * LANE, LANE), LANE))
        return carry

    lax.fori_loop(0, width // LANE, step, 0)


def spread(column, rows):
    return jnp.broadcast_to(column, (rows, LANE))


def beside(me):
    return me + 1 - 2 * lax.rem(me, 2), me + 2 - 4 * (me // 2)


class Gather:
    def __init__(self, n, own_ref, dest, ssem, rsem):
        me = lax.axis_index("tensor")
        w = own_ref.shape[1]
        self.square = n == 4
        if self.square:
            x, y = beside(me)
            half = w // 2
            part = lambda i: own_ref.at[:, i * half:(i + 1) * half]
            to = lambda i, src, owner, at, peer: send(
                src, dest(owner, at * half, half), ssem.at[i], rsem.at[i], peer
            )
            self.copies = [
                to(0, part(0), me, 0, x), to(1, part(1), me, 1, y),
                to(2, part(1), me, 1, x), to(3, part(0), me, 0, y),
            ]
            self.passed = [
                to(4, dest(x, 0, half), x, 0, y), to(5, dest(y, half, half), y, 1, x)
            ]
        else:
            self.copies = [
                send(own_ref, dest(me, 0, w), ssem.at[k - 1], rsem.at[k - 1], lax.rem(me + k, n))
                for k in range(1, n)
            ]

    def start(self):
        for copy in self.copies:
            copy.start()

    def relay(self):
        if self.square:
            for copy, passed in zip(self.copies, self.passed):
                copy.wait_recv()
                passed.start()

    def wait(self):
        if self.square:
            for copy in self.copies:
                copy.wait_send()
            for copy in self.copies[2:]:
                copy.wait_recv()
            wait_all(self.passed)
        else:
            wait_all(self.copies)


class Scatter:
    def __init__(self, n, w, part_ref, slots, come, go, ssem, rsem):
        me = lax.axis_index("tensor")
        self.n, self.w, self.part, self.slots, self.come, self.go = n, w, part_ref, slots, come, go
        self.square = n == 4
        cols = lambda owner, at, size: part_ref.at[:, pl.ds(pl.multiple_of(owner * w + at, LANE), size)]
        if self.square:
            x, y = beside(me)
            far = 3 - me
            half = w // 2
            self.half, self.x, self.y = half, x, y
            to = lambda i, src, dst, peer: send(src, dst, ssem.at[i], rsem.at[i], peer)
            low, high = slice(0, half), slice(half, w)
            self.first = [
                to(0, cols(far, 0, half), come.at[0], x), to(1, cols(far, half, half), come.at[1], y)
            ]
            self.second = [
                to(2, cols(x, 0, half), slots.at[0, :, low], x),
                to(3, cols(y, half, half), slots.at[1, :, high], y),
            ]
            self.third = [
                to(4, go.at[0], slots.at[0, :, high], x), to(5, go.at[1], slots.at[1, :, low], y)
            ]
            self.order = [(far, 0), (far, 1), (x, 0), (y, 1), (x, 1), (y, 0), (me, 0), (me, 1)]
        else:
            self.first = [
                send(cols(lax.rem(me + k, n), 0, w), slots.at[k - 1], ssem.at[k - 1], rsem.at[k - 1],
                     lax.rem(me + k, n))
                for k in range(1, n)
            ]
            self.second = self.third = []

    def start(self):
        for copy in self.first + self.second:
            copy.start()

    def relay(self):
        if self.square:
            half = self.half
            for i, (owner, at) in enumerate(((self.x, half), (self.y, 0))):
                self.first[1 - i].wait_recv()

                def add(cols, i=i, owner=owner, at=at):
                    wide = pl.ds(pl.multiple_of(owner * self.w + at + cols.start, LANE), LANE)
                    self.go[i, :, cols] = (
                        self.part[:, wide].astype(F32) + self.come[1 - i, :, cols].astype(F32)
                    ).astype(BF)

                chunks(half, add)
                self.third[i].start()

    def wait(self):
        if self.square:
            for copy in self.first:
                copy.wait_send()
            wait_all(self.second + self.third)
        else:
            wait_all(self.first)

    def total(self, cols, wide):
        total = self.part[:, wide].astype(F32)
        for k in range(self.slots.shape[0]):
            total = total + self.slots[k, :, cols].astype(F32)
        return total


def scatter_room(n, rows, w):
    count, half = (2, w // 2) if n == 4 else (n - 1, LANE)
    return [
        pltpu.VMEM((count, rows, w), BF), pltpu.VMEM((2, rows, half), BF), pltpu.VMEM((2, rows, half), BF),
        sems(6 if n == 4 else n - 1), sems(6 if n == 4 else n - 1),
    ]


def gather_sems(n):
    return [sems(6 if n == 4 else n - 1)] * 2


def stream(count, fetch, compute):
    fetch(0, 0).start()

    def step(i, carry):
        slot = lax.rem(i, 2)

        @pl.when(i + 1 < count)
        def _():
            fetch(i + 1, 1 - slot).start()

        fetch(i, slot).wait()
        compute(i, slot)
        return carry

    lax.fori_loop(0, count, step, 0)


def wait_all(copies):
    for copy in copies:
        copy.wait()


def row_stats(n, rows, w, all_ref, acc, mean_ref, inv_ref):
    acc[...] = jnp.zeros_like(acc)

    def add(cols):
        total = all_ref[0, :, cols].astype(F32)
        for k in range(1, n):
            total = total + all_ref[k, :, cols].astype(F32)
        acc[...] += total

    chunks(w, add)
    mean_ref[...] = spread(jnp.sum(acc[...], axis=1, keepdims=True) * (1.0 / D), rows)
    acc[...] = jnp.zeros_like(acc)

    def square(cols):
        mean = mean_ref[...]
        total = jnp.zeros_like(mean)
        for k in range(n):
            center = all_ref[k, :, cols].astype(F32) - mean
            total = total + center * center
        acc[...] += total

    chunks(w, square)
    var = jnp.sum(acc[...], axis=1, keepdims=True) * (1.0 / D)
    inv_ref[...] = spread(lax.rsqrt(var + EPS), rows)


def write_act(n, w, all_ref, mean_ref, inv_ref, gain_ref, bias_ref, act_ref):
    def act(cols):
        for k in range(n):
            wide = pl.ds(pl.multiple_of(k * w + cols.start, LANE), LANE)
            center = all_ref[k, :, cols].astype(F32) - mean_ref[...]
            act_ref[:, wide] = (
                center * inv_ref[...] * gain_ref[:, wide] + bias_ref[:, wide]
            ).astype(BF)

    chunks(w, act)


def part_rows(w_ref, out_ref, ibuf, obuf, isem, osem, also):
    size = ibuf.shape[1]
    count = w_ref.shape[0] // size

    def rows_of(i):
        return pl.ds(pl.multiple_of(i * size, size), size)

    def fetch(i, slot):
        return pltpu.make_async_copy(w_ref.at[rows_of(i)], ibuf.at[slot], isem.at[slot])

    def put(i, slot):
        return pltpu.make_async_copy(obuf.at[slot], out_ref.at[:, rows_of(i)], osem.at[slot])

    fetch(0, 0).start()

    def step(i, carry):
        slot = lax.rem(i, 2)
        also(i)

        @pl.when(i + 1 < count)
        def _():
            fetch(i + 1, 1 - slot).start()

        fetch(i, slot).wait()

        @pl.when(i >= 2)
        def _():
            put(i - 2, slot).wait()

        obuf[slot] = jnp.swapaxes(ibuf[slot], 0, 1)
        put(i, slot).start()
        return carry

    lax.fori_loop(0, count, step, 0)
    for i in (count - 2, count - 1):
        put(i, i % 2).wait()


def first_norm_kernel(
    n, x_ref, gain_ref, bias_ref, cot_ref, w_ref, act_ref, mean_ref, inv_ref, parted_ref, cots_ref, late_ref,
    all_ref, acc, ssem, rsem, ibuf, obuf, isem, osem, csem, crem,
):
    rows, w = x_ref.shape
    me = lax.axis_index("tensor")
    greet(n)
    dest = lambda owner, at, size: all_ref.at[owner, :, pl.ds(at, size)]
    gather = Gather(n, x_ref, dest, ssem, rsem)
    gather.start()
    all_ref[me] = x_ref[...]
    early_ref = cot_ref.at[:, :cots_ref.shape[2]]
    into = lambda owner, at, size: cots_ref.at[owner, :, pl.ds(at, size)]
    early = Gather(n, early_ref, into, csem, crem)

    def between(i):
        @pl.when(i == 6)
        def _():
            gather.relay()
            early.start()

    cots_ref[me] = early_ref[...]
    late_ref[...] = cot_ref[:, cots_ref.shape[2]:]
    part_rows(w_ref, parted_ref, ibuf, obuf, isem, osem, between)
    gather.wait()
    row_stats(n, rows, w, all_ref, acc, mean_ref, inv_ref)
    early.relay()
    write_act(n, w, all_ref, mean_ref, inv_ref, gain_ref, bias_ref, act_ref)
    early.wait()


def second_norm_kernel(
    n, m, pieces, part_ref, x_ref, scale_ref, gain_ref, bias_ref, mlp_ref, cot_ref, cots_ref, mixed_ref,
    w_down_ref, attn_ref, res_ref, act_ref, mean_ref, inv_ref, hgrad_ref, kcot_ref, *refs,
):
    hops = m // 2 - 1
    rights, lefts, refs = refs[:hops], refs[hops:2 * hops], refs[2 * hops:]
    (slots, come, go, ssem, rsem, own_ref, all_ref, acc, ssem2, rsem2, hsem,
     css, crs, cls, bgrad, wbuf, wsem) = refs
    rows, w = x_ref.shape
    me = lax.axis_index("tensor")
    greet(n, m)
    scatter = Scatter(n, w, part_ref, slots, come, go, ssem, rsem)
    scatter.start()
    line = [
        Hop(k, m, rights[k - 2] if k > 1 else mixed_ref, lefts[k - 2] if k > 1 else mixed_ref,
            rights[k - 1], lefts[k - 1], hsem.at[k - 1])
        for k in range(1, hops + 1)
    ]
    line[0].start()

    ahead = cots_ref.shape[2]
    for owner in range(n):

        def early(cols, owner=owner):
            wide = pl.ds(pl.multiple_of(owner * w + cols.start, LANE), LANE)
            bgrad[:, wide] = (mlp_ref[:, wide] * cots_ref[owner, :, cols].astype(F32)).astype(BF)

        def late(cols, owner=owner):
            wide = pl.ds(pl.multiple_of(owner * w + ahead + cols.start, LANE), LANE)
            from_ = pl.ds(pl.multiple_of(owner * (w - ahead) + cols.start, LANE), LANE)
            bgrad[:, wide] = (mlp_ref[:, wide] * cot_ref[:, from_].astype(F32)).astype(BF)

        chunks(ahead, early)
        chunks(w - ahead, late)
    side = Exchange(m, pieces, bgrad, kcot_ref, css, crs, cls)
    side.start()
    tile = wbuf.shape[1]
    count = hgrad_ref.shape[1] // tile

    def fetch(i, slot):
        return pltpu.make_async_copy(
            w_down_ref.at[pl.ds(pl.multiple_of(i * tile, tile), tile), :], wbuf.at[slot], wsem.at[slot]
        )

    def compute(i, slot):
        hgrad_ref[:, pl.ds(pl.multiple_of(i * tile, tile), tile)] = lax.dot_general(
            bgrad[...], wbuf[slot], COLS, preferred_element_type=F32
        )

        @pl.when(i == count // 2)
        def _():
            scatter.relay()

    stream(count, fetch, compute)
    line[0].wait()
    if hops > 1:
        line[1].start()
    scatter.wait()

    def add(cols):
        wide = pl.ds(pl.multiple_of(me * w + cols.start, LANE), LANE)
        total = scatter.total(cols, wide)
        attn_ref[:, cols] = total
        res = x_ref[:, cols].astype(F32) + scale_ref[:, wide] * total
        res_ref[:, cols] = res
        own_ref[:, cols] = res.astype(BF)

    chunks(w, add)
    dest = lambda owner, at, size: all_ref.at[owner, :, pl.ds(at, size)]
    gather = Gather(n, own_ref, dest, ssem2, rsem2)
    gather.start()
    all_ref[me] = own_ref[...]
    gather.relay()
    for k in range(1, hops - 1):
        line[k].wait()
        line[k + 1].start()
    gather.wait()
    row_stats(n, rows, w, all_ref, acc, mean_ref, inv_ref)
    write_act(n, w, all_ref, mean_ref, inv_ref, gain_ref, bias_ref, act_ref)
    line[-1].wait()
    side.wait()


def norm_back(n, w, load_total, grad_ref, base_ref, mean_ref, inv_ref, gain_ref,
              sums, acc, acc2, stat_own, stats, ssem, rsem, out):
    rows = grad_ref.shape[0]
    me = lax.axis_index("tensor")
    acc[...] = jnp.zeros_like(acc)
    acc2[...] = jnp.zeros_like(acc2)

    def first(cols):
        wide = pl.ds(pl.multiple_of(me * w + cols.start, LANE), LANE)
        total = load_total(cols, wide)
        grad_ref[:, cols] = total
        normed = (base_ref[:, cols].astype(F32) - mean_ref[...]) * inv_ref[...]
        sums[0:1, cols] = jnp.sum(total * normed, axis=0, keepdims=True)
        sums[1:2, cols] = jnp.sum(total, axis=0, keepdims=True)
        scaled = total * gain_ref[:, wide]
        acc[...] += scaled
        acc2[...] += scaled * normed

    chunks(w, first)
    ones = jnp.ones((8, LANE), F32)
    high = lax.Precision.HIGHEST
    plain = lax.dot_general(ones, acc[...], COLS, precision=high, preferred_element_type=F32)
    cross = lax.dot_general(ones, acc2[...], COLS, precision=high, preferred_element_type=F32)
    line = lax.broadcasted_iota(jnp.int32, (8, rows), 0)
    stat_own[...] = jnp.where(line < 4, plain, cross)
    copies = [
        send(stat_own, stats.at[me], ssem.at[k - 1], rsem.at[k - 1], lax.rem(me + k, n))
        for k in range(1, n)
    ]
    for copy in copies:
        copy.start()
    wait_all(copies)
    both = stat_own[...]
    for k in range(1, n):
        both = both + stats[lax.rem(me + k, n)]
    both = both * (1.0 / D)
    pick = lax.broadcasted_iota(jnp.int32, (8, LANE), 0)
    acc[...] = lax.dot_general(
        both, (pick == 0).astype(F32), ROWS, precision=high, preferred_element_type=F32
    )
    acc2[...] = lax.dot_general(
        both, (pick == 4).astype(F32), ROWS, precision=high, preferred_element_type=F32
    )

    def second(cols):
        wide = pl.ds(pl.multiple_of(me * w + cols.start, LANE), LANE)
        normed = (base_ref[:, cols].astype(F32) - mean_ref[...]) * inv_ref[...]
        scaled = grad_ref[:, cols] * gain_ref[:, wide]
        out(cols, wide, inv_ref[...] * (scaled - acc[...] - normed * acc2[...]))

    chunks(w, second)


def second_back_kernel(
    n, m, gate_ref, up_ref, cot_ref, res_ref, attn_ref, mean_ref, inv_ref, gain_ref, scale_ref,
    right_ref, left_ref, gu_ref, w_ref, rgrad_ref, agrad_ref, sums_ref, gu_right, gu_left, *refs,
):
    hops = m // 2 - 1
    rights = (right_ref,) + refs[:hops - 1]
    lefts = (left_ref,) + refs[hops - 1:2 * hops - 2]
    (part_ref, slots, come, go, ssem, rsem, grad_ref, own_ref, acc, acc2, stat_own, stats,
     ssem2, rsem2, ssem3, rsem3, lsem, hsem, gsem, wbuf, wsem) = refs[2 * hops - 2:]
    w = cot_ref.shape[1]
    me = lax.axis_index("tensor")
    greet(n, m)
    line = [
        Hop(k, m, rights[k - 2], lefts[k - 2], rights[k - 1], lefts[k - 1], hsem.at[k - 2])
        for k in range(2, hops + 1)
    ]
    line[0].start()
    first = End(m, gu_ref, 0, gu_right, gu_left, gsem)
    first.start()
    scatter = Scatter(n, w, part_ref, slots, come, go, ssem, rsem)
    tile = wbuf.shape[2]
    count = D // tile

    def spot(i):
        if not scatter.square:
            return pl.ds(pl.multiple_of(i * tile, LANE), tile)
        at = 0
        for k, (owner, half) in enumerate(scatter.order):
            at = at + jnp.where(i == k, owner * w + half * tile, 0)
        return pl.ds(pl.multiple_of(at, LANE), tile)

    def fetch(i, slot):
        return pltpu.make_async_copy(w_ref.at[:, spot(i), :], wbuf.at[slot], wsem.at[slot])

    def compute(i, slot):
        part_ref[:, spot(i)] = (
            lax.dot_general(gate_ref[...], wbuf[slot, 0], COLS, preferred_element_type=F32)
            + lax.dot_general(up_ref[...], wbuf[slot, 1], COLS, preferred_element_type=F32)
        ).astype(BF)
        if scatter.square:
            for k, copy in enumerate(scatter.first + scatter.second):
                pl.when(i == k)(copy.start)
            pl.when(i == 5)(scatter.relay)

    stream(count, fetch, compute)
    if not scatter.square:
        scatter.start()
    scatter.wait()
    line[0].wait()
    for hop in line[1:2]:
        hop.start()
    sums_ref[...] = jnp.zeros_like(sums_ref)

    def out(cols, wide, back):
        res_grad = cot_ref[:, cols].astype(F32) + back
        rgrad_ref[:, cols] = res_grad
        sums_ref[2:3, cols] = jnp.sum(res_grad * attn_ref[:, cols], axis=0, keepdims=True)
        own_ref[:, cols] = (scale_ref[:, wide] * res_grad).astype(BF)

    norm_back(n, w, scatter.total, grad_ref, res_ref, mean_ref, inv_ref, gain_ref,
              sums_ref, acc, acc2, stat_own, stats, ssem2, rsem2, out)
    dest = lambda owner, at, size: agrad_ref.at[:, pl.ds(pl.multiple_of(owner * w + at, LANE), size)]
    gather = Gather(n, own_ref, dest, ssem3, rsem3)
    gather.start()
    local = pltpu.make_async_copy(own_ref, dest(me, 0, w), lsem)
    local.start()
    gather.relay()
    for k in range(1, len(line)):
        line[k].wait()
        if k + 1 < len(line):
            line[k + 1].start()
    local.wait()
    gather.wait()
    first.wait()


def first_back_kernel(
    n, grad_in, x_ref, mean_ref, inv_ref, gain_ref, small_ref,
    part_ref, cot_ref, scale_ref,
    igrad_ref, sums, out_ref,
    slots, come, go, ssem, rsem, grad_ref, acc, acc2, stat_own, stats, ssem2, rsem2,
):
    w = x_ref.shape[1]
    greet(n)
    scatter = Scatter(n, w, part_ref, slots, come, go, ssem, rsem)
    scatter.start()
    sums[...] = small_ref[...]
    scatter.relay()

    def load_total(cols, wide):
        return grad_in[:, cols].astype(F32)

    def out(cols, wide, back):
        igrad_ref[:, cols] = back

    norm_back(n, w, load_total, grad_ref, x_ref, mean_ref, inv_ref, gain_ref,
              sums, acc, acc2, stat_own, stats, ssem2, rsem2, out)
    scatter.wait()
    me = lax.axis_index("tensor")

    def add(cols):
        wide = pl.ds(pl.multiple_of(me * w + cols.start, LANE), LANE)
        total = scatter.total(cols, wide)
        out_ref[:, cols] = scale_ref[:, wide] * total
        sums[5:6, cols] = jnp.sum(cot_ref[:, cols].astype(F32) * total, axis=0, keepdims=True)

    chunks(w, add)


def mate_of(you):
    return you + 1 - 2 * lax.rem(you, 2)


def pair_grad_kernel(
    m, act_ref, gate_ref, up_ref, hidden_ref, out_ref, right_ref, left_ref,
    acts, mates, gates, ups, flip, obuf, asem, arem, gsem, grem, lsem, hsem, osem,
):
    line = m // 2
    you = lax.axis_index("dp")
    core, mate = lax.rem(you, 2), mate_of(you)
    width = acts.shape[-1]
    tile = 512
    greet(1, m)
    hop = Hop(1, m, hidden_ref, hidden_ref, right_ref, left_ref, hsem)
    copies = [
        send_dp(gate_ref, gates, gsem.at[0], grem.at[0], mate),
        send_dp(up_ref, ups, gsem.at[1], grem.at[1], mate),
    ]
    locals_ = []
    for k in range(line):
        theirs = pl.ds(pl.multiple_of((2 * k + 1 - core) * width, LANE), width)
        ours = pl.ds(pl.multiple_of((2 * k + core) * width, LANE), width)
        copies.append(send_dp(act_ref.at[:, theirs], mates.at[k], asem.at[k], arem.at[k], mate))
        locals_.append(pltpu.make_async_copy(act_ref.at[:, ours], acts.at[k], lsem.at[k]))
    for copy in locals_ + copies:
        copy.start()
    hop.start()
    for copy in locals_:
        copy.wait()

    def turn(which, source):
        def step(k, carry):
            flip[which, k] = source[k].T
            return carry

        lax.fori_loop(0, line, step, 0)

    turn(0, acts)
    for copy in copies:
        copy.wait()
    turn(1, mates)
    def put(k):
        slot = lax.rem(k, 2)
        return pltpu.make_async_copy(obuf.at[slot], out_ref.at[k], osem.at[slot])

    def chip(k, carry):
        slot = lax.rem(k, 2)

        @pl.when(k >= 2)
        def _():
            put(k - 2).wait()

        for j, (near, far) in enumerate(((gate_ref, gates), (up_ref, ups))):

            def step(i, carry, j=j, near=near, far=far):
                cols = pl.ds(pl.multiple_of(i * tile, tile), tile)
                obuf[slot, j, :, cols] = (
                    jnp.dot(flip[0, k], near[:, cols], preferred_element_type=F32)
                    + jnp.dot(flip[1, k], far[:, cols], preferred_element_type=F32)
                ).astype(BF)
                return carry

            lax.fori_loop(0, gate_ref.shape[1] // tile, step, 0)
        put(k).start()
        return carry

    lax.fori_loop(0, line, chip, 0)
    for k in range(max(line - 2, 0), line):
        put(k).wait()
    hop.wait()


class SmallSums:
    def __init__(self, n, m, sums, out, parts, total, dss, drs, tss, trs):
        self.out, self.sums, self.parts, self.total = out, sums, parts, total
        me, you = lax.axis_index("tensor"), lax.axis_index("dp")
        w = sums.shape[1]
        self.m, self.you = m, you
        self.mine = pl.ds(pl.multiple_of(me * w, w), w)
        self.dp = [
            send_dp(sums, parts.at[you], dss.at[k - 1], drs.at[k - 1], lax.rem(you + k, m))
            for k in range(1, m)
        ]
        self.tensor = [
            send(total, out.at[:, self.mine], tss.at[k - 1], trs.at[k - 1], lax.rem(me + k, n))
            for k in range(1, n)
        ]

    def start(self):
        for copy in self.dp:
            copy.start()

    def finish(self):
        self.parts[self.you] = self.sums[...]
        wait_all(self.dp)
        total = self.parts[0]
        for k in range(1, self.m):
            total = total + self.parts[k]
        self.total[...] = total
        for copy in self.tensor:
            copy.start()
        self.out[:, self.mine] = total
        wait_all(self.tensor)


def small_sums_kernel(n, m, sums, out_ref, parts, total, *room):
    greet(n, m)
    small = SmallSums(n, m, sums, out_ref, parts, total, *room)
    small.start()
    small.finish()


def gathered_grad_kernel(m, turned, first, last, *refs):
    hops = m // 2 - 1
    you = lax.axis_index("dp")
    core, mate, z = lax.rem(you, 2), mate_of(you), you // 2
    todo = []
    refs = list(refs)
    for k in range(first, last + 1):
        if k == 0:
            todo.append((None, refs.pop(0), z))
        else:
            todo.append((z >= k, refs.pop(0), z - k))
            todo.append((z <= hops - k, refs.pop(0), z + k))
    side_ref = refs.pop(0)
    out_ref, blocks, flip, lsem, ssem, rsem = refs
    greet(1, m)
    copies = []
    for at, (cond, src, chip) in enumerate(todo):
        near = pltpu.make_async_copy(src, blocks.at[at, core], lsem.at[at])
        far = send_dp(src, blocks.at[at, core], ssem.at[at], rsem.at[at], mate)
        copies.append((cond, near, far))

    def when(cond, body):
        body() if cond is None else pl.when(cond)(body)

    def go(near, far):
        near.start()
        far.start()

    def done(near, far):
        near.wait()
        far.wait()

    def unit_of(at):
        k = (at + 1) // 2 if first == 0 else first
        right = lax.rem(at, 2) == (1 if first == 0 else 0)
        there = (k == 0) | (right & (z >= k)) | (jnp.logical_not(right) & (z <= hops - k))
        return there, jnp.where(right, z - k, z + k)

    def turn(i, carry):
        at, c = i // 2, lax.rem(i, 2)
        there, chip = unit_of(at)

        @pl.when(there)
        def _():
            flip[at, c] = side_ref[2 * chip + c].T

        return carry

    for cond, near, far in copies:
        when(cond, functools.partial(go, near, far))
    lax.fori_loop(0, 2 * len(todo), turn, 0)
    for cond, near, far in copies:
        when(cond, functools.partial(done, near, far))
    tile = 512
    parts, width = out_ref.shape[0], blocks.shape[-1]
    count = width // tile
    out_ref[...] = jnp.zeros_like(out_ref)

    def unit(i, carry):
        at, j, at_col = i // (parts * count), lax.rem(i // count, parts), lax.rem(i, count)
        there, _ = unit_of(at)

        @pl.when(there)
        def _():
            cols = pl.ds(pl.multiple_of(at_col * tile, tile), tile)
            total = jnp.dot(
                flip[at, 0], blocks[at, 0, j, :, cols], preferred_element_type=F32
            ) + jnp.dot(flip[at, 1], blocks[at, 1, j, :, cols], preferred_element_type=F32)
            if turned:
                out_ref[j, cols, :] += total.T
            else:
                out_ref[j, :, cols] += total

        return carry

    lax.fori_loop(0, len(todo) * parts * count, unit, 0)


def qkv_kernel(act_ref, w_ref, cos_ref, sin_ref, out_ref):
    raw = jnp.dot(act_ref[...], w_ref[...], preferred_element_type=F32)
    part = pl.program_id(0)

    @pl.when(part < 2)
    def _():
        for h in range(raw.shape[1] // HD):
            cols = slice(h * HD, (h + 1) * HD)
            t = raw[:, cols]
            out_ref[:, cols] = (
                t * cos_ref[...] + pltpu.roll(t, HD // 2, 1) * sin_ref[...]
            ).astype(BF)

    @pl.when(part == 2)
    def _():
        out_ref[...] = raw.astype(BF)


def qkv_matmul(act, w_j, cos2, sin2):
    rows = act.shape[0]
    inner = w_j.shape[2]
    tile = min(512, inner)
    return pl.pallas_call(
        qkv_kernel,
        grid=(3, inner // tile),
        out_shape=jax.ShapeDtypeStruct((3, rows, inner), BF),
        in_specs=[
            pl.BlockSpec((rows, D), lambda j, i: (0, 0)),
            pl.BlockSpec((None, D, tile), lambda j, i: (j, 0, i)),
            pl.BlockSpec((rows, HD), lambda j, i: (0, 0)),
            pl.BlockSpec((rows, HD), lambda j, i: (0, 0)),
        ],
        out_specs=pl.BlockSpec((None, rows, tile), lambda j, i: (j, 0, i)),
        compiler_params=pltpu.CompilerParams(vmem_limit_bytes=40 << 20),
        cost_estimate=pl.CostEstimate(
            flops=2 * rows * D * 3 * inner, bytes_accessed=6 * D * inner, transcendentals=0
        ),
    )(pltpu.with_memory_space_constraint(act, pltpu.HBM), w_j, cos2, sin2)


def attention_probs(q, k, same):
    scores = lax.dot_general(k, q, COLS, preferred_element_type=F32) * (HD ** (-0.5))
    scores = jnp.where(same, scores, -jnp.inf)
    top = jnp.max(scores, axis=0, keepdims=True)
    weight = jnp.exp(scores - top)
    return weight / jnp.sum(weight, axis=0, keepdims=True)


def same_image(rows):
    one = lax.broadcasted_iota(jnp.int32, (rows, rows), 0)
    two = lax.broadcasted_iota(jnp.int32, (rows, rows), 1)
    image = lambda i: sum((i >= SEQ * k).astype(jnp.int32) for k in range(1, rows // SEQ))
    return image(one) == image(two)


def attention_kernel(qkv_ref, w_hbm, mixed_ref, part_ref, w_ref, wsem):
    rows, inner = mixed_ref.shape
    weights = pltpu.make_async_copy(w_hbm, w_ref, wsem)
    weights.start()

    def head(h, carry):
        cols = pl.ds(pl.multiple_of(h * HD, HD), HD)
        probs = attention_probs(qkv_ref[0, :, cols], qkv_ref[1, :, cols], same_image(rows))
        value = qkv_ref[2, :, cols].astype(F32).T.astype(BF)
        mixed = jnp.dot(value, probs.astype(BF), preferred_element_type=F32)
        mixed_ref[:, cols] = mixed.T.astype(BF)
        return carry

    lax.fori_loop(0, inner // HD, head, 0)
    weights.wait()

    def tile(i, carry):
        cols = pl.ds(pl.multiple_of(i * 512, 512), 512)
        part_ref[:, cols] = jnp.dot(
            mixed_ref[...], w_ref[:, cols], preferred_element_type=F32
        ).astype(BF)
        return carry

    lax.fori_loop(0, D // 512, tile, 0)


def attention_back_kernel(
    m, pieces, agrad_ref, qkv_ref, cos_ref, sin_ref, full_ref, w_ref,
    out_ref, kattn_ref, mgrad, ass, ars, als, wbuf, wsem,
):
    rows, inner = mgrad.shape
    greet(1, m)
    side = Exchange(m, pieces, full_ref, kattn_ref, ass, ars, als)
    side.start()
    step = min(256, inner)

    def fetch(i, slot):
        some = pl.ds(pl.multiple_of(i * step, step), step)
        return pltpu.make_async_copy(w_ref.at[some, :], wbuf.at[slot], wsem.at[slot])

    def tile(i, slot):
        cols = pl.ds(pl.multiple_of(i * step, step), step)
        mgrad[:, cols] = lax.dot_general(
            agrad_ref[...], wbuf[slot], COLS, preferred_element_type=F32
        ).astype(BF)

    stream(inner // step, fetch, tile)

    def back(t):
        return t * cos_ref[...] - pltpu.roll(t, HD // 2, 1) * sin_ref[...]

    def head(h, carry):
        cols = pl.ds(pl.multiple_of(h * HD, HD), HD)
        q, k, v = qkv_ref[0, :, cols], qkv_ref[1, :, cols], qkv_ref[2, :, cols]
        grad = mgrad[:, cols]
        probs = attention_probs(q, k, same_image(rows))
        prob_grad = lax.dot_general(v, grad, COLS, preferred_element_type=F32)
        delta = jnp.sum(probs * prob_grad, axis=0, keepdims=True)
        score_grad = (probs * (prob_grad - delta)).astype(BF)
        scale = HD ** (-0.5)
        flipped = k.astype(F32).T.astype(BF)
        q_grad = jnp.dot(flipped, score_grad, preferred_element_type=F32).T * scale
        k_grad = jnp.dot(score_grad, q, preferred_element_type=F32) * scale
        out_ref[0, :, cols] = back(q_grad).astype(BF)
        out_ref[1, :, cols] = back(k_grad).astype(BF)
        out_ref[2, :, cols] = jnp.dot(
            probs.astype(BF), grad, preferred_element_type=F32
        ).astype(BF)
        return carry

    lax.fori_loop(0, inner // HD, head, 0)
    side.wait()


def gate_kernel(
    m, pieces, act_ref, w_ref, hgrad_ref, full_ref, hidden_ref, gate_ref, up_ref, kact_ref, ass, ars, als
):
    side = Exchange(m, pieces, full_ref, kact_ref, ass, ars, als)

    @pl.when(pl.program_id(0) == 0)
    def _():
        greet(1, m)
        side.start()

    gate = jnp.dot(act_ref[...], w_ref[0], preferred_element_type=F32)
    up = jnp.dot(act_ref[...], w_ref[1], preferred_element_type=F32)
    sig = jax.nn.sigmoid(gate)
    grad = hgrad_ref[...]
    hidden_ref[...] = (gate * sig * up).astype(BF)
    gate_ref[...] = (grad * up * sig * (1.0 + gate * (1.0 - sig))).astype(BF)
    up_ref[...] = (grad * gate * sig).astype(BF)
    pl.when(pl.program_id(0) == pl.num_programs(0) - 1)(side.wait)


def gate_matmul(act, w_j, hidden_grad, act_one, m, pieces):
    rows, width = hidden_grad.shape
    tile = min(256, width)
    block = pl.BlockSpec((rows, tile), lambda i: (0, i))
    return pl.pallas_call(
        functools.partial(gate_kernel, m, pieces),
        grid=(width // tile,),
        out_shape=[pltpu.HBM((rows, width), BF)] * 3 + [jax.ShapeDtypeStruct((m, rows, LANE), BF)],
        in_specs=[
            pl.BlockSpec((rows, D), lambda i: (0, 0)),
            pl.BlockSpec((2, D, tile), lambda i: (0, 0, i)),
            block,
            hb(),
        ],
        out_specs=[block] * 3 + [hb()],
        scratch_shapes=[sems(m - 1), sems(m - 1), pltpu.SemaphoreType.DMA],
        compiler_params=pltpu.CompilerParams(
            collective_id=12, has_side_effects=True, vmem_limit_bytes=48 << 20
        ),
    )(*[pltpu.with_memory_space_constraint(v, pltpu.HBM) for v in (act, w_j, hidden_grad)], act_one)


def back_kernel(g_ref, w_ref, out_ref):
    total = None
    for j in range(g_ref.shape[0]):
        term = lax.dot_general(g_ref[j], w_ref[j], COLS, preferred_element_type=F32)
        total = term if total is None else total + term
    out_ref[...] = total.astype(BF)


def back_matmul(grads, w_j):
    parts, rows, inner = grads.shape
    tile = 512
    return pl.pallas_call(
        back_kernel,
        grid=(D // tile,),
        out_shape=jax.ShapeDtypeStruct((rows, D), BF),
        in_specs=[
            pl.BlockSpec((parts, rows, inner), lambda i: (0, 0, 0)),
            pl.BlockSpec((parts, tile, inner), lambda i: (0, i, 0)),
        ],
        out_specs=pl.BlockSpec((rows, tile), lambda i: (0, i)),
        compiler_params=pltpu.CompilerParams(vmem_limit_bytes=40 << 20),
        cost_estimate=pl.CostEstimate(
            flops=rows * D * parts * inner * 100 // 500,
            bytes_accessed=800_000,
            transcendentals=0,
        ),
    )(grads, w_j)


def vm():
    return pl.BlockSpec(memory_space=pltpu.VMEM)


def hb():
    return pl.BlockSpec(memory_space=pltpu.HBM)


def sems(*shape):
    return pltpu.SemaphoreType.DMA(shape)


def call(kernel, ident, outs, scratch, args, micros=30):
    shapes = [jax.ShapeDtypeStruct(o[0], o[1]) for o in outs]
    return list(pl.pallas_call(
        kernel,
        out_shape=shapes,
        in_specs=[hb() if a[1] else vm() for a in args],
        out_specs=[hb() if len(o) > 2 else vm() for o in outs],
        scratch_shapes=scratch,
        compiler_params=pltpu.CompilerParams(
            collective_id=ident, has_side_effects=True, vmem_limit_bytes=56 << 20
        ),
        cost_estimate=pl.CostEstimate(
            flops=micros * 100_000_000, bytes_accessed=800_000, transcendentals=0
        ),
    )(*[a[0] for a in args]))


def join_kernel(one, two, three, out_ref):
    total = one[...].astype(F32) + two[...].astype(F32) + three[...].astype(F32)
    out_ref[...] = jnp.swapaxes(total, 0, 1)


def join(one, two, three):
    _, rows, width = one.shape
    size = 64
    block = pl.BlockSpec((2, size, width), lambda i: (0, i, 0))
    return pl.pallas_call(
        join_kernel,
        grid=(rows // size,),
        out_shape=jax.ShapeDtypeStruct((rows, 2, width), F32),
        in_specs=[block] * 3,
        out_specs=pl.BlockSpec((size, 2, width), lambda i: (i, 0, 0)),
        compiler_params=pltpu.CompilerParams(vmem_limit_bytes=32 << 20),
    )(*[pltpu.with_memory_space_constraint(v, pltpu.HBM) for v in (one, two, three)])


class LineReduce:
    def __init__(self, part, right, left, m):
        self.part, self.line, self.t = part, m // 2, 2
        self.z = lax.axis_index("dp") // 2
        right, left = (jnp.concatenate(pieces, axis=1).astype(F32) for pieces in (right, left))
        self.right = jnp.where(self.z >= 1, right, 0.0)
        self.left = jnp.where(self.z <= self.line - 2, left, 0.0)

    def take(self, i):
        i = jnp.clip(i, 0, self.line - 1)
        return lax.dynamic_index_in_dim(self.part, i, 0, keepdims=False).astype(F32)

    def step(self, after):
        line, t = self.line, self.t
        right = (self.take(self.z + line - t) + self.right).astype(BF)
        left = (self.take(self.z - line + t) + self.left).astype(BF)
        right, left = lax.optimization_barrier((right, left) + tuple(after))[:2]
        self.given = right, left
        self.right = lax.ppermute(
            right, "dp", [(2 * i + c, 2 * i + 2 + c) for i in range(t) for c in range(2)]
        ).astype(F32)
        self.left = lax.ppermute(
            left, "dp",
            [(2 * i + c, 2 * i - 2 + c) for i in range(line - t, line) for c in range(2)],
        ).astype(F32)
        self.t += 1

    def finish(self, after):
        while self.t < self.line:
            self.step(after)
        own = lax.dynamic_index_in_dim(self.part, self.z, 0, keepdims=False)
        return join(own, self.right.astype(BF), self.left.astype(BF))


def line_gather(own, m, meanwhile):
    line = m // 2
    right = left = own
    rights, lefts = [], []
    for k in range(1, line):
        right = lax.ppermute(right, "dp", [(i, i + 2) for i in range(2 * (k - 1), m - 2)])
        left = lax.ppermute(left, "dp", [(i, i - 2) for i in range(2, m - 2 * (k - 1))])
        if k in meanwhile and k < line - 1:
            right, left = lax.optimization_barrier((right, left) + meanwhile[k](right, left))[:2]
        rights.append(right)
        lefts.append(left)
    return rights, lefts


def local(
    tokens_in, ln1_gain, ln1_bias, w_qkv, w_out, scale_attn, ln2_gain, ln2_bias, w_gu, w_down,
    scale_mlp, out_cotangent, *, n, m,
):
    rows, w = tokens_in.shape
    images = rows // SEQ
    inner = w_qkv.shape[2]
    heads = inner // HD
    hidden_width = w_gu.shape[2]
    scale = HD ** (-0.5)
    line = m // 2
    hops = line - 1
    shard = D // m
    pieces = min(n, shard // LANE)
    cosines, sines = rope_tables()
    cos2 = jnp.tile(jnp.concatenate([cosines, cosines], axis=1), (images, 1))
    sin2 = jnp.tile(jnp.concatenate([-sines, sines], axis=1), (images, 1))
    wide = (rows, n * w)
    own = (rows, w)
    lanes = (rows, LANE)
    row = lambda v: v.reshape(1, D)
    V = lambda *a: [(x, False) for x in a]
    H = lambda *a: [(x, True) for x in a]

    w_j = jnp.transpose(w_qkv, (1, 0, 2))

    ahead = w // 2
    act_one, mean_one, inv_one, gu_j, cots, cot_late = call(
        functools.partial(first_norm_kernel, n), 1,
        [(wide, BF), (lanes, F32), (lanes, F32), ((2, D, hidden_width), BF, True), ((n, rows, ahead), BF),
         ((rows, w - ahead), BF)],
        [pltpu.VMEM((n,) + own, BF), pltpu.VMEM(lanes, F32)] + gather_sems(n)
        + [pltpu.VMEM((2, 256, 2, hidden_width), BF), pltpu.VMEM((2, 2, 256, hidden_width), BF),
           sems(2), sems(2)] + gather_sems(n),
        V(tokens_in, row(ln1_gain), row(ln1_bias), out_cotangent) + H(w_gu), 50,
    )
    cot_all = lax.all_gather(cot_late, "tensor", axis=1, tiled=True)
    qkv = qkv_matmul(act_one, w_j, cos2, sin2)
    mixed, attn_part = pl.pallas_call(
        attention_kernel,
        out_shape=[jax.ShapeDtypeStruct((rows, inner), BF), jax.ShapeDtypeStruct(wide, BF)],
        in_specs=[vm(), hb()],
        out_specs=[vm()] * 2,
        scratch_shapes=[pltpu.VMEM(w_out.shape, BF), pltpu.SemaphoreType.DMA],
        compiler_params=pltpu.CompilerParams(vmem_limit_bytes=48 << 20),
    )(qkv, w_out)
    tile = min(512, hidden_width)
    outs = call(
        functools.partial(second_norm_kernel, n, m, pieces), 2,
        [(own, F32), (own, F32), (wide, BF), (lanes, F32), (lanes, F32), ((rows, hidden_width), F32)]
        + [((m, rows, LANE), BF, True)] + [((rows, inner), BF, True)] * (2 * hops),
        scatter_room(n, rows, w)
        + [pltpu.VMEM(own, BF), pltpu.VMEM((n,) + own, BF), pltpu.VMEM(lanes, F32)]
        + gather_sems(n) + [sems(hops, 4)]
        + [sems(m - 1), sems(m - 1), pltpu.SemaphoreType.DMA]
        + [pltpu.VMEM(wide, BF), pltpu.VMEM((2, tile, D), BF), sems(2)],
        V(attn_part, tokens_in, row(scale_attn), row(ln2_gain), row(ln2_bias), row(scale_mlp), cot_all, cots)
        + H(mixed, w_down), 80,
    )
    attn_sum, residual, act_two, mean_two, inv_two, hidden_grad, kcot = outs[:7]
    mixed_right, mixed_left = outs[7:7 + hops], outs[7 + hops:]
    side = lambda k: lax.all_gather(k, "tensor", axis=2, tiled=True)[:, :, :shard]

    hidden, gate_grad, up_grad, kact = gate_matmul(act_two, gu_j, hidden_grad, act_one, m, pieces)
    block = (rows, hidden_width)
    gu_part, hidden_r, hidden_l = call(
        functools.partial(pair_grad_kernel, m), 3,
        [((line, 2, shard, hidden_width), BF, True), (block, BF, True), (block, BF, True)],
        [pltpu.VMEM((line, rows, shard), BF), pltpu.VMEM((line, rows, shard), BF),
         pltpu.VMEM(block, BF), pltpu.VMEM(block, BF), pltpu.VMEM((2, line, shard, rows), BF),
         pltpu.VMEM((2, 2, shard, hidden_width), BF),
         sems(line), sems(line), sems(2), sems(2), sems(line), sems(4), sems(2)],
        H(act_two) + V(gate_grad, up_grad) + H(hidden), 40,
    )
    cut = shard * 5 // 8
    tile = w // 2 if n == 4 else min(512, w)
    outs = call(
        functools.partial(second_back_kernel, n, m), 4,
        [(own, F32), (wide, BF), ((8, w), F32)] + [((2, cut, hidden_width), BF, True)] * 2
        + [(block, BF, True)] * (2 * hops - 2),
        [pltpu.VMEM(wide, BF)] + scatter_room(n, rows, w)
        + [pltpu.VMEM(own, F32), pltpu.VMEM(own, BF),
         pltpu.VMEM(lanes, F32), pltpu.VMEM(lanes, F32), pltpu.VMEM((8, rows), F32),
         pltpu.VMEM((n, 8, rows), F32)] + [sems(n - 1)] * 2 + gather_sems(n)
        + [pltpu.SemaphoreType.DMA, sems(hops - 1, 4), sems(4)]
        + [pltpu.VMEM((2, 2, tile, hidden_width), BF), sems(2)],
        V(gate_grad, up_grad, out_cotangent, residual, attn_sum, mean_two, inv_two, row(ln2_gain), row(scale_attn))
        + H(hidden_r, hidden_l, gu_part, gu_j), 80,
    )
    res_grad, attn_grad, sums_two, gu_right, gu_left = outs[:5]
    hidden_right = [hidden_r] + outs[5:4 + hops]
    hidden_left = [hidden_l] + outs[4 + hops:]
    raw_grad, kattn = call(
        functools.partial(attention_back_kernel, m, pieces), 5,
        [((3, rows, inner), BF), ((m, rows, LANE), BF, True)],
        [pltpu.VMEM((rows, inner), BF), sems(m - 1), sems(m - 1), pltpu.SemaphoreType.DMA,
         pltpu.VMEM((2, min(256, inner), D), BF), sems(2)],
        V(attn_grad, qkv, cos2, sin2) + H(attn_grad, w_out), 25,
    )
    kcot, kact, raw_grad = lax.optimization_barrier((kcot, kact, raw_grad))
    side_cot, side_attn, side_act = side(kcot), side(kattn), side(kact)
    def gathered(ident, mine, rights, lefts, sides, turned, first=0, last=hops):
        parts, _, width = mine.shape
        shape = (parts, width, shard) if turned else (parts, shard, width)
        blocks = []
        for k in range(first, last + 1):
            blocks += [rights[k - 1], lefts[k - 1]] if k else [mine]
        count = len(blocks)
        (out,) = call(
            functools.partial(gathered_grad_kernel, m, turned, first, last), ident, [(shape, F32)],
            [pltpu.VMEM((count, 2) + mine.shape, BF), pltpu.VMEM((count, 2, shard, rows), BF),
             sems(count), sems(count), sems(count)],
            H(*blocks) + V(sides), 30,
        )
        return out

    lead = lambda arrays: [a[None] for a in arrays]
    done = {}

    def after_one(right, left):
        part = back_matmul(raw_grad, w_j)
        done["grad"] = lax.psum_scatter(part, "tensor", scatter_dimension=1, tiled=True)
        done["attn"], done["hidden"] = lax.optimization_barrier(
            (side_attn, hidden, part, right, left)
        )[:2]
        ends = lax.optimization_barrier(
            (gu_part[line - 1, :, cut:], gu_part[0, :, cut:], right, left, part)
        )
        done["rest"] = (
            lax.ppermute(ends[0], "dp", [(c, 2 + c) for c in range(2)]),
            lax.ppermute(ends[1], "dp", [(m - 2 + c, m - 4 + c) for c in range(2)]),
        )
        return (part,)

    def after_two(right, left):
        done["proj"] = gathered(
            7, mixed[None], lead(mixed_right), lead(mixed_left), done["attn"], False
        )[0].T
        done["part"] = jnp.dot(done["hidden"], w_down, preferred_element_type=F32).astype(BF)
        rest = lax.optimization_barrier(done["rest"] + (done["proj"], done["part"]))
        gu_line = LineReduce(gu_part, (gu_right, rest[0]), (gu_left, rest[1]), m)
        gu_line.step((right, left))
        done["gu"] = gu_line
        late = lax.optimization_barrier((side_cot,) + gu_line.given)
        done["down"] = gathered(
            6, hidden[None], lead(hidden_right), lead(hidden_left), late[0], False
        )[0].T
        return ()

    raw_right, raw_left = line_gather(raw_grad, m, {1: after_one, 2: after_two})
    act_one_grad, down_sum = done["grad"], done["down"]
    proj_sum = done["proj"]
    branch_part = done["part"]
    qkv_part = gathered(8, raw_grad, raw_right, raw_left, side_act, False, 0, hops - 1)
    gu_sum = done["gu"].finish((raw_right[-1], raw_left[-1], down_sum, proj_sum, qkv_part))

    small = jnp.concatenate([jnp.zeros((2, w), F32), sums_two[0:3], jnp.zeros((3, w), F32)], axis=0)
    input_grad, sums, layer_out = call(
        functools.partial(first_back_kernel, n), 9,
        [(own, F32), ((8, w), F32), (own, F32)],
        scatter_room(n, rows, w)
        + [pltpu.VMEM(own, F32),
           pltpu.VMEM(lanes, F32), pltpu.VMEM(lanes, F32), pltpu.VMEM((8, rows), F32),
           pltpu.VMEM((n, 8, rows), F32)] + [sems(n - 1)] * 2,
        V(act_one_grad, tokens_in, mean_one, inv_one, row(ln1_gain), small,
          branch_part, out_cotangent, row(scale_mlp)), 20,
    )
    input_grad = res_grad + input_grad
    layer_out = residual + layer_out
    qkv_sum = qkv_part + gathered(
        10, raw_grad, raw_right, raw_left, side_act, False, hops, hops
    )
    qkv_sum, input_grad, layer_out, down_sum, proj_sum, sums = lax.optimization_barrier(
        (qkv_sum, input_grad, layer_out, down_sum, proj_sum, sums)
    )
    (small_sums,) = call(
        functools.partial(small_sums_kernel, n, m), 11, [((8, n * w), F32)],
        [pltpu.VMEM((m, 8, w), F32), pltpu.VMEM((8, w), F32)] + [sems(m - 1)] * 2 + [sems(n - 1)] * 2,
        V(sums), 10,
    )
    return (
        layer_out,
        input_grad,
        small_sums[0],
        small_sums[1],
        jnp.transpose(qkv_sum, (1, 0, 2)),
        proj_sum,
        small_sums[4],
        small_sums[2],
        small_sums[3],
        gu_sum,
        down_sum,
        small_sums[5],
    )


def solution(mesh):
    placed = (
        P("dp", "tensor"),
        P(),
        P(),
        P(None, None, "tensor"),
        P("tensor", None),
        P(),
        P(),
        P(),
        P(None, None, "tensor"),
        P("tensor", None),
        P(),
        P("dp", "tensor"),
    )
    return jax.shard_map(
        functools.partial(local, n=mesh.shape["tensor"], m=mesh.shape["dp"]),
        mesh=mesh,
        in_specs=placed,
        out_specs=(
            P("dp", "tensor"),
            P("dp", "tensor"),
            P(),
            P(),
            P("dp", None, "tensor"),
            P("tensor", "dp"),
            P(),
            P(),
            P(),
            P("dp", None, "tensor"),
            P("tensor", "dp"),
            P(),
        ),
        check_vma=False,
    )
```
